32 devices in a mesh: dp: 8 (over z, x), mem: 4 (over y, core).
Axes of the slice: x: 2, y: 2, z: 4, core: 2. Of those that a mesh axis runs over, the one named last changes fastest.
Arguments:
- target_in: bfloat16 [16384, 512], P(('dp', 'mem')), may hold values from -6 to 6
- memory: bfloat16 [16384, 512], P(('dp', 'mem')), may hold values from -6 to 6
- out_grad: bfloat16 [16384, 512], P(('dp', 'mem')), may hold values from -6 to 6
- self_query: bfloat16 [512, 512], P(('dp', 'mem')), may hold values from -0.25 to 0.25
- self_key: bfloat16 [512, 512], P(('dp', 'mem')), may hold values from -0.25 to 0.25
- self_value: bfloat16 [512, 512], P(('dp', 'mem')), may hold values from -0.25 to 0.25
- self_out: bfloat16 [512, 512], P(('dp', 'mem')), may hold values from -0.75 to 0.75
- cross_query: bfloat16 [512, 512], P(('dp', 'mem')), may hold values from -0.25 to 0.25
- cross_key: bfloat16 [512, 512], P(('dp', 'mem')), may hold values from -0.25 to 0.25
- cross_value: bfloat16 [512, 512], P(('dp', 'mem')), may hold values from -0.25 to 0.25
- cross_out: bfloat16 [512, 512], P(('dp', 'mem')), may hold values from -0.75 to 0.75
- ffn_in: bfloat16 [512, 2048], P(('dp', 'mem')), may hold values from -0.25 to 0.25
- ffn_out: bfloat16 [2048, 512], P(('dp', 'mem')), may hold values from -0.125 to 0.125
- attn_gain: bfloat16 [512], P(('dp', 'mem')), may hold values from 0.5 to 1.5
- attn_shift: bfloat16 [512], P(('dp', 'mem')), may hold values from -3 to 3
- cross_gain: bfloat16 [512], P(('dp', 'mem')), may hold values from 0.5 to 1.5
- cross_shift: bfloat16 [512], P(('dp', 'mem')), may hold values from -3 to 3
- ffn_gain: bfloat16 [512], P(('dp', 'mem')), may hold values from 0.5 to 1.5
- ffn_shift: bfloat16 [512], P(('dp', 'mem')), may hold values from -3 to 3
- tgt_lens: int32 [8, 64], P('dp'), may hold values from 1 to 256, as said below
- src_lens: int32 [8, 64], P('dp'), may hold values from 1 to 112, as said below
- src_offsets: int32 [8, 64], P('dp'), may hold values from 0 to 1936, as said below
Outputs:
- layer_out: bfloat16 [16384, 512], P(('dp', 'mem'))
- target_grad: float32 [16384, 512], P(('dp', 'mem'))
- memory_grad: float32 [16384, 512], P(('dp', 'mem'))
- self_query_grad: float32 [512, 512], P(('dp', 'mem'))
- self_key_grad: float32 [512, 512], P(('dp', 'mem'))
- self_value_grad: float32 [512, 512], P(('dp', 'mem'))
- self_out_grad: float32 [512, 512], P(('dp', 'mem'))
- cross_query_grad: float32 [512, 512], P(('dp', 'mem'))
- cross_key_grad: float32 [512, 512], P(('dp', 'mem'))
- cross_value_grad: float32 [512, 512], P(('dp', 'mem'))
- cross_out_grad: float32 [512, 512], P(('dp', 'mem'))
- ffn_in_grad: float32 [512, 2048], P(('dp', 'mem'))
- ffn_out_grad: float32 [2048, 512], P(('dp', 'mem'))
- attn_gain_grad: float32 [512], P(('dp', 'mem'))
- attn_shift_grad: float32 [512], P(('dp', 'mem'))
- cross_gain_grad: float32 [512], P(('dp', 'mem'))
- cross_shift_grad: float32 [512], P(('dp', 'mem'))
- ffn_gain_grad: float32 [512], P(('dp', 'mem'))
- ffn_shift_grad: float32 [512], P(('dp', 'mem'))
The draws below stay inside these ranges and needn't reach their ends.
Inputs may be any that keep to these rules, and one draw needn't show every extreme that they name: `tgt_lens`: the 16 entries of one device fill its 512 target rows exactly; every device has a sentence of 256 rows. `src_lens`: the source lengths of a group sum to at most 2048. The source rows [src_offsets, src_offsets + src_lens) of a group's sentences are disjoint and lie within the group's 2048 source rows, in no particular order.
All inputs are finite; a program needn't handle non-finite values.
Results may differ from the reference program's by a relative error of at most 0.03.
Values may be sent and summed in bfloat16 or wider, within the bound.
A program may use at most 128 MiB of HBM per device.

```python
import jax
import jax.numpy as jnp
from jax import lax

D = 512
HEADS = 8
HEAD = 64
FF = 2048
TOK_DEV = 512
SENT_DEV = 16
GROUPS = 8
GSENT = 64
SRC_GRP = 2048
TOKENS = 16384
SOURCE = 16384
N_DP = 8
N_MEM = 4
DEVICES = 32


def sentence_plan(key):
    base = jax.random.fold_in(key, 11)
    streams = jax.random.split(base, 5)
    devices_all = GROUPS * N_MEM
    others = SENT_DEV - 1
    longest = TOK_DEV // 2
    spare_rows = TOK_DEV - longest - others
    powers = jax.random.randint(streams[0], (devices_all, others), 0, 7)
    weights = jax.random.randint(streams[1], (devices_all, others), 1, 5) * jnp.power(2, powers)
    weight_sum = jnp.sum(weights, axis=1, keepdims=True)
    shares = spare_rows * weights // weight_sum
    leftover = spare_rows - jnp.sum(shares, axis=1, keepdims=True)
    rank_pos = lax.broadcasted_iota(jnp.int32, (devices_all, others), 1)
    shorter = 1 + shares + (rank_pos < leftover).astype(jnp.int32)
    where_long = jax.random.randint(streams[2], (devices_all, 1), 0, SENT_DEV)
    slot_pos = lax.broadcasted_iota(jnp.int32, (devices_all, SENT_DEV), 1)
    pick_pos = jnp.clip(slot_pos - (slot_pos > where_long).astype(jnp.int32), 0, others - 1)
    lengths = jnp.where(slot_pos == where_long, longest, jnp.take_along_axis(shorter, pick_pos, axis=1))
    target = lengths.reshape(GROUPS, GSENT)
    is_long = (slot_pos == where_long).reshape(GROUPS, GSENT)
    ratios = jnp.where(is_long, 7, jax.random.randint(streams[3], (GROUPS, GSENT), 6, 8))
    source = jnp.maximum(1, target * ratios // 16)
    column = lax.broadcasted_iota(jnp.int32, (GROUPS, GSENT), 1)
    first_long = where_long.reshape(GROUPS, N_MEM)[:, 0:1]
    last_one = column == first_long
    scores = jax.random.randint(streams[4], (GROUPS, GSENT), 0, 65536) * GSENT + column
    scores = scores + last_one.astype(jnp.int32) * (65536 * GSENT)
    ordering = jnp.argsort(scores, axis=1)
    placed = jnp.take_along_axis(source, ordering, axis=1)
    begins = jnp.cumsum(placed, axis=1) - placed
    inverse = jnp.argsort(ordering, axis=1)
    offsets = jnp.take_along_axis(begins, inverse, axis=1)
    offsets = jnp.where(last_one, SRC_GRP - source, offsets)
    return (target.astype(jnp.int32), source.astype(jnp.int32), offsets.astype(jnp.int32))


def draw_tgt_lens(key, part):
    return sentence_plan(key)[0]


def draw_src_lens(key, part):
    return sentence_plan(key)[1]


def draw_src_offsets(key, part):
    return sentence_plan(key)[2]


def strengthened(drawn, key, source, target, blocks, factor):
    owner, partner = [(jnp.arange(drawn.shape[dim]) // (drawn.shape[dim] // blocks)).reshape([-1 if axis == dim else 1 for axis in range(drawn.ndim)]) for dim in (source, target)]
    chosen = jax.random.permutation(key, blocks)[partner]
    strong = (owner == chosen) | (owner == (partner + blocks // 2) % blocks)
    return jnp.where(strong, factor * drawn, drawn)


def block_scale(key, dims, shards, smallest, high):
    level = 1.0
    for dim, parts in shards:
        draws = jax.random.uniform(jax.random.fold_in(jax.random.fold_in(key, 6), dim), (parts,), jnp.float32, smallest / len(shards), high / len(shards))
        level = level * jnp.repeat(jnp.exp(draws), dims[dim] // parts).reshape((-1,) + (1,) * (len(dims) - 1 - dim))
    return level


def noise(stream_key, extent, scale, reach, shards=(), kind=jnp.bfloat16):
    loudness = block_scale(stream_key, extent, shards, -0.22, 0.18) if shards else 1.0
    drawn = jax.random.normal(stream_key, extent, jnp.float32) * scale * loudness
    return jnp.minimum(jnp.maximum(drawn, -reach), reach).astype(kind)


def noise_with(stream_key, shape, deviation, reach, shards, heavy, kind=jnp.bfloat16):
    values = deviation * jax.random.normal(stream_key, shape, jnp.float32)
    if shards:
        values = values * block_scale(stream_key, shape, shards, -0.22, 0.18)
    return jnp.clip(strengthened(values, jax.random.fold_in(stream_key, 3), *heavy), -reach, reach).astype(kind)


def setup_inputs(seed: int = 0) -> dict:
    arg_keys = jax.random.split(jax.random.key(seed), 23)
    target_in = noise_with(arg_keys[0], (TOKENS, D), 1.0, 6.0, ((0, 32),), (0, 1, 32, 2.75))
    memory = noise_with(arg_keys[1], (SOURCE, D), 1.0, 6.0, ((0, 32),), (0, 1, 32, 2.75))
    out_grad = noise(arg_keys[2], (TOKENS, D), 1.0, 6.0, ((0, 32),))
    self_query = noise(arg_keys[3], (D, D), D ** -0.5, 0.25, ((0, 32),))
    self_key = noise(arg_keys[4], (D, D), D ** -0.5, 0.25, ((0, 32),))
    self_value = noise(arg_keys[5], (D, D), D ** -0.5, 0.25, ((0, 32),))
    self_out = noise(arg_keys[6], (D, D), (D // 8) ** -0.5, 0.75, ((0, 32),))
    cross_query = noise(arg_keys[7], (D, D), D ** -0.5, 0.25, ((0, 32),))
    cross_key = noise(arg_keys[8], (D, D), D ** -0.5, 0.25, ((0, 32),))
    cross_value = noise(arg_keys[9], (D, D), D ** -0.5, 0.25, ((0, 32),))
    cross_out = noise(arg_keys[10], (D, D), (D // 8) ** -0.5, 0.75, ((0, 32),))
    ffn_in = noise(arg_keys[11], (D, FF), D ** -0.5, 0.25, ((0, 32),))
    ffn_out = noise(arg_keys[12], (FF, D), FF ** -0.5, 0.125, ((0, 32),))
    attn_gain = jnp.clip(1.0 + 0.1 * jax.random.normal(arg_keys[13], (D,), jnp.float32), 0.5, 1.5).astype(jnp.bfloat16)
    attn_shift = noise(arg_keys[14], (D,), 0.5, 3.0, ((0, 32),))
    cross_gain = jnp.clip(1.0 + 0.1 * jax.random.normal(arg_keys[15], (D,), jnp.float32), 0.5, 1.5).astype(jnp.bfloat16)
    cross_shift = noise(arg_keys[16], (D,), 0.5, 3.0, ((0, 32),))
    ffn_gain = jnp.clip(1.0 + 0.1 * jax.random.normal(arg_keys[17], (D,), jnp.float32), 0.5, 1.5).astype(jnp.bfloat16)
    ffn_shift = noise(arg_keys[18], (D,), 0.5, 3.0, ((0, 32),))
    tgt_lens = draw_tgt_lens(jax.random.fold_in(arg_keys[22], 71), 0)
    src_lens = draw_src_lens(jax.random.fold_in(arg_keys[22], 71), 0)
    src_offsets = draw_src_offsets(jax.random.fold_in(arg_keys[22], 71), 0)
    return dict(target_in=target_in, memory=memory, out_grad=out_grad, self_query=self_query, self_key=self_key, self_value=self_value, self_out=self_out, cross_query=cross_query, cross_key=cross_key, cross_value=cross_value, cross_out=cross_out, ffn_in=ffn_in, ffn_out=ffn_out, attn_gain=attn_gain, attn_shift=attn_shift, cross_gain=cross_gain, cross_shift=cross_shift, ffn_gain=ffn_gain, ffn_shift=ffn_shift, tgt_lens=tgt_lens, src_lens=src_lens, src_offsets=src_offsets)


@jax.custom_vjp
def low(v):
    return lax.optimization_barrier(v.astype(jnp.bfloat16)).astype(jnp.float32)

@jax.custom_vjp
def low_back(v):
    return v

def low_keep(v):
    return (low(v), None)

def low_pass(kept, grad):
    return (grad,)

def back_keep(v):
    return (v, None)

def back_low(kept, grad):
    return (low(grad),)
low.defvjp(low_keep, low_pass)
low_back.defvjp(back_keep, back_low)
precise = lax.Precision.HIGHEST
eps_norm = 1e-05
score_scale = 0.125

def product(left, right):
    return jnp.dot(left, right, precision=precise)

def layer_norm(values, gain, shift):
    centre = values - lax.optimization_barrier(jnp.mean(values, axis=-1, keepdims=True))
    spread = lax.optimization_barrier(jnp.mean(centre * centre, axis=-1, keepdims=True))
    return centre * lax.rsqrt(spread + eps_norm) * gain + shift

def geometry(tgt_lens, src_lens, src_offsets):
    lengths = tgt_lens.reshape(DEVICES, SENT_DEV).astype(jnp.int32)
    starts = (jnp.cumsum(lengths, axis=1) - lengths).astype(jnp.int32)
    position = jnp.arange(TOK_DEV, dtype=jnp.int32)
    inside = (position[None, :, None] >= starts[:, None, :]).astype(jnp.int32)
    sentence_of = lax.optimization_barrier(jnp.sum(inside, axis=2)).astype(jnp.int32) - 1
    picker = sentence_of[:, :, None] == jnp.arange(SENT_DEV, dtype=jnp.int32)[None, None, :]
    self_low = lax.optimization_barrier(jnp.sum(jnp.where(picker, starts[:, None, :], 0), axis=2)).astype(jnp.int32)
    self_high = jnp.broadcast_to(position[None, :] + 1, (DEVICES, TOK_DEV)).astype(jnp.int32)
    offsets = src_offsets.reshape(DEVICES, SENT_DEV).astype(jnp.int32)
    spans = src_lens.reshape(DEVICES, SENT_DEV).astype(jnp.int32)
    cross_low = lax.optimization_barrier(jnp.sum(jnp.where(picker, offsets[:, None, :], 0), axis=2)).astype(jnp.int32)
    cross_high = cross_low + lax.optimization_barrier(jnp.sum(jnp.where(picker, spans[:, None, :], 0), axis=2)).astype(jnp.int32)
    return (self_low, self_high, cross_low, cross_high)

def attention(queries, keys, values, low_edge, high_edge):
    q_heads = queries.reshape(queries.shape[0], HEADS, HEAD)
    k_heads = keys.reshape(keys.shape[0], HEADS, HEAD)
    v_heads = values.reshape(values.shape[0], HEADS, HEAD)
    raw_scores = low_back(jnp.einsum('qhd,khd->hqk', q_heads, k_heads, precision=precise) * score_scale)
    position = jnp.arange(keys.shape[0], dtype=jnp.int32)
    allowed = (position[None, :] >= low_edge[:, None]) & (position[None, :] < high_edge[:, None])
    expo_val = jnp.where(allowed[None], jnp.exp(raw_scores), 0.0)
    totals = lax.optimization_barrier(jnp.sum(expo_val, axis=2))
    numerator = low_back(jnp.einsum('hqk,khd->qhd', low(expo_val), v_heads, precision=precise))
    return (numerator / totals.T[:, :, None]).reshape(queries.shape[0], D)

def forward(target, memory_f, params, plan):
    self_query, self_key, self_value, self_out, cross_query, cross_key, cross_value, cross_out, ffn_in, ffn_out, attn_gain, attn_shift, cross_gain, cross_shift, ffn_gain, ffn_shift = params
    self_low, self_high, cross_low, cross_high = plan
    queries_self = low_back(low(product(target, self_query)))
    keys_self = low_back(low(product(target, self_key)))
    values_self = low_back(low(product(target, self_value)))

    def self_piece(pieces):
        return attention(pieces[0], pieces[1], pieces[2], pieces[3], pieces[4])
    o_self = lax.map(jax.checkpoint(self_piece), (queries_self.reshape(DEVICES, TOK_DEV, D), keys_self.reshape(DEVICES, TOK_DEV, D), values_self.reshape(DEVICES, TOK_DEV, D), self_low, self_high)).reshape(-1, D)
    o_self = low_back(low(o_self))
    after_self = layer_norm(target + low_back(product(o_self, self_out)), attn_gain, attn_shift)
    queries_cross = low_back(low(product(low(after_self), cross_query)))
    keys_cross = low_back(low(product(memory_f, cross_key)))
    values_cross = low_back(low(product(memory_f, cross_value)))

    def cross_group(pieces):
        group_keys = pieces[1]
        group_values = pieces[2]

        def cross_piece(member_items):
            return attention(member_items[0], group_keys, group_values, member_items[1], member_items[2])
        return lax.map(jax.checkpoint(cross_piece), (pieces[0], pieces[3], pieces[4]))
    o_cross = lax.map(cross_group, (queries_cross.reshape(N_DP, N_MEM, TOK_DEV, D), keys_cross.reshape(N_DP, SRC_GRP, D), values_cross.reshape(N_DP, SRC_GRP, D), cross_low.reshape(N_DP, N_MEM, TOK_DEV), cross_high.reshape(N_DP, N_MEM, TOK_DEV))).reshape(-1, D)
    o_cross = low_back(low(o_cross))
    after_cross = layer_norm(after_self + low_back(product(o_cross, cross_out)), cross_gain, cross_shift)
    hidden = low_back(product(low(after_cross), ffn_in))
    branch = low_back(product(low(jax.nn.silu(hidden)), ffn_out))
    return layer_norm(after_cross + branch, ffn_gain, ffn_shift)

def reference(target_in, memory, out_grad, self_query, self_key, self_value, self_out, cross_query, cross_key, cross_value, cross_out, ffn_in, ffn_out, attn_gain, attn_shift, cross_gain, cross_shift, ffn_gain, ffn_shift, tgt_lens, src_lens, src_offsets):
    plan = geometry(tgt_lens, src_lens, src_offsets)
    params = tuple((weight.astype(jnp.float32) for weight in (self_query, self_key, self_value, self_out, cross_query, cross_key, cross_value, cross_out, ffn_in, ffn_out, attn_gain, attn_shift, cross_gain, cross_shift, ffn_gain, ffn_shift)))

    def wrapped(target, memory_f, weights):
        return forward(target, memory_f, weights, plan)
    result, pullback = jax.vjp(wrapped, target_in.astype(jnp.float32), memory.astype(jnp.float32), params)
    target_grad, memory_grad, grads = pullback(out_grad.astype(jnp.float32))
    return (result.astype(jnp.bfloat16), target_grad, memory_grad, grads[0], grads[1], grads[2], grads[3], grads[4], grads[5], grads[6], grads[7], grads[8], grads[9], grads[10], grads[11], grads[12], grads[13], grads[14], grads[15])
```

```python
import jax
import jax.numpy as jnp
from jax import lax
from jax.experimental import pallas as pl
from jax.experimental.pallas import tpu as pltpu
from jax.sharding import PartitionSpec as P

MESH = pl.DeviceIdType.MESH
SLAB = 512
NORM = 128
LANES = NORM + 16 * SLAB
ROWS = 16


def here():
    dp, mem = lax.axis_index("dp"), lax.axis_index("mem")
    return dp // 2, dp % 2, mem // 2, mem % 2


def device(z, x, y, c):
    return (z * 2 + x, y * 2 + c)


def greet(peers):
    barrier = pltpu.get_barrier_semaphore()
    for peer in peers:
        pl.semaphore_signal(barrier, inc=1, device_id=peer, device_id_type=MESH)
    pl.semaphore_wait(barrier, len(peers))


def remote(src, dst, sems, index, peer):
    send, recv = sems
    return pltpu.make_async_remote_copy(
        src_ref=src,
        dst_ref=dst,
        send_sem=send.at[index],
        recv_sem=recv.at[index],
        device_id=peer,
        device_id_type=MESH,
    )


GATHER_ROUNDS = ((0, 640, 2176), (2176, 2688, 4224), (4224, 5248, 8320))


def gather_kernel(*refs):
    shards = refs[:11]
    norm_ref, memory_ref = refs[11], refs[12]
    out, mem_out = refs[13], refs[14]
    local_sem, mem_local = refs[15], refs[16]
    zs = refs[17:19]
    first, second, across = refs[19:21], refs[21:23], refs[23:25]
    mems = refs[25:27]
    shards = shards[:10]
    z, x, y, c = here()
    xp, yp, cp_ = device(z, 1 - x, y, c), device(z, x, 1 - y, c), device(z, x, y, 1 - c)
    zp = [device((z + k) % 4, x, y, c) for k in (1, 2, 3)]
    own = out.at[z, x, y, c]

    local = []

    def bring(src, start, width):
        local.append(
            pltpu.make_async_copy(src, own.at[:, pl.ds(start, width)], local_sem.at[len(local)])
        )

    bring(norm_ref, 0, NORM)
    for i in range(8):
        bring(shards[i], NORM + SLAB * i, SLAB)
    bring(shards[8], NORM + SLAB * 8, 4 * SLAB)
    for k in range(4):
        bring(shards[9].at[pl.ds(ROWS * k, ROWS)], NORM + SLAB * (12 + k), SLAB)
    for one in local:
        one.start()
    keep = pltpu.make_async_copy(memory_ref, mem_out.at[y, c], mem_local)
    keep.start()
    greet([xp, yp, cp_] + zp)
    for one in local:
        one.wait()

    sent = []

    def go(copy):
        copy.start()
        sent.append(copy)

    def zcopy(r, k, source_z):
        a, _, b = GATHER_ROUNDS[r]
        ref = out.at[source_z, x, y, c, :, pl.ds(a, b - a)]
        return remote(ref, ref, zs, (r, k), zp[k])

    def one(r, stage, part, zz, other, kk):
        a, m, b = GATHER_ROUNDS[r]
        lanes = pl.ds(a, m - a) if part == 0 else pl.ds(m, b - m)
        if part == 0:
            ref = out.at[zz, other, y, c, :, lanes]
            peer = xp if stage == 0 else yp
        else:
            ref = out.at[zz, x, other, c, :, lanes]
            peer = yp if stage == 0 else xp
        if stage == 0:
            return remote(ref, ref, first, (r, part, kk), peer)
        return remote(ref, ref, second, (r, part, kk), peer)

    def over(r, zz, xx, yy, cc, kk, part):
        a, m, b = GATHER_ROUNDS[r]
        lanes = pl.ds(a, m - a) if part == 0 else pl.ds(m, b - m)
        ref = out.at[zz, xx, yy, cc, :, lanes]
        return remote(ref, ref, across, (r, kk, part), cp_)

    zz = [z, (z + 1) % 4, (z + 2) % 4, (z + 3) % 4]

    mem_own = mem_out.at[y, c]

    def block(r, k, hop):
        for part in (0, 1):
            mine = x if part == 0 else y
            go(one(r, 0, part, zz[k], mine, k))
            go(one(r, 1, part, zz[k], mine, 2 * k))

    rounds = range(len(GATHER_ROUNDS))
    for r in rounds:
        for k in range(3):
            go(zcopy(r, k, z))
        block(r, 0, 0)
        if r == 0:
            keep.wait()
            go(remote(mem_own, mem_own, mems, 0, yp))
            go(remote(mem_own, mem_own, mems, 1, cp_))
    for r in rounds:
        for part in (0, 1):
            go(over(r, z, x, y, c, 0, part))

    def arrive_z(r):
        for j in (0, 2, 1):
            k = 3 - j
            zcopy(r, j, zz[k]).wait_recv()
            block(r, k, 0)
            for part in (0, 1):
                go(over(r, zz[k], x, y, c, 4 * k, part))

    def arrive_first(r):
        for k in (0, 1, 3, 2):
            for part in (0, 1):
                theirs = (1 - x) if part == 0 else (1 - y)
                one(r, 0, part, zz[k], theirs, k).wait_recv()
                go(one(r, 1, part, zz[k], theirs, 2 * k + 1))
                if part == 0:
                    go(over(r, zz[k], 1 - x, y, c, 4 * k + 1, 0))
                else:
                    go(over(r, zz[k], x, 1 - y, c, 4 * k + 2, 1))

    def arrive_second(r):
        for k in (0, 1, 3, 2):
            for h in (0, 1):
                for part in (0, 1):
                    if part == 0:
                        xx = x if h == 0 else 1 - x
                        a, m, b = GATHER_ROUNDS[r]
                        ref = out.at[zz[k], xx, 1 - y, c, :, pl.ds(a, m - a)]
                        remote(ref, ref, second, (r, 0, 2 * k + h), yp).wait_recv()
                        go(over(r, zz[k], xx, 1 - y, c, 4 * k + 2 + h, 0))
                    else:
                        yy = y if h == 0 else 1 - y
                        a, m, b = GATHER_ROUNDS[r]
                        ref = out.at[zz[k], 1 - x, yy, c, :, pl.ds(m, b - m)]
                        remote(ref, ref, second, (r, 1, 2 * k + h), xp).wait_recv()
                        go(over(r, zz[k], 1 - x, yy, c, 4 * k + 1 + 2 * h, 1))

    def arrive_over(r):
        for k in range(4):
            for o, (xx, yy) in enumerate(((x, y), (1 - x, y), (x, 1 - y), (1 - x, 1 - y))):
                for part in (0, 1):
                    over(r, zz[k], xx, yy, 1 - c, 4 * k + o, part).wait_recv()

    arrive_z(0)
    arrive_z(1)
    arrive_first(0)
    arrive_z(2)
    arrive_first(1)
    arrive_second(0)
    there = mem_out.at[1 - y, c]
    remote(there, there, mems, 0, yp).wait_recv()
    go(remote(there, there, mems, 2, cp_))
    arrive_first(2)
    arrive_second(1)
    arrive_over(0)
    arrive_second(2)
    arrive_over(1)
    arrive_over(2)
    across_own = mem_out.at[y, 1 - c]
    remote(across_own, across_own, mems, 1, cp_).wait_recv()
    across_far = mem_out.at[1 - y, 1 - c]
    remote(across_far, across_far, mems, 2, cp_).wait_recv()
    for copy in sent:
        copy.wait_send()


def gather_all(shards, norms, memory):
    any_space = pl.BlockSpec(memory_space=pl.ANY)
    dma = pltpu.SemaphoreType.DMA
    n = len(GATHER_ROUNDS)

    def kernel(*refs):
        gather_kernel(*refs[:10], None, *refs[10:])

    gathered, whole_memory = pl.pallas_call(
        kernel,
        out_shape=(
            jax.ShapeDtypeStruct((4, 2, 2, 2, ROWS, LANES), jnp.bfloat16),
            jax.ShapeDtypeStruct((2, 2) + memory.shape, jnp.bfloat16),
        ),
        in_specs=[any_space] * 12,
        out_specs=(any_space, any_space),
        scratch_shapes=[
            dma((14,)),
            dma(()),
            dma((n, 3)),
            dma((n, 3)),
            dma((n, 2, 4)),
            dma((n, 2, 4)),
            dma((n, 2, 8)),
            dma((n, 2, 8)),
            dma((n, 16, 2)),
            dma((n, 16, 2)),
            dma((3,)),
            dma((3,)),
        ],
        compiler_params=pltpu.CompilerParams(collective_id=1, has_side_effects=True),
        name="gather",
    )(*shards, norms, memory)
    return gathered.reshape(32, ROWS, LANES), whole_memory.reshape(-1, SLAB)
SCATTER_ROUNDS = ((4224, 4736, 6272), (6272, 6784, 8320), (2176, 2688, 4224), (0, 640, 2176))


def scatter_kernel(grads, mem_grads, out, mem_out, acc, from_core, from_first, from_second, from_z,
                   macc, mfrom_core, mfrom_y, own_sems, mown_sem, core_s, core_r, first_s, first_r,
                   second_s, second_r, zs_s, zs_r, mem_s, mem_r):
    z, x, y, c = here()
    xp, yp, cp_ = device(z, 1 - x, y, c), device(z, x, 1 - y, c), device(z, x, y, 1 - c)
    zp = [device((z + k) % 4, x, y, c) for k in (1, 2, 3)]
    count = len(SCATTER_ROUNDS)
    core_sems, first_sems, second_sems = (core_s, core_r), (first_s, first_r), (second_s, second_r)
    z_sems, mem_sems = (zs_s, zs_r), (mem_s, mem_r)
    sent = []

    def go(copy):
        copy.start()
        sent.append(copy)

    def span(r, part=None):
        a, m, b = SCATTER_ROUNDS[r]
        return {None: (a, b - a), 0: (a, m - a), 1: (m, b - m)}[part]

    def own(r):
        a, n = span(r)
        return pltpu.make_async_copy(
            grads.at[:, :, :, c, :, pl.ds(a, n)], acc.at[:, :, :, :, pl.ds(a, n)], own_sems.at[r])

    def core(r):
        a, n = span(r)
        return remote(grads.at[:, :, :, 1 - c, :, pl.ds(a, n)],
                      from_core.at[:, :, :, :, pl.ds(a, n)], core_sems, r, cp_)

    def first(r, part):
        lanes = pl.ds(*span(r, part))
        src = acc.at[:, :, 1 - y, :, lanes] if part == 0 else acc.at[:, 1 - x, :, :, lanes]
        return remote(src, from_first.at[:, :, :, lanes], first_sems, (r, part),
                      yp if part == 0 else xp)

    def second(r, part):
        lanes = pl.ds(*span(r, part))
        src = acc.at[:, 1 - x, y, :, lanes] if part == 0 else acc.at[:, x, 1 - y, :, lanes]
        return remote(src, from_second.at[:, :, lanes], second_sems, (r, part),
                      xp if part == 0 else yp)

    def along(r, k):
        lanes = pl.ds(*span(r))
        return remote(acc.at[(z + k + 1) % 4, x, y, :, lanes], from_z.at[k, :, lanes], z_sems,
                      (r, k), zp[k])

    mem_own = pltpu.make_async_copy(mem_grads.at[:, c], macc, mown_sem)
    mem_core = remote(mem_grads.at[:, 1 - c], mfrom_core, mem_sems, 0, cp_)
    mem_far = remote(macc.at[1 - y], mfrom_y, mem_sems, 1, yp)

    own(0).start()
    mem_own.start()
    for r in range(1, count):
        own(r).start()
    greet([xp, yp, cp_] + zp)
    go(core(0))
    go(mem_core)
    for r in range(1, count):
        go(core(r))

    def add_core(r):
        own(r).wait()
        core(r).wait_recv()
        for part in (0, 1):
            lanes = pl.ds(*span(r, part))
            for theirs in (True, False):
                def body(zi, carry, part=part, lanes=lanes, theirs=theirs):
                    for o in (0, 1):
                        if part == 0:
                            xi, yi = o, (1 - y) if theirs else y
                        else:
                            xi, yi = (1 - x) if theirs else x, o
                        acc[zi, xi, yi, :, lanes] = (
                            acc[zi, xi, yi, :, lanes] + from_core[zi, xi, yi, :, lanes])
                    return carry
                lax.fori_loop(0, 4, body, 0)
                if theirs:
                    go(first(r, part))

    def add_first(r):
        for part in (0, 1):
            first(r, part).wait_recv()
            lanes = pl.ds(*span(r, part))
            for theirs in (True, False):
                def body(zi, carry, part=part, lanes=lanes, theirs=theirs):
                    if part == 0:
                        xi, yi = (1 - x) if theirs else x, y
                        slot = xi
                    else:
                        xi, yi = x, (1 - y) if theirs else y
                        slot = yi
                    acc[zi, xi, yi, :, lanes] = (
                        acc[zi, xi, yi, :, lanes] + from_first[zi, slot, :, lanes])
                    return carry
                lax.fori_loop(0, 4, body, 0)
                if theirs:
                    go(second(r, part))

    def add_second(r):
        for part in (0, 1):
            second(r, part).wait_recv()
            lanes = pl.ds(*span(r, part))

            def body(zi, carry, lanes=lanes):
                acc[zi, x, y, :, lanes] = acc[zi, x, y, :, lanes] + from_second[zi, :, lanes]
                return carry
            lax.fori_loop(0, 4, body, 0)
        for k in (1, 0, 2):
            go(along(r, k))

    def add_z(r):
        lanes = pl.ds(*span(r))
        total = acc[z, x, y, :, lanes].astype(jnp.float32)
        for k in (0, 2, 1):
            along(r, k).wait_recv()
            total = total + from_z[k, :, lanes].astype(jnp.float32)
        out[:, lanes] = total

    def memory_core():
        mem_own.wait()
        mem_core.wait_recv()
        for theirs in (True, False):
            side = (1 - y) if theirs else y

            def body(i, carry, side=side):
                rows = pl.ds(pl.multiple_of(i * 64, 64), 64)
                macc[side, rows] = macc[side, rows] + mfrom_core[side, rows]
                return carry
            lax.fori_loop(0, 8, body, 0)
            if theirs:
                go(mem_far)

    def memory_end():
        mem_far.wait_recv()

        def body(i, carry):
            rows = pl.ds(pl.multiple_of(i * 64, 64), 64)
            mem_out[rows] = macc[y, rows].astype(jnp.float32) + mfrom_y[rows].astype(jnp.float32)
            return carry
        lax.fori_loop(0, 8, body, 0)

    for t in range(count + 3):
        if t < count:
            add_core(t)
        if t == 0:
            memory_core()
        if 0 <= t - 1 < count:
            add_first(t - 1)
        if 0 <= t - 2 < count:
            add_second(t - 2)
        if 0 <= t - 3 < count:
            add_z(t - 3)
        if t == 3:
            memory_end()
    for copy in sent:
        copy.wait_send()


def scatter_all(grads, mem_grads):
    any_space = pl.BlockSpec(memory_space=pl.ANY)
    vmem = pl.BlockSpec(memory_space=pltpu.VMEM)
    dma = pltpu.SemaphoreType.DMA
    n = len(SCATTER_ROUNDS)
    rows = mem_grads.shape[2]
    low = jnp.bfloat16
    return pl.pallas_call(
        scatter_kernel,
        out_shape=(
            jax.ShapeDtypeStruct((ROWS, LANES), jnp.float32),
            jax.ShapeDtypeStruct((rows, SLAB), jnp.float32),
        ),
        in_specs=[any_space] * 2,
        out_specs=(vmem, vmem),
        scratch_shapes=[
            pltpu.VMEM((4, 2, 2, ROWS, LANES), low),
            pltpu.VMEM((4, 2, 2, ROWS, LANES), low),
            pltpu.VMEM((4, 2, ROWS, LANES), low),
            pltpu.VMEM((4, ROWS, LANES), low),
            pltpu.VMEM((3, ROWS, LANES), low),
            pltpu.VMEM((2, rows, SLAB), low),
            pltpu.VMEM((2, rows, SLAB), low),
            pltpu.VMEM((rows, SLAB), low),
            dma((n,)),
            dma(()),
            dma((n,)),
            dma((n,)),
            dma((n, 2)),
            dma((n, 2)),
            dma((n, 2)),
            dma((n, 2)),
            dma((n, 3)),
            dma((n, 3)),
            dma((2,)),
            dma((2,)),
        ],
        compiler_params=pltpu.CompilerParams(
            collective_id=2, has_side_effects=True, vmem_limit_bytes=48 << 20),
        name="scatter",
    )(grads, mem_grads)


def two_by_two(mesh_axes):
    return mesh_axes == (8, 4)


def gather_any(shards, norms, memory):
    everyone = ("dp", "mem")
    packed = jnp.concatenate([norms] + list(shards[:9]), axis=1)
    rows = lax.all_gather(packed, everyone, axis=0, tiled=True).reshape(32, ROWS, -1)
    last = lax.all_gather(shards[9], everyone, axis=0, tiled=True)
    last = last.reshape(32, 4, ROWS, SLAB).transpose(0, 2, 1, 3).reshape(32, ROWS, 4 * SLAB)
    return (
        jnp.concatenate([rows, last], axis=2),
        lax.all_gather(memory, "mem", axis=0, tiled=True),
    )


def scatter_any(grads, mem_grads):
    everyone = ("dp", "mem")
    wide = grads.reshape(32, ROWS, LANES).astype(jnp.float32)
    cut = LANES - 4 * SLAB
    rows = lax.psum_scatter(
        wide[:, :, :cut].reshape(512, cut), everyone, scatter_dimension=0, tiled=True
    )
    last = wide[:, :, cut:].reshape(32, ROWS, 4, SLAB).transpose(0, 2, 1, 3).reshape(2048, SLAB)
    last = lax.psum_scatter(last, everyone, scatter_dimension=0, tiled=True)
    mem = lax.psum_scatter(
        mem_grads.astype(jnp.float32), "mem", scatter_dimension=0, tiled=True
    )
    return rows, last, mem
HEADS = 8
HEAD = 64
eps_norm = 1e-05
score_scale = 0.125


def layer_norm(values, gain, shift):
    centre = values - jnp.mean(values, axis=-1, keepdims=True)
    spread = jnp.mean(centre * centre, axis=-1, keepdims=True)
    return centre * lax.rsqrt(spread + eps_norm) * gain + shift


def head_split(values):
    return values.reshape(values.shape[0], HEADS, HEAD)


def matmul(left, right):
    return jnp.dot(left, right, preferred_element_type=jnp.float32)


def left_grad(inputs, grads):
    return jnp.einsum("ra,rb->ab", inputs, grads, preferred_element_type=jnp.float32)


def back_through(grads, weight):
    return jnp.einsum("rb,ab->ra", grads, weight, preferred_element_type=jnp.float32)


def exp_scores(q_block, keys, low_edge, high_edge):
    raw = jnp.einsum("qhd,khd->hqk", head_split(q_block), head_split(keys),
                     preferred_element_type=jnp.float32) * score_scale
    position = lax.broadcasted_iota(jnp.int32, (q_block.shape[0], keys.shape[0]), 1)
    allowed = (position >= low_edge[:, None]) & (position < high_edge[:, None])
    return jnp.where(allowed[None], jnp.exp(raw), 0.0)


def attend(queries, keys, values, low_edge, high_edge):
    expo = exp_scores(queries, keys, low_edge, high_edge)
    numer = jnp.einsum("hqk,khd->qhd", expo.astype(jnp.bfloat16), head_split(values),
                       preferred_element_type=jnp.float32)
    totals = jnp.sum(expo, axis=2).T
    return (numer / totals[:, :, None]).reshape(queries.shape[0], -1), totals


def attend_back(queries, keys, values, low_edge, high_edge, upstream, output, totals):
    expo = exp_scores(queries, keys, low_edge, high_edge)
    up = head_split(upstream.astype(jnp.float32))
    numer_grad = (up / totals[:, :, None]).astype(jnp.bfloat16)
    corr = -jnp.sum(up * head_split(output), axis=2) / totals
    flow = jnp.einsum("qhd,khd->hqk", numer_grad, head_split(values),
                      preferred_element_type=jnp.float32) + corr.T[:, :, None]
    ds = (expo * flow).astype(jnp.bfloat16)
    dq = jnp.einsum("hqk,khd->qhd", ds, head_split(keys), preferred_element_type=jnp.float32)
    dk = jnp.einsum("hqk,qhd->khd", ds, head_split(queries), preferred_element_type=jnp.float32)
    dv = jnp.einsum("hqk,qhd->khd", expo.astype(jnp.bfloat16), numer_grad,
                    preferred_element_type=jnp.float32)
    flat = lambda v: v.reshape(v.shape[0], -1)
    return ((flat(dq) * score_scale).astype(jnp.bfloat16), (flat(dk) * score_scale).astype(jnp.bfloat16),
            flat(dv).astype(jnp.bfloat16))


def local(target_in, memory, out_grad, *rest):
    weights, (tgt_lens, src_lens, src_offsets) = rest[:16], rest[16:]
    member = lax.axis_index("mem")
    per_device = tgt_lens.shape[1] // lax.axis_size("mem")
    pick = lambda table: lax.dynamic_slice_in_dim(table[0], member * per_device, per_device, 0)
    lengths, spans, offsets = pick(tgt_lens), pick(src_lens), pick(src_offsets)
    norms = jnp.stack(weights[10:], axis=1)
    norms = jnp.pad(norms, ((0, 0), (0, NORM - norms.shape[1])))
    fast = two_by_two((lax.axis_size("dp"), lax.axis_size("mem")))
    gathered, all_memory = (gather_all if fast else gather_any)(weights[:10], norms, memory)
    W = gathered.reshape(512, LANES)
    mat = lambda i: W[:, NORM + SLAB * i : NORM + SLAB * (i + 1)]
    wsq, wsk, wsv, wso, wcq, wck, wcv, wco = [mat(i) for i in range(8)]
    w1 = W[:, NORM + 8 * SLAB : NORM + 12 * SLAB]
    w2 = gathered[:, :, NORM + 12 * SLAB :].reshape(32, 16, 4, SLAB).transpose(0, 2, 1, 3).reshape(2048, SLAB)
    ga, sa, gc, sc, gf, sf = [W[:, i].astype(jnp.float32) for i in range(6)]
    rows = target_in.shape[0]
    starts = jnp.cumsum(lengths) - lengths
    position = lax.iota(jnp.int32, rows)
    sentence = jnp.sum((position[:, None] >= starts[None, :]).astype(jnp.int32), axis=1) - 1
    picker = sentence[:, None] == lax.iota(jnp.int32, per_device)[None, :]
    choose = lambda v: jnp.sum(jnp.where(picker, v[None, :], 0), axis=1)
    self_low, self_high = choose(starts), position + 1
    cross_low = choose(offsets)
    cross_high = cross_low + choose(spans)
    low = jnp.bfloat16
    q, k, v = [matmul(target_in, w).astype(low) for w in (wsq, wsk, wsv)]
    o_self_f, tot_self = attend(q, k, v, self_low, self_high)
    o_self = o_self_f.astype(low)
    after_self, pull_self = jax.vjp(layer_norm, target_in.astype(jnp.float32) + matmul(o_self, wso), ga, sa)
    a_b = after_self.astype(low)
    qc = matmul(a_b, wcq).astype(low)
    kc, vc = matmul(all_memory, wck).astype(low), matmul(all_memory, wcv).astype(low)
    if fast:
        o_c_f, tot_c = attend(qc, kc, vc, cross_low, cross_high)
    else:
        cut = lambda v: v.reshape((4, -1) + v.shape[1:])
        o_c_f, tot_c = lax.map(
            lambda p: attend(p[0], kc, vc, p[1], p[2]), (cut(qc), cut(cross_low), cut(cross_high))
        )
        o_c_f, tot_c = o_c_f.reshape(rows, -1), tot_c.reshape(rows, -1)
    o_c = o_c_f.astype(low)
    after_cross, pull_cross = jax.vjp(layer_norm, after_self + matmul(o_c, wco), gc, sc)
    c_b = after_cross.astype(low)
    hidden = matmul(c_b, w1)
    activated, pull_silu = jax.vjp(jax.nn.silu, hidden)
    act = activated.astype(low)
    final, pull_ffn = jax.vjp(layer_norm, after_cross + matmul(act, w2), gf, sf)
    d_pre_out, g_gf, g_sf = pull_ffn(out_grad.astype(jnp.float32))
    d_branch = d_pre_out.astype(low)
    g_w2 = left_grad(act, d_branch)
    d_hidden = pull_silu(back_through(d_branch, w2))[0].astype(low)
    g_w1 = left_grad(c_b, d_hidden)
    d_pre_cross, g_gc, g_sc = pull_cross(d_pre_out + back_through(d_hidden, w1))
    d_cb = d_pre_cross.astype(low)
    g_wco = left_grad(o_c, d_cb)
    d_oc = back_through(d_cb, wco).astype(low)
    if fast:
        dq_c, dk_c, dv_c = attend_back(qc, kc, vc, cross_low, cross_high, d_oc, o_c_f, tot_c)
    else:
        def piece(carry, p):
            dq, dk, dv = attend_back(p[0], kc, vc, p[1], p[2], p[3], p[4], p[5])
            return (carry[0] + dk, carry[1] + dv), dq

        empty = jnp.zeros(kc.shape, jnp.bfloat16)
        (dk_c, dv_c), dq_c = lax.scan(
            piece,
            (empty, empty),
            tuple(cut(v) for v in (qc, cross_low, cross_high, d_oc, o_c_f, tot_c)),
        )
        dq_c = dq_c.reshape(rows, -1)
    g_wcq, g_wck, g_wcv = left_grad(a_b, dq_c), left_grad(all_memory, dk_c), left_grad(all_memory, dv_c)
    mem_grad = back_through(dk_c, wck) + back_through(dv_c, wcv)
    d_pre_self, g_ga, g_sa = pull_self(d_pre_cross + back_through(dq_c, wcq))
    d_sb = d_pre_self.astype(low)
    g_wso = left_grad(o_self, d_sb)
    d_os = back_through(d_sb, wso).astype(low)
    dq, dk, dv = attend_back(q, k, v, self_low, self_high, d_os, o_self_f, tot_self)
    g_wsq, g_wsk, g_wsv = left_grad(target_in, dq), left_grad(target_in, dk), left_grad(target_in, dv)
    target_grad = d_pre_self + back_through(dq, wsq) + back_through(dk, wsk) + back_through(dv, wsv)
    n_g = jnp.pad(jnp.stack([g_ga, g_sa, g_gc, g_sc, g_gf, g_sf], axis=1), ((0, 0), (0, NORM - 6)))
    g_w2p = g_w2.reshape(32, 4, 16, SLAB).transpose(0, 2, 1, 3).reshape(512, 4 * SLAB)
    grads = jnp.concatenate([g.astype(low) for g in (n_g, g_wsq, g_wsk, g_wsv, g_wso, g_wcq, g_wck, g_wcv, g_wco, g_w1, g_w2p)], axis=1)
    part = lambda i, n=1: out[:, NORM + SLAB * i : NORM + SLAB * (i + n)]
    if fast:
        out, mem_out = scatter_all(grads.reshape(4, 2, 2, 2, 16, LANES), mem_grad.astype(low).reshape(2, 2, rows, SLAB))
        w2_grad = jnp.concatenate([part(12 + k) for k in range(4)], axis=0)
    else:
        out, w2_grad, mem_out = scatter_any(grads, mem_grad.astype(low))
    return (final.astype(low), target_grad, mem_out) + tuple(part(i) for i in range(8)) + (part(8, 4), w2_grad) + tuple(out[:, i] for i in range(6))


def solution(mesh):
    both = P(("dp", "mem"), None)
    flat = P(("dp", "mem"))
    in_specs = (both,) * 13 + (flat,) * 6 + (P("dp", None),) * 3
    out_specs = (both,) * 13 + (flat,) * 6
    return jax.shard_map(local, mesh=mesh, in_specs=in_specs, out_specs=out_specs, check_vma=False)
```

```python
import jax
import jax.numpy as jnp
from jax import lax
from jax.experimental import pallas as pl
from jax.experimental.pallas import tpu as pltpu
from jax.sharding import PartitionSpec as P

MESH = pl.DeviceIdType.MESH
SLAB = 512
NORM = 128
LANES = NORM + 16 * SLAB
ROWS = 16


def here():
    dp, mem = lax.axis_index("dp"), lax.axis_index("mem")
    return dp // 2, dp % 2, mem // 2, mem % 2


def device(z, x, y, c):
    return (z * 2 + x, y * 2 + c)


def greet(peers):
    barrier = pltpu.get_barrier_semaphore()
    for peer in peers:
        pl.semaphore_signal(barrier, inc=1, device_id=peer, device_id_type=MESH)
    pl.semaphore_wait(barrier, len(peers))


def remote(src, dst, sems, index, peer):
    send, recv = sems
    return pltpu.make_async_remote_copy(
        src_ref=src,
        dst_ref=dst,
        send_sem=send.at[index],
        recv_sem=recv.at[index],
        device_id=peer,
        device_id_type=MESH,
    )


GATHER_ROUNDS = ((0, 640, 2176), (2176, 2688, 4224), (4224, 5248, 8320))


def gather_kernel(*refs):
    shards = refs[:11]
    norm_ref, memory_ref = refs[11], refs[12]
    out, mem_out = refs[13], refs[14]
    local_sem, mem_local = refs[15], refs[16]
    zs = refs[17:19]
    first, second, across = refs[19:21], refs[21:23], refs[23:25]
    mems = refs[25:27]
    shards = shards[:10]
    z, x, y, c = here()
    xp, yp, cp_ = device(z, 1 - x, y, c), device(z, x, 1 - y, c), device(z, x, y, 1 - c)
    zp = [device((z + k) % 4, x, y, c) for k in (1, 2, 3)]
    own = out.at[z, x, y, c]

    local = []

    def bring(src, start, width):
        local.append(
            pltpu.make_async_copy(src, own.at[:, pl.ds(start, width)], local_sem.at[len(local)])
        )

    bring(norm_ref, 0, NORM)
    for i in range(8):
        bring(shards[i], NORM + SLAB * i, SLAB)
    bring(shards[8], NORM + SLAB * 8, 4 * SLAB)
    for k in range(4):
        bring(shards[9].at[pl.ds(ROWS * k, ROWS)], NORM + SLAB * (12 + k), SLAB)
    for one in local:
        one.start()
    keep = pltpu.make_async_copy(memory_ref, mem_out.at[y, c], mem_local)
    keep.start()
    greet([xp, yp, cp_] + zp)
    for one in local:
        one.wait()

    sent = []

    def go(copy):
        copy.start()
        sent.append(copy)

    def zcopy(r, k, source_z):
        a, _, b = GATHER_ROUNDS[r]
        ref = out.at[source_z, x, y, c, :, pl.ds(a, b - a)]
        return remote(ref, ref, zs, (r, k), zp[k])

    def one(r, stage, part, zz, other, kk):
        a, m, b = GATHER_ROUNDS[r]
        lanes = pl.ds(a, m - a) if part == 0 else pl.ds(m, b - m)
        if part == 0:
            ref = out.at[zz, other, y, c, :, lanes]
            peer = xp if stage == 0 else yp
        else:
            ref = out.at[zz, x, other, c, :, lanes]
            peer = yp if stage == 0 else xp
        if stage == 0:
            return remote(ref, ref, first, (r, part, kk), peer)
        return remote(ref, ref, second, (r, part, kk), peer)

    def over(r, zz, xx, yy, cc, kk, part):
        a, m, b = GATHER_ROUNDS[r]
        lanes = pl.ds(a, m - a) if part == 0 else pl.ds(m, b - m)
        ref = out.at[zz, xx, yy, cc, :, lanes]
        return remote(ref, ref, across, (r, kk, part), cp_)

    zz = [z, (z + 1) % 4, (z + 2) % 4, (z + 3) % 4]

    mem_own = mem_out.at[y, c]

    def block(r, k, hop):
        for part in (0, 1):
            mine = x if part == 0 else y
            go(one(r, 0, part, zz[k], mine, k))
            go(one(r, 1, part, zz[k], mine, 2 * k))

    rounds = range(len(GATHER_ROUNDS))
    for r in rounds:
        for k in range(3):
            go(zcopy(r, k, z))
        block(r, 0, 0)
        if r == 0:
            keep.wait()
            go(remote(mem_own, mem_own, mems, 0, yp))
            go(remote(mem_own, mem_own, mems, 1, cp_))
    for r in rounds:
        for part in (0, 1):
            go(over(r, z, x, y, c, 0, part))

    def arrive_z(r):
        for j in (0, 2, 1):
            k = 3 - j
            zcopy(r, j, zz[k]).wait_recv()
            block(r, k, 0)
            for part in (0, 1):
                go(over(r, zz[k], x, y, c, 4 * k, part))

    def arrive_first(r):
        for k in (0, 1, 3, 2):
            for part in (0, 1):
                theirs = (1 - x) if part == 0 else (1 - y)
                one(r, 0, part, zz[k], theirs, k).wait_recv()
                go(one(r, 1, part, zz[k], theirs, 2 * k + 1))
                if part == 0:
                    go(over(r, zz[k], 1 - x, y, c, 4 * k + 1, 0))
                else:
                    go(over(r, zz[k], x, 1 - y, c, 4 * k + 2, 1))

    def arrive_second(r):
        for k in (0, 1, 3, 2):
            for h in (0, 1):
                for part in (0, 1):
                    if part == 0:
                        xx = x if h == 0 else 1 - x
                        a, m, b = GATHER_ROUNDS[r]
                        ref = out.at[zz[k], xx, 1 - y, c, :, pl.ds(a, m - a)]
                        remote(ref, ref, second, (r, 0, 2 * k + h), yp).wait_recv()
                        go(over(r, zz[k], xx, 1 - y, c, 4 * k + 2 + h, 0))
                    else:
                        yy = y if h == 0 else 1 - y
                        a, m, b = GATHER_ROUNDS[r]
                        ref = out.at[zz[k], 1 - x, yy, c, :, pl.ds(m, b - m)]
                        remote(ref, ref, second, (r, 1, 2 * k + h), xp).wait_recv()
                        go(over(r, zz[k], 1 - x, yy, c, 4 * k + 1 + 2 * h, 1))

    def arrive_over(r):
        for k in range(4):
            for o, (xx, yy) in enumerate(((x, y), (1 - x, y), (x, 1 - y), (1 - x, 1 - y))):
                for part in (0, 1):
                    over(r, zz[k], xx, yy, 1 - c, 4 * k + o, part).wait_recv()

    arrive_z(0)
    arrive_z(1)
    arrive_first(0)
    arrive_z(2)
    arrive_first(1)
    arrive_second(0)
    there = mem_out.at[1 - y, c]
    remote(there, there, mems, 0, yp).wait_recv()
    go(remote(there, there, mems, 2, cp_))
    arrive_first(2)
    arrive_second(1)
    arrive_over(0)
    arrive_second(2)
    arrive_over(1)
    arrive_over(2)
    across_own = mem_out.at[y, 1 - c]
    remote(across_own, across_own, mems, 1, cp_).wait_recv()
    across_far = mem_out.at[1 - y, 1 - c]
    remote(across_far, across_far, mems, 2, cp_).wait_recv()
    for copy in sent:
        copy.wait_send()


def gather_all(shards, norms, memory):
    any_space = pl.BlockSpec(memory_space=pl.ANY)
    dma = pltpu.SemaphoreType.DMA
    n = len(GATHER_ROUNDS)

    def kernel(*refs):
        gather_kernel(*refs[:10], None, *refs[10:])

    gathered, whole_memory = pl.pallas_call(
        kernel,
        out_shape=(
            jax.ShapeDtypeStruct((4, 2, 2, 2, ROWS, LANES), jnp.bfloat16),
            jax.ShapeDtypeStruct((2, 2) + memory.shape, jnp.bfloat16),
        ),
        in_specs=[any_space] * 12,
        out_specs=(any_space, any_space),
        scratch_shapes=[
            dma((14,)),
            dma(()),
            dma((n, 3)),
            dma((n, 3)),
            dma((n, 2, 4)),
            dma((n, 2, 4)),
            dma((n, 2, 8)),
            dma((n, 2, 8)),
            dma((n, 16, 2)),
            dma((n, 16, 2)),
            dma((3,)),
            dma((3,)),
        ],
        compiler_params=pltpu.CompilerParams(collective_id=1, has_side_effects=True),
        name="gather",
    )(*shards, norms, memory)
    return gathered.reshape(32, ROWS, LANES), whole_memory.reshape(-1, SLAB)
SCATTER_ROUNDS = ((4224, 4736, 6272), (6272, 6784, 8320), (2176, 2688, 4224), (0, 640, 2176))


def scatter_kernel(grads, mem_grads, out, mem_out, acc, from_core, from_first, from_second, from_z,
                   macc, mfrom_core, mfrom_y, own_sems, mown_sem, core_s, core_r, first_s, first_r,
                   second_s, second_r, zs_s, zs_r, mem_s, mem_r):
    z, x, y, c = here()
    xp, yp, cp_ = device(z, 1 - x, y, c), device(z, x, 1 - y, c), device(z, x, y, 1 - c)
    zp = [device((z + k) % 4, x, y, c) for k in (1, 2, 3)]
    count = len(SCATTER_ROUNDS)
    core_sems, first_sems, second_sems = (core_s, core_r), (first_s, first_r), (second_s, second_r)
    z_sems, mem_sems = (zs_s, zs_r), (mem_s, mem_r)
    sent = []

    def go(copy):
        copy.start()
        sent.append(copy)

    def span(r, part=None):
        a, m, b = SCATTER_ROUNDS[r]
        return {None: (a, b - a), 0: (a, m - a), 1: (m, b - m)}[part]

    def own(r):
        a, n = span(r)
        return pltpu.make_async_copy(
            grads.at[:, :, :, c, :, pl.ds(a, n)], acc.at[:, :, :, :, pl.ds(a, n)], own_sems.at[r])

    def core(r):
        a, n = span(r)
        return remote(grads.at[:, :, :, 1 - c, :, pl.ds(a, n)],
                      from_core.at[:, :, :, :, pl.ds(a, n)], core_sems, r, cp_)

    def first(r, part):
        lanes = pl.ds(*span(r, part))
        src = acc.at[:, :, 1 - y, :, lanes] if part == 0 else acc.at[:, 1 - x, :, :, lanes]
        return remote(src, from_first.at[:, :, :, lanes], first_sems, (r, part),
                      yp if part == 0 else xp)

    def second(r, part):
        lanes = pl.ds(*span(r, part))
        src = acc.at[:, 1 - x, y, :, lanes] if part == 0 else acc.at[:, x, 1 - y, :, lanes]
        return remote(src, from_second.at[:, :, lanes], second_sems, (r, part),
                      xp if part == 0 else yp)

    def along(r, k):
        lanes = pl.ds(*span(r))
        return remote(acc.at[(z + k + 1) % 4, x, y, :, lanes], from_z.at[k, :, lanes], z_sems,
                      (r, k), zp[k])

    mem_own = pltpu.make_async_copy(mem_grads.at[:, c], macc, mown_sem)
    mem_core = remote(mem_grads.at[:, 1 - c], mfrom_core, mem_sems, 0, cp_)
    mem_far = remote(macc.at[1 - y], mfrom_y, mem_sems, 1, yp)

    own(0).start()
    mem_own.start()
    for r in range(1, count):
        own(r).start()
    greet([xp, yp, cp_] + zp)
    go(core(0))
    go(mem_core)
    for r in range(1, count):
        go(core(r))

    def add_core(r):
        own(r).wait()
        core(r).wait_recv()
        for part in (0, 1):
            lanes = pl.ds(*span(r, part))
            for theirs in (True, False):
                def body(zi, carry, part=part, lanes=lanes, theirs=theirs):
                    for o in (0, 1):
                        if part == 0:
                            xi, yi = o, (1 - y) if theirs else y
                        else:
                            xi, yi = (1 - x) if theirs else x, o
                        acc[zi, xi, yi, :, lanes] = (
                            acc[zi, xi, yi, :, lanes] + from_core[zi, xi, yi, :, lanes])
                    return carry
                lax.fori_loop(0, 4, body, 0)
                if theirs:
                    go(first(r, part))

    def add_first(r):
        for part in (0, 1):
            first(r, part).wait_recv()
            lanes = pl.ds(*span(r, part))
            for theirs in (True, False):
                def body(zi, carry, part=part, lanes=lanes, theirs=theirs):
                    if part == 0:
                        xi, yi = (1 - x) if theirs else x, y
                        slot = xi
                    else:
                        xi, yi = x, (1 - y) if theirs else y
                        slot = yi
                    acc[zi, xi, yi, :, lanes] = (
                        acc[zi, xi, yi, :, lanes] + from_first[zi, slot, :, lanes])
                    return carry
                lax.fori_loop(0, 4, body, 0)
                if theirs:
                    go(second(r, part))

    def add_second(r):
        for part in (0, 1):
            second(r, part).wait_recv()
            lanes = pl.ds(*span(r, part))

            def body(zi, carry, lanes=lanes):
                acc[zi, x, y, :, lanes] = acc[zi, x, y, :, lanes] + from_second[zi, :, lanes]
                return carry
            lax.fori_loop(0, 4, body, 0)
        for k in (1, 0, 2):
            go(along(r, k))

    def add_z(r):
        lanes = pl.ds(*span(r))
        total = acc[z, x, y, :, lanes].astype(jnp.float32)
        for k in (0, 2, 1):
            along(r, k).wait_recv()
            total = total + from_z[k, :, lanes].astype(jnp.float32)
        out[:, lanes] = total

    def memory_core():
        mem_own.wait()
        mem_core.wait_recv()
        for theirs in (True, False):
            side = (1 - y) if theirs else y

            def body(i, carry, side=side):
                rows = pl.ds(pl.multiple_of(i * 64, 64), 64)
                macc[side, rows] = macc[side, rows] + mfrom_core[side, rows]
                return carry
            lax.fori_loop(0, 8, body, 0)
            if theirs:
                go(mem_far)

    def memory_end():
        mem_far.wait_recv()

        def body(i, carry):
            rows = pl.ds(pl.multiple_of(i * 64, 64), 64)
            mem_out[rows] = macc[y, rows].astype(jnp.float32) + mfrom_y[rows].astype(jnp.float32)
            return carry
        lax.fori_loop(0, 8, body, 0)

    for t in range(count + 3):
        if t < count:
            add_core(t)
        if t == 0:
            memory_core()
        if 0 <= t - 1 < count:
            add_first(t - 1)
        if 0 <= t - 2 < count:
            add_second(t - 2)
        if 0 <= t - 3 < count:
            add_z(t - 3)
        if t == 3:
            memory_end()
    for copy in sent:
        copy.wait_send()


def scatter_all(grads, mem_grads):
    any_space = pl.BlockSpec(memory_space=pl.ANY)
    vmem = pl.BlockSpec(memory_space=pltpu.VMEM)
    dma = pltpu.SemaphoreType.DMA
    n = len(SCATTER_ROUNDS)
    rows = mem_grads.shape[2]
    low = jnp.bfloat16
    return pl.pallas_call(
        scatter_kernel,
        out_shape=(
            jax.ShapeDtypeStruct((ROWS, LANES), jnp.float32),
            jax.ShapeDtypeStruct((rows, SLAB), jnp.float32),
        ),
        in_specs=[any_space] * 2,
        out_specs=(vmem, vmem),
        scratch_shapes=[
            pltpu.VMEM((4, 2, 2, ROWS, LANES), low),
            pltpu.VMEM((4, 2, 2, ROWS, LANES), low),
            pltpu.VMEM((4, 2, ROWS, LANES), low),
            pltpu.VMEM((4, ROWS, LANES), low),
            pltpu.VMEM((3, ROWS, LANES), low),
            pltpu.VMEM((2, rows, SLAB), low),
            pltpu.VMEM((2, rows, SLAB), low),
            pltpu.VMEM((rows, SLAB), low),
            dma((n,)),
            dma(()),
            dma((n,)),
            dma((n,)),
            dma((n, 2)),
            dma((n, 2)),
            dma((n, 2)),
            dma((n, 2)),
            dma((n, 3)),
            dma((n, 3)),
            dma((2,)),
            dma((2,)),
        ],
        compiler_params=pltpu.CompilerParams(
            collective_id=2, has_side_effects=True, vmem_limit_bytes=48 << 20),
        name="scatter",
    )(grads, mem_grads)


def two_by_two(mesh_axes):
    return mesh_axes == (8, 4)


def gather_any(shards, norms, memory):
    everyone = ("dp", "mem")
    packed = jnp.concatenate([norms] + list(shards[:9]), axis=1)
    rows = lax.all_gather(packed, everyone, axis=0, tiled=True).reshape(32, ROWS, -1)
    last = lax.all_gather(shards[9], everyone, axis=0, tiled=True)
    last = last.reshape(32, 4, ROWS, SLAB).transpose(0, 2, 1, 3).reshape(32, ROWS, 4 * SLAB)
    return (
        jnp.concatenate([rows, last], axis=2),
        lax.all_gather(memory, "mem", axis=0, tiled=True),
    )


def scatter_any(grads, mem_grads):
    everyone = ("dp", "mem")
    wide = grads.reshape(32, ROWS, LANES).astype(jnp.float32)
    cut = LANES - 4 * SLAB
    rows = lax.psum_scatter(
        wide[:, :, :cut].reshape(512, cut), everyone, scatter_dimension=0, tiled=True
    )
    last = wide[:, :, cut:].reshape(32, ROWS, 4, SLAB).transpose(0, 2, 1, 3).reshape(2048, SLAB)
    last = lax.psum_scatter(last, everyone, scatter_dimension=0, tiled=True)
    mem = lax.psum_scatter(
        mem_grads.astype(jnp.float32), "mem", scatter_dimension=0, tiled=True
    )
    return rows, last, mem
HEADS = 8
HEAD = 64
eps_norm = 1e-05
score_scale = 0.125


def layer_norm(values, gain, shift):
    centre = values - jnp.mean(values, axis=-1, keepdims=True)
    spread = jnp.mean(centre * centre, axis=-1, keepdims=True)
    return centre * lax.rsqrt(spread + eps_norm) * gain + shift


def head_split(values):
    return values.reshape(values.shape[0], HEADS, HEAD)


def matmul(left, right):
    return jnp.dot(left, right, preferred_element_type=jnp.float32)


def left_grad(inputs, grads):
    return jnp.einsum("ra,rb->ab", inputs, grads, preferred_element_type=jnp.float32)


def back_through(grads, weight):
    return jnp.einsum("rb,ab->ra", grads, weight, preferred_element_type=jnp.float32)


def exp_scores(q_block, keys, low_edge, high_edge):
    raw = jnp.einsum("qhd,khd->hqk", head_split(q_block), head_split(keys),
                     preferred_element_type=jnp.float32) * score_scale
    position = lax.broadcasted_iota(jnp.int32, (q_block.shape[0], keys.shape[0]), 1)
    allowed = (position >= low_edge[:, None]) & (position < high_edge[:, None])
    return jnp.where(allowed[None], jnp.exp(raw), 0.0)


def attend(queries, keys, values, low_edge, high_edge):
    expo = exp_scores(queries, keys, low_edge, high_edge)
    numer = jnp.einsum("hqk,khd->qhd", expo.astype(jnp.bfloat16), head_split(values),
                       preferred_element_type=jnp.float32)
    totals = jnp.sum(expo, axis=2).T
    return (numer / totals[:, :, None]).reshape(queries.shape[0], -1), totals


def attend_back(queries, keys, values, low_edge, high_edge, upstream, output, totals):
    expo = exp_scores(queries, keys, low_edge, high_edge)
    up = head_split(upstream.astype(jnp.float32))
    numer_grad = (up / totals[:, :, None]).astype(jnp.bfloat16)
    corr = -jnp.sum(up * head_split(output), axis=2) / totals
    flow = jnp.einsum("qhd,khd->hqk", numer_grad, head_split(values),
                      preferred_element_type=jnp.float32) + corr.T[:, :, None]
    ds = (expo * flow).astype(jnp.bfloat16)
    dq = jnp.einsum("hqk,khd->qhd", ds, head_split(keys), preferred_element_type=jnp.float32)
    dk = jnp.einsum("hqk,qhd->khd", ds, head_split(queries), preferred_element_type=jnp.float32)
    dv = jnp.einsum("hqk,qhd->khd", expo.astype(jnp.bfloat16), numer_grad,
                    preferred_element_type=jnp.float32)
    flat = lambda v: v.reshape(v.shape[0], -1)
    return ((flat(dq) * score_scale).astype(jnp.bfloat16), (flat(dk) * score_scale).astype(jnp.bfloat16),
            flat(dv).astype(jnp.bfloat16))


def plain(target_in, memory, out_grad, *rest):
    weights, (tgt_lens, src_lens, src_offsets) = rest[:16], rest[16:]
    member = lax.axis_index("mem")
    per_device = tgt_lens.shape[1] // lax.axis_size("mem")
    pick = lambda table: lax.dynamic_slice_in_dim(table[0], member * per_device, per_device, 0)
    lengths, spans, offsets = pick(tgt_lens), pick(src_lens), pick(src_offsets)
    norms = jnp.stack(weights[10:], axis=1)
    norms = jnp.pad(norms, ((0, 0), (0, NORM - norms.shape[1])))
    gathered, all_memory = gather_any(weights[:10], norms, memory)
    W = gathered.reshape(512, LANES)
    mat = lambda i: W[:, NORM + SLAB * i : NORM + SLAB * (i + 1)]
    wsq, wsk, wsv, wso, wcq, wck, wcv, wco = [mat(i) for i in range(8)]
    w1 = W[:, NORM + 8 * SLAB : NORM + 12 * SLAB]
    w2 = gathered[:, :, NORM + 12 * SLAB :].reshape(32, 16, 4, SLAB).transpose(0, 2, 1, 3).reshape(2048, SLAB)
    ga, sa, gc, sc, gf, sf = [W[:, i].astype(jnp.float32) for i in range(6)]
    rows = target_in.shape[0]
    starts = jnp.cumsum(lengths) - lengths
    position = lax.iota(jnp.int32, rows)
    sentence = jnp.sum((position[:, None] >= starts[None, :]).astype(jnp.int32), axis=1) - 1
    picker = sentence[:, None] == lax.iota(jnp.int32, per_device)[None, :]
    choose = lambda v: jnp.sum(jnp.where(picker, v[None, :], 0), axis=1)
    self_low, self_high = choose(starts), position + 1
    cross_low = choose(offsets)
    cross_high = cross_low + choose(spans)
    low = jnp.bfloat16
    q, k, v = [matmul(target_in, w).astype(low) for w in (wsq, wsk, wsv)]
    o_self_f, tot_self = attend(q, k, v, self_low, self_high)
    o_self = o_self_f.astype(low)
    after_self, pull_self = jax.vjp(layer_norm, target_in.astype(jnp.float32) + matmul(o_self, wso), ga, sa)
    a_b = after_self.astype(low)
    qc = matmul(a_b, wcq).astype(low)
    kc, vc = matmul(all_memory, wck).astype(low), matmul(all_memory, wcv).astype(low)
    cut = lambda v: v.reshape((4, -1) + v.shape[1:])
    o_c_f, tot_c = lax.map(
        lambda p: attend(p[0], kc, vc, p[1], p[2]), (cut(qc), cut(cross_low), cut(cross_high))
    )
    o_c_f, tot_c = o_c_f.reshape(rows, -1), tot_c.reshape(rows, -1)
    o_c = o_c_f.astype(low)
    after_cross, pull_cross = jax.vjp(layer_norm, after_self + matmul(o_c, wco), gc, sc)
    c_b = after_cross.astype(low)
    hidden = matmul(c_b, w1)
    activated, pull_silu = jax.vjp(jax.nn.silu, hidden)
    act = activated.astype(low)
    final, pull_ffn = jax.vjp(layer_norm, after_cross + matmul(act, w2), gf, sf)
    d_pre_out, g_gf, g_sf = pull_ffn(out_grad.astype(jnp.float32))
    d_branch = d_pre_out.astype(low)
    g_w2 = left_grad(act, d_branch)
    d_hidden = pull_silu(back_through(d_branch, w2))[0].astype(low)
    g_w1 = left_grad(c_b, d_hidden)
    d_pre_cross, g_gc, g_sc = pull_cross(d_pre_out + back_through(d_hidden, w1))
    d_cb = d_pre_cross.astype(low)
    g_wco = left_grad(o_c, d_cb)
    d_oc = back_through(d_cb, wco).astype(low)

    def piece(carry, p):
        dq, dk, dv = attend_back(p[0], kc, vc, p[1], p[2], p[3], p[4], p[5])
        return (carry[0] + dk, carry[1] + dv), dq

    empty = jnp.zeros(kc.shape, jnp.bfloat16)
    (dk_c, dv_c), dq_c = lax.scan(
        piece,
        (empty, empty),
        tuple(cut(v) for v in (qc, cross_low, cross_high, d_oc, o_c_f, tot_c)),
    )
    dq_c = dq_c.reshape(rows, -1)
    g_wcq, g_wck, g_wcv = left_grad(a_b, dq_c), left_grad(all_memory, dk_c), left_grad(all_memory, dv_c)
    mem_grad = back_through(dk_c, wck) + back_through(dv_c, wcv)
    d_pre_self, g_ga, g_sa = pull_self(d_pre_cross + back_through(dq_c, wcq))
    d_sb = d_pre_self.astype(low)
    g_wso = left_grad(o_self, d_sb)
    d_os = back_through(d_sb, wso).astype(low)
    dq, dk, dv = attend_back(q, k, v, self_low, self_high, d_os, o_self_f, tot_self)
    g_wsq, g_wsk, g_wsv = left_grad(target_in, dq), left_grad(target_in, dk), left_grad(target_in, dv)
    target_grad = d_pre_self + back_through(dq, wsq) + back_through(dk, wsk) + back_through(dv, wsv)
    n_g = jnp.pad(jnp.stack([g_ga, g_sa, g_gc, g_sc, g_gf, g_sf], axis=1), ((0, 0), (0, NORM - 6)))
    g_w2p = g_w2.reshape(32, 4, 16, SLAB).transpose(0, 2, 1, 3).reshape(512, 4 * SLAB)
    grads = jnp.concatenate([g.astype(low) for g in (n_g, g_wsq, g_wsk, g_wsv, g_wso, g_wcq, g_wck, g_wcv, g_wco, g_w1, g_w2p)], axis=1)
    part = lambda i, n=1: out[:, NORM + SLAB * i : NORM + SLAB * (i + n)]
    out, w2_grad, mem_out = scatter_any(grads, mem_grad.astype(low))
    return (final.astype(low), target_grad, mem_out) + tuple(part(i) for i in range(8)) + (part(8, 4), w2_grad) + tuple(out[:, i] for i in range(6))


TILE = 128
EPS = 1e-05
HIDE = -1e30
LOW = jnp.bfloat16
F32 = jnp.float32
DEV = 32
CUT = NORM + 12 * SLAB


def mm(a, b):
    return jnp.dot(a, b, preferred_element_type=F32)


def mmt(a, b):
    return lax.dot_general(a, b, (((1,), (1,)), ((), ())), preferred_element_type=F32)


def tmm(a, b):
    return lax.dot_general(a, b, (((0,), (0,)), ((), ())), preferred_element_type=F32)


def lane_iota(shape):
    return lax.broadcasted_iota(jnp.int32, shape, len(shape) - 1)


def row_iota(shape):
    return lax.broadcasted_iota(jnp.int32, shape, 0)


def halves():
    lane = lane_iota((1, TILE))
    even = jnp.where(lane < 64, 1.0, 0.0).astype(LOW)
    odd = jnp.where(lane < 64, 0.0, 1.0).astype(LOW)
    return even, odd


def stacked(block, even, odd):
    return jnp.concatenate([block * even, block * odd], axis=0)


def fold(pair):
    lane = lane_iota((TILE, TILE))
    return jnp.where(lane < 64, pair[:TILE], pair[TILE:])


def totals_block(even, odd):
    wide = lambda v: jnp.broadcast_to(v, (TILE, TILE))
    return jnp.concatenate([wide(even), wide(odd)], axis=0)


def corr_block():
    lane = lane_iota((TILE, TILE))
    a = jnp.where(lane < 2, 1.0, 0.0).astype(LOW)
    b = jnp.where((lane >= 64) & (lane < 66), 1.0, 0.0).astype(LOW)
    return jnp.concatenate([a, b], axis=0)


def tile_forward(rows, keys, bias, q, k, v, num, tot):
    even, odd = halves()
    ones = totals_block(even, odd)
    bias2 = jnp.concatenate([bias, bias], axis=1)
    for h in range(4):
        cols = pl.ds(TILE * h, TILE)
        s = mmt(q[rows, cols], stacked(k[keys, cols], even, odd))
        e = jnp.exp(s + bias2).astype(LOW)
        both = mm(e, jnp.concatenate([stacked(v[keys, cols], even, odd), ones], axis=1))
        num[rows, cols] += both[:, :TILE]
        tot[rows, cols] += both[:, TILE:]


def tile_backward(rows, keys, bias, q, k, v, dnx, dq, dk, dv):
    even, odd = halves()
    ones = corr_block()
    bias2 = jnp.concatenate([bias, bias], axis=1)
    for h in range(4):
        cols = pl.ds(TILE * h, TILE)
        qb = q[rows, cols]
        ks = stacked(k[keys, cols], even, odd)
        e = jnp.exp(mmt(qb, ks) + bias2)
        vs = jnp.concatenate([stacked(v[keys, cols], even, odd), ones], axis=1)
        flow = mmt(dnx[rows, pl.ds(2 * TILE * h, 2 * TILE)], vs)
        ds = (e * flow).astype(LOW)
        dq[rows, cols] += mm(ds, ks)
        dk[keys, cols] += fold(tmm(ds, qb))
        dv[keys, cols] += fold(tmm(e.astype(LOW), dnx[rows, pl.ds(2 * TILE * h, TILE)]))


def each(count, body):
    def step(i, carry):
        body(i)
        return carry
    lax.fori_loop(0, count, step, 0)


def zero(ref, step=128):
    def body(i):
        rows = pl.ds(pl.multiple_of(i * step, step), step)
        ref[rows] = jnp.zeros((step,) + ref.shape[1:], ref.dtype)
    each(ref.shape[0] // step, body)


def compute_kernel(lens_ref, spans_ref, offs_ref, target, out_grad, memory, gathered,
                   layer_out, target_grad, grads, mem_grads,
                   w, w2, x, og, mem, qs, ks, vs, qc, kc, vc, big, act, dhid, dv,
                   num_s, tot_s, num_c, tot_c, xh1, xh2, t1, dpre, dq, rs1, rs2, low_s, o_b, oc_b, a_b, c_b,
                   g_b, dnx, ng, gb, lout,
                   starts, in_sem, w_sem, out_sem):
    n_src = mem.shape[0]
    rows_all = x.shape[0]
    n_sent = starts.shape[0] - 1
    member = lax.axis_index("mem")
    base = member * n_sent

    loads = {}

    def load(name, src, dst, sem):
        loads[name] = pltpu.make_async_copy(src, dst, sem)
        loads[name].start()

    load("x", target, x, in_sem.at[0])
    load("norm", gathered.at[:, :, pl.ds(0, NORM)], w.at[:, :, pl.ds(0, NORM)], w_sem.at[12])
    for i in range(3):
        lanes = pl.ds(NORM + SLAB * i, SLAB)
        load(i, gathered.at[:, :, lanes], w.at[:, :, lanes], w_sem.at[i])
    load("mem", memory, mem, in_sem.at[1])
    for i in (3, 5, 6, 4, 7):
        lanes = pl.ds(NORM + SLAB * i, SLAB)
        load(i, gathered.at[:, :, lanes], w.at[:, :, lanes], w_sem.at[i])
    lanes = pl.ds(NORM + SLAB * 8, 4 * SLAB)
    load("w1", gathered.at[:, :, lanes], w.at[:, :, lanes], w_sem.at[8])
    for k in range(4):
        load(("w2", k), gathered.at[:, :, pl.ds(CUT + SLAB * k, SLAB)], w2.at[:, k], w_sem.at[13 + k])
    load("og", out_grad, og, in_sem.at[2])

    outs = []

    def send(src, dst):
        copy = pltpu.make_async_copy(src, dst, out_sem.at[len(outs)])
        copy.start()
        outs.append(copy)

    def weight(i, part=None, width=256):
        if part is None:
            return w[:, :, pl.ds(NORM + SLAB * i, SLAB)].reshape(SLAB, SLAB)
        start = pl.multiple_of(NORM + SLAB * i + part * width, TILE)
        return w[:, :, pl.ds(start, width)].reshape(SLAB, width)

    def weight_rows(i, part, width=256, lanes=SLAB):
        devs = pl.ds(pl.multiple_of(part * (width // ROWS), width // ROWS), width // ROWS)
        return w[devs, :, pl.ds(NORM + SLAB * i, lanes)].reshape(width, lanes)

    def put_weight(i, part, value, width=256):
        start = pl.multiple_of(NORM + SLAB * i + part * width, TILE)
        w[:, :, pl.ds(start, width)] = value.astype(LOW).reshape(DEV, ROWS, width)

    def columns(part, width=256):
        return pl.ds(pl.multiple_of(part * width, width), width)

    def block(i, width=TILE):
        return pl.ds(pl.multiple_of(i * width, width), width)

    def count(j, at):
        starts[j] = at
        return at + lens_ref[0, base + j]
    starts[n_sent] = lax.fori_loop(0, n_sent, count, jnp.int32(0))

    def lows(i):
        row = i * TILE + row_iota((TILE, TILE))

        def pick(j, found):
            return jnp.where(row >= starts[j], starts[j], found)
        low_s[block(i)] = lax.fori_loop(0, n_sent, pick, jnp.zeros((TILE, TILE), jnp.int32))
    each(rows_all // TILE, lows)
    zero(num_s)
    zero(tot_s)
    zero(num_c)
    zero(tot_c)
    ng[...] = jnp.zeros_like(ng)

    loads["norm"].wait()
    gb[...] = jnp.transpose(w[:, :, pl.ds(0, NORM)].reshape(SLAB, NORM).astype(F32))[:8]
    loads["x"].wait()
    for i, dst in ((0, qs), (1, ks), (2, vs)):
        loads[i].wait()

        def project(n, i=i, dst=dst):
            value = mm(x[...], weight(i, n)).astype(LOW)
            dst[:, columns(n)] = value * jnp.asarray(0.125, LOW) if i == 0 else value
        each(2, project)

    def self_bias(i, kt):
        key = kt * TILE + lane_iota((TILE, TILE))
        row = i * TILE + row_iota((TILE, TILE))
        return jnp.where((key >= low_s[block(i)]) & (key <= row), 0.0, HIDE)

    def first_key(i):
        def pick(j, found):
            return jnp.where(starts[j] <= i * TILE, starts[j], found)
        return lax.fori_loop(0, n_sent, pick, jnp.int32(0)) // TILE

    def self_tiles(body):
        def outer(i, carry):
            def inner(kt, carry):
                body(block(i), block(kt), self_bias(i, kt))
                return carry
            return lax.fori_loop(first_key(i), i + 1, inner, carry)
        lax.fori_loop(0, rows_all // TILE, outer, 0)

    def cross_tiles(body):
        def outer(j, carry):
            begin, end = starts[j], starts[j + 1]
            low = offs_ref[0, base + j]
            high = low + spans_ref[0, base + j]
            at = pl.multiple_of(jnp.minimum((low // ROWS) * ROWS, n_src - TILE), ROWS)

            def inner(b, carry):
                key = at + lane_iota((TILE, TILE))
                row = b * TILE + row_iota((TILE, TILE))
                inside = (key >= low) & (key < high) & (row >= begin) & (row < end)
                body(block(b), pl.ds(at, TILE), jnp.where(inside, 0.0, HIDE))
                return carry
            return lax.fori_loop(begin // TILE, (end - 1) // TILE + 1, inner, carry)
        lax.fori_loop(0, n_sent, outer, 0)

    self_tiles(lambda r, k, bias: tile_forward(r, k, bias, qs, ks, vs, num_s, tot_s))

    def divide(num, tot, out):
        def body(i):
            r = block(i, 64)
            o = num[r] / tot[r]
            num[r] = o
            out[r] = o.astype(LOW)
        each(rows_all // 64, body)

    divide(num_s, tot_s, o_b)

    def normalize(y):
        mean = jnp.mean(y, axis=1, keepdims=True)
        centre = y - mean
        r = lax.rsqrt(jnp.mean(centre * centre, axis=1, keepdims=True) + EPS)
        return centre * r, r

    def back_norm(u, gain, xh, r):
        gu = u * gain
        a = jnp.mean(gu, axis=1, keepdims=True)
        b = jnp.mean(gu * xh, axis=1, keepdims=True)
        return (gu - a - xh * b) * r

    loads[3].wait()

    def self_out(n):
        t1[:, columns(n)] = x[:, columns(n)].astype(F32) + mm(o_b[...], weight(3, n))
    each(2, self_out)

    def norm_self(i):
        r = block(i, 64)
        xh, rs = normalize(t1[r])
        xh1[r] = xh
        rs1[r] = jnp.broadcast_to(rs, (64, TILE))
        after = xh * gb[0:1] + gb[1:2]
        t1[r] = after
        a_b[r] = after.astype(LOW)
    each(rows_all // 64, norm_self)

    for i in (4, 5, 6):
        loads[i].wait()
    loads["mem"].wait()

    def query(n):
        qc[:, columns(n)] = mm(a_b[...], weight(4, n)).astype(LOW) * jnp.asarray(0.125, LOW)
    each(2, query)

    def keys(i):
        r = block(i // 2, SLAB)
        n = i % 2
        kc[r, columns(n)] = mm(mem[r], weight(5, n)).astype(LOW)
        vc[r, columns(n)] = mm(mem[r], weight(6, n)).astype(LOW)
    each(2 * n_src // SLAB, keys)

    cross_tiles(lambda r, k, bias: tile_forward(r, k, bias, qc, kc, vc, num_c, tot_c))
    divide(num_c, tot_c, oc_b)
    loads[7].wait()

    def cross_out(n):
        t1[:, columns(n)] += mm(oc_b[...], weight(7, n))
    each(2, cross_out)

    def norm_cross(i):
        r = block(i, 64)
        xh, rs = normalize(t1[r])
        xh2[r] = xh
        rs2[r] = jnp.broadcast_to(rs, (64, TILE))
        after = xh * gb[2:3] + gb[3:4]
        t1[r] = after
        c_b[r] = after.astype(LOW)
    each(rows_all // 64, norm_cross)

    loads["w1"].wait()

    def hidden(n):
        v = mm(c_b[...], weight(8, n))
        sig = 1.0 / (1.0 + jnp.exp(-v))
        act[:, columns(n)] = (v * sig).astype(LOW)
        big[block(n // 2, SLAB), columns(n % 2)] = sig * (1.0 + v * (1.0 - sig))
    each(8, hidden)
    for k in range(4):
        loads[("w2", k)].wait()

    def ffn_out(n):
        cols = columns(n)
        t1[:, cols] += mm(act[...], w2[:, :, :, cols].reshape(4 * SLAB, 256))
    each(2, ffn_out)
    loads["og"].wait()

    def norm_ffn(i):
        r = block(i, 64)
        xh, rs = normalize(t1[r])
        gain = gb[4:5]
        lout[r] = (xh * gain + gb[5:6]).astype(LOW)
        u = og[r].astype(F32)
        ng[4:5] += jnp.sum(u * xh, axis=0, keepdims=True)
        ng[5:6] += jnp.sum(u, axis=0, keepdims=True)
        d = back_norm(u, gain, xh, rs)
        dpre[r] = d
        g_b[r] = d.astype(LOW)
    each(rows_all // 64, norm_ffn)
    send(lout, layer_out)

    def hidden_back(n):
        devs = pl.ds(pl.multiple_of(n * 4, 4), 4)
        part = mmt(g_b[...], w2[devs].reshape(256, SLAB))
        d = (part * big[block(n // 2, SLAB), columns(n % 2)]).astype(LOW)
        dhid[:, columns(n)] = d
        w2[devs] = tmm(act[:, columns(n)], g_b[...]).astype(LOW).reshape(4, 4, ROWS, SLAB)
    each(8, hidden_back)
    for k in range(4):
        send(w2.at[:, k], grads.at[:, :, pl.ds(CUT + SLAB * k, SLAB)])

    def input_back(n):
        dpre[:, columns(n)] += mmt(dhid[...], weight_rows(8, n, 256, 4 * SLAB))
    each(2, input_back)

    def first_grad(n):
        put_weight(8, n, tmm(c_b[...], dhid[:, columns(n)]))
    each(8, first_grad)
    lanes = pl.ds(NORM + SLAB * 8, 4 * SLAB)
    send(w.at[:, :, lanes], grads.at[:, :, lanes])

    def back_cross(i):
        r = block(i, 64)
        u, xh = dpre[r], xh2[r]
        ng[2:3] += jnp.sum(u * xh, axis=0, keepdims=True)
        ng[3:4] += jnp.sum(u, axis=0, keepdims=True)
        d = back_norm(u, gb[2:3], xh, rs2[r][:, :1])
        dpre[r] = d
        g_b[r] = d.astype(LOW)
    each(rows_all // 64, back_cross)

    def out_back(i, o_low, num, tot):
        lane = lane_iota((TILE, TILE))
        same = jnp.where((lane < 64) == (row_iota((TILE, TILE)) < 64), 1.0, 0.0).astype(LOW)
        half = lane % 64

        def body(n):
            up = mmt(g_b[...], weight_rows(i, n)).astype(LOW).astype(F32)
            for h in range(2):
                cols = pl.ds(pl.multiple_of(n * 256 + h * TILE, TILE), TILE)
                wide = lambda k: pl.ds(pl.multiple_of(n * 512 + h * 256 + k * TILE, TILE), TILE)
                d = up[:, h * TILE:(h + 1) * TILE]
                t = tot[:, cols]
                dnx[:, wide(0)] = (d / t).astype(LOW)
                p = d * num[:, cols]
                p1 = p.astype(LOW)
                p2 = (p - p1.astype(F32)).astype(LOW)
                corr = -(mm(p1, same) + mm(p2, same)) / t
                c1 = corr.astype(LOW)
                c2 = (corr - c1.astype(F32)).astype(LOW)
                place = lane_iota(c1.shape) % 64
                nothing = jnp.zeros_like(c1)
                dnx[:, wide(1)] = jnp.where(place == 0, c1, jnp.where(place == 1, c2, nothing))
        each(2, body)

        def grad(n):
            put_weight(i, n, tmm(o_low[...], g_b[:, columns(n)]))
        each(2, grad)

    def send_slab(i):
        lanes = pl.ds(NORM + SLAB * i, SLAB)
        send(w.at[:, :, lanes], grads.at[:, :, lanes])

    out_back(7, oc_b, num_c, tot_c)
    send_slab(7)
    zero(dq)
    zero(big)
    zero(dv)
    cross_tiles(lambda r, k, bias: tile_backward(r, k, bias, qc, kc, vc, dnx, dq, big, dv))

    def scaled(src, dst, factor, step=64):
        def body(i):
            r = block(i, step)
            dst[r] = (src[r] * factor).astype(LOW)
        each(src.shape[0] // step, body)

    scaled(dq, qc, 0.125)
    scaled(big, kc, 1.0)
    scaled(dv, vc, 1.0)

    def query_back(n):
        dpre[:, columns(n)] += mmt(qc[...], weight_rows(4, n))
    each(2, query_back)

    def query_grad(n):
        put_weight(4, n, tmm(a_b[...], qc[:, columns(n)]))
    each(2, query_grad)
    send_slab(4)

    def memory_back(i):
        r = block(i // 2, SLAB)
        n = i % 2
        big[r, columns(n)] = mmt(kc[r], weight_rows(5, n)) + mmt(vc[r], weight_rows(6, n))
    each(2 * n_src // SLAB, memory_back)

    def memory_low(i):
        r = block(i, SLAB)
        dhid[:, pl.ds(0, SLAB)] = big[r].astype(LOW)
        copy = pltpu.make_async_copy(dhid.at[:, pl.ds(0, SLAB)], mem_grads.at[r], in_sem.at[3])
        copy.start()
        copy.wait()
    each(n_src // SLAB, memory_low)

    def key_grad(n):
        put_weight(5, n, tmm(mem[...], kc[:, columns(n)]))
        put_weight(6, n, tmm(mem[...], vc[:, columns(n)]))
    each(2, key_grad)
    send_slab(5)
    send_slab(6)

    def back_self(i):
        r = block(i, 64)
        u, xh = dpre[r], xh1[r]
        ng[0:1] += jnp.sum(u * xh, axis=0, keepdims=True)
        ng[1:2] += jnp.sum(u, axis=0, keepdims=True)
        d = back_norm(u, gb[0:1], xh, rs1[r][:, :1])
        dpre[r] = d
        g_b[r] = d.astype(LOW)
    each(rows_all // 64, back_self)
    out_back(3, o_b, num_s, tot_s)
    send_slab(3)
    zero(dq)
    dk_s, dv_s = t1, dv.at[pl.ds(0, rows_all)]
    zero(dk_s)
    zero(dv_s)
    self_tiles(lambda r, k, bias: tile_backward(r, k, bias, qs, ks, vs, dnx, dq, dk_s, dv_s))
    scaled(dq, qs, 0.125)
    scaled(dk_s, ks, 1.0)
    scaled(dv_s, vs, 1.0)

    def target_back(n):
        total = mmt(qs[...], weight_rows(0, n)) + mmt(ks[...], weight_rows(1, n))
        dpre[:, columns(n)] += total + mmt(vs[...], weight_rows(2, n))
    each(2, target_back)
    send(dpre, target_grad)
    for i, src in ((0, qs), (1, ks), (2, vs)):
        def grad(n, i=i, src=src):
            put_weight(i, n, tmm(x[...], src[:, columns(n)]))
        each(2, grad)
        send_slab(i)
    padded = jnp.concatenate([ng[...], jnp.zeros((NORM - 8, SLAB), F32)], axis=0)
    w[:, :, pl.ds(0, NORM)] = jnp.transpose(padded).astype(LOW).reshape(DEV, ROWS, NORM)
    send(w.at[:, :, pl.ds(0, NORM)], grads.at[:, :, pl.ds(0, NORM)])
    for copy in outs:
        copy.wait()


def compute(lens, spans, offs, target, out_grad, memory, gathered):
    rows, n_src = target.shape[0], memory.shape[0]
    n_sent = 16
    any_space = pl.BlockSpec(memory_space=pl.ANY)
    smem = pl.BlockSpec(memory_space=pltpu.SMEM)
    dma = pltpu.SemaphoreType.DMA
    f32 = lambda *s: pltpu.VMEM(s, F32)
    low = lambda *s: pltpu.VMEM(s, LOW)
    return pl.pallas_call(
        compute_kernel,
        out_shape=(
            jax.ShapeDtypeStruct((rows, SLAB), LOW),
            jax.ShapeDtypeStruct((rows, SLAB), F32),
            jax.ShapeDtypeStruct((DEV, ROWS, LANES), LOW),
            jax.ShapeDtypeStruct((n_src, SLAB), LOW),
        ),
        in_specs=[smem] * 3 + [any_space] * 4,
        out_specs=(any_space,) * 4,
        scratch_shapes=[
            low(DEV, ROWS, CUT),
            low(DEV, 4, ROWS, SLAB),
            low(rows, SLAB),
            low(rows, SLAB),
            low(n_src, SLAB),
            low(rows, SLAB),
            low(rows, SLAB),
            low(rows, SLAB),
            low(rows, SLAB),
            low(n_src, SLAB),
            low(n_src, SLAB),
            f32(max(n_src, 4 * SLAB), SLAB),
            low(rows, 4 * SLAB),
            low(rows, 4 * SLAB),
            f32(n_src, SLAB),
            f32(rows, SLAB),
            f32(rows, SLAB),
            f32(rows, SLAB),
            f32(rows, SLAB),
            f32(rows, SLAB),
            f32(rows, SLAB),
            f32(rows, SLAB),
            f32(rows, SLAB),
            f32(rows, SLAB),
            f32(rows, TILE),
            f32(rows, TILE),
            pltpu.VMEM((rows, TILE), jnp.int32),
            low(rows, SLAB),
            low(rows, SLAB),
            low(rows, SLAB),
            low(rows, SLAB),
            low(rows, SLAB),
            low(rows, 2 * SLAB),
            f32(8, SLAB),
            f32(8, SLAB),
            low(rows, SLAB),
            pltpu.SMEM((n_sent + 1,), jnp.int32),
            dma((4,)),
            dma((17,)),
            dma((17,)),
        ],
        compiler_params=pltpu.CompilerParams(vmem_limit_bytes=60 << 20),
        name="compute",
    )(lens, spans, offs, target, out_grad, memory, gathered)


def local(target_in, memory, out_grad, *rest):
    fast = two_by_two((lax.axis_size("dp"), lax.axis_size("mem")))
    if not fast:
        return plain(target_in, memory, out_grad, *rest)
    weights, tables = rest[:16], rest[16:]
    norms = jnp.stack(weights[10:], axis=1)
    norms = jnp.pad(norms, ((0, 0), (0, NORM - norms.shape[1])))
    gathered, all_memory = gather_all(weights[:10], norms, memory)
    layer_out, target_grad, grads, mem_grads = compute(*tables, target_in, out_grad, all_memory, gathered)
    rows = target_in.shape[0]
    out, mem_out = scatter_all(
        grads.reshape(4, 2, 2, 2, ROWS, LANES), mem_grads.reshape(2, 2, rows, SLAB))
    part = lambda i, n=1: out[:, NORM + SLAB * i : NORM + SLAB * (i + n)]
    w2_grad = jnp.concatenate([part(12 + k) for k in range(4)], axis=0)
    return (
        (layer_out, target_grad, mem_out)
        + tuple(part(i) for i in range(8))
        + (part(8, 4), w2_grad)
        + tuple(out[:, i] for i in range(6))
    )


def solution(mesh):
    both = P(("dp", "mem"), None)
    flat = P(("dp", "mem"))
    in_specs = (both,) * 13 + (flat,) * 6 + (P("dp", None),) * 3
    out_specs = (both,) * 13 + (flat,) * 6
    return jax.shard_map(local, mesh=mesh, in_specs=in_specs, out_specs=out_specs, check_vma=False)
```

```python
import functools

import jax
import jax.numpy as jnp
from jax import lax
from jax.experimental import pallas as pl
from jax.experimental.pallas import tpu as pltpu
from jax.sharding import PartitionSpec as P

MESH = pl.DeviceIdType.MESH
SLAB = 512
NORM = 128
LANES = NORM + 16 * SLAB
ROWS = 16


def here():
    dp, mem = lax.axis_index("dp"), lax.axis_index("mem")
    return dp // 2, dp % 2, mem // 2, mem % 2


def device(z, x, y, c):
    return (z * 2 + x, y * 2 + c)


def greet(peers):
    barrier = pltpu.get_barrier_semaphore()
    for peer in peers:
        pl.semaphore_signal(barrier, inc=1, device_id=peer, device_id_type=MESH)
    pl.semaphore_wait(barrier, len(peers))


def remote(src, dst, sems, index, peer):
    send, recv = sems
    return pltpu.make_async_remote_copy(
        src_ref=src,
        dst_ref=dst,
        send_sem=send.at[index],
        recv_sem=recv.at[index],
        device_id=peer,
        device_id_type=MESH,
    )


def cuts(widths, share):
    spans, at = [], 0
    for tiles in widths:
        n = tiles * 128
        spans.append((at, at + max(1, round(tiles * share)) * 128, at + n))
        at += n
    assert at == LANES
    return tuple(spans)


GATHER_ROUNDS = cuts((33, 32), 0.25)


def gather_kernel(*refs):
    shards, norm_ref, memory_ref = refs[:10], refs[10], refs[11]
    out, mem_out, local_sem, mem_local = refs[12:16]
    z_sems, first_sems, second_sems = refs[16:18], refs[18:20], refs[20:22]
    across, mems = refs[22:24], refs[24:26]
    z, x, y, c = here()
    xp, yp, cp_ = device(z, 1 - x, y, c), device(z, x, 1 - y, c), device(z, x, y, 1 - c)
    own = out.at[z, x, y, c]
    rounds = range(len(GATHER_ROUNDS))

    local = []

    def bring(src, start, width):
        local.append(
            pltpu.make_async_copy(src, own.at[:, pl.ds(start, width)], local_sem.at[len(local)])
        )

    bring(norm_ref, 0, NORM)
    for i in range(8):
        bring(shards[i], NORM + SLAB * i, SLAB)
    bring(shards[8], NORM + SLAB * 8, 4 * SLAB)
    for k in range(4):
        bring(shards[9].at[pl.ds(ROWS * k, ROWS)], NORM + SLAB * (12 + k), SLAB)
    for one in local:
        one.start()
    keep = pltpu.make_async_copy(memory_ref, mem_out.at[y, c], mem_local)
    keep.start()
    zn = [device((z + k) % 4, x, y, c) for k in (1, 3)]
    greet([xp, yp, cp_] + zn)
    for one in local:
        one.wait()

    def column(slot):
        return z if slot == 0 else (z - slot if slot < 4 else z + (slot - 3))

    def there(slot):
        return None if slot == 0 else (z >= slot if slot < 4 else z <= 6 - slot)

    def both(a, b):
        return b if a is None else (a if b is None else jnp.logical_and(a, b))

    def guarded(cond, body):
        if cond is None:
            body()
        else:
            pl.when(cond)(body)

    sent = []

    def go(make, cond=None):
        guarded(cond, lambda: make().start())
        sent.append((cond, make))

    def along(slot, r, up):
        a, _, b = GATHER_ROUNDS[r]
        ref = out.at[column(slot), x, y, c, :, pl.ds(a, b - a)]
        d = 0 if slot == 0 else (slot if slot < 4 else slot - 3)
        peer = device((z + (1 if up else 3)) % 4, x, y, c)
        return remote(ref, ref, z_sems, (0 if up else 1, d, r), peer)

    def arrived(slot, r):
        a, _, b = GATHER_ROUNDS[r]
        ref = out.at[column(slot), x, y, c, :, pl.ds(a, b - a)]
        up = slot < 4
        index = (0 if up else 1, (slot if up else slot - 3) - 1, r)
        return remote(ref, ref, z_sems, index, xp)

    def first(slot, r, part, arriving=False):
        a, m, b = GATHER_ROUNDS[r]
        zz = column(slot)
        if part == 0:
            ref = out.at[zz, (1 - x) if arriving else x, y, c, :, pl.ds(a, m - a)]
        else:
            ref = out.at[zz, x, (1 - y) if arriving else y, c, :, pl.ds(m, b - m)]
        return remote(ref, ref, first_sems, (slot, part, r), xp if part == 0 else yp)

    def second(slot, r, part, hop, arriving=False):
        a, m, b = GATHER_ROUNDS[r]
        zz = column(slot)
        if part == 0:
            side = (1 - x) if hop else x
            ref = out.at[zz, side, (1 - y) if arriving else y, c, :, pl.ds(a, m - a)]
        else:
            side = (1 - y) if hop else y
            ref = out.at[zz, (1 - x) if arriving else x, side, c, :, pl.ds(m, b - m)]
        return remote(ref, ref, second_sems, (slot, part, hop, r), yp if part == 0 else xp)

    def over(slot, r, arriving=False):
        a, _, b = GATHER_ROUNDS[r]
        ref = out.at[column(slot), :, :, (1 - c) if arriving else c, :, pl.ds(a, b - a)]
        return remote(ref, ref, across, (slot, r), cp_)

    def spread(slot, r):
        cond = there(slot)
        for part in (1, 0):
            go(functools.partial(first, slot, r, part), cond)
        for part in (1, 0):
            go(functools.partial(second, slot, r, part, 0), cond)

    def from_z(d):
        for r in rounds:
            for slot in (d, d + 3):
                cond = there(slot)
                guarded(cond, lambda slot=slot, r=r: arrived(slot, r).wait_recv())
                if d < 3:
                    onward = z < 3 if slot < 4 else z > 0
                    go(functools.partial(along, slot, r, slot < 4), both(cond, onward))
                spread(slot, r)

    def pass_on(slots):
        for r in rounds:
            for slot in slots:
                cond = there(slot)
                for part in (1, 0):
                    guarded(cond, lambda s=slot, r=r, p=part: first(s, r, p, True).wait_recv())
                    go(functools.partial(second, slot, r, part, 1), cond)

    def hand_over(slots):
        for r in rounds:
            for slot in slots:
                cond = there(slot)
                for part in (0, 1):
                    for hop in (0, 1):
                        guarded(cond, lambda s=slot, r=r, p=part, h=hop: second(s, r, p, h, True).wait_recv())
                go(functools.partial(over, slot, r), cond)

    for r in rounds:
        go(functools.partial(along, 0, r, True), z < 3)
        go(functools.partial(along, 0, r, False), z > 0)
        spread(0, r)
    mem_own = mem_out.at[y, c]
    from_z(1)
    pass_on((0,))
    from_z(2)
    pass_on((1, 4))
    hand_over((0,))
    keep.wait()
    go(lambda: remote(mem_own, mem_own, mems, 0, yp))
    go(lambda: remote(mem_own, mem_own, mems, 1, cp_))
    from_z(3)
    pass_on((2, 5))
    hand_over((1, 4))
    far = mem_out.at[1 - y, c]
    remote(far, far, mems, 0, yp).wait_recv()
    go(lambda: remote(far, far, mems, 2, cp_))
    pass_on((3, 6))
    hand_over((2, 5))
    hand_over((3, 6))
    for slot in (0, 1, 4, 2, 5, 3, 6):
        for r in rounds:
            guarded(there(slot), lambda s=slot, r=r: over(s, r, True).wait_recv())
    for i, side in ((1, y), (2, 1 - y)):
        block = mem_out.at[side, 1 - c]
        remote(block, block, mems, i, cp_).wait_recv()
    for cond, make in sent:
        guarded(cond, lambda make=make: make().wait_send())


def gather_all(shards, norms, memory):
    any_space = pl.BlockSpec(memory_space=pl.ANY)
    dma = pltpu.SemaphoreType.DMA
    n = len(GATHER_ROUNDS)
    both = lambda *s: [dma(s), dma(s)]
    gathered, whole_memory = pl.pallas_call(
        gather_kernel,
        out_shape=(
            jax.ShapeDtypeStruct((4, 2, 2, 2, ROWS, LANES), jnp.bfloat16),
            jax.ShapeDtypeStruct((2, 2) + memory.shape, jnp.bfloat16),
        ),
        in_specs=[any_space] * 12,
        out_specs=(any_space, any_space),
        scratch_shapes=[dma((14,)), dma(())]
        + both(2, 3, n) + both(7, 2, n) + both(7, 2, 2, n) + both(7, n) + both(3),
        compiler_params=pltpu.CompilerParams(collective_id=1, has_side_effects=True),
        name="gather",
    )(*shards, norms, memory)
    return gathered.reshape(32, ROWS, LANES), whole_memory.reshape(-1, SLAB)
SCATTER_ROUNDS = ((4224, 4736, 6272), (6272, 6784, 8320), (2176, 2688, 4224), (0, 640, 2176))


def scatter_kernel(grads, mem_grads, out, mem_out, acc, from_core, from_first, from_second, from_z,
                   macc, mfrom_core, mfrom_y, own_sems, mown_sem, core_s, core_r, first_s, first_r,
                   second_s, second_r, zs_s, zs_r, mem_s, mem_r):
    z, x, y, c = here()
    xp, yp, cp_ = device(z, 1 - x, y, c), device(z, x, 1 - y, c), device(z, x, y, 1 - c)
    zp = [device((z + k) % 4, x, y, c) for k in (1, 2, 3)]
    count = len(SCATTER_ROUNDS)
    core_sems, first_sems, second_sems = (core_s, core_r), (first_s, first_r), (second_s, second_r)
    z_sems, mem_sems = (zs_s, zs_r), (mem_s, mem_r)
    sent = []

    def go(copy):
        copy.start()
        sent.append(copy)

    def span(r, part=None):
        a, m, b = SCATTER_ROUNDS[r]
        return {None: (a, b - a), 0: (a, m - a), 1: (m, b - m)}[part]

    def own(r):
        a, n = span(r)
        return pltpu.make_async_copy(
            grads.at[:, :, :, c, :, pl.ds(a, n)], acc.at[:, :, :, :, pl.ds(a, n)], own_sems.at[r])

    def core(r):
        a, n = span(r)
        return remote(grads.at[:, :, :, 1 - c, :, pl.ds(a, n)],
                      from_core.at[:, :, :, :, pl.ds(a, n)], core_sems, r, cp_)

    def first(r, part):
        lanes = pl.ds(*span(r, part))
        src = acc.at[:, :, 1 - y, :, lanes] if part == 0 else acc.at[:, 1 - x, :, :, lanes]
        return remote(src, from_first.at[:, :, :, lanes], first_sems, (r, part),
                      yp if part == 0 else xp)

    def second(r, part):
        lanes = pl.ds(*span(r, part))
        src = acc.at[:, 1 - x, y, :, lanes] if part == 0 else acc.at[:, x, 1 - y, :, lanes]
        return remote(src, from_second.at[:, :, lanes], second_sems, (r, part),
                      xp if part == 0 else yp)

    def along(r, k):
        lanes = pl.ds(*span(r))
        return remote(acc.at[(z + k + 1) % 4, x, y, :, lanes], from_z.at[k, :, lanes], z_sems,
                      (r, k), zp[k])

    mem_own = pltpu.make_async_copy(mem_grads.at[:, c], macc, mown_sem)
    mem_core = remote(mem_grads.at[:, 1 - c], mfrom_core, mem_sems, 0, cp_)
    mem_far = remote(macc.at[1 - y], mfrom_y, mem_sems, 1, yp)

    own(0).start()
    mem_own.start()
    for r in range(1, count):
        own(r).start()
    greet([xp, yp, cp_] + zp)
    go(core(0))
    go(mem_core)
    for r in range(1, count):
        go(core(r))

    def add_core(r):
        own(r).wait()
        core(r).wait_recv()
        for part in (0, 1):
            lanes = pl.ds(*span(r, part))
            for theirs in (True, False):
                def body(zi, carry, part=part, lanes=lanes, theirs=theirs):
                    for o in (0, 1):
                        if part == 0:
                            xi, yi = o, (1 - y) if theirs else y
                        else:
                            xi, yi = (1 - x) if theirs else x, o
                        acc[zi, xi, yi, :, lanes] = (
                            acc[zi, xi, yi, :, lanes] + from_core[zi, xi, yi, :, lanes])
                    return carry
                lax.fori_loop(0, 4, body, 0)
                if theirs:
                    go(first(r, part))

    def add_first(r):
        for part in (0, 1):
            first(r, part).wait_recv()
            lanes = pl.ds(*span(r, part))
            for theirs in (True, False):
                def body(zi, carry, part=part, lanes=lanes, theirs=theirs):
                    if part == 0:
                        xi, yi = (1 - x) if theirs else x, y
                        slot = xi
                    else:
                        xi, yi = x, (1 - y) if theirs else y
                        slot = yi
                    acc[zi, xi, yi, :, lanes] = (
                        acc[zi, xi, yi, :, lanes] + from_first[zi, slot, :, lanes])
                    return carry
                lax.fori_loop(0, 4, body, 0)
                if theirs:
                    go(second(r, part))

    def add_second(r):
        for part in (0, 1):
            second(r, part).wait_recv()
            lanes = pl.ds(*span(r, part))

            def body(zi, carry, lanes=lanes):
                acc[zi, x, y, :, lanes] = acc[zi, x, y, :, lanes] + from_second[zi, :, lanes]
                return carry
            lax.fori_loop(0, 4, body, 0)
        for k in (1, 0, 2):
            go(along(r, k))

    def add_z(r):
        lanes = pl.ds(*span(r))
        total = acc[z, x, y, :, lanes].astype(jnp.float32)
        for k in (0, 2, 1):
            along(r, k).wait_recv()
            total = total + from_z[k, :, lanes].astype(jnp.float32)
        out[:, lanes] = total

    def memory_core():
        mem_own.wait()
        mem_core.wait_recv()
        for theirs in (True, False):
            side = (1 - y) if theirs else y

            def body(i, carry, side=side):
                rows = pl.ds(pl.multiple_of(i * 64, 64), 64)
                macc[side, rows] = macc[side, rows] + mfrom_core[side, rows]
                return carry
            lax.fori_loop(0, 8, body, 0)
            if theirs:
                go(mem_far)

    def memory_end():
        mem_far.wait_recv()

        def body(i, carry):
            rows = pl.ds(pl.multiple_of(i * 64, 64), 64)
            mem_out[rows] = macc[y, rows].astype(jnp.float32) + mfrom_y[rows].astype(jnp.float32)
            return carry
        lax.fori_loop(0, 8, body, 0)

    for t in range(count + 3):
        if t < count:
            add_core(t)
        if t == 0:
            memory_core()
        if 0 <= t - 1 < count:
            add_first(t - 1)
        if 0 <= t - 2 < count:
            add_second(t - 2)
        if 0 <= t - 3 < count:
            add_z(t - 3)
        if t == 3:
            memory_end()
    for copy in sent:
        copy.wait_send()


def scatter_all(grads, mem_grads):
    any_space = pl.BlockSpec(memory_space=pl.ANY)
    vmem = pl.BlockSpec(memory_space=pltpu.VMEM)
    dma = pltpu.SemaphoreType.DMA
    n = len(SCATTER_ROUNDS)
    rows = mem_grads.shape[2]
    low = jnp.bfloat16
    return pl.pallas_call(
        scatter_kernel,
        out_shape=(
            jax.ShapeDtypeStruct((ROWS, LANES), jnp.float32),
            jax.ShapeDtypeStruct((rows, SLAB), jnp.float32),
        ),
        in_specs=[any_space] * 2,
        out_specs=(vmem, vmem),
        scratch_shapes=[
            pltpu.VMEM((4, 2, 2, ROWS, LANES), low),
            pltpu.VMEM((4, 2, 2, ROWS, LANES), low),
            pltpu.VMEM((4, 2, ROWS, LANES), low),
            pltpu.VMEM((4, ROWS, LANES), low),
            pltpu.VMEM((3, ROWS, LANES), low),
            pltpu.VMEM((2, rows, SLAB), low),
            pltpu.VMEM((2, rows, SLAB), low),
            pltpu.VMEM((rows, SLAB), low),
            dma((n,)),
            dma(()),
            dma((n,)),
            dma((n,)),
            dma((n, 2)),
            dma((n, 2)),
            dma((n, 2)),
            dma((n, 2)),
            dma((n, 3)),
            dma((n, 3)),
            dma((2,)),
            dma((2,)),
        ],
        compiler_params=pltpu.CompilerParams(
            collective_id=2, has_side_effects=True, vmem_limit_bytes=48 << 20),
        name="scatter",
    )(grads, mem_grads)


def two_by_two(mesh_axes):
    return mesh_axes == (8, 4)


def gather_any(shards, norms, memory):
    everyone = ("dp", "mem")
    packed = jnp.concatenate([norms] + list(shards[:9]), axis=1)
    rows = lax.all_gather(packed, everyone, axis=0, tiled=True).reshape(32, ROWS, -1)
    last = lax.all_gather(shards[9], everyone, axis=0, tiled=True)
    last = last.reshape(32, 4, ROWS, SLAB).transpose(0, 2, 1, 3).reshape(32, ROWS, 4 * SLAB)
    return (
        jnp.concatenate([rows, last], axis=2),
        lax.all_gather(memory, "mem", axis=0, tiled=True),
    )


def scatter_any(grads, mem_grads):
    everyone = ("dp", "mem")
    wide = grads.reshape(32, ROWS, LANES).astype(jnp.float32)
    cut = LANES - 4 * SLAB
    rows = lax.psum_scatter(
        wide[:, :, :cut].reshape(512, cut), everyone, scatter_dimension=0, tiled=True
    )
    last = wide[:, :, cut:].reshape(32, ROWS, 4, SLAB).transpose(0, 2, 1, 3).reshape(2048, SLAB)
    last = lax.psum_scatter(last, everyone, scatter_dimension=0, tiled=True)
    mem = lax.psum_scatter(
        mem_grads.astype(jnp.float32), "mem", scatter_dimension=0, tiled=True
    )
    return rows, last, mem
HEADS = 8
HEAD = 64
eps_norm = 1e-05
score_scale = 0.125


def layer_norm(values, gain, shift):
    centre = values - jnp.mean(values, axis=-1, keepdims=True)
    spread = jnp.mean(centre * centre, axis=-1, keepdims=True)
    return centre * lax.rsqrt(spread + eps_norm) * gain + shift


def head_split(values):
    return values.reshape(values.shape[0], HEADS, HEAD)


def matmul(left, right):
    return jnp.dot(left, right, preferred_element_type=jnp.float32)


def left_grad(inputs, grads):
    return jnp.einsum("ra,rb->ab", inputs, grads, preferred_element_type=jnp.float32)


def back_through(grads, weight):
    return jnp.einsum("rb,ab->ra", grads, weight, preferred_element_type=jnp.float32)


def exp_scores(q_block, keys, low_edge, high_edge):
    raw = jnp.einsum("qhd,khd->hqk", head_split(q_block), head_split(keys),
                     preferred_element_type=jnp.float32) * score_scale
    position = lax.broadcasted_iota(jnp.int32, (q_block.shape[0], keys.shape[0]), 1)
    allowed = (position >= low_edge[:, None]) & (position < high_edge[:, None])
    return jnp.where(allowed[None], jnp.exp(raw), 0.0)


def attend(queries, keys, values, low_edge, high_edge):
    expo = exp_scores(queries, keys, low_edge, high_edge)
    numer = jnp.einsum("hqk,khd->qhd", expo.astype(jnp.bfloat16), head_split(values),
                       preferred_element_type=jnp.float32)
    totals = jnp.sum(expo, axis=2).T
    return (numer / totals[:, :, None]).reshape(queries.shape[0], -1), totals


def attend_back(queries, keys, values, low_edge, high_edge, upstream, output, totals):
    expo = exp_scores(queries, keys, low_edge, high_edge)
    up = head_split(upstream.astype(jnp.float32))
    numer_grad = (up / totals[:, :, None]).astype(jnp.bfloat16)
    corr = -jnp.sum(up * head_split(output), axis=2) / totals
    flow = jnp.einsum("qhd,khd->hqk", numer_grad, head_split(values),
                      preferred_element_type=jnp.float32) + corr.T[:, :, None]
    ds = (expo * flow).astype(jnp.bfloat16)
    dq = jnp.einsum("hqk,khd->qhd", ds, head_split(keys), preferred_element_type=jnp.float32)
    dk = jnp.einsum("hqk,qhd->khd", ds, head_split(queries), preferred_element_type=jnp.float32)
    dv = jnp.einsum("hqk,qhd->khd", expo.astype(jnp.bfloat16), numer_grad,
                    preferred_element_type=jnp.float32)
    flat = lambda v: v.reshape(v.shape[0], -1)
    return ((flat(dq) * score_scale).astype(jnp.bfloat16), (flat(dk) * score_scale).astype(jnp.bfloat16),
            flat(dv).astype(jnp.bfloat16))


def plain(target_in, memory, out_grad, *rest):
    weights, (tgt_lens, src_lens, src_offsets) = rest[:16], rest[16:]
    member = lax.axis_index("mem")
    per_device = tgt_lens.shape[1] // lax.axis_size("mem")
    pick = lambda table: lax.dynamic_slice_in_dim(table[0], member * per_device, per_device, 0)
    lengths, spans, offsets = pick(tgt_lens), pick(src_lens), pick(src_offsets)
    norms = jnp.stack(weights[10:], axis=1)
    norms = jnp.pad(norms, ((0, 0), (0, NORM - norms.shape[1])))
    gathered, all_memory = gather_any(weights[:10], norms, memory)
    W = gathered.reshape(512, LANES)
    mat = lambda i: W[:, NORM + SLAB * i : NORM + SLAB * (i + 1)]
    wsq, wsk, wsv, wso, wcq, wck, wcv, wco = [mat(i) for i in range(8)]
    w1 = W[:, NORM + 8 * SLAB : NORM + 12 * SLAB]
    w2 = gathered[:, :, NORM + 12 * SLAB :].reshape(32, 16, 4, SLAB).transpose(0, 2, 1, 3).reshape(2048, SLAB)
    ga, sa, gc, sc, gf, sf = [W[:, i].astype(jnp.float32) for i in range(6)]
    rows = target_in.shape[0]
    starts = jnp.cumsum(lengths) - lengths
    position = lax.iota(jnp.int32, rows)
    sentence = jnp.sum((position[:, None] >= starts[None, :]).astype(jnp.int32), axis=1) - 1
    picker = sentence[:, None] == lax.iota(jnp.int32, per_device)[None, :]
    choose = lambda v: jnp.sum(jnp.where(picker, v[None, :], 0), axis=1)
    self_low, self_high = choose(starts), position + 1
    cross_low = choose(offsets)
    cross_high = cross_low + choose(spans)
    low = jnp.bfloat16
    q, k, v = [matmul(target_in, w).astype(low) for w in (wsq, wsk, wsv)]
    o_self_f, tot_self = attend(q, k, v, self_low, self_high)
    o_self = o_self_f.astype(low)
    after_self, pull_self = jax.vjp(layer_norm, target_in.astype(jnp.float32) + matmul(o_self, wso), ga, sa)
    a_b = after_self.astype(low)
    qc = matmul(a_b, wcq).astype(low)
    kc, vc = matmul(all_memory, wck).astype(low), matmul(all_memory, wcv).astype(low)
    cut = lambda v: v.reshape((4, -1) + v.shape[1:])
    o_c_f, tot_c = lax.map(
        lambda p: attend(p[0], kc, vc, p[1], p[2]), (cut(qc), cut(cross_low), cut(cross_high))
    )
    o_c_f, tot_c = o_c_f.reshape(rows, -1), tot_c.reshape(rows, -1)
    o_c = o_c_f.astype(low)
    after_cross, pull_cross = jax.vjp(layer_norm, after_self + matmul(o_c, wco), gc, sc)
    c_b = after_cross.astype(low)
    hidden = matmul(c_b, w1)
    activated, pull_silu = jax.vjp(jax.nn.silu, hidden)
    act = activated.astype(low)
    final, pull_ffn = jax.vjp(layer_norm, after_cross + matmul(act, w2), gf, sf)
    d_pre_out, g_gf, g_sf = pull_ffn(out_grad.astype(jnp.float32))
    d_branch = d_pre_out.astype(low)
    g_w2 = left_grad(act, d_branch)
    d_hidden = pull_silu(back_through(d_branch, w2))[0].astype(low)
    g_w1 = left_grad(c_b, d_hidden)
    d_pre_cross, g_gc, g_sc = pull_cross(d_pre_out + back_through(d_hidden, w1))
    d_cb = d_pre_cross.astype(low)
    g_wco = left_grad(o_c, d_cb)
    d_oc = back_through(d_cb, wco).astype(low)

    def piece(carry, p):
        dq, dk, dv = attend_back(p[0], kc, vc, p[1], p[2], p[3], p[4], p[5])
        return (carry[0] + dk, carry[1] + dv), dq

    empty = jnp.zeros(kc.shape, jnp.bfloat16)
    (dk_c, dv_c), dq_c = lax.scan(
        piece,
        (empty, empty),
        tuple(cut(v) for v in (qc, cross_low, cross_high, d_oc, o_c_f, tot_c)),
    )
    dq_c = dq_c.reshape(rows, -1)
    g_wcq, g_wck, g_wcv = left_grad(a_b, dq_c), left_grad(all_memory, dk_c), left_grad(all_memory, dv_c)
    mem_grad = back_through(dk_c, wck) + back_through(dv_c, wcv)
    d_pre_self, g_ga, g_sa = pull_self(d_pre_cross + back_through(dq_c, wcq))
    d_sb = d_pre_self.astype(low)
    g_wso = left_grad(o_self, d_sb)
    d_os = back_through(d_sb, wso).astype(low)
    dq, dk, dv = attend_back(q, k, v, self_low, self_high, d_os, o_self_f, tot_self)
    g_wsq, g_wsk, g_wsv = left_grad(target_in, dq), left_grad(target_in, dk), left_grad(target_in, dv)
    target_grad = d_pre_self + back_through(dq, wsq) + back_through(dk, wsk) + back_through(dv, wsv)
    n_g = jnp.pad(jnp.stack([g_ga, g_sa, g_gc, g_sc, g_gf, g_sf], axis=1), ((0, 0), (0, NORM - 6)))
    g_w2p = g_w2.reshape(32, 4, 16, SLAB).transpose(0, 2, 1, 3).reshape(512, 4 * SLAB)
    grads = jnp.concatenate([g.astype(low) for g in (n_g, g_wsq, g_wsk, g_wsv, g_wso, g_wcq, g_wck, g_wcv, g_wco, g_w1, g_w2p)], axis=1)
    part = lambda i, n=1: out[:, NORM + SLAB * i : NORM + SLAB * (i + n)]
    out, w2_grad, mem_out = scatter_any(grads, mem_grad.astype(low))
    return (final.astype(low), target_grad, mem_out) + tuple(part(i) for i in range(8)) + (part(8, 4), w2_grad) + tuple(out[:, i] for i in range(6))


TILE = 128
RT = 256
CHUNK = 256
EPS = 1e-05
HIDE = -1e30
LOW = jnp.bfloat16
F32 = jnp.float32
DEV = 32
CUT = NORM + 12 * SLAB


def mm(a, b):
    return jnp.dot(a, b, preferred_element_type=F32)


def mmt(a, b):
    return lax.dot_general(a, b, (((1,), (1,)), ((), ())), preferred_element_type=F32)


def tmm(a, b):
    return lax.dot_general(a, b, (((0,), (0,)), ((), ())), preferred_element_type=F32)


def lane_iota(shape):
    return lax.broadcasted_iota(jnp.int32, shape, len(shape) - 1)


def row_iota(shape):
    return lax.broadcasted_iota(jnp.int32, shape, 0)


def halves():
    lane = lane_iota((1, TILE))
    even = jnp.where(lane < 64, 1.0, 0.0).astype(LOW)
    odd = jnp.where(lane < 64, 0.0, 1.0).astype(LOW)
    return even, odd


def stacked(block, even, odd):
    return jnp.concatenate([block * even, block * odd], axis=0)


def fold(pair):
    lane = lane_iota((TILE, TILE))
    return jnp.where(lane < 64, pair[:TILE], pair[TILE:])


def totals_block(even, odd):
    wide = lambda v: jnp.broadcast_to(v, (TILE, TILE))
    return jnp.concatenate([wide(even), wide(odd)], axis=0)


def corr_block():
    lane = lane_iota((TILE, TILE))
    a = jnp.where(lane < 2, 1.0, 0.0).astype(LOW)
    b = jnp.where((lane >= 64) & (lane < 66), 1.0, 0.0).astype(LOW)
    return jnp.concatenate([a, b], axis=0)


def tile_forward(rows, keys, bias, q, k, v, num, tot):
    even, odd = halves()
    ones = totals_block(even, odd)
    bias2 = jnp.concatenate([bias, bias], axis=1)
    for h in range(4):
        cols = pl.ds(TILE * h, TILE)
        s = mmt(q[rows, cols], stacked(k[keys, cols], even, odd))
        e = jnp.exp(s + bias2).astype(LOW)
        both = mm(e, jnp.concatenate([stacked(v[keys, cols], even, odd), ones], axis=1))
        num[rows, cols] += both[:, :TILE]
        tot[rows, cols] += both[:, TILE:]


def tile_backward(rows, keys, bias, q, k, v, dnx, dq, dk, dv):
    even, odd = halves()
    ones = corr_block()
    bias2 = jnp.concatenate([bias, bias], axis=1)
    for h in range(4):
        cols = pl.ds(TILE * h, TILE)
        qb = q[rows, cols]
        ks = stacked(k[keys, cols], even, odd)
        e = jnp.exp(mmt(qb, ks) + bias2)
        vs = jnp.concatenate([stacked(v[keys, cols], even, odd), ones], axis=1)
        flow = mmt(dnx[rows, pl.ds(2 * TILE * h, 2 * TILE)], vs)
        ds = (e * flow).astype(LOW)
        dq[rows, cols] += mm(ds, ks)
        dk[keys, cols] += fold(tmm(ds, qb))
        dv[keys, cols] += fold(tmm(e.astype(LOW), dnx[rows, pl.ds(2 * TILE * h, TILE)]))


def each(count, body):
    def step(i, carry):
        body(i)
        return carry
    lax.fori_loop(0, count, step, 0)


def zero(ref, step=128):
    def body(i):
        rows = pl.ds(pl.multiple_of(i * step, step), step)
        ref[rows] = jnp.zeros((step,) + ref.shape[1:], ref.dtype)
    each(ref.shape[0] // step, body)


def compute_kernel(lens_ref, spans_ref, offs_ref, target, out_grad, memory, gathered,
                   layer_out, target_grad, grads, mem_grads,
                   w, w2, x, og, mem, qs, ks, vs, qc, kc, vc, big, act, dhid, dv,
                   num_s, tot_s, num_c, tot_c, xh1, xh2, t1, dpre, dq, rs1, rs2, low_s, o_b, oc_b, a_b, c_b,
                   g_b, dnx, ng, gb, lout,
                   low_c, high_c, memc, sel, idx,
                   starts, packed, in_sem, w_sem, out_sem):
    n_src = mem.shape[0]
    rows_all = x.shape[0]
    n_sent = starts.shape[0] - 1
    member = lax.axis_index("mem")
    base = member * n_sent

    loads = {}

    def load(name, src, dst, sem):
        loads[name] = pltpu.make_async_copy(src, dst, sem)
        loads[name].start()

    load("x", target, x, in_sem.at[0])
    load("norm", gathered.at[:, :, pl.ds(0, NORM)], w.at[:, :, pl.ds(0, NORM)], w_sem.at[12])
    for i in range(3):
        lanes = pl.ds(NORM + SLAB * i, SLAB)
        load(i, gathered.at[:, :, lanes], w.at[:, :, lanes], w_sem.at[i])
    load("mem", memory, mem, in_sem.at[1])
    for i in (3, 5, 6, 4, 7):
        lanes = pl.ds(NORM + SLAB * i, SLAB)
        load(i, gathered.at[:, :, lanes], w.at[:, :, lanes], w_sem.at[i])
    lanes = pl.ds(NORM + SLAB * 8, 4 * SLAB)
    load("w1", gathered.at[:, :, lanes], w.at[:, :, lanes], w_sem.at[8])
    for k in range(4):
        load(("w2", k), gathered.at[:, :, pl.ds(CUT + SLAB * k, SLAB)], w2.at[:, k], w_sem.at[13 + k])
    load("og", out_grad, og, in_sem.at[2])

    outs = []

    def send(src, dst):
        copy = pltpu.make_async_copy(src, dst, out_sem.at[len(outs)])
        copy.start()
        outs.append(copy)

    def weight(i, part=None, width=256):
        if part is None:
            return w[:, :, pl.ds(NORM + SLAB * i, SLAB)].reshape(SLAB, SLAB)
        start = pl.multiple_of(NORM + SLAB * i + part * width, TILE)
        return w[:, :, pl.ds(start, width)].reshape(SLAB, width)

    def weight_rows(i, part, width=256, lanes=SLAB):
        devs = pl.ds(pl.multiple_of(part * (width // ROWS), width // ROWS), width // ROWS)
        return w[devs, :, pl.ds(NORM + SLAB * i, lanes)].reshape(width, lanes)

    def put_weight(i, part, value, width=256):
        start = pl.multiple_of(NORM + SLAB * i + part * width, TILE)
        w[:, :, pl.ds(start, width)] = value.astype(LOW).reshape(DEV, ROWS, width)

    def columns(part, width=256):
        return pl.ds(pl.multiple_of(part * width, width), width)

    def block(i, width=TILE):
        return pl.ds(pl.multiple_of(i * width, width), width)

    def count(j, at):
        starts[j] = at
        return at + lens_ref[0, base + j]
    starts[n_sent] = lax.fori_loop(0, n_sent, count, jnp.int32(0))

    def count_packed(j, at):
        packed[j] = at
        return at + spans_ref[0, base + j]
    n_keys = lax.fori_loop(0, n_sent, count_packed, jnp.int32(0))
    packed[n_sent] = n_keys
    chunks = (n_keys + CHUNK - 1) // CHUNK

    def lows(i):
        row = i * TILE + row_iota((TILE, TILE))
        nothing = jnp.zeros((TILE, TILE), jnp.int32)

        def pick(j, found):
            here_on = row >= starts[j]
            values = (starts[j], packed[j], packed[j + 1])
            return tuple(jnp.where(here_on, v, f) for v, f in zip(values, found))
        low_s[block(i)], low_c[block(i)], high_c[block(i)] = lax.fori_loop(
            0, n_sent, pick, (nothing, nothing, nothing))
    each(rows_all // TILE, lows)
    zero(num_s)
    zero(tot_s)
    zero(num_c)
    zero(tot_c)
    ng[...] = jnp.zeros_like(ng)

    loads["norm"].wait()
    gb[...] = jnp.transpose(w[:, :, pl.ds(0, NORM)].reshape(SLAB, NORM).astype(F32))[:8]
    loads["x"].wait()
    for i, dst in ((0, qs), (1, ks), (2, vs)):
        loads[i].wait()

        def project(n, i=i, dst=dst):
            value = mm(x[...], weight(i, n)).astype(LOW)
            dst[:, columns(n)] = value * jnp.asarray(0.125, LOW) if i == 0 else value
        each(2, project)

    def last_at(table, row):
        def pick(j, found):
            return jnp.where(starts[j] <= row, table(j), found)
        return lax.fori_loop(0, n_sent, pick, jnp.int32(0))

    def tiles(body, bias, first, last):
        def outer(i, carry):
            def inner(kt, carry):
                body(block(i, RT), block(kt), bias(i, kt))
                return carry
            return lax.fori_loop(first(i) // TILE, (last(i) - 1) // TILE + 1, inner, carry)
        lax.fori_loop(0, rows_all // RT, outer, 0)

    def self_tiles(body):
        def bias(i, kt):
            key = kt * TILE + lane_iota((RT, TILE))
            row = i * RT + row_iota((RT, TILE))
            return jnp.where((key >= low_s[block(i, RT)]) & (key <= row), 0.0, HIDE)
        tiles(body, bias, lambda i: last_at(lambda j: starts[j], i * RT), lambda i: (i + 1) * RT)

    def cross_tiles(body):
        def bias(i, kt):
            key = kt * TILE + lane_iota((RT, TILE))
            r = block(i, RT)
            return jnp.where((key >= low_c[r]) & (key < high_c[r]), 0.0, HIDE)
        tiles(body, bias, lambda i: last_at(lambda j: packed[j], i * RT),
              lambda i: last_at(lambda j: packed[j + 1], (i + 1) * RT - 1))

    self_tiles(lambda r, k, bias: tile_forward(r, k, bias, qs, ks, vs, num_s, tot_s))

    def divide(num, tot, out):
        def body(i):
            r = block(i, 64)
            o = num[r] / tot[r]
            num[r] = o
            out[r] = o.astype(LOW)
        each(rows_all // 64, body)

    divide(num_s, tot_s, o_b)

    def normalize(y):
        mean = jnp.mean(y, axis=1, keepdims=True)
        centre = y - mean
        r = lax.rsqrt(jnp.mean(centre * centre, axis=1, keepdims=True) + EPS)
        return centre * r, r

    def back_norm(u, gain, xh, r):
        gu = u * gain
        a = jnp.mean(gu, axis=1, keepdims=True)
        b = jnp.mean(gu * xh, axis=1, keepdims=True)
        return (gu - a - xh * b) * r

    loads[3].wait()

    def self_out(n):
        t1[:, columns(n)] = x[:, columns(n)].astype(F32) + mm(o_b[...], weight(3, n))
    each(2, self_out)

    def norm_self(i):
        r = block(i, 64)
        xh, rs = normalize(t1[r])
        xh1[r] = xh
        rs1[r] = jnp.broadcast_to(rs, (64, TILE))
        after = xh * gb[0:1] + gb[1:2]
        t1[r] = after
        a_b[r] = after.astype(LOW)
    each(rows_all // 64, norm_self)

    for i in (4, 5, 6):
        loads[i].wait()
    loads["mem"].wait()

    def query(n):
        qc[:, columns(n)] = mm(a_b[...], weight(4, n)).astype(LOW) * jnp.asarray(0.125, LOW)
    each(2, query)

    def choose(ct):
        r = block(ct, CHUNK)
        for g in range(n_src // TILE):
            hit = idx[r] == g * TILE + lane_iota((CHUNK, TILE))
            sel[:, g * TILE:(g + 1) * TILE] = jnp.where(hit, 1.0, 0.0).astype(LOW)

    def keys(ct):
        r = block(ct, CHUNK)
        key = ct * CHUNK + row_iota((CHUNK, TILE))

        def pick(j, found):
            return jnp.where(key >= packed[j], offs_ref[0, base + j] - packed[j] + key, found)
        at = lax.fori_loop(0, n_sent, pick, jnp.zeros((CHUNK, TILE), jnp.int32))
        idx[r] = jnp.where(key < n_keys, at, -1)
        choose(ct)

        def bring(n):
            memc[r, columns(n)] = mm(sel[...], mem[:, columns(n)]).astype(LOW)
        each(2, bring)

        def project(n):
            kc[r, columns(n)] = mm(memc[r], weight(5, n)).astype(LOW)
            vc[r, columns(n)] = mm(memc[r], weight(6, n)).astype(LOW)
        each(2, project)
    each(chunks, keys)

    cross_tiles(lambda r, k, bias: tile_forward(r, k, bias, qc, kc, vc, num_c, tot_c))
    divide(num_c, tot_c, oc_b)
    loads[7].wait()

    def cross_out(n):
        t1[:, columns(n)] += mm(oc_b[...], weight(7, n))
    each(2, cross_out)

    def norm_cross(i):
        r = block(i, 64)
        xh, rs = normalize(t1[r])
        xh2[r] = xh
        rs2[r] = jnp.broadcast_to(rs, (64, TILE))
        after = xh * gb[2:3] + gb[3:4]
        t1[r] = after
        c_b[r] = after.astype(LOW)
    each(rows_all // 64, norm_cross)

    loads["w1"].wait()

    def hidden(n):
        v = mm(c_b[...], weight(8, n))
        sig = 1.0 / (1.0 + jnp.exp(-v))
        act[:, columns(n)] = (v * sig).astype(LOW)
        big[block(n // 2, SLAB), columns(n % 2)] = sig * (1.0 + v * (1.0 - sig))
    each(8, hidden)
    for k in range(4):
        loads[("w2", k)].wait()

    def ffn_out(n):
        cols = columns(n)
        t1[:, cols] += mm(act[...], w2[:, :, :, cols].reshape(4 * SLAB, 256))
    each(2, ffn_out)
    loads["og"].wait()

    def norm_ffn(i):
        r = block(i, 64)
        xh, rs = normalize(t1[r])
        gain = gb[4:5]
        lout[r] = (xh * gain + gb[5:6]).astype(LOW)
        u = og[r].astype(F32)
        ng[4:5] += jnp.sum(u * xh, axis=0, keepdims=True)
        ng[5:6] += jnp.sum(u, axis=0, keepdims=True)
        d = back_norm(u, gain, xh, rs)
        dpre[r] = d
        g_b[r] = d.astype(LOW)
    each(rows_all // 64, norm_ffn)
    send(lout, layer_out)

    def hidden_back(n):
        devs = pl.ds(pl.multiple_of(n * 4, 4), 4)
        part = mmt(g_b[...], w2[devs].reshape(256, SLAB))
        d = (part * big[block(n // 2, SLAB), columns(n % 2)]).astype(LOW)
        dhid[:, columns(n)] = d
        w2[devs] = tmm(act[:, columns(n)], g_b[...]).astype(LOW).reshape(4, 4, ROWS, SLAB)
    each(8, hidden_back)
    for k in range(4):
        send(w2.at[:, k], grads.at[:, :, pl.ds(CUT + SLAB * k, SLAB)])

    def input_back(n):
        dpre[:, columns(n)] += mmt(dhid[...], weight_rows(8, n, 256, 4 * SLAB))
    each(2, input_back)

    def first_grad(n):
        put_weight(8, n, tmm(c_b[...], dhid[:, columns(n)]))
    each(8, first_grad)
    lanes = pl.ds(NORM + SLAB * 8, 4 * SLAB)
    send(w.at[:, :, lanes], grads.at[:, :, lanes])

    def back_cross(i):
        r = block(i, 64)
        u, xh = dpre[r], xh2[r]
        ng[2:3] += jnp.sum(u * xh, axis=0, keepdims=True)
        ng[3:4] += jnp.sum(u, axis=0, keepdims=True)
        d = back_norm(u, gb[2:3], xh, rs2[r][:, :1])
        dpre[r] = d
        g_b[r] = d.astype(LOW)
    each(rows_all // 64, back_cross)

    def out_back(i, o_low, num, tot):
        lane = lane_iota((TILE, TILE))
        same = jnp.where((lane < 64) == (row_iota((TILE, TILE)) < 64), 1.0, 0.0).astype(LOW)
        half = lane % 64

        def body(n):
            up = mmt(g_b[...], weight_rows(i, n)).astype(LOW).astype(F32)
            for h in range(2):
                cols = pl.ds(pl.multiple_of(n * 256 + h * TILE, TILE), TILE)
                wide = lambda k: pl.ds(pl.multiple_of(n * 512 + h * 256 + k * TILE, TILE), TILE)
                d = up[:, h * TILE:(h + 1) * TILE]
                t = tot[:, cols]
                dnx[:, wide(0)] = (d / t).astype(LOW)
                p = d * num[:, cols]
                p1 = p.astype(LOW)
                p2 = (p - p1.astype(F32)).astype(LOW)
                corr = -(mm(p1, same) + mm(p2, same)) / t
                c1 = corr.astype(LOW)
                c2 = (corr - c1.astype(F32)).astype(LOW)
                place = lane_iota(c1.shape) % 64
                nothing = jnp.zeros_like(c1)
                dnx[:, wide(1)] = jnp.where(place == 0, c1, jnp.where(place == 1, c2, nothing))
        each(2, body)

        def grad(n):
            put_weight(i, n, tmm(o_low[...], g_b[:, columns(n)]))
        each(2, grad)

    def send_slab(i):
        lanes = pl.ds(NORM + SLAB * i, SLAB)
        send(w.at[:, :, lanes], grads.at[:, :, lanes])

    out_back(7, oc_b, num_c, tot_c)
    send_slab(7)
    zero(dq)

    def clear(ct):
        r = block(ct, CHUNK)
        big[r] = jnp.zeros((CHUNK, SLAB), F32)
        dv[r] = jnp.zeros((CHUNK, SLAB), F32)
    each(chunks, clear)
    cross_tiles(lambda r, k, bias: tile_backward(r, k, bias, qc, kc, vc, dnx, dq, big, dv))

    def scaled(src, dst, factor, step=64):
        def body(i):
            r = block(i, step)
            dst[r] = (src[r] * factor).astype(LOW)
        each(src.shape[0] // step, body)

    scaled(dq, qc, 0.125)

    def query_back(n):
        dpre[:, columns(n)] += mmt(qc[...], weight_rows(4, n))
    each(2, query_back)

    def query_grad(n):
        put_weight(4, n, tmm(a_b[...], qc[:, columns(n)]))
    each(2, query_grad)
    send_slab(4)

    zero(num_c)
    zero(tot_c)

    def memory_back(ct):
        r = block(ct, CHUNK)
        kc[r] = big[r].astype(LOW)
        vc[r] = dv[r].astype(LOW)

        def key_grad(n):
            cols = columns(n)
            num_c[:, cols] += tmm(memc[r], kc[r, cols])
            tot_c[:, cols] += tmm(memc[r], vc[r, cols])
        each(2, key_grad)

        def rows_grad(n):
            memc[r, columns(n)] = (
                mmt(kc[r], weight_rows(5, n)) + mmt(vc[r], weight_rows(6, n))).astype(LOW)
        each(2, rows_grad)
        choose(ct)

        def spread(n):
            rows = block(n, 256)
            found = tmm(sel[:, columns(n)], memc[r]).astype(LOW)
            mem[rows] = jnp.where(ct == 0, found, mem[rows] + found)
        each(n_src // 256, spread)
    each(chunks, memory_back)
    send(mem, mem_grads)

    def key_store(n):
        put_weight(5, n, num_c[:, columns(n)])
        put_weight(6, n, tot_c[:, columns(n)])
    each(2, key_store)
    send_slab(5)
    send_slab(6)

    def back_self(i):
        r = block(i, 64)
        u, xh = dpre[r], xh1[r]
        ng[0:1] += jnp.sum(u * xh, axis=0, keepdims=True)
        ng[1:2] += jnp.sum(u, axis=0, keepdims=True)
        d = back_norm(u, gb[0:1], xh, rs1[r][:, :1])
        dpre[r] = d
        g_b[r] = d.astype(LOW)
    each(rows_all // 64, back_self)
    out_back(3, o_b, num_s, tot_s)
    send_slab(3)
    zero(dq)
    dk_s, dv_s = t1, dv.at[pl.ds(0, rows_all)]
    zero(dk_s)
    zero(dv_s)
    self_tiles(lambda r, k, bias: tile_backward(r, k, bias, qs, ks, vs, dnx, dq, dk_s, dv_s))
    scaled(dq, qs, 0.125)
    scaled(dk_s, ks, 1.0)
    scaled(dv_s, vs, 1.0)

    def target_back(n):
        total = mmt(qs[...], weight_rows(0, n)) + mmt(ks[...], weight_rows(1, n))
        dpre[:, columns(n)] += total + mmt(vs[...], weight_rows(2, n))
    each(2, target_back)
    send(dpre, target_grad)
    for i, src in ((0, qs), (1, ks), (2, vs)):
        def grad(n, i=i, src=src):
            put_weight(i, n, tmm(x[...], src[:, columns(n)]))
        each(2, grad)
        send_slab(i)
    padded = jnp.concatenate([ng[...], jnp.zeros((NORM - 8, SLAB), F32)], axis=0)
    w[:, :, pl.ds(0, NORM)] = jnp.transpose(padded).astype(LOW).reshape(DEV, ROWS, NORM)
    send(w.at[:, :, pl.ds(0, NORM)], grads.at[:, :, pl.ds(0, NORM)])
    for copy in outs:
        copy.wait()


def compute(lens, spans, offs, target, out_grad, memory, gathered):
    rows, n_src = target.shape[0], memory.shape[0]
    n_sent = 16
    n_keys = n_sent * 112
    any_space = pl.BlockSpec(memory_space=pl.ANY)
    smem = pl.BlockSpec(memory_space=pltpu.SMEM)
    dma = pltpu.SemaphoreType.DMA
    f32 = lambda *s: pltpu.VMEM(s, F32)
    low = lambda *s: pltpu.VMEM(s, LOW)
    return pl.pallas_call(
        compute_kernel,
        out_shape=(
            jax.ShapeDtypeStruct((rows, SLAB), LOW),
            jax.ShapeDtypeStruct((rows, SLAB), F32),
            jax.ShapeDtypeStruct((DEV, ROWS, LANES), LOW),
            jax.ShapeDtypeStruct((n_src, SLAB), LOW),
        ),
        in_specs=[smem] * 3 + [any_space] * 4,
        out_specs=(any_space,) * 4,
        scratch_shapes=[
            low(DEV, ROWS, CUT),
            low(DEV, 4, ROWS, SLAB),
            low(rows, SLAB),
            low(rows, SLAB),
            low(n_src, SLAB),
            low(rows, SLAB),
            low(rows, SLAB),
            low(rows, SLAB),
            low(rows, SLAB),
            low(n_keys, SLAB),
            low(n_keys, SLAB),
            f32(4 * SLAB, SLAB),
            low(rows, 4 * SLAB),
            low(rows, 4 * SLAB),
            f32(n_keys, SLAB),
            f32(rows, SLAB),
            f32(rows, SLAB),
            f32(rows, SLAB),
            f32(rows, SLAB),
            f32(rows, SLAB),
            f32(rows, SLAB),
            f32(rows, SLAB),
            f32(rows, SLAB),
            f32(rows, SLAB),
            f32(rows, TILE),
            f32(rows, TILE),
            pltpu.VMEM((rows, TILE), jnp.int32),
            low(rows, SLAB),
            low(rows, SLAB),
            low(rows, SLAB),
            low(rows, SLAB),
            low(rows, SLAB),
            low(rows, 2 * SLAB),
            f32(8, SLAB),
            f32(8, SLAB),
            low(rows, SLAB),
            pltpu.VMEM((rows, TILE), jnp.int32),
            pltpu.VMEM((rows, TILE), jnp.int32),
            low(n_keys, SLAB),
            low(CHUNK, n_src),
            pltpu.VMEM((n_keys, TILE), jnp.int32),
            pltpu.SMEM((n_sent + 1,), jnp.int32),
            pltpu.SMEM((n_sent + 1,), jnp.int32),
            dma((4,)),
            dma((17,)),
            dma((17,)),
        ],
        compiler_params=pltpu.CompilerParams(vmem_limit_bytes=60 << 20),
        name="compute",
    )(lens, spans, offs, target, out_grad, memory, gathered)


def local(target_in, memory, out_grad, *rest):
    fast = two_by_two((lax.axis_size("dp"), lax.axis_size("mem")))
    if not fast:
        return plain(target_in, memory, out_grad, *rest)
    weights, tables = rest[:16], rest[16:]
    norms = jnp.stack(weights[10:], axis=1)
    norms = jnp.pad(norms, ((0, 0), (0, NORM - norms.shape[1])))
    gathered, all_memory = gather_all(weights[:10], norms, memory)
    layer_out, target_grad, grads, mem_grads = compute(*tables, target_in, out_grad, all_memory, gathered)
    rows = target_in.shape[0]
    out, mem_out = scatter_all(
        grads.reshape(4, 2, 2, 2, ROWS, LANES), mem_grads.reshape(2, 2, rows, SLAB))
    part = lambda i, n=1: out[:, NORM + SLAB * i : NORM + SLAB * (i + n)]
    w2_grad = jnp.concatenate([part(12 + k) for k in range(4)], axis=0)
    return (
        (layer_out, target_grad, mem_out)
        + tuple(part(i) for i in range(8))
        + (part(8, 4), w2_grad)
        + tuple(out[:, i] for i in range(6))
    )


def solution(mesh):
    both = P(("dp", "mem"), None)
    flat = P(("dp", "mem"))
    in_specs = (both,) * 13 + (flat,) * 6 + (P("dp", None),) * 3
    out_specs = (both,) * 13 + (flat,) * 6
    return jax.shard_map(local, mesh=mesh, in_specs=in_specs, out_specs=out_specs, check_vma=False)
```

```python
import functools

import jax
import jax.numpy as jnp
from jax import lax
from jax.experimental import pallas as pl
from jax.experimental.pallas import tpu as pltpu
from jax.sharding import PartitionSpec as P

MESH = pl.DeviceIdType.MESH
SLAB = 512
NORM = 128
LANES = NORM + 16 * SLAB
ROWS = 16


def here():
    dp, mem = lax.axis_index("dp"), lax.axis_index("mem")
    return dp // 2, dp % 2, mem // 2, mem % 2


def device(z, x, y, c):
    return (z * 2 + x, y * 2 + c)


def greet(peers):
    barrier = pltpu.get_barrier_semaphore()
    for peer in peers:
        pl.semaphore_signal(barrier, inc=1, device_id=peer, device_id_type=MESH)
    pl.semaphore_wait(barrier, len(peers))


def remote(src, dst, sems, index, peer):
    send, recv = sems
    return pltpu.make_async_remote_copy(
        src_ref=src,
        dst_ref=dst,
        send_sem=send.at[index],
        recv_sem=recv.at[index],
        device_id=peer,
        device_id_type=MESH,
    )


def cuts(widths, share):
    spans, at = [], 0
    for tiles in widths:
        n = tiles * 128
        spans.append((at, at + max(1, round(tiles * share)) * 128, at + n))
        at += n
    assert at == LANES
    return tuple(spans)


GATHER_ROUNDS = cuts((33, 32), 0.25)


def gather_kernel(*refs):
    shards, norm_ref, memory_ref = refs[:10], refs[10], refs[11]
    out, mem_out, local_sem, mem_local = refs[12:16]
    z_sems, first_sems, second_sems = refs[16:18], refs[18:20], refs[20:22]
    across, mems = refs[22:24], refs[24:26]
    z, x, y, c = here()
    xp, yp, cp_ = device(z, 1 - x, y, c), device(z, x, 1 - y, c), device(z, x, y, 1 - c)
    own = out.at[z, x, y, c]
    rounds = range(len(GATHER_ROUNDS))

    local = []

    def bring(src, start, width):
        local.append(
            pltpu.make_async_copy(src, own.at[:, pl.ds(start, width)], local_sem.at[len(local)])
        )

    bring(norm_ref, 0, NORM)
    for i in range(8):
        bring(shards[i], NORM + SLAB * i, SLAB)
    bring(shards[8], NORM + SLAB * 8, 4 * SLAB)
    for k in range(4):
        bring(shards[9].at[pl.ds(ROWS * k, ROWS)], NORM + SLAB * (12 + k), SLAB)
    for one in local:
        one.start()
    keep = pltpu.make_async_copy(memory_ref, mem_out.at[y, c], mem_local)
    keep.start()
    zn = [device((z + k) % 4, x, y, c) for k in (1, 3)]
    greet([xp, yp, cp_] + zn)
    for one in local:
        one.wait()

    def column(slot):
        return z if slot == 0 else (z - slot if slot < 4 else z + (slot - 3))

    def there(slot):
        return None if slot == 0 else (z >= slot if slot < 4 else z <= 6 - slot)

    def both(a, b):
        return b if a is None else (a if b is None else jnp.logical_and(a, b))

    def guarded(cond, body):
        if cond is None:
            body()
        else:
            pl.when(cond)(body)

    sent = []

    def go(make, cond=None):
        guarded(cond, lambda: make().start())
        sent.append((cond, make))

    def along(slot, r, up):
        a, _, b = GATHER_ROUNDS[r]
        ref = out.at[column(slot), x, y, c, :, pl.ds(a, b - a)]
        d = 0 if slot == 0 else (slot if slot < 4 else slot - 3)
        peer = device((z + (1 if up else 3)) % 4, x, y, c)
        return remote(ref, ref, z_sems, (0 if up else 1, d, r), peer)

    def arrived(slot, r):
        a, _, b = GATHER_ROUNDS[r]
        ref = out.at[column(slot), x, y, c, :, pl.ds(a, b - a)]
        up = slot < 4
        index = (0 if up else 1, (slot if up else slot - 3) - 1, r)
        return remote(ref, ref, z_sems, index, xp)

    def first(slot, r, part, arriving=False):
        a, m, b = GATHER_ROUNDS[r]
        zz = column(slot)
        if part == 0:
            ref = out.at[zz, (1 - x) if arriving else x, y, c, :, pl.ds(a, m - a)]
        else:
            ref = out.at[zz, x, (1 - y) if arriving else y, c, :, pl.ds(m, b - m)]
        return remote(ref, ref, first_sems, (slot, part, r), xp if part == 0 else yp)

    def second(slot, r, part, hop, arriving=False):
        a, m, b = GATHER_ROUNDS[r]
        zz = column(slot)
        if part == 0:
            side = (1 - x) if hop else x
            ref = out.at[zz, side, (1 - y) if arriving else y, c, :, pl.ds(a, m - a)]
        else:
            side = (1 - y) if hop else y
            ref = out.at[zz, (1 - x) if arriving else x, side, c, :, pl.ds(m, b - m)]
        return remote(ref, ref, second_sems, (slot, part, hop, r), yp if part == 0 else xp)

    def over(slot, r, arriving=False):
        a, _, b = GATHER_ROUNDS[r]
        ref = out.at[column(slot), :, :, (1 - c) if arriving else c, :, pl.ds(a, b - a)]
        return remote(ref, ref, across, (slot, r), cp_)

    def spread(slot, r):
        cond = there(slot)
        for part in (1, 0):
            go(functools.partial(first, slot, r, part), cond)
        for part in (1, 0):
            go(functools.partial(second, slot, r, part, 0), cond)

    def from_z(d):
        for r in rounds:
            for slot in (d, d + 3):
                cond = there(slot)
                guarded(cond, lambda slot=slot, r=r: arrived(slot, r).wait_recv())
                if d < 3:
                    onward = z < 3 if slot < 4 else z > 0
                    go(functools.partial(along, slot, r, slot < 4), both(cond, onward))
                spread(slot, r)

    def pass_on(slots):
        for r in rounds:
            for slot in slots:
                cond = there(slot)
                for part in (1, 0):
                    guarded(cond, lambda s=slot, r=r, p=part: first(s, r, p, True).wait_recv())
                    go(functools.partial(second, slot, r, part, 1), cond)

    def hand_over(slots):
        for r in rounds:
            for slot in slots:
                cond = there(slot)
                for part in (0, 1):
                    for hop in (0, 1):
                        guarded(cond, lambda s=slot, r=r, p=part, h=hop: second(s, r, p, h, True).wait_recv())
                go(functools.partial(over, slot, r), cond)

    for r in rounds:
        go(functools.partial(along, 0, r, True), z < 3)
        go(functools.partial(along, 0, r, False), z > 0)
        spread(0, r)
    mem_own = mem_out.at[y, c]
    from_z(1)
    pass_on((0,))
    from_z(2)
    pass_on((1, 4))
    hand_over((0,))
    keep.wait()
    go(lambda: remote(mem_own, mem_own, mems, 0, yp))
    go(lambda: remote(mem_own, mem_own, mems, 1, cp_))
    from_z(3)
    pass_on((2, 5))
    hand_over((1, 4))
    far = mem_out.at[1 - y, c]
    remote(far, far, mems, 0, yp).wait_recv()
    go(lambda: remote(far, far, mems, 2, cp_))
    pass_on((3, 6))
    hand_over((2, 5))
    hand_over((3, 6))
    for slot in (0, 1, 4, 2, 5, 3, 6):
        for r in rounds:
            guarded(there(slot), lambda s=slot, r=r: over(s, r, True).wait_recv())
    for i, side in ((1, y), (2, 1 - y)):
        block = mem_out.at[side, 1 - c]
        remote(block, block, mems, i, cp_).wait_recv()
    for cond, make in sent:
        guarded(cond, lambda make=make: make().wait_send())


def gather_all(shards, norms, memory):
    any_space = pl.BlockSpec(memory_space=pl.ANY)
    dma = pltpu.SemaphoreType.DMA
    n = len(GATHER_ROUNDS)
    both = lambda *s: [dma(s), dma(s)]
    gathered, whole_memory = pl.pallas_call(
        gather_kernel,
        out_shape=(
            jax.ShapeDtypeStruct((4, 2, 2, 2, ROWS, LANES), jnp.bfloat16),
            jax.ShapeDtypeStruct((2, 2) + memory.shape, jnp.bfloat16),
        ),
        in_specs=[any_space] * 12,
        out_specs=(any_space, any_space),
        scratch_shapes=[dma((14,)), dma(())]
        + both(2, 3, n) + both(7, 2, n) + both(7, 2, 2, n) + both(7, n) + both(3),
        compiler_params=pltpu.CompilerParams(collective_id=1, has_side_effects=True),
        name="gather",
    )(*shards, norms, memory)
    return gathered.reshape(32, ROWS, LANES), whole_memory.reshape(-1, SLAB)


def two_by_two(mesh_axes):
    return mesh_axes == (8, 4)


def gather_any(shards, norms, memory):
    everyone = ("dp", "mem")
    packed = jnp.concatenate([norms] + list(shards[:9]), axis=1)
    rows = lax.all_gather(packed, everyone, axis=0, tiled=True).reshape(32, ROWS, -1)
    last = lax.all_gather(shards[9], everyone, axis=0, tiled=True)
    last = last.reshape(32, 4, ROWS, SLAB).transpose(0, 2, 1, 3).reshape(32, ROWS, 4 * SLAB)
    return (
        jnp.concatenate([rows, last], axis=2),
        lax.all_gather(memory, "mem", axis=0, tiled=True),
    )


def scatter_any(grads, mem_grads):
    everyone = ("dp", "mem")
    wide = grads.reshape(32, ROWS, LANES).astype(jnp.float32)
    cut = LANES - 4 * SLAB
    rows = lax.psum_scatter(
        wide[:, :, :cut].reshape(512, cut), everyone, scatter_dimension=0, tiled=True
    )
    last = wide[:, :, cut:].reshape(32, ROWS, 4, SLAB).transpose(0, 2, 1, 3).reshape(2048, SLAB)
    last = lax.psum_scatter(last, everyone, scatter_dimension=0, tiled=True)
    mem = lax.psum_scatter(
        mem_grads.astype(jnp.float32), "mem", scatter_dimension=0, tiled=True
    )
    return rows, last, mem
HEADS = 8
HEAD = 64
eps_norm = 1e-05
score_scale = 0.125


def layer_norm(values, gain, shift):
    centre = values - jnp.mean(values, axis=-1, keepdims=True)
    spread = jnp.mean(centre * centre, axis=-1, keepdims=True)
    return centre * lax.rsqrt(spread + eps_norm) * gain + shift


def head_split(values):
    return values.reshape(values.shape[0], HEADS, HEAD)


def matmul(left, right):
    return jnp.dot(left, right, preferred_element_type=jnp.float32)


def left_grad(inputs, grads):
    return jnp.einsum("ra,rb->ab", inputs, grads, preferred_element_type=jnp.float32)


def back_through(grads, weight):
    return jnp.einsum("rb,ab->ra", grads, weight, preferred_element_type=jnp.float32)


def exp_scores(q_block, keys, low_edge, high_edge):
    raw = jnp.einsum("qhd,khd->hqk", head_split(q_block), head_split(keys),
                     preferred_element_type=jnp.float32) * score_scale
    position = lax.broadcasted_iota(jnp.int32, (q_block.shape[0], keys.shape[0]), 1)
    allowed = (position >= low_edge[:, None]) & (position < high_edge[:, None])
    return jnp.where(allowed[None], jnp.exp(raw), 0.0)


def attend(queries, keys, values, low_edge, high_edge):
    expo = exp_scores(queries, keys, low_edge, high_edge)
    numer = jnp.einsum("hqk,khd->qhd", expo.astype(jnp.bfloat16), head_split(values),
                       preferred_element_type=jnp.float32)
    totals = jnp.sum(expo, axis=2).T
    return (numer / totals[:, :, None]).reshape(queries.shape[0], -1), totals


def attend_back(queries, keys, values, low_edge, high_edge, upstream, output, totals):
    expo = exp_scores(queries, keys, low_edge, high_edge)
    up = head_split(upstream.astype(jnp.float32))
    numer_grad = (up / totals[:, :, None]).astype(jnp.bfloat16)
    corr = -jnp.sum(up * head_split(output), axis=2) / totals
    flow = jnp.einsum("qhd,khd->hqk", numer_grad, head_split(values),
                      preferred_element_type=jnp.float32) + corr.T[:, :, None]
    ds = (expo * flow).astype(jnp.bfloat16)
    dq = jnp.einsum("hqk,khd->qhd", ds, head_split(keys), preferred_element_type=jnp.float32)
    dk = jnp.einsum("hqk,qhd->khd", ds, head_split(queries), preferred_element_type=jnp.float32)
    dv = jnp.einsum("hqk,qhd->khd", expo.astype(jnp.bfloat16), numer_grad,
                    preferred_element_type=jnp.float32)
    flat = lambda v: v.reshape(v.shape[0], -1)
    return ((flat(dq) * score_scale).astype(jnp.bfloat16), (flat(dk) * score_scale).astype(jnp.bfloat16),
            flat(dv).astype(jnp.bfloat16))


def plain(target_in, memory, out_grad, *rest):
    weights, (tgt_lens, src_lens, src_offsets) = rest[:16], rest[16:]
    member = lax.axis_index("mem")
    per_device = tgt_lens.shape[1] // lax.axis_size("mem")
    pick = lambda table: lax.dynamic_slice_in_dim(table[0], member * per_device, per_device, 0)
    lengths, spans, offsets = pick(tgt_lens), pick(src_lens), pick(src_offsets)
    norms = jnp.stack(weights[10:], axis=1)
    norms = jnp.pad(norms, ((0, 0), (0, NORM - norms.shape[1])))
    gathered, all_memory = gather_any(weights[:10], norms, memory)
    W = gathered.reshape(512, LANES)
    mat = lambda i: W[:, NORM + SLAB * i : NORM + SLAB * (i + 1)]
    wsq, wsk, wsv, wso, wcq, wck, wcv, wco = [mat(i) for i in range(8)]
    w1 = W[:, NORM + 8 * SLAB : NORM + 12 * SLAB]
    w2 = gathered[:, :, NORM + 12 * SLAB :].reshape(32, 16, 4, SLAB).transpose(0, 2, 1, 3).reshape(2048, SLAB)
    ga, sa, gc, sc, gf, sf = [W[:, i].astype(jnp.float32) for i in range(6)]
    rows = target_in.shape[0]
    starts = jnp.cumsum(lengths) - lengths
    position = lax.iota(jnp.int32, rows)
    sentence = jnp.sum((position[:, None] >= starts[None, :]).astype(jnp.int32), axis=1) - 1
    picker = sentence[:, None] == lax.iota(jnp.int32, per_device)[None, :]
    choose = lambda v: jnp.sum(jnp.where(picker, v[None, :], 0), axis=1)
    self_low, self_high = choose(starts), position + 1
    cross_low = choose(offsets)
    cross_high = cross_low + choose(spans)
    low = jnp.bfloat16
    q, k, v = [matmul(target_in, w).astype(low) for w in (wsq, wsk, wsv)]
    o_self_f, tot_self = attend(q, k, v, self_low, self_high)
    o_self = o_self_f.astype(low)
    after_self, pull_self = jax.vjp(layer_norm, target_in.astype(jnp.float32) + matmul(o_self, wso), ga, sa)
    a_b = after_self.astype(low)
    qc = matmul(a_b, wcq).astype(low)
    kc, vc = matmul(all_memory, wck).astype(low), matmul(all_memory, wcv).astype(low)
    cut = lambda v: v.reshape((4, -1) + v.shape[1:])
    o_c_f, tot_c = lax.map(
        lambda p: attend(p[0], kc, vc, p[1], p[2]), (cut(qc), cut(cross_low), cut(cross_high))
    )
    o_c_f, tot_c = o_c_f.reshape(rows, -1), tot_c.reshape(rows, -1)
    o_c = o_c_f.astype(low)
    after_cross, pull_cross = jax.vjp(layer_norm, after_self + matmul(o_c, wco), gc, sc)
    c_b = after_cross.astype(low)
    hidden = matmul(c_b, w1)
    activated, pull_silu = jax.vjp(jax.nn.silu, hidden)
    act = activated.astype(low)
    final, pull_ffn = jax.vjp(layer_norm, after_cross + matmul(act, w2), gf, sf)
    d_pre_out, g_gf, g_sf = pull_ffn(out_grad.astype(jnp.float32))
    d_branch = d_pre_out.astype(low)
    g_w2 = left_grad(act, d_branch)
    d_hidden = pull_silu(back_through(d_branch, w2))[0].astype(low)
    g_w1 = left_grad(c_b, d_hidden)
    d_pre_cross, g_gc, g_sc = pull_cross(d_pre_out + back_through(d_hidden, w1))
    d_cb = d_pre_cross.astype(low)
    g_wco = left_grad(o_c, d_cb)
    d_oc = back_through(d_cb, wco).astype(low)

    def piece(carry, p):
        dq, dk, dv = attend_back(p[0], kc, vc, p[1], p[2], p[3], p[4], p[5])
        return (carry[0] + dk, carry[1] + dv), dq

    empty = jnp.zeros(kc.shape, jnp.bfloat16)
    (dk_c, dv_c), dq_c = lax.scan(
        piece,
        (empty, empty),
        tuple(cut(v) for v in (qc, cross_low, cross_high, d_oc, o_c_f, tot_c)),
    )
    dq_c = dq_c.reshape(rows, -1)
    g_wcq, g_wck, g_wcv = left_grad(a_b, dq_c), left_grad(all_memory, dk_c), left_grad(all_memory, dv_c)
    mem_grad = back_through(dk_c, wck) + back_through(dv_c, wcv)
    d_pre_self, g_ga, g_sa = pull_self(d_pre_cross + back_through(dq_c, wcq))
    d_sb = d_pre_self.astype(low)
    g_wso = left_grad(o_self, d_sb)
    d_os = back_through(d_sb, wso).astype(low)
    dq, dk, dv = attend_back(q, k, v, self_low, self_high, d_os, o_self_f, tot_self)
    g_wsq, g_wsk, g_wsv = left_grad(target_in, dq), left_grad(target_in, dk), left_grad(target_in, dv)
    target_grad = d_pre_self + back_through(dq, wsq) + back_through(dk, wsk) + back_through(dv, wsv)
    n_g = jnp.pad(jnp.stack([g_ga, g_sa, g_gc, g_sc, g_gf, g_sf], axis=1), ((0, 0), (0, NORM - 6)))
    g_w2p = g_w2.reshape(32, 4, 16, SLAB).transpose(0, 2, 1, 3).reshape(512, 4 * SLAB)
    grads = jnp.concatenate([g.astype(low) for g in (n_g, g_wsq, g_wsk, g_wsv, g_wso, g_wcq, g_wck, g_wcv, g_wco, g_w1, g_w2p)], axis=1)
    part = lambda i, n=1: out[:, NORM + SLAB * i : NORM + SLAB * (i + n)]
    out, w2_grad, mem_out = scatter_any(grads, mem_grad.astype(low))
    return (final.astype(low), target_grad, mem_out) + tuple(part(i) for i in range(8)) + (part(8, 4), w2_grad) + tuple(out[:, i] for i in range(6))


TILE = 128
RT = 256
CHUNK = 256
EPS = 1e-05
HIDE = -1e30
LOW = jnp.bfloat16
F32 = jnp.float32
DEV = 32
CUT = NORM + 12 * SLAB


def mm(a, b):
    return jnp.dot(a, b, preferred_element_type=F32)


def mmt(a, b):
    return lax.dot_general(a, b, (((1,), (1,)), ((), ())), preferred_element_type=F32)


def tmm(a, b):
    return lax.dot_general(a, b, (((0,), (0,)), ((), ())), preferred_element_type=F32)


def lane_iota(shape):
    return lax.broadcasted_iota(jnp.int32, shape, len(shape) - 1)


def row_iota(shape):
    return lax.broadcasted_iota(jnp.int32, shape, 0)


def halves():
    lane = lane_iota((1, TILE))
    even = jnp.where(lane < 64, 1.0, 0.0).astype(LOW)
    odd = jnp.where(lane < 64, 0.0, 1.0).astype(LOW)
    return even, odd


def stacked(block, even, odd):
    return jnp.concatenate([block * even, block * odd], axis=0)


def fold(pair):
    lane = lane_iota((TILE, TILE))
    return jnp.where(lane < 64, pair[:TILE], pair[TILE:])


def totals_block(even, odd):
    wide = lambda v: jnp.broadcast_to(v, (TILE, TILE))
    return jnp.concatenate([wide(even), wide(odd)], axis=0)


def corr_block():
    lane = lane_iota((TILE, TILE))
    a = jnp.where(lane < 2, 1.0, 0.0).astype(LOW)
    b = jnp.where((lane >= 64) & (lane < 66), 1.0, 0.0).astype(LOW)
    return jnp.concatenate([a, b], axis=0)


def tile_forward(rows, keys, bias, q, k, v, num, tot):
    even, odd = halves()
    ones = totals_block(even, odd)
    bias2 = jnp.concatenate([bias, bias], axis=1)
    for h in range(4):
        cols = pl.ds(TILE * h, TILE)
        s = mmt(q[rows, cols], stacked(k[keys, cols], even, odd))
        e = jnp.exp(s + bias2).astype(LOW)
        both = mm(e, jnp.concatenate([stacked(v[keys, cols], even, odd), ones], axis=1))
        num[rows, cols] += both[:, :TILE]
        tot[rows, cols] += both[:, TILE:]


def tile_backward(rows, keys, bias, q, k, v, dnx, dq, dk, dv):
    even, odd = halves()
    ones = corr_block()
    bias2 = jnp.concatenate([bias, bias], axis=1)
    for h in range(4):
        cols = pl.ds(TILE * h, TILE)
        qb = q[rows, cols]
        ks = stacked(k[keys, cols], even, odd)
        e = jnp.exp(mmt(qb, ks) + bias2)
        vs = jnp.concatenate([stacked(v[keys, cols], even, odd), ones], axis=1)
        flow = mmt(dnx[rows, pl.ds(2 * TILE * h, 2 * TILE)], vs)
        ds = (e * flow).astype(LOW)
        dq[rows, cols] += mm(ds, ks)
        dk[keys, cols] += fold(tmm(ds, qb))
        dv[keys, cols] += fold(tmm(e.astype(LOW), dnx[rows, pl.ds(2 * TILE * h, TILE)]))


def each(count, body):
    def step(i, carry):
        body(i)
        return carry
    if isinstance(count, int) and count <= 2:
        for i in range(count):
            body(i)
        return
    lax.fori_loop(0, count, step, 0, unroll=8 if isinstance(count, int) else 1)


def zero(ref, step=128):
    def body(i):
        rows = pl.ds(pl.multiple_of(i * step, step), step)
        ref[rows] = jnp.zeros((step,) + ref.shape[1:], ref.dtype)
    each(ref.shape[0] // step, body)


def columns(part, width=256):
    return pl.ds(pl.multiple_of(part * width, width), width)


def block(i, width=TILE):
    return pl.ds(pl.multiple_of(i * width, width), width)


def back_norm(u, gain, xh, r):
    gu = u * gain
    a = jnp.mean(gu, axis=1, keepdims=True)
    b = jnp.mean(gu * xh, axis=1, keepdims=True)
    return (gu - a - xh * b) * r


def out_back(g_b, weight_rows, num, tot, dnx):
    lane = lane_iota((TILE, TILE))
    same = jnp.where((lane < 64) == (row_iota((TILE, TILE)) < 64), 1.0, 0.0).astype(LOW)

    def body(n):
        up = mmt(g_b[...], weight_rows(n)).astype(LOW).astype(F32)
        for h in range(2):
            cols = pl.ds(pl.multiple_of(n * 256 + h * TILE, TILE), TILE)
            wide = lambda k: pl.ds(pl.multiple_of(n * 512 + h * 256 + k * TILE, TILE), TILE)
            d = up[:, h * TILE:(h + 1) * TILE]
            t = tot[:, cols]
            dnx[:, wide(0)] = (d / t).astype(LOW)
            p = d * num[:, cols]
            p1 = p.astype(LOW)
            p2 = (p - p1.astype(F32)).astype(LOW)
            corr = -(mm(p1, same) + mm(p2, same)) / t
            c1 = corr.astype(LOW)
            c2 = (corr - c1.astype(F32)).astype(LOW)
            place = lane_iota(c1.shape) % 64
            nothing = jnp.zeros_like(c1)
            dnx[:, wide(1)] = jnp.where(place == 0, c1, jnp.where(place == 1, c2, nothing))
    each(2, body)


def compute_kernel(lens_ref, spans_ref, offs_ref, target, out_grad, memory, gathered,
                   layer_out, grads, mem_grads, *rest):
    (dpre_out, xh1_out, rs1_out, num_out, tot_out, q_out, k_out, v_out, o_out, gb_out, ng_out, low_out,
                   w, w2, x, og, mem, qs, ks, vs, qc, kc, vc, big, act, dhid, dv,
                   num_s, tot_s, num_c, tot_c, xh1, xh2, t1, dpre, dq, rs1, rs2, low_s, o_b, oc_b, a_b, c_b,
                   g_b, dnx, ng, gb, lout,
                   low_c, high_c, memc, sel, idx,
     starts, packed, in_sem, w_sem, out_sem) = rest
    n_src = mem.shape[0]
    rows_all = x.shape[0]
    n_sent = starts.shape[0] - 1
    member = lax.axis_index("mem")
    base = member * n_sent

    loads = {}

    def load(name, src, dst, sem):
        loads[name] = pltpu.make_async_copy(src, dst, sem)
        loads[name].start()

    load("x", target, x, in_sem.at[0])
    load("norm", gathered.at[:, :, pl.ds(0, NORM)], w.at[:, :, pl.ds(0, NORM)], w_sem.at[12])
    for i in range(3):
        lanes = pl.ds(NORM + SLAB * i, SLAB)
        load(i, gathered.at[:, :, lanes], w.at[:, :, lanes], w_sem.at[i])
    load("mem", memory, mem, in_sem.at[1])
    for i in (3, 5, 6, 4, 7):
        lanes = pl.ds(NORM + SLAB * i, SLAB)
        load(i, gathered.at[:, :, lanes], w.at[:, :, lanes], w_sem.at[i])
    lanes = pl.ds(NORM + SLAB * 8, 4 * SLAB)
    load("w1", gathered.at[:, :, lanes], w.at[:, :, lanes], w_sem.at[8])
    for k in range(4):
        load(("w2", k), gathered.at[:, :, pl.ds(CUT + SLAB * k, SLAB)], w2.at[:, k], w_sem.at[13 + k])
    load("og", out_grad, og, in_sem.at[2])

    outs = []

    def send(src, dst):
        copy = pltpu.make_async_copy(src, dst, out_sem.at[len(outs)])
        copy.start()
        outs.append(copy)

    def weight(i, part=None, width=256):
        if part is None:
            return w[:, :, pl.ds(NORM + SLAB * i, SLAB)].reshape(SLAB, SLAB)
        start = pl.multiple_of(NORM + SLAB * i + part * width, TILE)
        return w[:, :, pl.ds(start, width)].reshape(SLAB, width)

    def weight_rows(i, part, width=256, lanes=SLAB):
        devs = pl.ds(pl.multiple_of(part * (width // ROWS), width // ROWS), width // ROWS)
        return w[devs, :, pl.ds(NORM + SLAB * i, lanes)].reshape(width, lanes)

    def put_weight(i, part, value, width=256):
        start = pl.multiple_of(NORM + SLAB * i + part * width, TILE)
        w[:, :, pl.ds(start, width)] = value.astype(LOW).reshape(DEV, ROWS, width)

    def count(j, at):
        starts[j] = at
        return at + lens_ref[0, base + j]
    starts[n_sent] = lax.fori_loop(0, n_sent, count, jnp.int32(0))

    def count_packed(j, at):
        packed[j] = at
        return at + spans_ref[0, base + j]
    n_keys = lax.fori_loop(0, n_sent, count_packed, jnp.int32(0))
    packed[n_sent] = n_keys
    chunks = (n_keys + CHUNK - 1) // CHUNK

    def lows(i):
        row = i * TILE + row_iota((TILE, TILE))
        nothing = jnp.zeros((TILE, TILE), jnp.int32)

        def pick(j, found):
            here_on = row >= starts[j]
            values = (starts[j], packed[j], packed[j + 1])
            return tuple(jnp.where(here_on, v, f) for v, f in zip(values, found))
        low_s[block(i)], low_c[block(i)], high_c[block(i)] = lax.fori_loop(
            0, n_sent, pick, (nothing, nothing, nothing))
    each(rows_all // TILE, lows)
    zero(num_s)
    zero(tot_s)
    zero(num_c)
    zero(tot_c)
    ng[...] = jnp.zeros_like(ng)

    loads["norm"].wait()
    gb[...] = jnp.transpose(w[:, :, pl.ds(0, NORM)].reshape(SLAB, NORM).astype(F32))[:8]
    loads["x"].wait()
    for i, dst in ((0, qs), (1, ks), (2, vs)):
        loads[i].wait()

        def project(n, i=i, dst=dst):
            value = mm(x[...], weight(i, n)).astype(LOW)
            dst[:, columns(n)] = value * jnp.asarray(0.125, LOW) if i == 0 else value
        each(2, project)

    def last_at(table, row):
        def pick(j, found):
            return jnp.where(starts[j] <= row, table(j), found)
        return lax.fori_loop(0, n_sent, pick, jnp.int32(0))

    def tiles(body, bias, first, last):
        def outer(i, carry):
            def inner(kt, carry):
                body(block(i, RT), block(kt), bias(i, kt))
                return carry
            return lax.fori_loop(first(i) // TILE, (last(i) - 1) // TILE + 1, inner, carry)
        lax.fori_loop(0, rows_all // RT, outer, 0)

    def self_tiles(body):
        def bias(i, kt):
            key = kt * TILE + lane_iota((RT, TILE))
            row = i * RT + row_iota((RT, TILE))
            return jnp.where((key >= low_s[block(i, RT)]) & (key <= row), 0.0, HIDE)
        tiles(body, bias, lambda i: last_at(lambda j: starts[j], i * RT), lambda i: (i + 1) * RT)

    def cross_tiles(body):
        def bias(i, kt):
            key = kt * TILE + lane_iota((RT, TILE))
            r = block(i, RT)
            return jnp.where((key >= low_c[r]) & (key < high_c[r]), 0.0, HIDE)
        tiles(body, bias, lambda i: last_at(lambda j: packed[j], i * RT),
              lambda i: last_at(lambda j: packed[j + 1], (i + 1) * RT - 1))

    self_tiles(lambda r, k, bias: tile_forward(r, k, bias, qs, ks, vs, num_s, tot_s))

    def divide(num, tot, out):
        def body(i):
            r = block(i, 64)
            o = num[r] / tot[r]
            num[r] = o
            out[r] = o.astype(LOW)
        each(rows_all // 64, body)

    divide(num_s, tot_s, o_b)
    for src, dst in ((num_s, num_out), (tot_s, tot_out), (qs, q_out), (ks, k_out), (vs, v_out),
                     (o_b, o_out), (gb, gb_out), (low_s, low_out)):
        send(src, dst)

    def normalize(y):
        mean = jnp.mean(y, axis=1, keepdims=True)
        centre = y - mean
        r = lax.rsqrt(jnp.mean(centre * centre, axis=1, keepdims=True) + EPS)
        return centre * r, r

    loads[3].wait()

    def self_out(n):
        t1[:, columns(n)] = x[:, columns(n)].astype(F32) + mm(o_b[...], weight(3, n))
    each(2, self_out)

    def norm_self(i):
        r = block(i, 64)
        xh, rs = normalize(t1[r])
        xh1[r] = xh
        rs1[r] = jnp.broadcast_to(rs, (64, TILE))
        after = xh * gb[0:1] + gb[1:2]
        t1[r] = after
        a_b[r] = after.astype(LOW)
    each(rows_all // 64, norm_self)

    send(xh1, xh1_out)
    send(rs1, rs1_out)
    for i in (4, 5, 6):
        loads[i].wait()
    loads["mem"].wait()

    def query(n):
        qc[:, columns(n)] = mm(a_b[...], weight(4, n)).astype(LOW) * jnp.asarray(0.125, LOW)
    each(2, query)

    def choose(ct):
        r = block(ct, CHUNK)
        for g in range(n_src // TILE):
            hit = idx[r] == g * TILE + lane_iota((CHUNK, TILE))
            sel[:, g * TILE:(g + 1) * TILE] = jnp.where(hit, 1.0, 0.0).astype(LOW)

    def keys(ct):
        r = block(ct, CHUNK)
        key = ct * CHUNK + row_iota((CHUNK, TILE))

        def pick(j, found):
            return jnp.where(key >= packed[j], offs_ref[0, base + j] - packed[j] + key, found)
        at = lax.fori_loop(0, n_sent, pick, jnp.zeros((CHUNK, TILE), jnp.int32))
        idx[r] = jnp.where(key < n_keys, at, -1)
        choose(ct)

        def bring(n):
            memc[r, columns(n)] = mm(sel[...], mem[:, columns(n)]).astype(LOW)
        each(2, bring)

        def project(n):
            kc[r, columns(n)] = mm(memc[r], weight(5, n)).astype(LOW)
            vc[r, columns(n)] = mm(memc[r], weight(6, n)).astype(LOW)
        each(2, project)
    each(chunks, keys)

    cross_tiles(lambda r, k, bias: tile_forward(r, k, bias, qc, kc, vc, num_c, tot_c))
    divide(num_c, tot_c, oc_b)
    loads[7].wait()

    def cross_out(n):
        t1[:, columns(n)] += mm(oc_b[...], weight(7, n))
    each(2, cross_out)

    def norm_cross(i):
        r = block(i, 64)
        xh, rs = normalize(t1[r])
        xh2[r] = xh
        rs2[r] = jnp.broadcast_to(rs, (64, TILE))
        after = xh * gb[2:3] + gb[3:4]
        t1[r] = after
        c_b[r] = after.astype(LOW)
    each(rows_all // 64, norm_cross)

    loads["w1"].wait()

    def hidden(n):
        v = mm(c_b[...], weight(8, n))
        sig = 1.0 / (1.0 + jnp.exp(-v))
        act[:, columns(n)] = (v * sig).astype(LOW)
        big[block(n // 2, SLAB), columns(n % 2)] = sig * (1.0 + v * (1.0 - sig))
    each(8, hidden)
    for k in range(4):
        loads[("w2", k)].wait()

    def ffn_out(n):
        cols = columns(n)
        t1[:, cols] += mm(act[...], w2[:, :, :, cols].reshape(4 * SLAB, 256))
    each(2, ffn_out)
    loads["og"].wait()

    def norm_ffn(i):
        r = block(i, 64)
        xh, rs = normalize(t1[r])
        gain = gb[4:5]
        lout[r] = (xh * gain + gb[5:6]).astype(LOW)
        u = og[r].astype(F32)
        ng[4:5] += jnp.sum(u * xh, axis=0, keepdims=True)
        ng[5:6] += jnp.sum(u, axis=0, keepdims=True)
        d = back_norm(u, gain, xh, rs)
        dpre[r] = d
        g_b[r] = d.astype(LOW)
    each(rows_all // 64, norm_ffn)
    send(lout, layer_out)

    def hidden_back(n):
        devs = pl.ds(pl.multiple_of(n * 4, 4), 4)
        part = mmt(g_b[...], w2[devs].reshape(256, SLAB))
        d = (part * big[block(n // 2, SLAB), columns(n % 2)]).astype(LOW)
        dhid[:, columns(n)] = d
        w2[devs] = tmm(act[:, columns(n)], g_b[...]).astype(LOW).reshape(4, 4, ROWS, SLAB)
    each(8, hidden_back)
    for k in range(4):
        send(w2.at[:, k], grads.at[:, :, pl.ds(CUT + SLAB * k, SLAB)])

    def input_back(n):
        dpre[:, columns(n)] += mmt(dhid[...], weight_rows(8, n, 256, 4 * SLAB))
    each(2, input_back)

    def first_grad(n):
        put_weight(8, n, tmm(c_b[...], dhid[:, columns(n)]))
    each(8, first_grad)
    lanes = pl.ds(NORM + SLAB * 8, 4 * SLAB)
    send(w.at[:, :, lanes], grads.at[:, :, lanes])

    def back_cross(i):
        r = block(i, 64)
        u, xh = dpre[r], xh2[r]
        ng[2:3] += jnp.sum(u * xh, axis=0, keepdims=True)
        ng[3:4] += jnp.sum(u, axis=0, keepdims=True)
        d = back_norm(u, gb[2:3], xh, rs2[r][:, :1])
        dpre[r] = d
        g_b[r] = d.astype(LOW)
    each(rows_all // 64, back_cross)

    out_back(g_b, lambda n: weight_rows(7, n), num_c, tot_c, dnx)

    def out_grad_store(n):
        put_weight(7, n, tmm(oc_b[...], g_b[:, columns(n)]))
    each(2, out_grad_store)

    def send_slab(i):
        lanes = pl.ds(NORM + SLAB * i, SLAB)
        send(w.at[:, :, lanes], grads.at[:, :, lanes])

    send_slab(7)
    zero(dq)

    def clear(ct):
        r = block(ct, CHUNK)
        big[r] = jnp.zeros((CHUNK, SLAB), F32)
        dv[r] = jnp.zeros((CHUNK, SLAB), F32)
    each(chunks, clear)
    cross_tiles(lambda r, k, bias: tile_backward(r, k, bias, qc, kc, vc, dnx, dq, big, dv))

    def scaled(src, dst, factor, step=64):
        def body(i):
            r = block(i, step)
            dst[r] = (src[r] * factor).astype(LOW)
        each(src.shape[0] // step, body)

    scaled(dq, qc, 0.125)

    def query_back(n):
        dpre[:, columns(n)] += mmt(qc[...], weight_rows(4, n))
    each(2, query_back)

    send(dpre, dpre_out)

    def query_grad(n):
        put_weight(4, n, tmm(a_b[...], qc[:, columns(n)]))
    each(2, query_grad)
    send_slab(4)

    zero(num_c)
    zero(tot_c)

    def memory_back(ct):
        r = block(ct, CHUNK)
        kc[r] = big[r].astype(LOW)
        vc[r] = dv[r].astype(LOW)

        def key_grad(n):
            cols = columns(n)
            num_c[:, cols] += tmm(memc[r], kc[r, cols])
            tot_c[:, cols] += tmm(memc[r], vc[r, cols])
        each(2, key_grad)

        def rows_grad(n):
            memc[r, columns(n)] = (
                mmt(kc[r], weight_rows(5, n)) + mmt(vc[r], weight_rows(6, n))).astype(LOW)
        each(2, rows_grad)
        choose(ct)

        def spread(n):
            rows = block(n, 256)
            found = tmm(sel[:, columns(n)], memc[r]).astype(LOW)
            mem[rows] = jnp.where(ct == 0, found, mem[rows] + found)
        each(n_src // 256, spread)
    each(chunks, memory_back)
    send(mem, mem_grads)

    def key_store(n):
        put_weight(5, n, num_c[:, columns(n)])
        put_weight(6, n, tot_c[:, columns(n)])
    each(2, key_store)
    send_slab(5)
    send_slab(6)

    send(ng, ng_out)
    for copy in outs:
        copy.wait()


def state_shapes(rows):
    full = lambda dtype, lanes=SLAB, n=rows: jax.ShapeDtypeStruct((n, lanes), dtype)
    return (
        full(F32),
        full(F32),
        full(F32, TILE),
        full(F32),
        full(F32),
        full(LOW),
        full(LOW),
        full(LOW),
        full(LOW),
        full(F32, SLAB, 8),
        full(F32, SLAB, 8),
        full(jnp.int32, TILE),
    )


def compute(lens, spans, offs, target, out_grad, memory, gathered):
    rows, n_src = target.shape[0], memory.shape[0]
    n_sent = 16
    n_keys = n_sent * 112
    any_space = pl.BlockSpec(memory_space=pl.ANY)
    smem = pl.BlockSpec(memory_space=pltpu.SMEM)
    dma = pltpu.SemaphoreType.DMA
    f32 = lambda *s: pltpu.VMEM(s, F32)
    low = lambda *s: pltpu.VMEM(s, LOW)
    return pl.pallas_call(
        compute_kernel,
        out_shape=(
            jax.ShapeDtypeStruct((rows, SLAB), LOW),
            jax.ShapeDtypeStruct((DEV, ROWS, LANES), LOW),
            jax.ShapeDtypeStruct((n_src, SLAB), LOW),
        ) + state_shapes(rows),
        in_specs=[smem] * 3 + [any_space] * 4,
        out_specs=(any_space,) * 15,
        scratch_shapes=[
            low(DEV, ROWS, CUT),
            low(DEV, 4, ROWS, SLAB),
            low(rows, SLAB),
            low(rows, SLAB),
            low(n_src, SLAB),
            low(rows, SLAB),
            low(rows, SLAB),
            low(rows, SLAB),
            low(rows, SLAB),
            low(n_keys, SLAB),
            low(n_keys, SLAB),
            f32(4 * SLAB, SLAB),
            low(rows, 4 * SLAB),
            low(rows, 4 * SLAB),
            f32(n_keys, SLAB),
            f32(rows, SLAB),
            f32(rows, SLAB),
            f32(rows, SLAB),
            f32(rows, SLAB),
            f32(rows, SLAB),
            f32(rows, SLAB),
            f32(rows, SLAB),
            f32(rows, SLAB),
            f32(rows, SLAB),
            f32(rows, TILE),
            f32(rows, TILE),
            pltpu.VMEM((rows, TILE), jnp.int32),
            low(rows, SLAB),
            low(rows, SLAB),
            low(rows, SLAB),
            low(rows, SLAB),
            low(rows, SLAB),
            low(rows, 2 * SLAB),
            f32(8, SLAB),
            f32(8, SLAB),
            low(rows, SLAB),
            pltpu.VMEM((rows, TILE), jnp.int32),
            pltpu.VMEM((rows, TILE), jnp.int32),
            low(n_keys, SLAB),
            low(CHUNK, n_src),
            pltpu.VMEM((n_keys, TILE), jnp.int32),
            pltpu.SMEM((n_sent + 1,), jnp.int32),
            pltpu.SMEM((n_sent + 1,), jnp.int32),
            dma((4,)),
            dma((17,)),
            dma((32,)),
        ],
        compiler_params=pltpu.CompilerParams(vmem_limit_bytes=60 << 20),
        name="compute",
    )(lens, spans, offs, target, out_grad, memory, gathered)
def scatter_rounds(share=0.25):
    spans = []
    for at, tiles in ((33, 6), (39, 12), (51, 14), (17, 16), (0, 11), (11, 6)):
        split = at + max(1, round(tiles * share))
        spans.append((at * 128, split * 128, (at + tiles) * 128))
    return tuple(spans)


SCATTER_ROUNDS = scatter_rounds()
SELF_LANES = NORM + 4 * SLAB
SELF_ROUNDS = (4, 5)


def scatter_kernel(grads, mem_grads, gathered, target, *rest):
    state, (out, mem_out, target_grad), rest = rest[:12], rest[12:15], rest[15:]
    (acc, from_core, from_first, from_second, from_z, macc, mfrom_core, mfrom_y), rest = rest[:8], rest[8:]
    held, rest = rest[:12], rest[12:]
    (w, tgt, gs, dq, dk, dv, dnx, g_b), rest = rest[:8], rest[8:]
    (own_sems, mown_sem, state_sems, core_s, core_r, first_s, first_r,
     second_s, second_r, zs_s, zs_r, mem_s, mem_r) = rest
    dpre, xh1, rs1, num_s, tot_s, qs, ks, vs, o_b, gb, ng, low_s = held
    z, x, y, c = here()
    xp, yp, cp_ = device(z, 1 - x, y, c), device(z, x, 1 - y, c), device(z, x, y, 1 - c)
    zp = [device((z + k) % 4, x, y, c) for k in (1, 2, 3)]
    count = len(SCATTER_ROUNDS)
    core_sems, first_sems, second_sems = (core_s, core_r), (first_s, first_r), (second_s, second_r)
    z_sems, mem_sems = (zs_s, zs_r), (mem_s, mem_r)
    sent = []

    def go(copy):
        copy.start()
        sent.append(copy)

    def span(r, part=None):
        a, m, b = SCATTER_ROUNDS[r]
        return {None: (a, b - a), 0: (a, m - a), 1: (m, b - m)}[part]

    def own(r):
        a, n = span(r)
        return pltpu.make_async_copy(
            grads.at[:, :, :, c, :, pl.ds(a, n)], acc.at[:, :, :, :, pl.ds(a, n)], own_sems.at[r])

    def core(r):
        a, n = span(r)
        source = gs if r in SELF_ROUNDS else grads
        return remote(source.at[:, :, :, 1 - c, :, pl.ds(a, n)],
                      from_core.at[:, :, :, :, pl.ds(a, n)], core_sems, r, cp_)

    def first(r, part):
        lanes = pl.ds(*span(r, part))
        src = acc.at[:, :, 1 - y, :, lanes] if part == 0 else acc.at[:, 1 - x, :, :, lanes]
        return remote(src, from_first.at[:, :, :, lanes], first_sems, (r, part),
                      yp if part == 0 else xp)

    def second(r, part):
        lanes = pl.ds(*span(r, part))
        src = acc.at[:, 1 - x, y, :, lanes] if part == 0 else acc.at[:, x, 1 - y, :, lanes]
        return remote(src, from_second.at[:, :, lanes], second_sems, (r, part),
                      xp if part == 0 else yp)

    def along(r, k):
        lanes = pl.ds(*span(r))
        return remote(acc.at[(z + k + 1) % 4, x, y, :, lanes], from_z.at[k, :, lanes], z_sems,
                      (r, k), zp[k])

    mem_own = pltpu.make_async_copy(mem_grads.at[:, c], macc, mown_sem)
    mem_core = remote(mem_grads.at[:, 1 - c], mfrom_core, mem_sems, 0, cp_)
    mem_far = remote(macc.at[1 - y], mfrom_y, mem_sems, 1, yp)

    def bring(i, src, dst):
        copy = pltpu.make_async_copy(src, dst, state_sems.at[i])
        copy.start()
        return copy

    early = [r for r in range(count) if r not in SELF_ROUNDS]
    own(0).start()
    mem_own.start()
    for r in early[1:]:
        own(r).start()
    copies = [bring(i, src, dst) for i, (src, dst) in enumerate(zip(state, held))]
    copies.append(bring(12, gathered.at[:, :, pl.ds(NORM, 4 * SLAB)], w))
    copies.append(bring(13, target, tgt))
    greet([xp, yp, cp_] + zp)
    go(core(early[0]))
    go(mem_core)
    for r in early[1:]:
        go(core(r))

    def add_core(r):
        if r not in SELF_ROUNDS:
            own(r).wait()
        core(r).wait_recv()
        for part in (0, 1):
            lanes = pl.ds(*span(r, part))
            for theirs in (True, False):
                def body(zi, carry, part=part, lanes=lanes, theirs=theirs):
                    for o in (0, 1):
                        if part == 0:
                            xi, yi = o, (1 - y) if theirs else y
                        else:
                            xi, yi = (1 - x) if theirs else x, o
                        mine = gs[zi, xi, yi, c, :, lanes] if r in SELF_ROUNDS else acc[zi, xi, yi, :, lanes]
                        acc[zi, xi, yi, :, lanes] = mine + from_core[zi, xi, yi, :, lanes]
                    return carry
                lax.fori_loop(0, 4, body, 0)
                if theirs:
                    go(first(r, part))

    def add_first(r):
        for part in (0, 1):
            first(r, part).wait_recv()
            lanes = pl.ds(*span(r, part))
            for theirs in (True, False):
                def body(zi, carry, part=part, lanes=lanes, theirs=theirs):
                    if part == 0:
                        xi, yi = (1 - x) if theirs else x, y
                        slot = xi
                    else:
                        xi, yi = x, (1 - y) if theirs else y
                        slot = yi
                    acc[zi, xi, yi, :, lanes] = (
                        acc[zi, xi, yi, :, lanes] + from_first[zi, slot, :, lanes])
                    return carry
                lax.fori_loop(0, 4, body, 0)
                if theirs:
                    go(second(r, part))

    def add_second(r):
        for part in (0, 1):
            second(r, part).wait_recv()
            lanes = pl.ds(*span(r, part))

            def body(zi, carry, lanes=lanes):
                acc[zi, x, y, :, lanes] = acc[zi, x, y, :, lanes] + from_second[zi, :, lanes]
                return carry
            lax.fori_loop(0, 4, body, 0)
        for k in (1, 0, 2):
            go(along(r, k))

    def add_z(r):
        lanes = pl.ds(*span(r))
        total = acc[z, x, y, :, lanes].astype(jnp.float32)
        for k in (0, 2, 1):
            along(r, k).wait_recv()
            total = total + from_z[k, :, lanes].astype(jnp.float32)
        out[:, lanes] = total

    def memory_core():
        mem_own.wait()
        mem_core.wait_recv()
        for theirs in (True, False):
            side = (1 - y) if theirs else y

            def body(i, carry, side=side):
                rows = pl.ds(pl.multiple_of(i * 64, 64), 64)
                macc[side, rows] = macc[side, rows] + mfrom_core[side, rows]
                return carry
            lax.fori_loop(0, 8, body, 0)
            if theirs:
                go(mem_far)

    def memory_end():
        mem_far.wait_recv()

        def body(i, carry):
            rows = pl.ds(pl.multiple_of(i * 64, 64), 64)
            mem_out[rows] = macc[y, rows].astype(jnp.float32) + mfrom_y[rows].astype(jnp.float32)
            return carry
        lax.fori_loop(0, 8, body, 0)

    def weight_rows(i, part):
        devs = pl.ds(part * 16, 16)
        return w[devs, :, pl.ds(SLAB * i, SLAB)].reshape(256, SLAB)

    def put(i, n, value):
        gs[:, :, :, :, :, pl.ds(NORM + SLAB * i + 256 * n, 256)] = value.astype(LOW).reshape(4, 2, 2, 2, ROWS, 256)

    rows_all = tgt.shape[0]

    def norm_back(i):
        r = block(i, 64)
        u, xh = dpre[r], xh1[r]
        ng[0:1] += jnp.sum(u * xh, axis=0, keepdims=True)
        ng[1:2] += jnp.sum(u, axis=0, keepdims=True)
        d = back_norm(u, gb[0:1], xh, rs1[r][:, :1])
        dpre[r] = d
        g_b[r] = d.astype(LOW)

    def self_norm():
        for copy in copies:
            copy.wait()
        each(rows_all // 64, norm_back)

    def self_out():
        out_back(g_b, lambda n: weight_rows(3, n), num_s, tot_s, dnx)
        for n in (0, 1):
            put(3, n, tmm(o_b[...], g_b[:, pl.ds(256 * n, 256)]))
        for ref in (dq, dk, dv):
            zero(ref)

    def self_tiles(i, first, last):
        def inner(kt, carry):
            r = pl.ds(i * RT, RT)
            key = kt * TILE + lane_iota((RT, TILE))
            row = i * RT + row_iota((RT, TILE))
            bias = jnp.where((key >= low_s[r]) & (key <= row), 0.0, HIDE)
            tile_backward(r, block(kt), bias, qs, ks, vs, dnx, dq, dk, dv)
            return carry
        lax.fori_loop(first, last, inner, 0)

    def self_grads():
        def lower(i):
            r = block(i, 64)
            qs[r] = (dq[r] * 0.125).astype(LOW)
            ks[r] = dk[r].astype(LOW)
            vs[r] = dv[r].astype(LOW)
        each(rows_all // 64, lower)
        for i, src in ((0, qs), (1, ks), (2, vs)):
            for n in (0, 1):
                put(i, n, tmm(tgt[...], src[:, pl.ds(256 * n, 256)]))
        padded = jnp.concatenate([ng[...], jnp.zeros((NORM - 8, SLAB), F32)], axis=0)
        gs[:, :, :, :, :, pl.ds(0, NORM)] = jnp.transpose(padded).astype(LOW).reshape(4, 2, 2, 2, ROWS, NORM)
        for r in SELF_ROUNDS:
            go(core(r))

    def self_target():
        for n in (0, 1):
            total = mmt(qs[...], weight_rows(0, n)) + mmt(ks[...], weight_rows(1, n))
            cols = pl.ds(256 * n, 256)
            target_grad[:, cols] = dpre[:, cols] + total + mmt(vs[...], weight_rows(2, n))

    add_core(0)
    memory_core()
    add_core(1)
    self_norm()
    add_first(0)
    add_core(2)
    self_out()
    add_second(0)
    add_first(1)
    add_core(3)
    self_tiles(0, 0, 2)
    add_second(1)
    add_first(2)
    self_tiles(1, 0, 4)
    add_z(0)
    add_second(2)
    add_first(3)
    self_grads()
    add_core(4)
    add_core(5)
    self_target()
    memory_end()
    add_z(1)
    add_second(3)
    add_first(4)
    add_first(5)
    add_z(2)
    add_second(4)
    add_z(3)
    add_second(5)
    add_z(4)
    add_z(5)
    for copy in sent:
        copy.wait_send()


def scatter_all(grads, mem_grads, gathered, target, state):
    any_space = pl.BlockSpec(memory_space=pl.ANY)
    vmem = pl.BlockSpec(memory_space=pltpu.VMEM)
    dma = pltpu.SemaphoreType.DMA
    n = len(SCATTER_ROUNDS)
    rows = mem_grads.shape[2]
    low = lambda *s: pltpu.VMEM(s, LOW)
    f32 = lambda *s: pltpu.VMEM(s, F32)
    return pl.pallas_call(
        scatter_kernel,
        out_shape=(
            jax.ShapeDtypeStruct((ROWS, LANES), F32),
            jax.ShapeDtypeStruct((rows, SLAB), F32),
            jax.ShapeDtypeStruct((rows, SLAB), F32),
        ),
        in_specs=[any_space] * 16,
        out_specs=(vmem,) * 3,
        scratch_shapes=[
            low(4, 2, 2, ROWS, LANES),
            low(4, 2, 2, ROWS, LANES),
            low(4, 2, ROWS, LANES),
            low(4, ROWS, LANES),
            low(3, ROWS, LANES),
            low(2, rows, SLAB),
            low(2, rows, SLAB),
            low(rows, SLAB),
        ]
        + [pltpu.VMEM(s.shape, s.dtype) for s in state_shapes(rows)]
        + [
            low(32, ROWS, 4 * SLAB),
            low(rows, SLAB),
            low(4, 2, 2, 2, ROWS, SELF_LANES),
            f32(rows, SLAB),
            f32(rows, SLAB),
            f32(rows, SLAB),
            low(rows, 2 * SLAB),
            low(rows, SLAB),
            dma((n,)),
            dma(()),
            dma((14,)),
            dma((n,)),
            dma((n,)),
            dma((n, 2)),
            dma((n, 2)),
            dma((n, 2)),
            dma((n, 2)),
            dma((n, 3)),
            dma((n, 3)),
            dma((2,)),
            dma((2,)),
        ],
        compiler_params=pltpu.CompilerParams(
            collective_id=2, has_side_effects=True, vmem_limit_bytes=56 << 20),
        name="scatter",
    )(grads, mem_grads, gathered, target, *state)


def local(target_in, memory, out_grad, *rest):
    fast = two_by_two((lax.axis_size("dp"), lax.axis_size("mem")))
    if not fast:
        return plain(target_in, memory, out_grad, *rest)
    weights, tables = rest[:16], rest[16:]
    norms = jnp.stack(weights[10:], axis=1)
    norms = jnp.pad(norms, ((0, 0), (0, NORM - norms.shape[1])))
    gathered, all_memory = gather_all(weights[:10], norms, memory)
    layer_out, grads, mem_grads, *state = compute(*tables, target_in, out_grad, all_memory, gathered)
    rows = target_in.shape[0]
    out, mem_out, target_grad = scatter_all(
        grads.reshape(4, 2, 2, 2, ROWS, LANES),
        mem_grads.reshape(2, 2, rows, SLAB),
        gathered,
        target_in,
        state,
    )
    part = lambda i, n=1: out[:, NORM + SLAB * i : NORM + SLAB * (i + n)]
    w2_grad = jnp.concatenate([part(12 + k) for k in range(4)], axis=0)
    return (
        (layer_out, target_grad, mem_out)
        + tuple(part(i) for i in range(8))
        + (part(8, 4), w2_grad)
        + tuple(out[:, i] for i in range(6))
    )


def solution(mesh):
    both = P(("dp", "mem"), None)
    flat = P(("dp", "mem"))
    in_specs = (both,) * 13 + (flat,) * 6 + (P("dp", None),) * 3
    out_specs = (both,) * 13 + (flat,) * 6
    return jax.shard_map(local, mesh=mesh, in_specs=in_specs, out_specs=out_specs, check_vma=False)
```

```python
import functools

import jax
import jax.numpy as jnp
from jax import lax
from jax.experimental import pallas as pl
from jax.experimental.pallas import tpu as pltpu
from jax.sharding import PartitionSpec as P

MESH = pl.DeviceIdType.MESH
SLAB = 512
NORM = 128
LANES = NORM + 16 * SLAB
ROWS = 16


def here():
    dp, mem = lax.axis_index("dp"), lax.axis_index("mem")
    return dp // 2, dp % 2, mem // 2, mem % 2


def device(z, x, y, c):
    return (z * 2 + x, y * 2 + c)


def greet(peers):
    barrier = pltpu.get_barrier_semaphore()
    for peer in peers:
        pl.semaphore_signal(barrier, inc=1, device_id=peer, device_id_type=MESH)
    pl.semaphore_wait(barrier, len(peers))


def remote(src, dst, sems, index, peer):
    send, recv = sems
    return pltpu.make_async_remote_copy(
        src_ref=src,
        dst_ref=dst,
        send_sem=send.at[index],
        recv_sem=recv.at[index],
        device_id=peer,
        device_id_type=MESH,
    )


def cuts(widths, share):
    spans, at = [], 0
    for tiles in widths:
        n = tiles * 128
        spans.append((at, at + max(1, round(tiles * share)) * 128, at + n))
        at += n
    assert at == LANES
    return tuple(spans)


GATHER_ROUNDS = cuts((33, 32), 0.25)


def gather_kernel(*refs):
    shards, norm_ref, memory_ref = refs[:10], refs[10], refs[11]
    out, mem_out, local_sem, mem_local = refs[12:16]
    z_sems, first_sems, second_sems = refs[16:18], refs[18:20], refs[20:22]
    across, mems = refs[22:24], refs[24:26]
    stage, mem_stage = refs[26:28]
    z, x, y, c = here()
    xp, yp, cp_ = device(z, 1 - x, y, c), device(z, x, 1 - y, c), device(z, x, y, 1 - c)
    own = out.at[z, x, y, c]
    rounds = range(len(GATHER_ROUNDS))

    local = []

    def bring(src, start, width):
        local.append(
            pltpu.make_async_copy(src, stage.at[:, pl.ds(start, width)], local_sem.at[len(local)])
        )

    bring(norm_ref, 0, NORM)
    for i in range(8):
        bring(shards[i], NORM + SLAB * i, SLAB)
    bring(shards[8], NORM + SLAB * 8, 4 * SLAB)
    for k in range(4):
        bring(shards[9].at[pl.ds(ROWS * k, ROWS)], NORM + SLAB * (12 + k), SLAB)
    for one in local:
        one.start()
    keep = pltpu.make_async_copy(memory_ref, mem_stage, mem_local.at[0])
    keep.start()
    zn = [device((z + k) % 4, x, y, c) for k in (1, 3)]
    greet([xp, yp, cp_] + zn)
    for one in local:
        one.wait()
    own_out = pltpu.make_async_copy(stage, own, mem_local.at[1])
    own_out.start()

    def column(slot):
        return z if slot == 0 else (z - slot if slot < 4 else z + (slot - 3))

    def there(slot):
        return None if slot == 0 else (z >= slot if slot < 4 else z <= 6 - slot)

    def both(a, b):
        return b if a is None else (a if b is None else jnp.logical_and(a, b))

    def guarded(cond, body):
        if cond is None:
            body()
        else:
            pl.when(cond)(body)

    sent = []

    def go(make, cond=None):
        guarded(cond, lambda: make().start())
        sent.append((cond, make))

    def along(slot, r, up):
        a, _, b = GATHER_ROUNDS[r]
        ref = out.at[column(slot), x, y, c, :, pl.ds(a, b - a)]
        src = stage.at[:, pl.ds(a, b - a)] if slot == 0 else ref
        d = 0 if slot == 0 else (slot if slot < 4 else slot - 3)
        peer = device((z + (1 if up else 3)) % 4, x, y, c)
        return remote(src, ref, z_sems, (0 if up else 1, d, r), peer)

    def arrived(slot, r):
        a, _, b = GATHER_ROUNDS[r]
        ref = out.at[column(slot), x, y, c, :, pl.ds(a, b - a)]
        up = slot < 4
        index = (0 if up else 1, (slot if up else slot - 3) - 1, r)
        return remote(ref, ref, z_sems, index, xp)

    def first(slot, r, part, arriving=False):
        a, m, b = GATHER_ROUNDS[r]
        zz = column(slot)
        if part == 0:
            ref = out.at[zz, (1 - x) if arriving else x, y, c, :, pl.ds(a, m - a)]
        else:
            ref = out.at[zz, x, (1 - y) if arriving else y, c, :, pl.ds(m, b - m)]
        lanes = pl.ds(a, m - a) if part == 0 else pl.ds(m, b - m)
        src = stage.at[:, lanes] if slot == 0 and not arriving else ref
        return remote(src, ref, first_sems, (slot, part, r), xp if part == 0 else yp)

    def second(slot, r, part, hop, arriving=False):
        a, m, b = GATHER_ROUNDS[r]
        zz = column(slot)
        if part == 0:
            side = (1 - x) if hop else x
            ref = out.at[zz, side, (1 - y) if arriving else y, c, :, pl.ds(a, m - a)]
        else:
            side = (1 - y) if hop else y
            ref = out.at[zz, (1 - x) if arriving else x, side, c, :, pl.ds(m, b - m)]
        lanes = pl.ds(a, m - a) if part == 0 else pl.ds(m, b - m)
        src = stage.at[:, lanes] if slot == 0 and not (arriving or hop) else ref
        return remote(src, ref, second_sems, (slot, part, hop, r), yp if part == 0 else xp)

    def over(slot, r, arriving=False):
        a, _, b = GATHER_ROUNDS[r]
        ref = out.at[column(slot), :, :, (1 - c) if arriving else c, :, pl.ds(a, b - a)]
        return remote(ref, ref, across, (slot, r), cp_)

    def spread(slot, r):
        cond = there(slot)
        for part in (1, 0):
            go(functools.partial(first, slot, r, part), cond)
        for part in (1, 0):
            go(functools.partial(second, slot, r, part, 0), cond)

    def from_z(d):
        for r in rounds:
            for slot in (d, d + 3):
                cond = there(slot)
                guarded(cond, lambda slot=slot, r=r: arrived(slot, r).wait_recv())
                if d < 3:
                    onward = z < 3 if slot < 4 else z > 0
                    go(functools.partial(along, slot, r, slot < 4), both(cond, onward))
                spread(slot, r)

    def pass_on(slots):
        for r in rounds:
            for slot in slots:
                cond = there(slot)
                for part in (1, 0):
                    guarded(cond, lambda s=slot, r=r, p=part: first(s, r, p, True).wait_recv())
                    go(functools.partial(second, slot, r, part, 1), cond)

    def hand_over(slots):
        for r in rounds:
            for slot in slots:
                cond = there(slot)
                for part in (0, 1):
                    for hop in (0, 1):
                        guarded(cond, lambda s=slot, r=r, p=part, h=hop: second(s, r, p, h, True).wait_recv())
                go(functools.partial(over, slot, r), cond)

    for r in rounds:
        go(functools.partial(along, 0, r, True), z < 3)
        go(functools.partial(along, 0, r, False), z > 0)
        spread(0, r)
    mem_own = mem_out.at[y, c]
    from_z(1)
    pass_on((0,))
    from_z(2)
    pass_on((1, 4))
    own_out.wait()
    hand_over((0,))
    keep.wait()
    kept = pltpu.make_async_copy(mem_stage, mem_own, mem_local.at[2])
    kept.start()
    go(lambda: remote(mem_stage, mem_own, mems, 0, yp))
    go(lambda: remote(mem_stage, mem_own, mems, 1, cp_))
    from_z(3)
    pass_on((2, 5))
    hand_over((1, 4))
    far = mem_out.at[1 - y, c]
    remote(far, far, mems, 0, yp).wait_recv()
    go(lambda: remote(far, far, mems, 2, cp_))
    pass_on((3, 6))
    hand_over((2, 5))
    hand_over((3, 6))
    for slot in (0, 1, 4, 2, 5, 3, 6):
        for r in rounds:
            guarded(there(slot), lambda s=slot, r=r: over(s, r, True).wait_recv())
    for i, side in ((1, y), (2, 1 - y)):
        block = mem_out.at[side, 1 - c]
        remote(block, block, mems, i, cp_).wait_recv()
    kept.wait()
    for cond, make in sent:
        guarded(cond, lambda make=make: make().wait_send())


def gather_all(shards, norms, memory):
    any_space = pl.BlockSpec(memory_space=pl.ANY)
    dma = pltpu.SemaphoreType.DMA
    n = len(GATHER_ROUNDS)
    both = lambda *s: [dma(s), dma(s)]
    gathered, whole_memory = pl.pallas_call(
        gather_kernel,
        out_shape=(
            jax.ShapeDtypeStruct((4, 2, 2, 2, ROWS, LANES), jnp.bfloat16),
            jax.ShapeDtypeStruct((2, 2) + memory.shape, jnp.bfloat16),
        ),
        in_specs=[any_space] * 12,
        out_specs=(any_space, any_space),
        scratch_shapes=[dma((14,)), dma((3,))]
        + both(2, 3, n) + both(7, 2, n) + both(7, 2, 2, n) + both(7, n) + both(3)
        + [pltpu.VMEM((ROWS, LANES), jnp.bfloat16), pltpu.VMEM(memory.shape, jnp.bfloat16)],
        compiler_params=pltpu.CompilerParams(collective_id=1, has_side_effects=True),
        name="gather",
    )(*shards, norms, memory)
    return gathered.reshape(32, ROWS, LANES), whole_memory.reshape(-1, SLAB)


def two_by_two(mesh_axes):
    return mesh_axes == (8, 4)


def gather_any(shards, norms, memory):
    everyone = ("dp", "mem")
    packed = jnp.concatenate([norms] + list(shards[:9]), axis=1)
    rows = lax.all_gather(packed, everyone, axis=0, tiled=True).reshape(32, ROWS, -1)
    last = lax.all_gather(shards[9], everyone, axis=0, tiled=True)
    last = last.reshape(32, 4, ROWS, SLAB).transpose(0, 2, 1, 3).reshape(32, ROWS, 4 * SLAB)
    return (
        jnp.concatenate([rows, last], axis=2),
        lax.all_gather(memory, "mem", axis=0, tiled=True),
    )


def scatter_any(grads, mem_grads):
    everyone = ("dp", "mem")
    wide = grads.reshape(32, ROWS, LANES).astype(jnp.float32)
    cut = LANES - 4 * SLAB
    rows = lax.psum_scatter(
        wide[:, :, :cut].reshape(512, cut), everyone, scatter_dimension=0, tiled=True
    )
    last = wide[:, :, cut:].reshape(32, ROWS, 4, SLAB).transpose(0, 2, 1, 3).reshape(2048, SLAB)
    last = lax.psum_scatter(last, everyone, scatter_dimension=0, tiled=True)
    mem = lax.psum_scatter(
        mem_grads.astype(jnp.float32), "mem", scatter_dimension=0, tiled=True
    )
    return rows, last, mem
HEADS = 8
HEAD = 64
eps_norm = 1e-05
score_scale = 0.125


def layer_norm(values, gain, shift):
    centre = values - jnp.mean(values, axis=-1, keepdims=True)
    spread = jnp.mean(centre * centre, axis=-1, keepdims=True)
    return centre * lax.rsqrt(spread + eps_norm) * gain + shift


def head_split(values):
    return values.reshape(values.shape[0], HEADS, HEAD)


def matmul(left, right):
    return jnp.dot(left, right, preferred_element_type=jnp.float32)


def left_grad(inputs, grads):
    return jnp.einsum("ra,rb->ab", inputs, grads, preferred_element_type=jnp.float32)


def back_through(grads, weight):
    return jnp.einsum("rb,ab->ra", grads, weight, preferred_element_type=jnp.float32)


def exp_scores(q_block, keys, low_edge, high_edge):
    raw = jnp.einsum("qhd,khd->hqk", head_split(q_block), head_split(keys),
                     preferred_element_type=jnp.float32) * score_scale
    position = lax.broadcasted_iota(jnp.int32, (q_block.shape[0], keys.shape[0]), 1)
    allowed = (position >= low_edge[:, None]) & (position < high_edge[:, None])
    return jnp.where(allowed[None], jnp.exp(raw), 0.0)


def attend(queries, keys, values, low_edge, high_edge):
    expo = exp_scores(queries, keys, low_edge, high_edge)
    numer = jnp.einsum("hqk,khd->qhd", expo.astype(jnp.bfloat16), head_split(values),
                       preferred_element_type=jnp.float32)
    totals = jnp.sum(expo, axis=2).T
    return (numer / totals[:, :, None]).reshape(queries.shape[0], -1), totals


def attend_back(queries, keys, values, low_edge, high_edge, upstream, output, totals):
    expo = exp_scores(queries, keys, low_edge, high_edge)
    up = head_split(upstream.astype(jnp.float32))
    numer_grad = (up / totals[:, :, None]).astype(jnp.bfloat16)
    corr = -jnp.sum(up * head_split(output), axis=2) / totals
    flow = jnp.einsum("qhd,khd->hqk", numer_grad, head_split(values),
                      preferred_element_type=jnp.float32) + corr.T[:, :, None]
    ds = (expo * flow).astype(jnp.bfloat16)
    dq = jnp.einsum("hqk,khd->qhd", ds, head_split(keys), preferred_element_type=jnp.float32)
    dk = jnp.einsum("hqk,qhd->khd", ds, head_split(queries), preferred_element_type=jnp.float32)
    dv = jnp.einsum("hqk,qhd->khd", expo.astype(jnp.bfloat16), numer_grad,
                    preferred_element_type=jnp.float32)
    flat = lambda v: v.reshape(v.shape[0], -1)
    return ((flat(dq) * score_scale).astype(jnp.bfloat16), (flat(dk) * score_scale).astype(jnp.bfloat16),
            flat(dv).astype(jnp.bfloat16))


def plain(target_in, memory, out_grad, *rest):
    weights, (tgt_lens, src_lens, src_offsets) = rest[:16], rest[16:]
    member = lax.axis_index("mem")
    per_device = tgt_lens.shape[1] // lax.axis_size("mem")
    pick = lambda table: lax.dynamic_slice_in_dim(table[0], member * per_device, per_device, 0)
    lengths, spans, offsets = pick(tgt_lens), pick(src_lens), pick(src_offsets)
    norms = jnp.stack(weights[10:], axis=1)
    norms = jnp.pad(norms, ((0, 0), (0, NORM - norms.shape[1])))
    gathered, all_memory = gather_any(weights[:10], norms, memory)
    W = gathered.reshape(512, LANES)
    mat = lambda i: W[:, NORM + SLAB * i : NORM + SLAB * (i + 1)]
    wsq, wsk, wsv, wso, wcq, wck, wcv, wco = [mat(i) for i in range(8)]
    w1 = W[:, NORM + 8 * SLAB : NORM + 12 * SLAB]
    w2 = gathered[:, :, NORM + 12 * SLAB :].reshape(32, 16, 4, SLAB).transpose(0, 2, 1, 3).reshape(2048, SLAB)
    ga, sa, gc, sc, gf, sf = [W[:, i].astype(jnp.float32) for i in range(6)]
    rows = target_in.shape[0]
    starts = jnp.cumsum(lengths) - lengths
    position = lax.iota(jnp.int32, rows)
    sentence = jnp.sum((position[:, None] >= starts[None, :]).astype(jnp.int32), axis=1) - 1
    picker = sentence[:, None] == lax.iota(jnp.int32, per_device)[None, :]
    choose = lambda v: jnp.sum(jnp.where(picker, v[None, :], 0), axis=1)
    self_low, self_high = choose(starts), position + 1
    cross_low = choose(offsets)
    cross_high = cross_low + choose(spans)
    low = jnp.bfloat16
    q, k, v = [matmul(target_in, w).astype(low) for w in (wsq, wsk, wsv)]
    o_self_f, tot_self = attend(q, k, v, self_low, self_high)
    o_self = o_self_f.astype(low)
    after_self, pull_self = jax.vjp(layer_norm, target_in.astype(jnp.float32) + matmul(o_self, wso), ga, sa)
    a_b = after_self.astype(low)
    qc = matmul(a_b, wcq).astype(low)
    kc, vc = matmul(all_memory, wck).astype(low), matmul(all_memory, wcv).astype(low)
    cut = lambda v: v.reshape((4, -1) + v.shape[1:])
    o_c_f, tot_c = lax.map(
        lambda p: attend(p[0], kc, vc, p[1], p[2]), (cut(qc), cut(cross_low), cut(cross_high))
    )
    o_c_f, tot_c = o_c_f.reshape(rows, -1), tot_c.reshape(rows, -1)
    o_c = o_c_f.astype(low)
    after_cross, pull_cross = jax.vjp(layer_norm, after_self + matmul(o_c, wco), gc, sc)
    c_b = after_cross.astype(low)
    hidden = matmul(c_b, w1)
    activated, pull_silu = jax.vjp(jax.nn.silu, hidden)
    act = activated.astype(low)
    final, pull_ffn = jax.vjp(layer_norm, after_cross + matmul(act, w2), gf, sf)
    d_pre_out, g_gf, g_sf = pull_ffn(out_grad.astype(jnp.float32))
    d_branch = d_pre_out.astype(low)
    g_w2 = left_grad(act, d_branch)
    d_hidden = pull_silu(back_through(d_branch, w2))[0].astype(low)
    g_w1 = left_grad(c_b, d_hidden)
    d_pre_cross, g_gc, g_sc = pull_cross(d_pre_out + back_through(d_hidden, w1))
    d_cb = d_pre_cross.astype(low)
    g_wco = left_grad(o_c, d_cb)
    d_oc = back_through(d_cb, wco).astype(low)

    def piece(carry, p):
        dq, dk, dv = attend_back(p[0], kc, vc, p[1], p[2], p[3], p[4], p[5])
        return (carry[0] + dk, carry[1] + dv), dq

    empty = jnp.zeros(kc.shape, jnp.bfloat16)
    (dk_c, dv_c), dq_c = lax.scan(
        piece,
        (empty, empty),
        tuple(cut(v) for v in (qc, cross_low, cross_high, d_oc, o_c_f, tot_c)),
    )
    dq_c = dq_c.reshape(rows, -1)
    g_wcq, g_wck, g_wcv = left_grad(a_b, dq_c), left_grad(all_memory, dk_c), left_grad(all_memory, dv_c)
    mem_grad = back_through(dk_c, wck) + back_through(dv_c, wcv)
    d_pre_self, g_ga, g_sa = pull_self(d_pre_cross + back_through(dq_c, wcq))
    d_sb = d_pre_self.astype(low)
    g_wso = left_grad(o_self, d_sb)
    d_os = back_through(d_sb, wso).astype(low)
    dq, dk, dv = attend_back(q, k, v, self_low, self_high, d_os, o_self_f, tot_self)
    g_wsq, g_wsk, g_wsv = left_grad(target_in, dq), left_grad(target_in, dk), left_grad(target_in, dv)
    target_grad = d_pre_self + back_through(dq, wsq) + back_through(dk, wsk) + back_through(dv, wsv)
    n_g = jnp.pad(jnp.stack([g_ga, g_sa, g_gc, g_sc, g_gf, g_sf], axis=1), ((0, 0), (0, NORM - 6)))
    g_w2p = g_w2.reshape(32, 4, 16, SLAB).transpose(0, 2, 1, 3).reshape(512, 4 * SLAB)
    grads = jnp.concatenate([g.astype(low) for g in (n_g, g_wsq, g_wsk, g_wsv, g_wso, g_wcq, g_wck, g_wcv, g_wco, g_w1, g_w2p)], axis=1)
    part = lambda i, n=1: out[:, NORM + SLAB * i : NORM + SLAB * (i + n)]
    out, w2_grad, mem_out = scatter_any(grads, mem_grad.astype(low))
    return (final.astype(low), target_grad, mem_out) + tuple(part(i) for i in range(8)) + (part(8, 4), w2_grad) + tuple(out[:, i] for i in range(6))


TILE = 128
RT = 256
CHUNK = 256
EPS = 1e-05
HIDE = -1e30
LOW = jnp.bfloat16
F32 = jnp.float32
DEV = 32
CUT = NORM + 12 * SLAB


def mm(a, b):
    return jnp.dot(a, b, preferred_element_type=F32)


def mmt(a, b):
    return lax.dot_general(a, b, (((1,), (1,)), ((), ())), preferred_element_type=F32)


def tmm(a, b):
    return lax.dot_general(a, b, (((0,), (0,)), ((), ())), preferred_element_type=F32)


def lane_iota(shape):
    return lax.broadcasted_iota(jnp.int32, shape, len(shape) - 1)


def row_iota(shape):
    return lax.broadcasted_iota(jnp.int32, shape, 0)


def halves():
    lane = lane_iota((1, TILE))
    even = jnp.where(lane < 64, 1.0, 0.0).astype(LOW)
    odd = jnp.where(lane < 64, 0.0, 1.0).astype(LOW)
    return even, odd


def stacked(block, even, odd):
    return jnp.concatenate([block * even, block * odd], axis=0)


def fold(pair):
    lane = lane_iota((TILE, TILE))
    return jnp.where(lane < 64, pair[:TILE], pair[TILE:])


def totals_block(even, odd):
    wide = lambda v: jnp.broadcast_to(v, (TILE, TILE))
    return jnp.concatenate([wide(even), wide(odd)], axis=0)


def corr_block():
    lane = lane_iota((TILE, TILE))
    a = jnp.where(lane < 2, 1.0, 0.0).astype(LOW)
    b = jnp.where((lane >= 64) & (lane < 66), 1.0, 0.0).astype(LOW)
    return jnp.concatenate([a, b], axis=0)


def tile_forward(rows, keys, bias, q, k, v, num, tot):
    even, odd = halves()
    ones = totals_block(even, odd)
    bias2 = jnp.concatenate([bias, bias], axis=1)
    for h in range(4):
        cols = pl.ds(TILE * h, TILE)
        s = mmt(q[rows, cols], stacked(k[keys, cols], even, odd))
        e = jnp.exp(s + bias2).astype(LOW)
        both = mm(e, jnp.concatenate([stacked(v[keys, cols], even, odd), ones], axis=1))
        num[rows, cols] += both[:, :TILE]
        tot[rows, cols] += both[:, TILE:]


def tile_backward(rows, keys, bias, q, k, v, dnx, dq, dk, dv):
    even, odd = halves()
    ones = corr_block()
    bias2 = jnp.concatenate([bias, bias], axis=1)
    for h in range(4):
        cols = pl.ds(TILE * h, TILE)
        qb = q[rows, cols]
        ks = stacked(k[keys, cols], even, odd)
        e = jnp.exp(mmt(qb, ks) + bias2)
        vs = jnp.concatenate([stacked(v[keys, cols], even, odd), ones], axis=1)
        flow = mmt(dnx[rows, pl.ds(2 * TILE * h, 2 * TILE)], vs)
        ds = (e * flow).astype(LOW)
        dq[rows, cols] += mm(ds, ks)
        dk[keys, cols] += fold(tmm(ds, qb))
        dv[keys, cols] += fold(tmm(e.astype(LOW), dnx[rows, pl.ds(2 * TILE * h, TILE)]))


def each(count, body):
    def step(i, carry):
        body(i)
        return carry
    if isinstance(count, int) and count <= 2:
        for i in range(count):
            body(i)
        return
    lax.fori_loop(0, count, step, 0, unroll=8 if isinstance(count, int) else 1)


def zero(ref, step=128):
    def body(i):
        rows = pl.ds(pl.multiple_of(i * step, step), step)
        ref[rows] = jnp.zeros((step,) + ref.shape[1:], ref.dtype)
    each(ref.shape[0] // step, body)


def columns(part, width=256):
    return pl.ds(pl.multiple_of(part * width, width), width)


def block(i, width=TILE):
    return pl.ds(pl.multiple_of(i * width, width), width)


def back_norm(u, gain, xh, r):
    gu = u * gain
    a = jnp.mean(gu, axis=1, keepdims=True)
    b = jnp.mean(gu * xh, axis=1, keepdims=True)
    return (gu - a - xh * b) * r


def out_back(g_b, weight_rows, num, tot, dnx):
    lane = lane_iota((TILE, TILE))
    same = jnp.where((lane < 64) == (row_iota((TILE, TILE)) < 64), 1.0, 0.0).astype(LOW)

    def body(n):
        up = mmt(g_b[...], weight_rows(n)).astype(LOW).astype(F32)
        for h in range(2):
            cols = pl.ds(pl.multiple_of(n * 256 + h * TILE, TILE), TILE)
            wide = lambda k: pl.ds(pl.multiple_of(n * 512 + h * 256 + k * TILE, TILE), TILE)
            d = up[:, h * TILE:(h + 1) * TILE]
            t = tot[:, cols]
            dnx[:, wide(0)] = (d / t).astype(LOW)
            p = d * num[:, cols]
            p1 = p.astype(LOW)
            p2 = (p - p1.astype(F32)).astype(LOW)
            corr = -(mm(p1, same) + mm(p2, same)) / t
            c1 = corr.astype(LOW)
            c2 = (corr - c1.astype(F32)).astype(LOW)
            place = lane_iota(c1.shape) % 64
            nothing = jnp.zeros_like(c1)
            dnx[:, wide(1)] = jnp.where(place == 0, c1, jnp.where(place == 1, c2, nothing))
    each(2, body)


def compute_kernel(lens_ref, spans_ref, offs_ref, target, out_grad, memory, gathered,
                   layer_out, grads, mem_grads, *rest):
    (dpre_out, xh1_out, rs1_out, num_out, tot_out, q_out, k_out, v_out, o_out, gb_out, ng_out, low_out,
                   w, w2, x, og, mem, qs, ks, vs, qc, kc, vc, big, act, dhid, dv,
                   num_s, tot_s, num_c, tot_c, xh1, xh2, t1, dpre, dq, rs1, rs2, low_s, o_b, oc_b, a_b, c_b,
                   g_b, dnx, ng, gb, lout,
                   low_c, high_c, memc, sel, idx,
     starts, packed, in_sem, w_sem, out_sem) = rest
    n_src = mem.shape[0]
    rows_all = x.shape[0]
    n_sent = starts.shape[0] - 1
    member = lax.axis_index("mem")
    base = member * n_sent

    loads = {}

    def load(name, src, dst, sem):
        loads[name] = pltpu.make_async_copy(src, dst, sem)
        loads[name].start()

    load("x", target, x, in_sem.at[0])
    load("norm", gathered.at[:, :, pl.ds(0, NORM)], w.at[:, :, pl.ds(0, NORM)], w_sem.at[12])
    for i in range(3):
        lanes = pl.ds(NORM + SLAB * i, SLAB)
        load(i, gathered.at[:, :, lanes], w.at[:, :, lanes], w_sem.at[i])
    load("mem", memory, mem, in_sem.at[1])
    for i in (3, 5, 6, 4, 7):
        lanes = pl.ds(NORM + SLAB * i, SLAB)
        load(i, gathered.at[:, :, lanes], w.at[:, :, lanes], w_sem.at[i])
    lanes = pl.ds(NORM + SLAB * 8, 4 * SLAB)
    load("w1", gathered.at[:, :, lanes], w.at[:, :, lanes], w_sem.at[8])
    for k in range(4):
        load(("w2", k), gathered.at[:, :, pl.ds(CUT + SLAB * k, SLAB)], w2.at[:, k], w_sem.at[13 + k])
    load("og", out_grad, og, in_sem.at[2])

    outs = []

    def send(src, dst):
        copy = pltpu.make_async_copy(src, dst, out_sem.at[len(outs)])
        copy.start()
        outs.append(copy)

    def weight(i, part=None, width=256):
        if part is None:
            return w[:, :, pl.ds(NORM + SLAB * i, SLAB)].reshape(SLAB, SLAB)
        start = pl.multiple_of(NORM + SLAB * i + part * width, TILE)
        return w[:, :, pl.ds(start, width)].reshape(SLAB, width)

    def weight_rows(i, part, width=256, lanes=SLAB):
        devs = pl.ds(pl.multiple_of(part * (width // ROWS), width // ROWS), width // ROWS)
        return w[devs, :, pl.ds(NORM + SLAB * i, lanes)].reshape(width, lanes)

    def put_weight(i, part, value, width=256):
        start = pl.multiple_of(NORM + SLAB * i + part * width, TILE)
        w[:, :, pl.ds(start, width)] = value.astype(LOW).reshape(DEV, ROWS, width)

    def count(j, at):
        starts[j] = at
        return at + lens_ref[0, base + j]
    starts[n_sent] = lax.fori_loop(0, n_sent, count, jnp.int32(0))

    def count_packed(j, at):
        packed[j] = at
        return at + spans_ref[0, base + j]
    n_keys = lax.fori_loop(0, n_sent, count_packed, jnp.int32(0))
    packed[n_sent] = n_keys
    chunks = (n_keys + CHUNK - 1) // CHUNK

    def lows(i):
        row = i * TILE + row_iota((TILE, TILE))
        nothing = jnp.zeros((TILE, TILE), jnp.int32)

        def pick(j, found):
            here_on = row >= starts[j]
            values = (starts[j], packed[j], packed[j + 1])
            return tuple(jnp.where(here_on, v, f) for v, f in zip(values, found))
        low_s[block(i)], low_c[block(i)], high_c[block(i)] = lax.fori_loop(
            0, n_sent, pick, (nothing, nothing, nothing))
    each(rows_all // TILE, lows)
    zero(num_s)
    zero(tot_s)
    zero(num_c)
    zero(tot_c)
    ng[...] = jnp.zeros_like(ng)

    loads["norm"].wait()
    for j in range(SLAB // TILE):
        total = jnp.zeros((8, TILE), F32)
        for k in range(8):
            one = w[8 * j + k, :, pl.ds(0, NORM)].astype(F32)[:8]
            total = total + (pltpu.roll(one, ROWS * k, 1) if k else one)
        gb[:, pl.ds(TILE * j, TILE)] = total
    loads["x"].wait()
    for i, dst in ((0, qs), (1, ks), (2, vs)):
        loads[i].wait()

        def project(n, i=i, dst=dst):
            value = mm(x[...], weight(i, n)).astype(LOW)
            dst[:, columns(n)] = value * jnp.asarray(0.125, LOW) if i == 0 else value
        each(2, project)

    def last_at(table, row):
        def pick(j, found):
            return jnp.where(starts[j] <= row, table(j), found)
        return lax.fori_loop(0, n_sent, pick, jnp.int32(0))

    def tiles(body, bias, first, last):
        def outer(i, carry):
            def inner(kt, carry):
                body(block(i, RT), block(kt), bias(i, kt))
                return carry
            return lax.fori_loop(first(i) // TILE, (last(i) - 1) // TILE + 1, inner, carry)
        lax.fori_loop(0, rows_all // RT, outer, 0)

    def self_tiles(body):
        def bias(i, kt):
            key = kt * TILE + lane_iota((RT, TILE))
            row = i * RT + row_iota((RT, TILE))
            return jnp.where((key >= low_s[block(i, RT)]) & (key <= row), 0.0, HIDE)
        tiles(body, bias, lambda i: last_at(lambda j: starts[j], i * RT), lambda i: (i + 1) * RT)

    def cross_tiles(body):
        def bias(i, kt):
            key = kt * TILE + lane_iota((RT, TILE))
            r = block(i, RT)
            return jnp.where((key >= low_c[r]) & (key < high_c[r]), 0.0, HIDE)
        tiles(body, bias, lambda i: last_at(lambda j: packed[j], i * RT),
              lambda i: last_at(lambda j: packed[j + 1], (i + 1) * RT - 1))

    self_tiles(lambda r, k, bias: tile_forward(r, k, bias, qs, ks, vs, num_s, tot_s))

    def divide(num, tot, out):
        def body(i):
            r = block(i, 64)
            o = num[r] / tot[r]
            num[r] = o
            out[r] = o.astype(LOW)
        each(rows_all // 64, body)

    divide(num_s, tot_s, o_b)
    for src, dst in ((num_s, num_out), (tot_s, tot_out), (qs, q_out), (ks, k_out), (vs, v_out),
                     (o_b, o_out), (gb, gb_out), (low_s, low_out)):
        send(src, dst)

    def normalize(y):
        mean = jnp.mean(y, axis=1, keepdims=True)
        centre = y - mean
        r = lax.rsqrt(jnp.mean(centre * centre, axis=1, keepdims=True) + EPS)
        return centre * r, r

    loads[3].wait()

    def self_out(n):
        t1[:, columns(n)] = x[:, columns(n)].astype(F32) + mm(o_b[...], weight(3, n))
    each(2, self_out)

    def norm_self(i):
        r = block(i, 64)
        xh, rs = normalize(t1[r])
        xh1[r] = xh
        rs1[r] = jnp.broadcast_to(rs, (64, TILE))
        after = xh * gb[0:1] + gb[1:2]
        t1[r] = after
        a_b[r] = after.astype(LOW)
    each(rows_all // 64, norm_self)

    send(xh1, xh1_out)
    send(rs1, rs1_out)
    for i in (4, 5, 6):
        loads[i].wait()
    loads["mem"].wait()

    def query(n):
        qc[:, columns(n)] = mm(a_b[...], weight(4, n)).astype(LOW) * jnp.asarray(0.125, LOW)
    each(2, query)

    def choose(ct):
        r = block(ct, CHUNK)
        for g in range(n_src // TILE):
            hit = idx[r] == g * TILE + lane_iota((CHUNK, TILE))
            sel[:, g * TILE:(g + 1) * TILE] = jnp.where(hit, 1.0, 0.0).astype(LOW)

    def keys(ct):
        r = block(ct, CHUNK)
        key = ct * CHUNK + row_iota((CHUNK, TILE))

        def pick(j, found):
            return jnp.where(key >= packed[j], offs_ref[0, base + j] - packed[j] + key, found)
        at = lax.fori_loop(0, n_sent, pick, jnp.zeros((CHUNK, TILE), jnp.int32))
        idx[r] = jnp.where(key < n_keys, at, -1)
        choose(ct)

        def bring(n):
            memc[r, columns(n)] = mm(sel[...], mem[:, columns(n)]).astype(LOW)
        each(2, bring)

        def project(n):
            kc[r, columns(n)] = mm(memc[r], weight(5, n)).astype(LOW)
            vc[r, columns(n)] = mm(memc[r], weight(6, n)).astype(LOW)
        each(2, project)
    each(chunks, keys)

    cross_tiles(lambda r, k, bias: tile_forward(r, k, bias, qc, kc, vc, num_c, tot_c))
    divide(num_c, tot_c, oc_b)
    loads[7].wait()

    def cross_out(n):
        t1[:, columns(n)] += mm(oc_b[...], weight(7, n))
    each(2, cross_out)

    def norm_cross(i):
        r = block(i, 64)
        xh, rs = normalize(t1[r])
        xh2[r] = xh
        rs2[r] = jnp.broadcast_to(rs, (64, TILE))
        after = xh * gb[2:3] + gb[3:4]
        t1[r] = after
        c_b[r] = after.astype(LOW)
    each(rows_all // 64, norm_cross)

    loads["w1"].wait()

    def hidden(n):
        v = mm(c_b[...], weight(8, n))
        sig = 1.0 / (1.0 + jnp.exp(-v))
        act[:, columns(n)] = (v * sig).astype(LOW)
        big[block(n // 2, SLAB), columns(n % 2)] = sig * (1.0 + v * (1.0 - sig))
    each(8, hidden)
    for k in range(4):
        loads[("w2", k)].wait()

    def ffn_out(n):
        cols = columns(n)
        t1[:, cols] += mm(act[...], w2[:, :, :, cols].reshape(4 * SLAB, 256))
    each(2, ffn_out)
    loads["og"].wait()

    def norm_ffn(i):
        r = block(i, 64)
        xh, rs = normalize(t1[r])
        gain = gb[4:5]
        lout[r] = (xh * gain + gb[5:6]).astype(LOW)
        u = og[r].astype(F32)
        ng[4:5] += jnp.sum(u * xh, axis=0, keepdims=True)
        ng[5:6] += jnp.sum(u, axis=0, keepdims=True)
        d = back_norm(u, gain, xh, rs)
        dpre[r] = d
        g_b[r] = d.astype(LOW)
    each(rows_all // 64, norm_ffn)
    send(lout, layer_out)

    def hidden_back(n):
        devs = pl.ds(pl.multiple_of(n * 4, 4), 4)
        part = mmt(g_b[...], w2[devs].reshape(256, SLAB))
        d = (part * big[block(n // 2, SLAB), columns(n % 2)]).astype(LOW)
        dhid[:, columns(n)] = d
        w2[devs] = tmm(act[:, columns(n)], g_b[...]).astype(LOW).reshape(4, 4, ROWS, SLAB)
    each(8, hidden_back)
    for k in range(4):
        send(w2.at[:, k], grads.at[:, :, pl.ds(CUT + SLAB * k, SLAB)])

    def input_back(n):
        dpre[:, columns(n)] += mmt(dhid[...], weight_rows(8, n, 256, 4 * SLAB))
    each(2, input_back)

    def first_grad(n):
        put_weight(8, n, tmm(c_b[...], dhid[:, columns(n)]))
    each(8, first_grad)
    lanes = pl.ds(NORM + SLAB * 8, 4 * SLAB)
    send(w.at[:, :, lanes], grads.at[:, :, lanes])

    def back_cross(i):
        r = block(i, 64)
        u, xh = dpre[r], xh2[r]
        ng[2:3] += jnp.sum(u * xh, axis=0, keepdims=True)
        ng[3:4] += jnp.sum(u, axis=0, keepdims=True)
        d = back_norm(u, gb[2:3], xh, rs2[r][:, :1])
        dpre[r] = d
        g_b[r] = d.astype(LOW)
    each(rows_all // 64, back_cross)

    out_back(g_b, lambda n: weight_rows(7, n), num_c, tot_c, dnx)

    def out_grad_store(n):
        put_weight(7, n, tmm(oc_b[...], g_b[:, columns(n)]))
    each(2, out_grad_store)

    def send_slab(i):
        lanes = pl.ds(NORM + SLAB * i, SLAB)
        send(w.at[:, :, lanes], grads.at[:, :, lanes])

    send_slab(7)
    zero(dq)

    def clear(ct):
        r = block(ct, CHUNK)
        big[r] = jnp.zeros((CHUNK, SLAB), F32)
        dv[r] = jnp.zeros((CHUNK, SLAB), F32)
    each(chunks, clear)
    cross_tiles(lambda r, k, bias: tile_backward(r, k, bias, qc, kc, vc, dnx, dq, big, dv))

    def scaled(src, dst, factor, step=64):
        def body(i):
            r = block(i, step)
            dst[r] = (src[r] * factor).astype(LOW)
        each(src.shape[0] // step, body)

    scaled(dq, qc, 0.125)

    def query_back(n):
        dpre[:, columns(n)] += mmt(qc[...], weight_rows(4, n))
    each(2, query_back)

    send(dpre, dpre_out)

    def query_grad(n):
        put_weight(4, n, tmm(a_b[...], qc[:, columns(n)]))
    each(2, query_grad)
    send_slab(4)

    zero(num_c)
    zero(tot_c)

    def memory_back(ct):
        r = block(ct, CHUNK)
        kc[r] = big[r].astype(LOW)
        vc[r] = dv[r].astype(LOW)

        def key_grad(n):
            cols = columns(n)
            num_c[:, cols] += tmm(memc[r], kc[r, cols])
            tot_c[:, cols] += tmm(memc[r], vc[r, cols])
        each(2, key_grad)

        def rows_grad(n):
            memc[r, columns(n)] = (
                mmt(kc[r], weight_rows(5, n)) + mmt(vc[r], weight_rows(6, n))).astype(LOW)
        each(2, rows_grad)
        choose(ct)

        def spread(n):
            rows = block(n, 256)
            found = tmm(sel[:, columns(n)], memc[r]).astype(LOW)
            mem[rows] = jnp.where(ct == 0, found, mem[rows] + found)
        each(n_src // 256, spread)
    each(chunks, memory_back)
    send(mem, mem_grads)

    def key_store(n):
        put_weight(5, n, num_c[:, columns(n)])
        put_weight(6, n, tot_c[:, columns(n)])
    each(2, key_store)
    send_slab(5)
    send_slab(6)

    send(ng, ng_out)
    for copy in outs:
        copy.wait()


def state_shapes(rows):
    full = lambda dtype, lanes=SLAB, n=rows: jax.ShapeDtypeStruct((n, lanes), dtype)
    return (
        full(F32),
        full(F32),
        full(F32, TILE),
        full(F32),
        full(F32),
        full(LOW),
        full(LOW),
        full(LOW),
        full(LOW),
        full(F32, SLAB, 8),
        full(F32, SLAB, 8),
        full(jnp.int32, TILE),
    )


def compute(lens, spans, offs, target, out_grad, memory, gathered):
    rows, n_src = target.shape[0], memory.shape[0]
    n_sent = 16
    n_keys = n_sent * 112
    any_space = pl.BlockSpec(memory_space=pl.ANY)
    smem = pl.BlockSpec(memory_space=pltpu.SMEM)
    dma = pltpu.SemaphoreType.DMA
    f32 = lambda *s: pltpu.VMEM(s, F32)
    low = lambda *s: pltpu.VMEM(s, LOW)
    return pl.pallas_call(
        compute_kernel,
        out_shape=(
            jax.ShapeDtypeStruct((rows, SLAB), LOW),
            jax.ShapeDtypeStruct((DEV, ROWS, LANES), LOW),
            jax.ShapeDtypeStruct((n_src, SLAB), LOW),
        ) + state_shapes(rows),
        in_specs=[smem] * 3 + [any_space] * 4,
        out_specs=(any_space,) * 15,
        scratch_shapes=[
            low(DEV, ROWS, CUT),
            low(DEV, 4, ROWS, SLAB),
            low(rows, SLAB),
            low(rows, SLAB),
            low(n_src, SLAB),
            low(rows, SLAB),
            low(rows, SLAB),
            low(rows, SLAB),
            low(rows, SLAB),
            low(n_keys, SLAB),
            low(n_keys, SLAB),
            f32(4 * SLAB, SLAB),
            low(rows, 4 * SLAB),
            low(rows, 4 * SLAB),
            f32(n_keys, SLAB),
            f32(rows, SLAB),
            f32(rows, SLAB),
            f32(rows, SLAB),
            f32(rows, SLAB),
            f32(rows, SLAB),
            f32(rows, SLAB),
            f32(rows, SLAB),
            f32(rows, SLAB),
            f32(rows, SLAB),
            f32(rows, TILE),
            f32(rows, TILE),
            pltpu.VMEM((rows, TILE), jnp.int32),
            low(rows, SLAB),
            low(rows, SLAB),
            low(rows, SLAB),
            low(rows, SLAB),
            low(rows, SLAB),
            low(rows, 2 * SLAB),
            f32(8, SLAB),
            f32(8, SLAB),
            low(rows, SLAB),
            pltpu.VMEM((rows, TILE), jnp.int32),
            pltpu.VMEM((rows, TILE), jnp.int32),
            low(n_keys, SLAB),
            low(CHUNK, n_src),
            pltpu.VMEM((n_keys, TILE), jnp.int32),
            pltpu.SMEM((n_sent + 1,), jnp.int32),
            pltpu.SMEM((n_sent + 1,), jnp.int32),
            dma((4,)),
            dma((17,)),
            dma((32,)),
        ],
        compiler_params=pltpu.CompilerParams(vmem_limit_bytes=60 << 20),
        name="compute",
    )(lens, spans, offs, target, out_grad, memory, gathered)
def scatter_rounds(share=0.25):
    spans = []
    for at, tiles in ((33, 6), (39, 12), (51, 14), (17, 16), (0, 11), (11, 6)):
        split = at + max(1, round(tiles * share))
        spans.append((at * 128, split * 128, (at + tiles) * 128))
    return tuple(spans)


SCATTER_ROUNDS = scatter_rounds()
SELF_LANES = NORM + 4 * SLAB
SELF_ROUNDS = (4, 5)


def scatter_kernel(grads, mem_grads, gathered, target, *rest):
    state, (out_ref, mem_ref, target_ref), rest = rest[:12], rest[12:15], rest[15:]
    (acc, from_core, from_first, from_second, from_z, macc, mfrom_core, mfrom_y), rest = rest[:8], rest[8:]
    held, rest = rest[:12], rest[12:]
    (w, tgt, gs, dq, dk, dv, dnx, g_b, out, mem_out), rest = rest[:10], rest[10:]
    target_grad = rest[0]
    rest = rest[1:]
    (out_sems, own_sems, mown_sem, state_sems, core_s, core_r, first_s, first_r,
     second_s, second_r, zs_s, zs_r, mem_s, mem_r) = rest
    dpre, xh1, rs1, num_s, tot_s, qs, ks, vs, o_b, gb, ng, low_s = held
    z, x, y, c = here()
    xp, yp, cp_ = device(z, 1 - x, y, c), device(z, x, 1 - y, c), device(z, x, y, 1 - c)
    zp = [device((z + k) % 4, x, y, c) for k in (1, 2, 3)]
    count = len(SCATTER_ROUNDS)
    core_sems, first_sems, second_sems = (core_s, core_r), (first_s, first_r), (second_s, second_r)
    z_sems, mem_sems = (zs_s, zs_r), (mem_s, mem_r)
    sent = []

    def go(copy):
        copy.start()
        sent.append(copy)

    def span(r, part=None):
        a, m, b = SCATTER_ROUNDS[r]
        return {None: (a, b - a), 0: (a, m - a), 1: (m, b - m)}[part]

    def own(r):
        a, n = span(r)
        return pltpu.make_async_copy(
            grads.at[:, :, :, c, :, pl.ds(a, n)], acc.at[:, :, :, :, pl.ds(a, n)], own_sems.at[r])

    def core(r):
        a, n = span(r)
        source = gs if r in SELF_ROUNDS else grads
        return remote(source.at[:, :, :, 1 - c, :, pl.ds(a, n)],
                      from_core.at[:, :, :, :, pl.ds(a, n)], core_sems, r, cp_)

    def first(r, part):
        lanes = pl.ds(*span(r, part))
        src = acc.at[:, :, 1 - y, :, lanes] if part == 0 else acc.at[:, 1 - x, :, :, lanes]
        return remote(src, from_first.at[:, :, :, lanes], first_sems, (r, part),
                      yp if part == 0 else xp)

    def second(r, part):
        lanes = pl.ds(*span(r, part))
        src = acc.at[:, 1 - x, y, :, lanes] if part == 0 else acc.at[:, x, 1 - y, :, lanes]
        return remote(src, from_second.at[:, :, lanes], second_sems, (r, part),
                      xp if part == 0 else yp)

    def along(r, k):
        lanes = pl.ds(*span(r))
        return remote(acc.at[(z + k + 1) % 4, x, y, :, lanes], from_z.at[k, :, lanes], z_sems,
                      (r, k), zp[k])

    mem_own = pltpu.make_async_copy(mem_grads.at[:, c], macc, mown_sem)
    mem_core = remote(mem_grads.at[:, 1 - c], mfrom_core, mem_sems, 0, cp_)
    mem_far = remote(macc.at[1 - y], mfrom_y, mem_sems, 1, yp)

    def bring(i, src, dst):
        copy = pltpu.make_async_copy(src, dst, state_sems.at[i])
        copy.start()
        return copy

    early = [r for r in range(count) if r not in SELF_ROUNDS]
    own(0).start()
    mem_own.start()
    for r in early[1:]:
        own(r).start()
    copies = [bring(i, src, dst) for i, (src, dst) in enumerate(zip(state, held))]
    copies.append(bring(12, gathered.at[:, :, pl.ds(NORM, 4 * SLAB)], w))
    copies.append(bring(13, target, tgt))
    greet([xp, yp, cp_] + zp)
    go(core(early[0]))
    go(mem_core)
    for r in early[1:]:
        go(core(r))

    def add_core(r):
        if r not in SELF_ROUNDS:
            own(r).wait()
        core(r).wait_recv()
        for part in (0, 1):
            lanes = pl.ds(*span(r, part))
            for theirs in (True, False):
                def body(zi, carry, part=part, lanes=lanes, theirs=theirs):
                    for o in (0, 1):
                        if part == 0:
                            xi, yi = o, (1 - y) if theirs else y
                        else:
                            xi, yi = (1 - x) if theirs else x, o
                        mine = gs[zi, xi, yi, c, :, lanes] if r in SELF_ROUNDS else acc[zi, xi, yi, :, lanes]
                        acc[zi, xi, yi, :, lanes] = mine + from_core[zi, xi, yi, :, lanes]
                    return carry
                lax.fori_loop(0, 4, body, 0)
                if theirs:
                    go(first(r, part))

    def add_first(r):
        for part in (0, 1):
            first(r, part).wait_recv()
            lanes = pl.ds(*span(r, part))
            for theirs in (True, False):
                def body(zi, carry, part=part, lanes=lanes, theirs=theirs):
                    if part == 0:
                        xi, yi = (1 - x) if theirs else x, y
                        slot = xi
                    else:
                        xi, yi = x, (1 - y) if theirs else y
                        slot = yi
                    acc[zi, xi, yi, :, lanes] = (
                        acc[zi, xi, yi, :, lanes] + from_first[zi, slot, :, lanes])
                    return carry
                lax.fori_loop(0, 4, body, 0)
                if theirs:
                    go(second(r, part))

    def add_second(r):
        for part in (0, 1):
            second(r, part).wait_recv()
            lanes = pl.ds(*span(r, part))

            def body(zi, carry, lanes=lanes):
                acc[zi, x, y, :, lanes] = acc[zi, x, y, :, lanes] + from_second[zi, :, lanes]
                return carry
            lax.fori_loop(0, 4, body, 0)
        for k in (1, 0, 2):
            go(along(r, k))

    def add_z(r):
        lanes = pl.ds(*span(r))
        total = acc[z, x, y, :, lanes].astype(jnp.float32)
        for k in (0, 2, 1):
            along(r, k).wait_recv()
            total = total + from_z[k, :, lanes].astype(jnp.float32)
        out[:, lanes] = total

    def memory_core():
        mem_own.wait()
        mem_core.wait_recv()
        for theirs in (True, False):
            side = (1 - y) if theirs else y

            def body(i, carry, side=side):
                rows = pl.ds(pl.multiple_of(i * 64, 64), 64)
                macc[side, rows] = macc[side, rows] + mfrom_core[side, rows]
                return carry
            lax.fori_loop(0, 8, body, 0)
            if theirs:
                go(mem_far)

    def memory_end():
        mem_far.wait_recv()

        def body(i, carry):
            rows = pl.ds(pl.multiple_of(i * 64, 64), 64)
            mem_out[rows] = macc[y, rows].astype(jnp.float32) + mfrom_y[rows].astype(jnp.float32)
            return carry
        lax.fori_loop(0, 8, body, 0)

    def weight_rows(i, part):
        devs = pl.ds(part * 16, 16)
        return w[devs, :, pl.ds(SLAB * i, SLAB)].reshape(256, SLAB)

    def put(i, n, value):
        gs[:, :, :, :, :, pl.ds(NORM + SLAB * i + 256 * n, 256)] = value.astype(LOW).reshape(4, 2, 2, 2, ROWS, 256)

    rows_all = tgt.shape[0]

    def norm_back(i):
        r = block(i, 64)
        u, xh = dpre[r], xh1[r]
        ng[0:1] += jnp.sum(u * xh, axis=0, keepdims=True)
        ng[1:2] += jnp.sum(u, axis=0, keepdims=True)
        d = back_norm(u, gb[0:1], xh, rs1[r][:, :1])
        dpre[r] = d
        g_b[r] = d.astype(LOW)

    def self_norm():
        for copy in copies:
            copy.wait()
        each(rows_all // 64, norm_back)

    def self_out():
        out_back(g_b, lambda n: weight_rows(3, n), num_s, tot_s, dnx)
        for n in (0, 1):
            put(3, n, tmm(o_b[...], g_b[:, pl.ds(256 * n, 256)]))
        for ref in (dq, dk, dv):
            zero(ref)

    def self_tiles(i, first, last):
        def inner(kt, carry):
            r = pl.ds(i * RT, RT)
            key = kt * TILE + lane_iota((RT, TILE))
            row = i * RT + row_iota((RT, TILE))
            bias = jnp.where((key >= low_s[r]) & (key <= row), 0.0, HIDE)
            tile_backward(r, block(kt), bias, qs, ks, vs, dnx, dq, dk, dv)
            return carry
        lax.fori_loop(first, last, inner, 0)

    def self_grads():
        def lower(i):
            r = block(i, 64)
            qs[r] = (dq[r] * 0.125).astype(LOW)
            ks[r] = dk[r].astype(LOW)
            vs[r] = dv[r].astype(LOW)
        each(rows_all // 64, lower)
        for i, src in ((0, qs), (1, ks), (2, vs)):
            for n in (0, 1):
                put(i, n, tmm(tgt[...], src[:, pl.ds(256 * n, 256)]))
        inside = lane_iota((8, TILE)) < ROWS
        for d in range(DEV):
            one = ng[:, pl.ds(TILE * (d // 8), TILE)]
            one = pltpu.roll(one, (TILE - ROWS * (d % 8)) % TILE, 1) if d % 8 else one
            one = jnp.concatenate([jnp.where(inside, one, 0.0), jnp.zeros((8, TILE), F32)], axis=0)
            gs[d // 8, d // 4 % 2, d // 2 % 2, d % 2, :, pl.ds(0, NORM)] = one.astype(LOW)
        for r in SELF_ROUNDS:
            go(core(r))

    def self_target():
        for n in (0, 1):
            total = mmt(qs[...], weight_rows(0, n)) + mmt(ks[...], weight_rows(1, n))
            cols = pl.ds(256 * n, 256)
            target_grad[:, cols] = dpre[:, cols] + total + mmt(vs[...], weight_rows(2, n))

    add_core(0)
    memory_core()
    add_core(1)
    self_norm()
    add_first(0)
    add_core(2)
    self_out()
    add_second(0)
    add_first(1)
    add_core(3)
    self_tiles(0, 0, 2)
    add_second(1)
    add_first(2)
    self_tiles(1, 0, 4)
    add_z(0)
    add_second(2)
    add_first(3)
    self_grads()
    add_core(4)
    add_core(5)
    self_target()
    to_target = pltpu.make_async_copy(target_grad, target_ref, out_sems.at[0])
    to_target.start()
    memory_end()
    to_memory = pltpu.make_async_copy(mem_out, mem_ref, out_sems.at[1])
    to_memory.start()
    add_z(1)
    add_second(3)
    add_first(4)
    add_first(5)
    add_z(2)
    add_second(4)
    add_z(3)
    add_second(5)
    add_z(4)
    add_z(5)
    to_rows = pltpu.make_async_copy(out, out_ref, out_sems.at[2])
    to_rows.start()
    for copy in (to_target, to_memory, to_rows):
        copy.wait()
    for copy in sent:
        copy.wait_send()


def scatter_all(grads, mem_grads, gathered, target, state):
    any_space = pl.BlockSpec(memory_space=pl.ANY)
    dma = pltpu.SemaphoreType.DMA
    n = len(SCATTER_ROUNDS)
    rows = mem_grads.shape[2]
    low = lambda *s: pltpu.VMEM(s, LOW)
    f32 = lambda *s: pltpu.VMEM(s, F32)
    return pl.pallas_call(
        scatter_kernel,
        out_shape=(
            jax.ShapeDtypeStruct((ROWS, LANES), F32),
            jax.ShapeDtypeStruct((rows, SLAB), F32),
            jax.ShapeDtypeStruct((rows, SLAB), F32),
        ),
        in_specs=[any_space] * 16,
        out_specs=(any_space,) * 3,
        scratch_shapes=[
            low(4, 2, 2, ROWS, LANES),
            low(4, 2, 2, ROWS, LANES),
            low(4, 2, ROWS, LANES),
            low(4, ROWS, LANES),
            low(3, ROWS, LANES),
            low(2, rows, SLAB),
            low(2, rows, SLAB),
            low(rows, SLAB),
        ]
        + [pltpu.VMEM(s.shape, s.dtype) for s in state_shapes(rows)]
        + [
            low(32, ROWS, 4 * SLAB),
            low(rows, SLAB),
            low(4, 2, 2, 2, ROWS, SELF_LANES),
            f32(rows, SLAB),
            f32(rows, SLAB),
            f32(rows, SLAB),
            low(rows, 2 * SLAB),
            low(rows, SLAB),
            f32(ROWS, LANES),
            f32(rows, SLAB),
            f32(rows, SLAB),
            dma((3,)),
            dma((n,)),
            dma(()),
            dma((14,)),
            dma((n,)),
            dma((n,)),
            dma((n, 2)),
            dma((n, 2)),
            dma((n, 2)),
            dma((n, 2)),
            dma((n, 3)),
            dma((n, 3)),
            dma((2,)),
            dma((2,)),
        ],
        compiler_params=pltpu.CompilerParams(
            collective_id=2, has_side_effects=True, vmem_limit_bytes=56 << 20),
        name="scatter",
    )(grads, mem_grads, gathered, target, *state)


def finish_kernel(rows_ref, mem_ref, target_ref, *rest):
    outs, (rows, mem, target, in_sems, out_sems) = rest[:18], rest[18:]
    copies = []
    loads = []
    half = target.shape[0] // 2
    pieces = [pl.ds(0, half), pl.ds(half, half)]
    cuts_ = [(NORM + SLAB * i, SLAB) for i in range(8)] + [(NORM + SLAB * 8, 4 * SLAB)]
    cuts_ += [(NORM + SLAB * (12 + k), SLAB) for k in range(4)]

    def load(src, dst):
        copy = pltpu.make_async_copy(src, dst, in_sems.at[len(loads)])
        copy.start()
        loads.append(copy)

    def bring(src, dst):
        copy = pltpu.make_async_copy(src, dst, out_sems.at[len(copies)])
        copy.start()
        copies.append(copy)

    for p in pieces:
        load(target_ref.at[p], target.at[p])
        load(mem_ref.at[p], mem.at[p])
    load(rows_ref, rows)
    for i, p in enumerate(pieces):
        loads[2 * i].wait()
        bring(target.at[p], outs[0].at[p])
        loads[2 * i + 1].wait()
        bring(mem.at[p], outs[1].at[p])
    loads[4].wait()
    for i, (start, width) in enumerate(cuts_):
        dst = outs[2 + i] if i < 9 else outs[11].at[pl.ds(ROWS * (i - 9), ROWS)]
        bring(rows.at[:, pl.ds(start, width)], dst)
    for i in range(6):
        outs[12 + i][...] = rows[i, pl.ds(0, ROWS)]
    for copy in copies:
        copy.wait()


def finish(rows, mem, target):
    any_space = pl.BlockSpec(memory_space=pl.ANY)
    shape = lambda *s: jax.ShapeDtypeStruct(s, F32)
    return pl.pallas_call(
        finish_kernel,
        out_shape=(shape(*target.shape), shape(*mem.shape))
        + (shape(ROWS, SLAB),) * 8
        + (shape(ROWS, 4 * SLAB), shape(4 * ROWS, SLAB))
        + (shape(ROWS),) * 6,
        in_specs=[any_space] * 3,
        out_specs=(any_space,) * 12 + (pl.BlockSpec(memory_space=pltpu.VMEM),) * 6,
        scratch_shapes=[
            pltpu.VMEM(rows.shape, F32),
            pltpu.VMEM(mem.shape, F32),
            pltpu.VMEM(target.shape, F32),
            pltpu.SemaphoreType.DMA((5,)),
            pltpu.SemaphoreType.DMA((17,)),
        ],
        name="finish",
    )(rows, mem, target)


def local(target_in, memory, out_grad, *rest):
    fast = two_by_two((lax.axis_size("dp"), lax.axis_size("mem")))
    if not fast:
        return plain(target_in, memory, out_grad, *rest)
    weights, tables = rest[:16], rest[16:]
    norms = sum(
        jnp.pad(one[None, :], ((i, ROWS - 1 - i), (0, NORM - ROWS)))
        for i, one in enumerate(weights[10:])
    )
    gathered, all_memory = gather_all(weights[:10], norms, memory)
    layer_out, grads, mem_grads, *state = compute(*tables, target_in, out_grad, all_memory, gathered)
    rows = target_in.shape[0]
    out, mem_out, target_grad = scatter_all(
        grads.reshape(4, 2, 2, 2, ROWS, LANES),
        mem_grads.reshape(2, 2, rows, SLAB),
        gathered,
        target_in,
        state,
    )
    return (layer_out,) + tuple(finish(out, mem_out, target_grad))


def solution(mesh):
    both = P(("dp", "mem"), None)
    flat = P(("dp", "mem"))
    in_specs = (both,) * 13 + (flat,) * 6 + (P("dp", None),) * 3
    out_specs = (both,) * 13 + (flat,) * 6
    return jax.shard_map(local, mesh=mesh, in_specs=in_specs, out_specs=out_specs, check_vma=False)
```

```python
import functools

import jax
import jax.numpy as jnp
from jax import lax
from jax.experimental import pallas as pl
from jax.experimental.pallas import tpu as pltpu
from jax.sharding import PartitionSpec as P

MESH = pl.DeviceIdType.MESH
SLAB = 512
NORM = 128
LANES = NORM + 16 * SLAB
ROWS = 16


def here():
    dp, mem = lax.axis_index("dp"), lax.axis_index("mem")
    return dp // 2, dp % 2, mem // 2, mem % 2


def device(z, x, y, c):
    return (z * 2 + x, y * 2 + c)


def greet(peers):
    barrier = pltpu.get_barrier_semaphore()
    for peer in peers:
        pl.semaphore_signal(barrier, inc=1, device_id=peer, device_id_type=MESH)
    pl.semaphore_wait(barrier, len(peers))


def remote(src, dst, sems, index, peer):
    send, recv = sems
    return pltpu.make_async_remote_copy(
        src_ref=src,
        dst_ref=dst,
        send_sem=send.at[index],
        recv_sem=recv.at[index],
        device_id=peer,
        device_id_type=MESH,
    )


def cuts(widths, share):
    spans, at = [], 0
    for tiles in widths:
        n = tiles * 128
        spans.append((at, at + max(1, round(tiles * share)) * 128, at + n))
        at += n
    assert at == LANES
    return tuple(spans)


GATHER_ROUNDS = cuts((17, 48), 0.25)


def gather_kernel(*refs):
    shards, norm_ref, memory_ref, lens_ref, target = refs[:10], *refs[10:14]
    out, mem_out = refs[14:16]
    state_out, refs = refs[16:28], refs[28:]
    local_sem, mem_local = refs[:2]
    z_sems, first_sems, second_sems = refs[2:4], refs[4:6], refs[6:8]
    across, mems = refs[8:10], refs[10:12]
    stage, mem_stage = refs[12:14]
    state, refs = refs[14:26], refs[26:]
    after, a_b, xh1, rs1, num, tot, qs, ks, vs, o_b, gb, low_s = state
    w, norms, tgt, starts, state_sems = refs
    z, x, y, c = here()
    xp, yp, cp_ = device(z, 1 - x, y, c), device(z, x, 1 - y, c), device(z, x, y, 1 - c)
    own = out.at[z, x, y, c]
    rounds = range(len(GATHER_ROUNDS))

    local = []

    def bring(src, start, width):
        local.append(
            pltpu.make_async_copy(src, stage.at[:, pl.ds(start, width)], local_sem.at[len(local)])
        )

    bring(norm_ref, 0, NORM)
    for i in range(8):
        bring(shards[i], NORM + SLAB * i, SLAB)
    bring(shards[8], NORM + SLAB * 8, 4 * SLAB)
    for k in range(4):
        bring(shards[9].at[pl.ds(ROWS * k, ROWS)], NORM + SLAB * (12 + k), SLAB)
    for one in local:
        one.start()
    keep = pltpu.make_async_copy(memory_ref, mem_stage, mem_local.at[0])
    keep.start()
    zn = [device((z + k) % 4, x, y, c) for k in (1, 3)]
    greet([xp, yp, cp_] + zn)
    for one in local:
        one.wait()
    own_out = pltpu.make_async_copy(stage, own, mem_local.at[1])
    own_out.start()

    def column(slot):
        return z if slot == 0 else (z - slot if slot < 4 else z + (slot - 3))

    def there(slot):
        return None if slot == 0 else (z >= slot if slot < 4 else z <= 6 - slot)

    def both(a, b):
        return b if a is None else (a if b is None else jnp.logical_and(a, b))

    def guarded(cond, body):
        if cond is None:
            body()
        else:
            pl.when(cond)(body)

    sent = []

    def go(make, cond=None):
        guarded(cond, lambda: make().start())
        sent.append((cond, make))

    def along(slot, r, up):
        a, _, b = GATHER_ROUNDS[r]
        ref = out.at[column(slot), x, y, c, :, pl.ds(a, b - a)]
        src = stage.at[:, pl.ds(a, b - a)] if slot == 0 else ref
        d = 0 if slot == 0 else (slot if slot < 4 else slot - 3)
        peer = device((z + (1 if up else 3)) % 4, x, y, c)
        return remote(src, ref, z_sems, (0 if up else 1, d, r), peer)

    def arrived(slot, r):
        a, _, b = GATHER_ROUNDS[r]
        ref = out.at[column(slot), x, y, c, :, pl.ds(a, b - a)]
        up = slot < 4
        index = (0 if up else 1, (slot if up else slot - 3) - 1, r)
        return remote(ref, ref, z_sems, index, xp)

    def first(slot, r, part, arriving=False):
        a, m, b = GATHER_ROUNDS[r]
        zz = column(slot)
        if part == 0:
            ref = out.at[zz, (1 - x) if arriving else x, y, c, :, pl.ds(a, m - a)]
        else:
            ref = out.at[zz, x, (1 - y) if arriving else y, c, :, pl.ds(m, b - m)]
        lanes = pl.ds(a, m - a) if part == 0 else pl.ds(m, b - m)
        src = stage.at[:, lanes] if slot == 0 and not arriving else ref
        return remote(src, ref, first_sems, (slot, part, r), xp if part == 0 else yp)

    def second(slot, r, part, hop, arriving=False):
        a, m, b = GATHER_ROUNDS[r]
        zz = column(slot)
        if part == 0:
            side = (1 - x) if hop else x
            ref = out.at[zz, side, (1 - y) if arriving else y, c, :, pl.ds(a, m - a)]
        else:
            side = (1 - y) if hop else y
            ref = out.at[zz, (1 - x) if arriving else x, side, c, :, pl.ds(m, b - m)]
        lanes = pl.ds(a, m - a) if part == 0 else pl.ds(m, b - m)
        src = stage.at[:, lanes] if slot == 0 and not (arriving or hop) else ref
        return remote(src, ref, second_sems, (slot, part, hop, r), yp if part == 0 else xp)

    def over(slot, r, arriving=False):
        a, _, b = GATHER_ROUNDS[r]
        ref = out.at[column(slot), :, :, (1 - c) if arriving else c, :, pl.ds(a, b - a)]
        return remote(ref, ref, across, (slot, r), cp_)

    def spread(slot, r):
        cond = there(slot)
        for part in (1, 0):
            go(functools.partial(first, slot, r, part), cond)
        for part in (1, 0):
            go(functools.partial(second, slot, r, part, 0), cond)

    def from_z(d, r):
            for slot in (d, d + 3):
                cond = there(slot)
                guarded(cond, lambda slot=slot, r=r: arrived(slot, r).wait_recv())
                if d < 3:
                    onward = z < 3 if slot < 4 else z > 0
                    go(functools.partial(along, slot, r, slot < 4), both(cond, onward))
                spread(slot, r)

    def pass_on(slots, r):
            for slot in slots:
                cond = there(slot)
                for part in (1, 0):
                    guarded(cond, lambda s=slot, r=r, p=part: first(s, r, p, True).wait_recv())
                    go(functools.partial(second, slot, r, part, 1), cond)

    def hand_over(slots, r):
            for slot in slots:
                cond = there(slot)
                for part in (0, 1):
                    for hop in (0, 1):
                        guarded(cond, lambda s=slot, r=r, p=part, h=hop: second(s, r, p, h, True).wait_recv())
                go(functools.partial(over, slot, r), cond)

    for r in rounds:
        go(functools.partial(along, 0, r, True), z < 3)
        go(functools.partial(along, 0, r, False), z > 0)
        spread(0, r)
    mem_own = mem_out.at[y, c]

    def memory_rows():
        keep.wait()
        kept = pltpu.make_async_copy(mem_stage, mem_own, mem_local.at[2])
        kept.start()
        go(lambda: remote(mem_stage, mem_own, mems, 0, yp))
        go(lambda: remote(mem_stage, mem_own, mems, 1, cp_))
        return kept

    def memory_far():
        far = mem_out.at[1 - y, c]
        remote(far, far, mems, 0, yp).wait_recv()
        go(lambda: remote(far, far, mems, 2, cp_))

    everyone = (0, 1, 4, 2, 5, 3, 6)

    def all_over(r):
        for slot in everyone:
            guarded(there(slot), lambda s=slot: over(s, r, True).wait_recv())

    rows_all = tgt.shape[0]
    n_sent = starts.shape[0]
    loads = [pltpu.make_async_copy(target, tgt, state_sems.at[12])]
    loads.append(pltpu.make_async_copy(out.at[:, :, :, :, :, pl.ds(NORM, 4 * SLAB)], w, state_sems.at[13]))
    loads.append(pltpu.make_async_copy(out.at[:, :, :, :, :, pl.ds(0, NORM)], norms, state_sems.at[14]))
    saves = [pltpu.make_async_copy(src, dst, state_sems.at[i]) for i, (src, dst) in enumerate(zip(state, state_out))]

    def weight(i, n):
        return w[:, :, :, :, :, pl.ds(SLAB * i + 256 * n, 256)].reshape(SLAB, 256)

    def prepare():
        base = lax.axis_index("mem") * n_sent

        def count(j, at):
            starts[j] = at
            return at + lens_ref[0, base + j]
        lax.fori_loop(0, n_sent, count, jnp.int32(0))
        for i in range(rows_all // TILE):
            row = i * TILE + row_iota((TILE, TILE))
            found = jnp.zeros((TILE, TILE), jnp.int32)
            for j in range(n_sent):
                found = jnp.where(row >= starts[j], starts[j], found)
            low_s[pl.ds(i * TILE, TILE)] = found
        zero(num)
        zero(tot)

    def project():
        for one in loads:
            one.wait()
        for j in range(SLAB // TILE):
            total = jnp.zeros((8, TILE), F32)
            for k in range(8):
                d = 8 * j + k
                one = norms[d // 8, d // 4 % 2, d // 2 % 2, d % 2].astype(F32)[:8]
                total = total + (pltpu.roll(one, ROWS * k, 1) if k else one)
            gb[:, pl.ds(TILE * j, TILE)] = total
        for i, dst in ((0, qs), (1, ks), (2, vs)):
            for n in (0, 1):
                value = mm(tgt[...], weight(i, n)).astype(LOW)
                dst[:, pl.ds(256 * n, 256)] = value * jnp.asarray(0.125, LOW) if i == 0 else value

    def self_tiles(i, first_tile, last_tile):
        def inner(kt, carry):
            r = pl.ds(i * RT, RT)
            key = kt * TILE + lane_iota((RT, TILE))
            row = i * RT + row_iota((RT, TILE))
            bias = jnp.where((key >= low_s[r]) & (key <= row), 0.0, HIDE)
            tile_forward(r, block(kt), bias, qs, ks, vs, num, tot)
            return carry
        lax.fori_loop(first_tile, last_tile, inner, 0)

    def project_out():
        divide(num, tot, o_b, rows_all)
        for n in (0, 1):
            cols = pl.ds(256 * n, 256)
            after[:, cols] = tgt[:, cols].astype(F32) + mm(o_b[...], weight(3, n))

    def norm_rows(i):
        r = block(i, 64)
        xh, rs = normalize(after[r])
        xh1[r] = xh
        rs1[r] = jnp.broadcast_to(rs, (64, TILE))
        value = xh * gb[0:1] + gb[1:2]
        after[r] = value
        a_b[r] = value.astype(LOW)

    loads[0].start()
    prepare()
    from_z(1, 0)
    from_z(1, 1)
    pass_on((0,), 0)
    from_z(2, 0)
    pass_on((0,), 1)
    pass_on((1, 4), 0)
    from_z(3, 0)
    from_z(2, 1)
    pass_on((2, 5), 0)
    own_out.wait()
    hand_over((0,), 0)
    pass_on((1, 4), 1)
    pass_on((3, 6), 0)
    kept = memory_rows()
    hand_over((1, 4), 0)
    hand_over((2, 5), 0)
    from_z(3, 1)
    hand_over((3, 6), 0)
    all_over(0)
    loads[1].start()
    loads[2].start()
    pass_on((2, 5), 1)
    project()
    hand_over((0,), 1)
    self_tiles(0, 0, 2)
    pass_on((3, 6), 1)
    self_tiles(1, 0, 4)
    hand_over((1, 4), 1)
    memory_far()
    project_out()
    each(rows_all // 64, norm_rows)
    hand_over((2, 5), 1)
    hand_over((3, 6), 1)
    for one in saves:
        one.start()
    all_over(1)
    for one in saves:
        one.wait()
    for i, side in ((1, y), (2, 1 - y)):
        last = mem_out.at[side, 1 - c]
        remote(last, last, mems, i, cp_).wait_recv()
    kept.wait()
    for cond, make in sent:
        guarded(cond, lambda make=make: make().wait_send())


def gather_all(shards, norms, memory, lens, target):
    any_space = pl.BlockSpec(memory_space=pl.ANY)
    dma = pltpu.SemaphoreType.DMA
    n = len(GATHER_ROUNDS)
    both = lambda *s: [dma(s), dma(s)]
    state = forward_shapes(target.shape[0])
    low = lambda *s: pltpu.VMEM(s, LOW)
    gathered, whole_memory, *saved = pl.pallas_call(
        gather_kernel,
        out_shape=(
            jax.ShapeDtypeStruct((4, 2, 2, 2, ROWS, LANES), jnp.bfloat16),
            jax.ShapeDtypeStruct((2, 2) + memory.shape, jnp.bfloat16),
        )
        + state,
        in_specs=[any_space] * 12 + [pl.BlockSpec(memory_space=pltpu.SMEM), any_space],
        out_specs=(any_space,) * 14,
        scratch_shapes=[dma((14,)), dma((3,))]
        + both(2, 3, n) + both(7, 2, n) + both(7, 2, 2, n) + both(7, n) + both(3)
        + [low(ROWS, LANES), low(*memory.shape)]
        + [pltpu.VMEM(s.shape, s.dtype) for s in state]
        + [
            low(4, 2, 2, 2, ROWS, 4 * SLAB),
            low(4, 2, 2, 2, ROWS, NORM),
            low(*target.shape),
            pltpu.SMEM((16,), jnp.int32),
            dma((15,)),
        ],
        compiler_params=pltpu.CompilerParams(
            collective_id=1, has_side_effects=True, vmem_limit_bytes=60 << 20),
        name="gather",
    )(*shards, norms, memory, lens, target)
    return gathered.reshape(32, ROWS, LANES), whole_memory.reshape(-1, SLAB), saved


def forward_shapes(rows):
    full = lambda dtype, lanes=SLAB, n=rows: jax.ShapeDtypeStruct((n, lanes), dtype)
    return (
        full(F32),
        full(LOW),
        full(F32),
        full(F32, TILE),
        full(F32),
        full(F32),
        full(LOW),
        full(LOW),
        full(LOW),
        full(LOW),
        full(F32, SLAB, 8),
        full(jnp.int32, TILE),
    )


def two_by_two(mesh_axes):
    return mesh_axes == (8, 4)


def gather_any(shards, norms, memory):
    everyone = ("dp", "mem")
    packed = jnp.concatenate([norms] + list(shards[:9]), axis=1)
    rows = lax.all_gather(packed, everyone, axis=0, tiled=True).reshape(32, ROWS, -1)
    last = lax.all_gather(shards[9], everyone, axis=0, tiled=True)
    last = last.reshape(32, 4, ROWS, SLAB).transpose(0, 2, 1, 3).reshape(32, ROWS, 4 * SLAB)
    return (
        jnp.concatenate([rows, last], axis=2),
        lax.all_gather(memory, "mem", axis=0, tiled=True),
    )


def scatter_any(grads, mem_grads):
    everyone = ("dp", "mem")
    wide = grads.reshape(32, ROWS, LANES).astype(jnp.float32)
    cut = LANES - 4 * SLAB
    rows = lax.psum_scatter(
        wide[:, :, :cut].reshape(512, cut), everyone, scatter_dimension=0, tiled=True
    )
    last = wide[:, :, cut:].reshape(32, ROWS, 4, SLAB).transpose(0, 2, 1, 3).reshape(2048, SLAB)
    last = lax.psum_scatter(last, everyone, scatter_dimension=0, tiled=True)
    mem = lax.psum_scatter(
        mem_grads.astype(jnp.float32), "mem", scatter_dimension=0, tiled=True
    )
    return rows, last, mem
HEADS = 8
HEAD = 64
eps_norm = 1e-05
score_scale = 0.125


def layer_norm(values, gain, shift):
    centre = values - jnp.mean(values, axis=-1, keepdims=True)
    spread = jnp.mean(centre * centre, axis=-1, keepdims=True)
    return centre * lax.rsqrt(spread + eps_norm) * gain + shift


def head_split(values):
    return values.reshape(values.shape[0], HEADS, HEAD)


def matmul(left, right):
    return jnp.dot(left, right, preferred_element_type=jnp.float32)


def left_grad(inputs, grads):
    return jnp.einsum("ra,rb->ab", inputs, grads, preferred_element_type=jnp.float32)


def back_through(grads, weight):
    return jnp.einsum("rb,ab->ra", grads, weight, preferred_element_type=jnp.float32)


def exp_scores(q_block, keys, low_edge, high_edge):
    raw = jnp.einsum("qhd,khd->hqk", head_split(q_block), head_split(keys),
                     preferred_element_type=jnp.float32) * score_scale
    position = lax.broadcasted_iota(jnp.int32, (q_block.shape[0], keys.shape[0]), 1)
    allowed = (position >= low_edge[:, None]) & (position < high_edge[:, None])
    return jnp.where(allowed[None], jnp.exp(raw), 0.0)


def attend(queries, keys, values, low_edge, high_edge):
    expo = exp_scores(queries, keys, low_edge, high_edge)
    numer = jnp.einsum("hqk,khd->qhd", expo.astype(jnp.bfloat16), head_split(values),
                       preferred_element_type=jnp.float32)
    totals = jnp.sum(expo, axis=2).T
    return (numer / totals[:, :, None]).reshape(queries.shape[0], -1), totals


def attend_back(queries, keys, values, low_edge, high_edge, upstream, output, totals):
    expo = exp_scores(queries, keys, low_edge, high_edge)
    up = head_split(upstream.astype(jnp.float32))
    numer_grad = (up / totals[:, :, None]).astype(jnp.bfloat16)
    corr = -jnp.sum(up * head_split(output), axis=2) / totals
    flow = jnp.einsum("qhd,khd->hqk", numer_grad, head_split(values),
                      preferred_element_type=jnp.float32) + corr.T[:, :, None]
    ds = (expo * flow).astype(jnp.bfloat16)
    dq = jnp.einsum("hqk,khd->qhd", ds, head_split(keys), preferred_element_type=jnp.float32)
    dk = jnp.einsum("hqk,qhd->khd", ds, head_split(queries), preferred_element_type=jnp.float32)
    dv = jnp.einsum("hqk,qhd->khd", expo.astype(jnp.bfloat16), numer_grad,
                    preferred_element_type=jnp.float32)
    flat = lambda v: v.reshape(v.shape[0], -1)
    return ((flat(dq) * score_scale).astype(jnp.bfloat16), (flat(dk) * score_scale).astype(jnp.bfloat16),
            flat(dv).astype(jnp.bfloat16))


def plain(target_in, memory, out_grad, *rest):
    weights, (tgt_lens, src_lens, src_offsets) = rest[:16], rest[16:]
    member = lax.axis_index("mem")
    per_device = tgt_lens.shape[1] // lax.axis_size("mem")
    pick = lambda table: lax.dynamic_slice_in_dim(table[0], member * per_device, per_device, 0)
    lengths, spans, offsets = pick(tgt_lens), pick(src_lens), pick(src_offsets)
    norms = jnp.stack(weights[10:], axis=1)
    norms = jnp.pad(norms, ((0, 0), (0, NORM - norms.shape[1])))
    gathered, all_memory = gather_any(weights[:10], norms, memory)
    W = gathered.reshape(512, LANES)
    mat = lambda i: W[:, NORM + SLAB * i : NORM + SLAB * (i + 1)]
    wsq, wsk, wsv, wso, wcq, wck, wcv, wco = [mat(i) for i in range(8)]
    w1 = W[:, NORM + 8 * SLAB : NORM + 12 * SLAB]
    w2 = gathered[:, :, NORM + 12 * SLAB :].reshape(32, 16, 4, SLAB).transpose(0, 2, 1, 3).reshape(2048, SLAB)
    ga, sa, gc, sc, gf, sf = [W[:, i].astype(jnp.float32) for i in range(6)]
    rows = target_in.shape[0]
    starts = jnp.cumsum(lengths) - lengths
    position = lax.iota(jnp.int32, rows)
    sentence = jnp.sum((position[:, None] >= starts[None, :]).astype(jnp.int32), axis=1) - 1
    picker = sentence[:, None] == lax.iota(jnp.int32, per_device)[None, :]
    choose = lambda v: jnp.sum(jnp.where(picker, v[None, :], 0), axis=1)
    self_low, self_high = choose(starts), position + 1
    cross_low = choose(offsets)
    cross_high = cross_low + choose(spans)
    low = jnp.bfloat16
    q, k, v = [matmul(target_in, w).astype(low) for w in (wsq, wsk, wsv)]
    o_self_f, tot_self = attend(q, k, v, self_low, self_high)
    o_self = o_self_f.astype(low)
    after_self, pull_self = jax.vjp(layer_norm, target_in.astype(jnp.float32) + matmul(o_self, wso), ga, sa)
    a_b = after_self.astype(low)
    qc = matmul(a_b, wcq).astype(low)
    kc, vc = matmul(all_memory, wck).astype(low), matmul(all_memory, wcv).astype(low)
    cut = lambda v: v.reshape((4, -1) + v.shape[1:])
    o_c_f, tot_c = lax.map(
        lambda p: attend(p[0], kc, vc, p[1], p[2]), (cut(qc), cut(cross_low), cut(cross_high))
    )
    o_c_f, tot_c = o_c_f.reshape(rows, -1), tot_c.reshape(rows, -1)
    o_c = o_c_f.astype(low)
    after_cross, pull_cross = jax.vjp(layer_norm, after_self + matmul(o_c, wco), gc, sc)
    c_b = after_cross.astype(low)
    hidden = matmul(c_b, w1)
    activated, pull_silu = jax.vjp(jax.nn.silu, hidden)
    act = activated.astype(low)
    final, pull_ffn = jax.vjp(layer_norm, after_cross + matmul(act, w2), gf, sf)
    d_pre_out, g_gf, g_sf = pull_ffn(out_grad.astype(jnp.float32))
    d_branch = d_pre_out.astype(low)
    g_w2 = left_grad(act, d_branch)
    d_hidden = pull_silu(back_through(d_branch, w2))[0].astype(low)
    g_w1 = left_grad(c_b, d_hidden)
    d_pre_cross, g_gc, g_sc = pull_cross(d_pre_out + back_through(d_hidden, w1))
    d_cb = d_pre_cross.astype(low)
    g_wco = left_grad(o_c, d_cb)
    d_oc = back_through(d_cb, wco).astype(low)

    def piece(carry, p):
        dq, dk, dv = attend_back(p[0], kc, vc, p[1], p[2], p[3], p[4], p[5])
        return (carry[0] + dk, carry[1] + dv), dq

    empty = jnp.zeros(kc.shape, jnp.bfloat16)
    (dk_c, dv_c), dq_c = lax.scan(
        piece,
        (empty, empty),
        tuple(cut(v) for v in (qc, cross_low, cross_high, d_oc, o_c_f, tot_c)),
    )
    dq_c = dq_c.reshape(rows, -1)
    g_wcq, g_wck, g_wcv = left_grad(a_b, dq_c), left_grad(all_memory, dk_c), left_grad(all_memory, dv_c)
    mem_grad = back_through(dk_c, wck) + back_through(dv_c, wcv)
    d_pre_self, g_ga, g_sa = pull_self(d_pre_cross + back_through(dq_c, wcq))
    d_sb = d_pre_self.astype(low)
    g_wso = left_grad(o_self, d_sb)
    d_os = back_through(d_sb, wso).astype(low)
    dq, dk, dv = attend_back(q, k, v, self_low, self_high, d_os, o_self_f, tot_self)
    g_wsq, g_wsk, g_wsv = left_grad(target_in, dq), left_grad(target_in, dk), left_grad(target_in, dv)
    target_grad = d_pre_self + back_through(dq, wsq) + back_through(dk, wsk) + back_through(dv, wsv)
    n_g = jnp.pad(jnp.stack([g_ga, g_sa, g_gc, g_sc, g_gf, g_sf], axis=1), ((0, 0), (0, NORM - 6)))
    g_w2p = g_w2.reshape(32, 4, 16, SLAB).transpose(0, 2, 1, 3).reshape(512, 4 * SLAB)
    grads = jnp.concatenate([g.astype(low) for g in (n_g, g_wsq, g_wsk, g_wsv, g_wso, g_wcq, g_wck, g_wcv, g_wco, g_w1, g_w2p)], axis=1)
    part = lambda i, n=1: out[:, NORM + SLAB * i : NORM + SLAB * (i + n)]
    out, w2_grad, mem_out = scatter_any(grads, mem_grad.astype(low))
    return (final.astype(low), target_grad, mem_out) + tuple(part(i) for i in range(8)) + (part(8, 4), w2_grad) + tuple(out[:, i] for i in range(6))


TILE = 128
RT = 256
CHUNK = 256
EPS = 1e-05
HIDE = -1e30
LOW = jnp.bfloat16
F32 = jnp.float32
DEV = 32
CUT = NORM + 12 * SLAB


def mm(a, b):
    return jnp.dot(a, b, preferred_element_type=F32)


def mmt(a, b):
    return lax.dot_general(a, b, (((1,), (1,)), ((), ())), preferred_element_type=F32)


def tmm(a, b):
    return lax.dot_general(a, b, (((0,), (0,)), ((), ())), preferred_element_type=F32)


def lane_iota(shape):
    return lax.broadcasted_iota(jnp.int32, shape, len(shape) - 1)


def row_iota(shape):
    return lax.broadcasted_iota(jnp.int32, shape, 0)


def halves():
    lane = lane_iota((1, TILE))
    even = jnp.where(lane < 64, 1.0, 0.0).astype(LOW)
    odd = jnp.where(lane < 64, 0.0, 1.0).astype(LOW)
    return even, odd


def stacked(block, even, odd):
    return jnp.concatenate([block * even, block * odd], axis=0)


def fold(pair):
    lane = lane_iota((TILE, TILE))
    return jnp.where(lane < 64, pair[:TILE], pair[TILE:])


def totals_block(even, odd):
    wide = lambda v: jnp.broadcast_to(v, (TILE, TILE))
    return jnp.concatenate([wide(even), wide(odd)], axis=0)


def corr_block():
    lane = lane_iota((TILE, TILE))
    a = jnp.where(lane < 2, 1.0, 0.0).astype(LOW)
    b = jnp.where((lane >= 64) & (lane < 66), 1.0, 0.0).astype(LOW)
    return jnp.concatenate([a, b], axis=0)


def tile_forward(rows, keys, bias, q, k, v, num, tot):
    even, odd = halves()
    ones = totals_block(even, odd)
    bias2 = jnp.concatenate([bias, bias], axis=1)
    for h in range(4):
        cols = pl.ds(TILE * h, TILE)
        s = mmt(q[rows, cols], stacked(k[keys, cols], even, odd))
        e = jnp.exp(s + bias2).astype(LOW)
        both = mm(e, jnp.concatenate([stacked(v[keys, cols], even, odd), ones], axis=1))
        num[rows, cols] += both[:, :TILE]
        tot[rows, cols] += both[:, TILE:]


def tile_backward(rows, keys, bias, q, k, v, dnx, dq, dk, dv):
    even, odd = halves()
    ones = corr_block()
    bias2 = jnp.concatenate([bias, bias], axis=1)
    for h in range(4):
        cols = pl.ds(TILE * h, TILE)
        qb = q[rows, cols]
        ks = stacked(k[keys, cols], even, odd)
        e = jnp.exp(mmt(qb, ks) + bias2)
        vs = jnp.concatenate([stacked(v[keys, cols], even, odd), ones], axis=1)
        flow = mmt(dnx[rows, pl.ds(2 * TILE * h, 2 * TILE)], vs)
        ds = (e * flow).astype(LOW)
        dq[rows, cols] += mm(ds, ks)
        dk[keys, cols] += fold(tmm(ds, qb))
        dv[keys, cols] += fold(tmm(e.astype(LOW), dnx[rows, pl.ds(2 * TILE * h, TILE)]))


def each(count, body):
    def step(i, carry):
        body(i)
        return carry
    if isinstance(count, int) and count <= 2:
        for i in range(count):
            body(i)
        return
    lax.fori_loop(0, count, step, 0, unroll=8 if isinstance(count, int) else 1)


def zero(ref, step=128):
    def body(i):
        rows = pl.ds(pl.multiple_of(i * step, step), step)
        ref[rows] = jnp.zeros((step,) + ref.shape[1:], ref.dtype)
    each(ref.shape[0] // step, body)


def columns(part, width=256):
    return pl.ds(pl.multiple_of(part * width, width), width)


def block(i, width=TILE):
    return pl.ds(pl.multiple_of(i * width, width), width)


def back_norm(u, gain, xh, r):
    gu = u * gain
    a = jnp.mean(gu, axis=1, keepdims=True)
    b = jnp.mean(gu * xh, axis=1, keepdims=True)
    return (gu - a - xh * b) * r


def out_back(g_b, weight_rows, num, tot, dnx):
    lane = lane_iota((TILE, TILE))
    same = jnp.where((lane < 64) == (row_iota((TILE, TILE)) < 64), 1.0, 0.0).astype(LOW)

    def body(n):
        up = mmt(g_b[...], weight_rows(n)).astype(LOW).astype(F32)
        for h in range(2):
            cols = pl.ds(pl.multiple_of(n * 256 + h * TILE, TILE), TILE)
            wide = lambda k: pl.ds(pl.multiple_of(n * 512 + h * 256 + k * TILE, TILE), TILE)
            d = up[:, h * TILE:(h + 1) * TILE]
            t = tot[:, cols]
            dnx[:, wide(0)] = (d / t).astype(LOW)
            p = d * num[:, cols]
            p1 = p.astype(LOW)
            p2 = (p - p1.astype(F32)).astype(LOW)
            corr = -(mm(p1, same) + mm(p2, same)) / t
            c1 = corr.astype(LOW)
            c2 = (corr - c1.astype(F32)).astype(LOW)
            place = lane_iota(c1.shape) % 64
            nothing = jnp.zeros_like(c1)
            dnx[:, wide(1)] = jnp.where(place == 0, c1, jnp.where(place == 1, c2, nothing))
    each(2, body)


def divide(num, tot, out, rows_all):
    def body(i):
        r = block(i, 64)
        o = num[r] / tot[r]
        num[r] = o
        out[r] = o.astype(LOW)
    each(rows_all // 64, body)


def normalize(y):
    mean = jnp.mean(y, axis=1, keepdims=True)
    centre = y - mean
    r = lax.rsqrt(jnp.mean(centre * centre, axis=1, keepdims=True) + EPS)
    return centre * r, r


def compute_kernel(lens_ref, spans_ref, offs_ref, out_grad, memory, gathered, after_ref, low_ref, gains_ref,
                   layer_out, grads, mem_grads, dpre_out, ng_out, *scratch):
    (w, w2, og, mem, qc, kc, vc, big, act, dhid, dv, num_c, tot_c, xh2, t1, dpre, dq, rs2,
     oc_b, a_b, c_b, g_b, dnx, ng, gb, lout, low_c, high_c, memc, sel, idx,
     starts, packed, in_sem, w_sem, out_sem) = scratch
    n_src = mem.shape[0]
    rows_all = og.shape[0]
    n_sent = starts.shape[0] - 1
    member = lax.axis_index("mem")
    base = member * n_sent

    loads = {}

    def load(name, src, dst, sem):
        loads[name] = pltpu.make_async_copy(src, dst, sem)
        loads[name].start()

    def load_slab(i, count=1):
        lanes = pl.ds(NORM + SLAB * i, SLAB * count)
        load(i, gathered.at[:, :, lanes], w.at[:, :, lanes], w_sem.at[i])

    load("a", low_ref, a_b, in_sem.at[0])
    load_slab(4)
    load("mem", memory, mem, in_sem.at[1])
    load_slab(5)
    load_slab(6)

    def load_rest():
        load("t1", after_ref, t1, in_sem.at[3])
        load("gb", gains_ref, gb, in_sem.at[4])
        load_slab(7)
        load_slab(8, 4)
        for k in range(4):
            load(("w2", k), gathered.at[:, :, pl.ds(CUT + SLAB * k, SLAB)], w2.at[:, k], w_sem.at[13 + k])
        load("og", out_grad, og, in_sem.at[2])

    outs = []

    def send(src, dst):
        copy = pltpu.make_async_copy(src, dst, out_sem.at[len(outs)])
        copy.start()
        outs.append(copy)

    def weight(i, part=None, width=256):
        if part is None:
            return w[:, :, pl.ds(NORM + SLAB * i, SLAB)].reshape(SLAB, SLAB)
        start = pl.multiple_of(NORM + SLAB * i + part * width, TILE)
        return w[:, :, pl.ds(start, width)].reshape(SLAB, width)

    def weight_rows(i, part, width=256, lanes=SLAB):
        devs = pl.ds(pl.multiple_of(part * (width // ROWS), width // ROWS), width // ROWS)
        return w[devs, :, pl.ds(NORM + SLAB * i, lanes)].reshape(width, lanes)

    def put_weight(i, part, value, width=256):
        start = pl.multiple_of(NORM + SLAB * i + part * width, TILE)
        w[:, :, pl.ds(start, width)] = value.astype(LOW).reshape(DEV, ROWS, width)

    def count(j, at):
        starts[j] = at
        return at + lens_ref[0, base + j]
    starts[n_sent] = lax.fori_loop(0, n_sent, count, jnp.int32(0))

    def count_packed(j, at):
        packed[j] = at
        return at + spans_ref[0, base + j]
    n_keys = lax.fori_loop(0, n_sent, count_packed, jnp.int32(0))
    packed[n_sent] = n_keys
    chunks = (n_keys + CHUNK - 1) // CHUNK

    def lows(i):
        row = i * TILE + row_iota((TILE, TILE))
        nothing = jnp.zeros((TILE, TILE), jnp.int32)

        def pick(j, found):
            here_on = row >= starts[j]
            values = (packed[j], packed[j + 1])
            return tuple(jnp.where(here_on, v, f) for v, f in zip(values, found))
        low_c[block(i)], high_c[block(i)] = lax.fori_loop(0, n_sent, pick, (nothing, nothing))
    each(rows_all // TILE, lows)
    zero(num_c)
    zero(tot_c)
    ng[...] = jnp.zeros_like(ng)

    def last_at(table, row):
        def pick(j, found):
            return jnp.where(starts[j] <= row, table(j), found)
        return lax.fori_loop(0, n_sent, pick, jnp.int32(0))

    def tiles(body, bias, first, last):
        def outer(i, carry):
            def inner(kt, carry):
                body(block(i, RT), block(kt), bias(i, kt))
                return carry
            return lax.fori_loop(first(i) // TILE, (last(i) - 1) // TILE + 1, inner, carry)
        lax.fori_loop(0, rows_all // RT, outer, 0)

    def cross_tiles(body):
        def bias(i, kt):
            key = kt * TILE + lane_iota((RT, TILE))
            r = block(i, RT)
            return jnp.where((key >= low_c[r]) & (key < high_c[r]), 0.0, HIDE)
        tiles(body, bias, lambda i: last_at(lambda j: packed[j], i * RT),
              lambda i: last_at(lambda j: packed[j + 1], (i + 1) * RT - 1))

    loads["a"].wait()
    loads[4].wait()

    def query(n):
        qc[:, columns(n)] = mm(a_b[...], weight(4, n)).astype(LOW) * jnp.asarray(0.125, LOW)
    each(2, query)
    load_rest()
    for name in ("mem", 5, 6):
        loads[name].wait()

    def choose(ct):
        r = block(ct, CHUNK)
        for g in range(n_src // TILE):
            hit = idx[r] == g * TILE + lane_iota((CHUNK, TILE))
            sel[:, g * TILE:(g + 1) * TILE] = jnp.where(hit, 1.0, 0.0).astype(LOW)

    def keys(ct):
        r = block(ct, CHUNK)
        key = ct * CHUNK + row_iota((CHUNK, TILE))

        def pick(j, found):
            return jnp.where(key >= packed[j], offs_ref[0, base + j] - packed[j] + key, found)
        at = lax.fori_loop(0, n_sent, pick, jnp.zeros((CHUNK, TILE), jnp.int32))
        idx[r] = jnp.where(key < n_keys, at, -1)
        choose(ct)

        def bring(n):
            memc[r, columns(n)] = mm(sel[...], mem[:, columns(n)]).astype(LOW)
        each(2, bring)

        def project(n):
            kc[r, columns(n)] = mm(memc[r], weight(5, n)).astype(LOW)
            vc[r, columns(n)] = mm(memc[r], weight(6, n)).astype(LOW)
        each(2, project)
    each(chunks, keys)

    cross_tiles(lambda r, k, bias: tile_forward(r, k, bias, qc, kc, vc, num_c, tot_c))
    divide(num_c, tot_c, oc_b, rows_all)
    for name in (7, "t1", "gb"):
        loads[name].wait()

    def cross_out(n):
        t1[:, columns(n)] += mm(oc_b[...], weight(7, n))
    each(2, cross_out)

    def norm_cross(i):
        r = block(i, 64)
        xh, rs = normalize(t1[r])
        xh2[r] = xh
        rs2[r] = jnp.broadcast_to(rs, (64, TILE))
        after = xh * gb[2:3] + gb[3:4]
        t1[r] = after
        c_b[r] = after.astype(LOW)
    each(rows_all // 64, norm_cross)

    loads[8].wait()

    def hidden(n):
        v = mm(c_b[...], weight(8, n))
        sig = 1.0 / (1.0 + jnp.exp(-v))
        act[:, columns(n)] = (v * sig).astype(LOW)
        big[block(n // 2, SLAB), columns(n % 2)] = sig * (1.0 + v * (1.0 - sig))
    each(8, hidden)
    for k in range(4):
        loads[("w2", k)].wait()

    def ffn_out(n):
        cols = columns(n)
        t1[:, cols] += mm(act[...], w2[:, :, :, cols].reshape(4 * SLAB, 256))
    each(2, ffn_out)
    loads["og"].wait()

    def norm_ffn(i):
        r = block(i, 64)
        xh, rs = normalize(t1[r])
        gain = gb[4:5]
        lout[r] = (xh * gain + gb[5:6]).astype(LOW)
        u = og[r].astype(F32)
        ng[4:5] += jnp.sum(u * xh, axis=0, keepdims=True)
        ng[5:6] += jnp.sum(u, axis=0, keepdims=True)
        d = back_norm(u, gain, xh, rs)
        dpre[r] = d
        g_b[r] = d.astype(LOW)
    each(rows_all // 64, norm_ffn)
    send(lout, layer_out)

    def hidden_back(n):
        devs = pl.ds(pl.multiple_of(n * 4, 4), 4)
        part = mmt(g_b[...], w2[devs].reshape(256, SLAB))
        d = (part * big[block(n // 2, SLAB), columns(n % 2)]).astype(LOW)
        dhid[:, columns(n)] = d
        w2[devs] = tmm(act[:, columns(n)], g_b[...]).astype(LOW).reshape(4, 4, ROWS, SLAB)
    each(8, hidden_back)
    for k in range(4):
        send(w2.at[:, k], grads.at[:, :, pl.ds(CUT + SLAB * k, SLAB)])

    def input_back(n):
        dpre[:, columns(n)] += mmt(dhid[...], weight_rows(8, n, 256, 4 * SLAB))
    each(2, input_back)

    def first_grad(n):
        put_weight(8, n, tmm(c_b[...], dhid[:, columns(n)]))
    each(8, first_grad)
    lanes = pl.ds(NORM + SLAB * 8, 4 * SLAB)
    send(w.at[:, :, lanes], grads.at[:, :, lanes])

    def back_cross(i):
        r = block(i, 64)
        u, xh = dpre[r], xh2[r]
        ng[2:3] += jnp.sum(u * xh, axis=0, keepdims=True)
        ng[3:4] += jnp.sum(u, axis=0, keepdims=True)
        d = back_norm(u, gb[2:3], xh, rs2[r][:, :1])
        dpre[r] = d
        g_b[r] = d.astype(LOW)
    each(rows_all // 64, back_cross)

    out_back(g_b, lambda n: weight_rows(7, n), num_c, tot_c, dnx)

    def out_grad_store(n):
        put_weight(7, n, tmm(oc_b[...], g_b[:, columns(n)]))
    each(2, out_grad_store)

    def send_slab(i):
        lanes = pl.ds(NORM + SLAB * i, SLAB)
        send(w.at[:, :, lanes], grads.at[:, :, lanes])

    send_slab(7)
    zero(dq)

    def clear(ct):
        r = block(ct, CHUNK)
        big[r] = jnp.zeros((CHUNK, SLAB), F32)
        dv[r] = jnp.zeros((CHUNK, SLAB), F32)
    each(chunks, clear)
    cross_tiles(lambda r, k, bias: tile_backward(r, k, bias, qc, kc, vc, dnx, dq, big, dv))

    def scaled(src, dst, factor, step=64):
        def body(i):
            r = block(i, step)
            dst[r] = (src[r] * factor).astype(LOW)
        each(src.shape[0] // step, body)

    scaled(dq, qc, 0.125)

    def query_back(n):
        dpre[:, columns(n)] += mmt(qc[...], weight_rows(4, n))
    each(2, query_back)

    send(dpre, dpre_out)

    def query_grad(n):
        put_weight(4, n, tmm(a_b[...], qc[:, columns(n)]))
    each(2, query_grad)
    send_slab(4)

    zero(num_c)
    zero(tot_c)

    def memory_back(ct):
        r = block(ct, CHUNK)
        kc[r] = big[r].astype(LOW)
        vc[r] = dv[r].astype(LOW)

        def key_grad(n):
            cols = columns(n)
            num_c[:, cols] += tmm(memc[r], kc[r, cols])
            tot_c[:, cols] += tmm(memc[r], vc[r, cols])
        each(2, key_grad)

        def rows_grad(n):
            memc[r, columns(n)] = (
                mmt(kc[r], weight_rows(5, n)) + mmt(vc[r], weight_rows(6, n))).astype(LOW)
        each(2, rows_grad)
        choose(ct)

        def spread(n):
            rows = block(n, 256)
            found = tmm(sel[:, columns(n)], memc[r]).astype(LOW)
            mem[rows] = jnp.where(ct == 0, found, mem[rows] + found)
        each(n_src // 256, spread)
    each(chunks, memory_back)
    send(mem, mem_grads)

    def key_store(n):
        put_weight(5, n, num_c[:, columns(n)])
        put_weight(6, n, tot_c[:, columns(n)])
    each(2, key_store)
    send_slab(5)
    send_slab(6)

    send(ng, ng_out)
    for copy in outs:
        copy.wait()


def state_shapes(rows):
    full = lambda dtype, lanes=SLAB, n=rows: jax.ShapeDtypeStruct((n, lanes), dtype)
    return (
        full(F32),
        full(F32),
        full(F32, TILE),
        full(F32),
        full(F32),
        full(LOW),
        full(LOW),
        full(LOW),
        full(LOW),
        full(F32, SLAB, 8),
        full(F32, SLAB, 8),
        full(jnp.int32, TILE),
    )


def compute(lens, spans, offs, out_grad, memory, gathered, after, after_low, gains):
    rows, n_src = out_grad.shape[0], memory.shape[0]
    n_sent = 16
    n_keys = n_sent * 112
    any_space = pl.BlockSpec(memory_space=pl.ANY)
    smem = pl.BlockSpec(memory_space=pltpu.SMEM)
    dma = pltpu.SemaphoreType.DMA
    f32 = lambda *s: pltpu.VMEM(s, F32)
    low = lambda *s: pltpu.VMEM(s, LOW)
    return pl.pallas_call(
        compute_kernel,
        out_shape=(
            jax.ShapeDtypeStruct((rows, SLAB), LOW),
            jax.ShapeDtypeStruct((DEV, ROWS, LANES), LOW),
            jax.ShapeDtypeStruct((n_src, SLAB), LOW),
            jax.ShapeDtypeStruct((rows, SLAB), F32),
            jax.ShapeDtypeStruct((8, SLAB), F32),
        ),
        in_specs=[smem] * 3 + [any_space] * 6,
        out_specs=(any_space,) * 5,
        scratch_shapes=[
            low(DEV, ROWS, CUT),
            low(DEV, 4, ROWS, SLAB),
            low(rows, SLAB),
            low(n_src, SLAB),
            low(rows, SLAB),
            low(n_keys, SLAB),
            low(n_keys, SLAB),
            f32(4 * SLAB, SLAB),
            low(rows, 4 * SLAB),
            low(rows, 4 * SLAB),
            f32(n_keys, SLAB),
            f32(rows, SLAB),
            f32(rows, SLAB),
            f32(rows, SLAB),
            f32(rows, SLAB),
            f32(rows, SLAB),
            f32(rows, SLAB),
            f32(rows, TILE),
            low(rows, SLAB),
            low(rows, SLAB),
            low(rows, SLAB),
            low(rows, SLAB),
            low(rows, 2 * SLAB),
            f32(8, SLAB),
            f32(8, SLAB),
            low(rows, SLAB),
            pltpu.VMEM((rows, TILE), jnp.int32),
            pltpu.VMEM((rows, TILE), jnp.int32),
            low(n_keys, SLAB),
            low(CHUNK, n_src),
            pltpu.VMEM((n_keys, TILE), jnp.int32),
            pltpu.SMEM((n_sent + 1,), jnp.int32),
            pltpu.SMEM((n_sent + 1,), jnp.int32),
            dma((5,)),
            dma((17,)),
            dma((32,)),
        ],
        compiler_params=pltpu.CompilerParams(vmem_limit_bytes=60 << 20),
        name="compute",
    )(lens, spans, offs, out_grad, memory, gathered, after, after_low, gains)
def scatter_rounds(share=0.25):
    spans = []
    for at, tiles in ((33, 6), (39, 12), (51, 14), (17, 16), (0, 11), (11, 6)):
        split = at + max(1, round(tiles * share))
        spans.append((at * 128, split * 128, (at + tiles) * 128))
    return tuple(spans)


SCATTER_ROUNDS = scatter_rounds()
SELF_LANES = NORM + 4 * SLAB
SELF_ROUNDS = (4, 5)


def scatter_kernel(grads, mem_grads, gathered, target, *rest):
    state, (out_ref, mem_ref, target_ref), rest = rest[:12], rest[12:15], rest[15:]
    (acc, from_core, from_first, from_second, from_z, macc, mfrom_core, mfrom_y), rest = rest[:8], rest[8:]
    held, rest = rest[:12], rest[12:]
    (w, tgt, gs, dq, dk, dv, dnx, g_b, out, mem_out), rest = rest[:10], rest[10:]
    target_grad = rest[0]
    rest = rest[1:]
    (out_sems, own_sems, mown_sem, state_sems, core_s, core_r, first_s, first_r,
     second_s, second_r, zs_s, zs_r, mem_s, mem_r) = rest
    dpre, xh1, rs1, num_s, tot_s, qs, ks, vs, o_b, gb, ng, low_s = held
    z, x, y, c = here()
    xp, yp, cp_ = device(z, 1 - x, y, c), device(z, x, 1 - y, c), device(z, x, y, 1 - c)
    zp = [device((z + k) % 4, x, y, c) for k in (1, 2, 3)]
    count = len(SCATTER_ROUNDS)
    core_sems, first_sems, second_sems = (core_s, core_r), (first_s, first_r), (second_s, second_r)
    z_sems, mem_sems = (zs_s, zs_r), (mem_s, mem_r)
    sent = []

    def go(copy):
        copy.start()
        sent.append(copy)

    def span(r, part=None):
        a, m, b = SCATTER_ROUNDS[r]
        return {None: (a, b - a), 0: (a, m - a), 1: (m, b - m)}[part]

    def own(r):
        a, n = span(r)
        return pltpu.make_async_copy(
            grads.at[:, :, :, c, :, pl.ds(a, n)], acc.at[:, :, :, :, pl.ds(a, n)], own_sems.at[r])

    def core(r):
        a, n = span(r)
        source = gs if r in SELF_ROUNDS else grads
        return remote(source.at[:, :, :, 1 - c, :, pl.ds(a, n)],
                      from_core.at[:, :, :, :, pl.ds(a, n)], core_sems, r, cp_)

    def first(r, part):
        lanes = pl.ds(*span(r, part))
        src = acc.at[:, :, 1 - y, :, lanes] if part == 0 else acc.at[:, 1 - x, :, :, lanes]
        return remote(src, from_first.at[:, :, :, lanes], first_sems, (r, part),
                      yp if part == 0 else xp)

    def second(r, part):
        lanes = pl.ds(*span(r, part))
        src = acc.at[:, 1 - x, y, :, lanes] if part == 0 else acc.at[:, x, 1 - y, :, lanes]
        return remote(src, from_second.at[:, :, lanes], second_sems, (r, part),
                      xp if part == 0 else yp)

    def along(r, k):
        lanes = pl.ds(*span(r))
        return remote(acc.at[(z + k + 1) % 4, x, y, :, lanes], from_z.at[k, :, lanes], z_sems,
                      (r, k), zp[k])

    mem_own = pltpu.make_async_copy(mem_grads.at[:, c], macc, mown_sem)
    mem_core = remote(mem_grads.at[:, 1 - c], mfrom_core, mem_sems, 0, cp_)
    mem_far = remote(macc.at[1 - y], mfrom_y, mem_sems, 1, yp)

    def bring(i, src, dst):
        copy = pltpu.make_async_copy(src, dst, state_sems.at[i])
        copy.start()
        return copy

    early = [r for r in range(count) if r not in SELF_ROUNDS]
    own(0).start()
    mem_own.start()
    for r in early[1:]:
        own(r).start()
    copies = [bring(i, src, dst) for i, (src, dst) in enumerate(zip(state, held))]
    copies.append(bring(12, gathered.at[:, :, pl.ds(NORM, 4 * SLAB)], w))
    copies.append(bring(13, target, tgt))
    greet([xp, yp, cp_] + zp)
    go(core(early[0]))
    go(mem_core)
    for r in early[1:]:
        go(core(r))

    def add_core(r):
        if r not in SELF_ROUNDS:
            own(r).wait()
        core(r).wait_recv()
        for part in (0, 1):
            lanes = pl.ds(*span(r, part))
            for theirs in (True, False):
                def body(zi, carry, part=part, lanes=lanes, theirs=theirs):
                    for o in (0, 1):
                        if part == 0:
                            xi, yi = o, (1 - y) if theirs else y
                        else:
                            xi, yi = (1 - x) if theirs else x, o
                        mine = gs[zi, xi, yi, c, :, lanes] if r in SELF_ROUNDS else acc[zi, xi, yi, :, lanes]
                        acc[zi, xi, yi, :, lanes] = mine + from_core[zi, xi, yi, :, lanes]
                    return carry
                lax.fori_loop(0, 4, body, 0)
                if theirs:
                    go(first(r, part))

    def add_first(r):
        for part in (0, 1):
            first(r, part).wait_recv()
            lanes = pl.ds(*span(r, part))
            for theirs in (True, False):
                def body(zi, carry, part=part, lanes=lanes, theirs=theirs):
                    if part == 0:
                        xi, yi = (1 - x) if theirs else x, y
                        slot = xi
                    else:
                        xi, yi = x, (1 - y) if theirs else y
                        slot = yi
                    acc[zi, xi, yi, :, lanes] = (
                        acc[zi, xi, yi, :, lanes] + from_first[zi, slot, :, lanes])
                    return carry
                lax.fori_loop(0, 4, body, 0)
                if theirs:
                    go(second(r, part))

    def add_second(r):
        for part in (0, 1):
            second(r, part).wait_recv()
            lanes = pl.ds(*span(r, part))

            def body(zi, carry, lanes=lanes):
                acc[zi, x, y, :, lanes] = acc[zi, x, y, :, lanes] + from_second[zi, :, lanes]
                return carry
            lax.fori_loop(0, 4, body, 0)
        for k in (1, 0, 2):
            go(along(r, k))

    def add_z(r):
        lanes = pl.ds(*span(r))
        total = acc[z, x, y, :, lanes].astype(jnp.float32)
        for k in (0, 2, 1):
            along(r, k).wait_recv()
            total = total + from_z[k, :, lanes].astype(jnp.float32)
        out[:, lanes] = total

    def memory_core():
        mem_own.wait()
        mem_core.wait_recv()
        for theirs in (True, False):
            side = (1 - y) if theirs else y

            def body(i, carry, side=side):
                rows = pl.ds(pl.multiple_of(i * 64, 64), 64)
                macc[side, rows] = macc[side, rows] + mfrom_core[side, rows]
                return carry
            lax.fori_loop(0, 8, body, 0)
            if theirs:
                go(mem_far)

    def memory_end():
        mem_far.wait_recv()

        def body(i, carry):
            rows = pl.ds(pl.multiple_of(i * 64, 64), 64)
            mem_out[rows] = macc[y, rows].astype(jnp.float32) + mfrom_y[rows].astype(jnp.float32)
            return carry
        lax.fori_loop(0, 8, body, 0)

    def weight_rows(i, part):
        devs = pl.ds(part * 16, 16)
        return w[devs, :, pl.ds(SLAB * i, SLAB)].reshape(256, SLAB)

    def put(i, n, value):
        gs[:, :, :, :, :, pl.ds(NORM + SLAB * i + 256 * n, 256)] = value.astype(LOW).reshape(4, 2, 2, 2, ROWS, 256)

    rows_all = tgt.shape[0]

    def norm_back(i):
        r = block(i, 64)
        u, xh = dpre[r], xh1[r]
        ng[0:1] += jnp.sum(u * xh, axis=0, keepdims=True)
        ng[1:2] += jnp.sum(u, axis=0, keepdims=True)
        d = back_norm(u, gb[0:1], xh, rs1[r][:, :1])
        dpre[r] = d
        g_b[r] = d.astype(LOW)

    def self_norm():
        for copy in copies:
            copy.wait()
        each(rows_all // 64, norm_back)

    def self_out():
        out_back(g_b, lambda n: weight_rows(3, n), num_s, tot_s, dnx)
        for n in (0, 1):
            put(3, n, tmm(o_b[...], g_b[:, pl.ds(256 * n, 256)]))
        for ref in (dq, dk, dv):
            zero(ref)

    def self_tiles(i, first, last):
        def inner(kt, carry):
            r = pl.ds(i * RT, RT)
            key = kt * TILE + lane_iota((RT, TILE))
            row = i * RT + row_iota((RT, TILE))
            bias = jnp.where((key >= low_s[r]) & (key <= row), 0.0, HIDE)
            tile_backward(r, block(kt), bias, qs, ks, vs, dnx, dq, dk, dv)
            return carry
        lax.fori_loop(first, last, inner, 0)

    def self_grads():
        def lower(i):
            r = block(i, 64)
            qs[r] = (dq[r] * 0.125).astype(LOW)
            ks[r] = dk[r].astype(LOW)
            vs[r] = dv[r].astype(LOW)
        each(rows_all // 64, lower)
        for i, src in ((0, qs), (1, ks), (2, vs)):
            for n in (0, 1):
                put(i, n, tmm(tgt[...], src[:, pl.ds(256 * n, 256)]))
        inside = lane_iota((8, TILE)) < ROWS
        for d in range(DEV):
            one = ng[:, pl.ds(TILE * (d // 8), TILE)]
            one = pltpu.roll(one, (TILE - ROWS * (d % 8)) % TILE, 1) if d % 8 else one
            one = jnp.concatenate([jnp.where(inside, one, 0.0), jnp.zeros((8, TILE), F32)], axis=0)
            gs[d // 8, d // 4 % 2, d // 2 % 2, d % 2, :, pl.ds(0, NORM)] = one.astype(LOW)
        for r in SELF_ROUNDS:
            go(core(r))

    def self_target():
        for n in (0, 1):
            total = mmt(qs[...], weight_rows(0, n)) + mmt(ks[...], weight_rows(1, n))
            cols = pl.ds(256 * n, 256)
            target_grad[:, cols] = dpre[:, cols] + total + mmt(vs[...], weight_rows(2, n))

    add_core(0)
    memory_core()
    add_core(1)
    self_norm()
    add_first(0)
    add_core(2)
    self_out()
    add_second(0)
    add_first(1)
    add_core(3)
    self_tiles(0, 0, 2)
    add_second(1)
    add_first(2)
    self_tiles(1, 0, 4)
    add_z(0)
    add_second(2)
    add_first(3)
    self_grads()
    add_core(4)
    add_core(5)
    self_target()
    to_target = pltpu.make_async_copy(target_grad, target_ref, out_sems.at[0])
    to_target.start()
    memory_end()
    to_memory = pltpu.make_async_copy(mem_out, mem_ref, out_sems.at[1])
    to_memory.start()
    add_z(1)
    add_second(3)
    add_first(4)
    add_first(5)
    add_z(2)
    add_second(4)
    add_z(3)
    add_second(5)
    add_z(4)
    add_z(5)
    to_rows = pltpu.make_async_copy(out, out_ref, out_sems.at[2])
    to_rows.start()
    for copy in (to_target, to_memory, to_rows):
        copy.wait()
    for copy in sent:
        copy.wait_send()


def scatter_all(grads, mem_grads, gathered, target, state):
    any_space = pl.BlockSpec(memory_space=pl.ANY)
    dma = pltpu.SemaphoreType.DMA
    n = len(SCATTER_ROUNDS)
    rows = mem_grads.shape[2]
    low = lambda *s: pltpu.VMEM(s, LOW)
    f32 = lambda *s: pltpu.VMEM(s, F32)
    return pl.pallas_call(
        scatter_kernel,
        out_shape=(
            jax.ShapeDtypeStruct((ROWS, LANES), F32),
            jax.ShapeDtypeStruct((rows, SLAB), F32),
            jax.ShapeDtypeStruct((rows, SLAB), F32),
        ),
        in_specs=[any_space] * 16,
        out_specs=(any_space,) * 3,
        scratch_shapes=[
            low(4, 2, 2, ROWS, LANES),
            low(4, 2, 2, ROWS, LANES),
            low(4, 2, ROWS, LANES),
            low(4, ROWS, LANES),
            low(3, ROWS, LANES),
            low(2, rows, SLAB),
            low(2, rows, SLAB),
            low(rows, SLAB),
        ]
        + [pltpu.VMEM(s.shape, s.dtype) for s in state_shapes(rows)]
        + [
            low(32, ROWS, 4 * SLAB),
            low(rows, SLAB),
            low(4, 2, 2, 2, ROWS, SELF_LANES),
            f32(rows, SLAB),
            f32(rows, SLAB),
            f32(rows, SLAB),
            low(rows, 2 * SLAB),
            low(rows, SLAB),
            f32(ROWS, LANES),
            f32(rows, SLAB),
            f32(rows, SLAB),
            dma((3,)),
            dma((n,)),
            dma(()),
            dma((14,)),
            dma((n,)),
            dma((n,)),
            dma((n, 2)),
            dma((n, 2)),
            dma((n, 2)),
            dma((n, 2)),
            dma((n, 3)),
            dma((n, 3)),
            dma((2,)),
            dma((2,)),
        ],
        compiler_params=pltpu.CompilerParams(
            collective_id=2, has_side_effects=True, vmem_limit_bytes=56 << 20),
        name="scatter",
    )(grads, mem_grads, gathered, target, *state)


def finish_kernel(rows_ref, mem_ref, target_ref, *rest):
    outs, (rows, mem, target, in_sems, out_sems) = rest[:18], rest[18:]
    copies = []
    loads = []
    half = target.shape[0] // 2
    pieces = [pl.ds(0, half), pl.ds(half, half)]
    cuts_ = [(NORM + SLAB * i, SLAB) for i in range(8)] + [(NORM + SLAB * 8, 4 * SLAB)]
    cuts_ += [(NORM + SLAB * (12 + k), SLAB) for k in range(4)]

    def load(src, dst):
        copy = pltpu.make_async_copy(src, dst, in_sems.at[len(loads)])
        copy.start()
        loads.append(copy)

    def bring(src, dst):
        copy = pltpu.make_async_copy(src, dst, out_sems.at[len(copies)])
        copy.start()
        copies.append(copy)

    for p in pieces:
        load(target_ref.at[p], target.at[p])
        load(mem_ref.at[p], mem.at[p])
    load(rows_ref, rows)
    for i, p in enumerate(pieces):
        loads[2 * i].wait()
        bring(target.at[p], outs[0].at[p])
        loads[2 * i + 1].wait()
        bring(mem.at[p], outs[1].at[p])
    loads[4].wait()
    for i, (start, width) in enumerate(cuts_):
        dst = outs[2 + i] if i < 9 else outs[11].at[pl.ds(ROWS * (i - 9), ROWS)]
        bring(rows.at[:, pl.ds(start, width)], dst)
    for i in range(6):
        outs[12 + i][...] = rows[i, pl.ds(0, ROWS)]
    for copy in copies:
        copy.wait()


def finish(rows, mem, target):
    any_space = pl.BlockSpec(memory_space=pl.ANY)
    shape = lambda *s: jax.ShapeDtypeStruct(s, F32)
    return pl.pallas_call(
        finish_kernel,
        out_shape=(shape(*target.shape), shape(*mem.shape))
        + (shape(ROWS, SLAB),) * 8
        + (shape(ROWS, 4 * SLAB), shape(4 * ROWS, SLAB))
        + (shape(ROWS),) * 6,
        in_specs=[any_space] * 3,
        out_specs=(any_space,) * 12 + (pl.BlockSpec(memory_space=pltpu.VMEM),) * 6,
        scratch_shapes=[
            pltpu.VMEM(rows.shape, F32),
            pltpu.VMEM(mem.shape, F32),
            pltpu.VMEM(target.shape, F32),
            pltpu.SemaphoreType.DMA((5,)),
            pltpu.SemaphoreType.DMA((17,)),
        ],
        name="finish",
    )(rows, mem, target)


def local(target_in, memory, out_grad, *rest):
    fast = two_by_two((lax.axis_size("dp"), lax.axis_size("mem")))
    if not fast:
        return plain(target_in, memory, out_grad, *rest)
    weights, tables = rest[:16], rest[16:]
    norms = sum(
        jnp.pad(one[None, :], ((i, ROWS - 1 - i), (0, NORM - ROWS)))
        for i, one in enumerate(weights[10:])
    )
    gathered, all_memory, saved = gather_all(weights[:10], norms, memory, tables[0], target_in)
    after, after_low, xh1, rs1, num, tot, q, k, v, o, gains, low_s = saved
    layer_out, grads, mem_grads, d_after, norm_grads = compute(
        *tables, out_grad, all_memory, gathered, after, after_low, gains
    )
    state = (d_after, xh1, rs1, num, tot, q, k, v, o, gains, norm_grads, low_s)
    rows = target_in.shape[0]
    out, mem_out, target_grad = scatter_all(
        grads.reshape(4, 2, 2, 2, ROWS, LANES),
        mem_grads.reshape(2, 2, rows, SLAB),
        gathered,
        target_in,
        state,
    )
    return (layer_out,) + tuple(finish(out, mem_out, target_grad))


def solution(mesh):
    both = P(("dp", "mem"), None)
    flat = P(("dp", "mem"))
    in_specs = (both,) * 13 + (flat,) * 6 + (P("dp", None),) * 3
    out_specs = (both,) * 13 + (flat,) * 6
    return jax.shard_map(local, mesh=mesh, in_specs=in_specs, out_specs=out_specs, check_vma=False)
```

```python
import functools

import jax
import jax.numpy as jnp
from jax import lax
from jax.experimental import pallas as pl
from jax.experimental.pallas import tpu as pltpu
from jax.sharding import PartitionSpec as P

MESH = pl.DeviceIdType.MESH
SLAB = 512
NORM = 128
LANES = NORM + 16 * SLAB
ROWS = 16


def here():
    dp, mem = lax.axis_index("dp"), lax.axis_index("mem")
    return dp // 2, dp % 2, mem // 2, mem % 2


def device(z, x, y, c):
    return (z * 2 + x, y * 2 + c)


def greet(peers):
    barrier = pltpu.get_barrier_semaphore()
    for peer in peers:
        pl.semaphore_signal(barrier, inc=1, device_id=peer, device_id_type=MESH)
    pl.semaphore_wait(barrier, len(peers))


def remote(src, dst, sems, index, peer):
    send, recv = sems
    return pltpu.make_async_remote_copy(
        src_ref=src,
        dst_ref=dst,
        send_sem=send.at[index],
        recv_sem=recv.at[index],
        device_id=peer,
        device_id_type=MESH,
    )


def cuts(widths, share):
    spans, at = [], 0
    for tiles in widths:
        n = tiles * 128
        spans.append((at, at + max(1, round(tiles * share)) * 128, at + n))
        at += n
    return tuple(spans)


GATHER_ROUNDS = cuts((17, 36), 0.22)
Z_LAST = (53 * 128, 59 * 128, 65 * 128)


def gather_kernel(*refs):
    shards, norm_ref, memory_ref, lens_ref, target = refs[:10], *refs[10:14]
    out, mem_out = refs[14:16]
    state_out, refs = refs[16:28], refs[28:]
    local_sem, mem_local = refs[:2]
    z_sems, first_sems, second_sems = refs[2:4], refs[4:6], refs[6:8]
    across, mems = refs[8:10], refs[10:12]
    stage, mem_stage = refs[12:14]
    state, refs = refs[14:26], refs[26:]
    after, a_b, xh1, rs1, num, tot, qs, ks, vs, o_b, gb, low_s = state
    w, norms, tgt, starts, state_sems, refs = *refs[:5], refs[5:]
    cf_sems, cs_sems, cz_sems, co_sems = refs[:2], refs[2:4], refs[4:6], refs[6:8]
    z, x, y, c = here()
    xp, yp, cp_ = device(z, 1 - x, y, c), device(z, x, 1 - y, c), device(z, x, y, 1 - c)
    own = out.at[z, x, y, c]
    rounds = range(len(GATHER_ROUNDS))

    local = []

    def bring(src, start, width):
        local.append(
            pltpu.make_async_copy(src, stage.at[:, pl.ds(start, width)], local_sem.at[len(local)])
        )

    bring(norm_ref, 0, NORM)
    for i in range(8):
        bring(shards[i], NORM + SLAB * i, SLAB)
    bring(shards[8], NORM + SLAB * 8, 4 * SLAB)
    for k in range(4):
        bring(shards[9].at[pl.ds(ROWS * k, ROWS)], NORM + SLAB * (12 + k), SLAB)
    for one in local:
        one.start()
    keep = pltpu.make_async_copy(memory_ref, mem_stage, mem_local.at[0])
    keep.start()
    zn = [device((z + k) % 4, x, y, c) for k in (1, 3)]
    greet([xp, yp, cp_] + zn)
    for one in local:
        one.wait()
    own_out = pltpu.make_async_copy(stage, own, mem_local.at[1])
    own_out.start()

    def column(slot):
        return z if slot == 0 else (z - slot if slot < 4 else z + (slot - 3))

    def there(slot):
        return None if slot == 0 else (z >= slot if slot < 4 else z <= 6 - slot)

    def both(a, b):
        return b if a is None else (a if b is None else jnp.logical_and(a, b))

    def guarded(cond, body):
        if cond is None:
            body()
        else:
            pl.when(cond)(body)

    sent = []

    def go(make, cond=None):
        guarded(cond, lambda: make().start())
        sent.append((cond, make))

    def along(slot, r, up):
        a, _, b = GATHER_ROUNDS[r]
        ref = out.at[column(slot), x, y, c, :, pl.ds(a, b - a)]
        src = stage.at[:, pl.ds(a, b - a)] if slot == 0 else ref
        d = 0 if slot == 0 else (slot if slot < 4 else slot - 3)
        peer = device((z + (1 if up else 3)) % 4, x, y, c)
        return remote(src, ref, z_sems, (0 if up else 1, d, r), peer)

    def arrived(slot, r):
        a, _, b = GATHER_ROUNDS[r]
        ref = out.at[column(slot), x, y, c, :, pl.ds(a, b - a)]
        up = slot < 4
        index = (0 if up else 1, (slot if up else slot - 3) - 1, r)
        return remote(ref, ref, z_sems, index, xp)

    def first(slot, r, part, arriving=False):
        a, m, b = GATHER_ROUNDS[r]
        zz = column(slot)
        if part == 0:
            ref = out.at[zz, (1 - x) if arriving else x, y, c, :, pl.ds(a, m - a)]
        else:
            ref = out.at[zz, x, (1 - y) if arriving else y, c, :, pl.ds(m, b - m)]
        lanes = pl.ds(a, m - a) if part == 0 else pl.ds(m, b - m)
        src = stage.at[:, lanes] if slot == 0 and not arriving else ref
        return remote(src, ref, first_sems, (slot, part, r), xp if part == 0 else yp)

    def second(slot, r, part, hop, arriving=False):
        a, m, b = GATHER_ROUNDS[r]
        zz = column(slot)
        if part == 0:
            side = (1 - x) if hop else x
            ref = out.at[zz, side, (1 - y) if arriving else y, c, :, pl.ds(a, m - a)]
        else:
            side = (1 - y) if hop else y
            ref = out.at[zz, (1 - x) if arriving else x, side, c, :, pl.ds(m, b - m)]
        lanes = pl.ds(a, m - a) if part == 0 else pl.ds(m, b - m)
        src = stage.at[:, lanes] if slot == 0 and not (arriving or hop) else ref
        return remote(src, ref, second_sems, (slot, part, hop, r), yp if part == 0 else xp)

    def over(slot, r, arriving=False):
        a, _, b = GATHER_ROUNDS[r]
        ref = out.at[column(slot), :, :, (1 - c) if arriving else c, :, pl.ds(a, b - a)]
        return remote(ref, ref, across, (slot, r), cp_)

    def spread(slot, r):
        cond = there(slot)
        for part in (1, 0):
            go(functools.partial(first, slot, r, part), cond)
        for part in (1, 0):
            go(functools.partial(second, slot, r, part, 0), cond)

    def from_z(d, r):
            for slot in (d, d + 3):
                cond = there(slot)
                guarded(cond, lambda slot=slot, r=r: arrived(slot, r).wait_recv())
                if d < 3:
                    onward = z < 3 if slot < 4 else z > 0
                    go(functools.partial(along, slot, r, slot < 4), both(cond, onward))
                spread(slot, r)

    def pass_on(slots, r):
            for slot in slots:
                cond = there(slot)
                for part in (1, 0):
                    guarded(cond, lambda s=slot, r=r, p=part: first(s, r, p, True).wait_recv())
                    go(functools.partial(second, slot, r, part, 1), cond)

    def hand_over(slots, r):
            for slot in slots:
                cond = there(slot)
                for part in (0, 1):
                    for hop in (0, 1):
                        guarded(cond, lambda s=slot, r=r, p=part, h=hop: second(s, r, p, h, True).wait_recv())
                go(functools.partial(over, slot, r), cond)

    cut_c = [pl.ds(Z_LAST[p], Z_LAST[p + 1] - Z_LAST[p]) for p in (0, 1)]
    lanes_c = pl.ds(Z_LAST[0], Z_LAST[2] - Z_LAST[0])

    def first_c(part, arriving=False):
        if part == 0:
            ref = out.at[z, (1 - x) if arriving else x, y, c, :, cut_c[0]]
        else:
            ref = out.at[z, x, (1 - y) if arriving else y, c, :, cut_c[1]]
        src = ref if arriving else stage.at[:, cut_c[part]]
        return remote(src, ref, cf_sems, part, xp if part == 0 else yp)

    def second_c(part, hop, arriving=False):
        if part == 0:
            ref = out.at[z, (1 - x) if hop else x, (1 - y) if arriving else y, c, :, cut_c[0]]
        else:
            ref = out.at[z, (1 - x) if arriving else x, (1 - y) if hop else y, c, :, cut_c[1]]
        src = ref if arriving or hop else stage.at[:, cut_c[part]]
        return remote(src, ref, cs_sems, (part, hop), yp if part == 0 else xp)

    def along_c(slot, up):
        ref = out.at[column(slot), :, :, c, :, lanes_c]
        d = 0 if slot == 0 else (slot if slot < 4 else slot - 3)
        peer = device((z + (1 if up else 3)) % 4, x, y, c)
        return remote(ref, ref, cz_sems, (0 if up else 1, d), peer)

    def arrived_c(slot):
        ref = out.at[column(slot), :, :, c, :, lanes_c]
        up = slot < 4
        return remote(ref, ref, cz_sems, (0 if up else 1, (slot if up else slot - 3) - 1), xp)

    def over_c(slot, arriving=False):
        ref = out.at[column(slot), :, :, (1 - c) if arriving else c, :, lanes_c]
        return remote(ref, ref, co_sems, slot, cp_)

    def pass_on_c():
        for part in (0, 1):
            first_c(part, True).wait_recv()
            go(functools.partial(second_c, part, 1))

    def plane_c():
        own_out.wait()
        for part in (0, 1):
            for hop in (0, 1):
                second_c(part, hop, True).wait_recv()
        go(functools.partial(along_c, 0, True), z < 3)
        go(functools.partial(along_c, 0, False), z > 0)
        go(functools.partial(over_c, 0))

    def from_z_c(d):
        for slot in (d, d + 3):
            cond = there(slot)
            guarded(cond, lambda slot=slot: arrived_c(slot).wait_recv())
            if d < 3:
                onward = z < 3 if slot < 4 else z > 0
                go(functools.partial(along_c, slot, slot < 4), both(cond, onward))
            go(functools.partial(over_c, slot), cond)

    for r in rounds:
        go(functools.partial(along, 0, r, True), z < 3)
        go(functools.partial(along, 0, r, False), z > 0)
        spread(0, r)
        if r == 0:
            for part in (0, 1):
                go(functools.partial(first_c, part))
            for part in (0, 1):
                go(functools.partial(second_c, part, 0))
    mem_own = mem_out.at[y, c]

    def memory_rows():
        keep.wait()
        kept = pltpu.make_async_copy(mem_stage, mem_own, mem_local.at[2])
        kept.start()
        go(lambda: remote(mem_stage, mem_own, mems, 0, yp))
        go(lambda: remote(mem_stage, mem_own, mems, 1, cp_))
        return kept

    def memory_far():
        far = mem_out.at[1 - y, c]
        remote(far, far, mems, 0, yp).wait_recv()
        go(lambda: remote(far, far, mems, 2, cp_))

    everyone = (0, 1, 4, 2, 5, 3, 6)

    def all_over(r):
        for slot in everyone:
            guarded(there(slot), lambda s=slot: over(s, r, True).wait_recv())

    rows_all = tgt.shape[0]
    n_sent = starts.shape[0]
    loads = [pltpu.make_async_copy(target, tgt, state_sems.at[12])]
    loads.append(pltpu.make_async_copy(out.at[:, :, :, :, :, pl.ds(NORM, 4 * SLAB)], w, state_sems.at[13]))
    loads.append(pltpu.make_async_copy(out.at[:, :, :, :, :, pl.ds(0, NORM)], norms, state_sems.at[14]))
    saves = [pltpu.make_async_copy(src, dst, state_sems.at[i]) for i, (src, dst) in enumerate(zip(state, state_out))]

    def weight(i, n):
        return w[:, :, :, :, :, pl.ds(SLAB * i + 256 * n, 256)].reshape(SLAB, 256)

    def prepare():
        base = lax.axis_index("mem") * n_sent

        def count(j, at):
            starts[j] = at
            return at + lens_ref[0, base + j]
        lax.fori_loop(0, n_sent, count, jnp.int32(0))
        for i in range(rows_all // TILE):
            row = i * TILE + row_iota((TILE, TILE))
            found = jnp.zeros((TILE, TILE), jnp.int32)
            for j in range(n_sent):
                found = jnp.where(row >= starts[j], starts[j], found)
            low_s[pl.ds(i * TILE, TILE)] = found
        zero(num)
        zero(tot)

    def project():
        for one in loads:
            one.wait()
        for j in range(SLAB // TILE):
            total = jnp.zeros((8, TILE), F32)
            for k in range(8):
                d = 8 * j + k
                one = norms[d // 8, d // 4 % 2, d // 2 % 2, d % 2].astype(F32)[:8]
                total = total + (pltpu.roll(one, ROWS * k, 1) if k else one)
            gb[:, pl.ds(TILE * j, TILE)] = total
        for i, dst in ((0, qs), (1, ks), (2, vs)):
            for n in (0, 1):
                value = mm(tgt[...], weight(i, n)).astype(LOW)
                dst[:, pl.ds(256 * n, 256)] = value * jnp.asarray(0.125, LOW) if i == 0 else value

    def self_tiles(i, first_tile, last_tile):
        def inner(kt, carry):
            r = pl.ds(i * RT, RT)
            key = kt * TILE + lane_iota((RT, TILE))
            row = i * RT + row_iota((RT, TILE))
            bias = jnp.where((key >= low_s[r]) & (key <= row), 0.0, HIDE)
            tile_forward(r, block(kt), bias, qs, ks, vs, num, tot)
            return carry
        lax.fori_loop(first_tile, last_tile, inner, 0)

    def project_out():
        divide(num, tot, o_b, rows_all)
        for n in (0, 1):
            cols = pl.ds(256 * n, 256)
            after[:, cols] = tgt[:, cols].astype(F32) + mm(o_b[...], weight(3, n))

    def norm_rows(i):
        r = block(i, 64)
        xh, rs = normalize(after[r])
        xh1[r] = xh
        rs1[r] = jnp.broadcast_to(rs, (64, TILE))
        value = xh * gb[0:1] + gb[1:2]
        after[r] = value
        a_b[r] = value.astype(LOW)

    loads[0].start()
    prepare()
    from_z(1, 0)
    pass_on_c()
    from_z(1, 1)
    pass_on((0,), 0)
    plane_c()
    from_z(2, 0)
    pass_on((0,), 1)
    pass_on((1, 4), 0)
    from_z(3, 0)
    from_z(2, 1)
    pass_on((2, 5), 0)
    hand_over((0,), 0)
    from_z_c(1)
    pass_on((1, 4), 1)
    pass_on((3, 6), 0)
    kept = memory_rows()
    hand_over((1, 4), 0)
    hand_over((2, 5), 0)
    from_z(3, 1)
    from_z_c(2)
    hand_over((3, 6), 0)
    all_over(0)
    loads[1].start()
    loads[2].start()
    pass_on((2, 5), 1)
    from_z_c(3)
    project()
    hand_over((0,), 1)
    self_tiles(0, 0, 2)
    pass_on((3, 6), 1)
    self_tiles(1, 0, 4)
    hand_over((1, 4), 1)
    memory_far()
    project_out()
    each(rows_all // 64, norm_rows)
    hand_over((2, 5), 1)
    hand_over((3, 6), 1)
    for one in saves:
        one.start()
    all_over(1)
    for slot in everyone:
        guarded(there(slot), lambda s=slot: over_c(s, True).wait_recv())
    for one in saves:
        one.wait()
    for i, side in ((1, y), (2, 1 - y)):
        last = mem_out.at[side, 1 - c]
        remote(last, last, mems, i, cp_).wait_recv()
    kept.wait()
    for cond, make in sent:
        guarded(cond, lambda make=make: make().wait_send())


def gather_all(shards, norms, memory, lens, target):
    any_space = pl.BlockSpec(memory_space=pl.ANY)
    dma = pltpu.SemaphoreType.DMA
    n = len(GATHER_ROUNDS)
    both = lambda *s: [dma(s), dma(s)]
    state = forward_shapes(target.shape[0])
    low = lambda *s: pltpu.VMEM(s, LOW)
    gathered, whole_memory, *saved = pl.pallas_call(
        gather_kernel,
        out_shape=(
            jax.ShapeDtypeStruct((4, 2, 2, 2, ROWS, LANES), jnp.bfloat16),
            jax.ShapeDtypeStruct((2, 2) + memory.shape, jnp.bfloat16),
        )
        + state,
        in_specs=[any_space] * 12 + [pl.BlockSpec(memory_space=pltpu.SMEM), any_space],
        out_specs=(any_space,) * 14,
        scratch_shapes=[dma((14,)), dma((3,))]
        + both(2, 3, n) + both(7, 2, n) + both(7, 2, 2, n) + both(7, n) + both(3)
        + [low(ROWS, LANES), low(*memory.shape)]
        + [pltpu.VMEM(s.shape, s.dtype) for s in state]
        + [
            low(4, 2, 2, 2, ROWS, 4 * SLAB),
            low(4, 2, 2, 2, ROWS, NORM),
            low(*target.shape),
            pltpu.SMEM((16,), jnp.int32),
            dma((15,)),
        ]
        + both(2) + both(2, 2) + both(2, 3) + both(7),
        compiler_params=pltpu.CompilerParams(
            collective_id=1, has_side_effects=True, vmem_limit_bytes=60 << 20),
        name="gather",
    )(*shards, norms, memory, lens, target)
    return gathered.reshape(32, ROWS, LANES), whole_memory.reshape(-1, SLAB), saved


def forward_shapes(rows):
    full = lambda dtype, lanes=SLAB, n=rows: jax.ShapeDtypeStruct((n, lanes), dtype)
    return (
        full(F32),
        full(LOW),
        full(F32),
        full(F32, TILE),
        full(F32),
        full(F32),
        full(LOW),
        full(LOW),
        full(LOW),
        full(LOW),
        full(F32, SLAB, 8),
        full(jnp.int32, TILE),
    )


def two_by_two(mesh_axes):
    return mesh_axes == (8, 4)


def gather_any(shards, norms, memory):
    everyone = ("dp", "mem")
    packed = jnp.concatenate([norms] + list(shards[:9]), axis=1)
    rows = lax.all_gather(packed, everyone, axis=0, tiled=True).reshape(32, ROWS, -1)
    last = lax.all_gather(shards[9], everyone, axis=0, tiled=True)
    last = last.reshape(32, 4, ROWS, SLAB).transpose(0, 2, 1, 3).reshape(32, ROWS, 4 * SLAB)
    return (
        jnp.concatenate([rows, last], axis=2),
        lax.all_gather(memory, "mem", axis=0, tiled=True),
    )


def scatter_any(grads, mem_grads):
    everyone = ("dp", "mem")
    wide = grads.reshape(32, ROWS, LANES).astype(jnp.float32)
    cut = LANES - 4 * SLAB
    rows = lax.psum_scatter(
        wide[:, :, :cut].reshape(512, cut), everyone, scatter_dimension=0, tiled=True
    )
    last = wide[:, :, cut:].reshape(32, ROWS, 4, SLAB).transpose(0, 2, 1, 3).reshape(2048, SLAB)
    last = lax.psum_scatter(last, everyone, scatter_dimension=0, tiled=True)
    mem = lax.psum_scatter(
        mem_grads.astype(jnp.float32), "mem", scatter_dimension=0, tiled=True
    )
    return rows, last, mem
HEADS = 8
HEAD = 64
eps_norm = 1e-05
score_scale = 0.125


def layer_norm(values, gain, shift):
    centre = values - jnp.mean(values, axis=-1, keepdims=True)
    spread = jnp.mean(centre * centre, axis=-1, keepdims=True)
    return centre * lax.rsqrt(spread + eps_norm) * gain + shift


def head_split(values):
    return values.reshape(values.shape[0], HEADS, HEAD)


def matmul(left, right):
    return jnp.dot(left, right, preferred_element_type=jnp.float32)


def left_grad(inputs, grads):
    return jnp.einsum("ra,rb->ab", inputs, grads, preferred_element_type=jnp.float32)


def back_through(grads, weight):
    return jnp.einsum("rb,ab->ra", grads, weight, preferred_element_type=jnp.float32)


def exp_scores(q_block, keys, low_edge, high_edge):
    raw = jnp.einsum("qhd,khd->hqk", head_split(q_block), head_split(keys),
                     preferred_element_type=jnp.float32) * score_scale
    position = lax.broadcasted_iota(jnp.int32, (q_block.shape[0], keys.shape[0]), 1)
    allowed = (position >= low_edge[:, None]) & (position < high_edge[:, None])
    return jnp.where(allowed[None], jnp.exp(raw), 0.0)


def attend(queries, keys, values, low_edge, high_edge):
    expo = exp_scores(queries, keys, low_edge, high_edge)
    numer = jnp.einsum("hqk,khd->qhd", expo.astype(jnp.bfloat16), head_split(values),
                       preferred_element_type=jnp.float32)
    totals = jnp.sum(expo, axis=2).T
    return (numer / totals[:, :, None]).reshape(queries.shape[0], -1), totals


def attend_back(queries, keys, values, low_edge, high_edge, upstream, output, totals):
    expo = exp_scores(queries, keys, low_edge, high_edge)
    up = head_split(upstream.astype(jnp.float32))
    numer_grad = (up / totals[:, :, None]).astype(jnp.bfloat16)
    corr = -jnp.sum(up * head_split(output), axis=2) / totals
    flow = jnp.einsum("qhd,khd->hqk", numer_grad, head_split(values),
                      preferred_element_type=jnp.float32) + corr.T[:, :, None]
    ds = (expo * flow).astype(jnp.bfloat16)
    dq = jnp.einsum("hqk,khd->qhd", ds, head_split(keys), preferred_element_type=jnp.float32)
    dk = jnp.einsum("hqk,qhd->khd", ds, head_split(queries), preferred_element_type=jnp.float32)
    dv = jnp.einsum("hqk,qhd->khd", expo.astype(jnp.bfloat16), numer_grad,
                    preferred_element_type=jnp.float32)
    flat = lambda v: v.reshape(v.shape[0], -1)
    return ((flat(dq) * score_scale).astype(jnp.bfloat16), (flat(dk) * score_scale).astype(jnp.bfloat16),
            flat(dv).astype(jnp.bfloat16))


def plain(target_in, memory, out_grad, *rest):
    weights, (tgt_lens, src_lens, src_offsets) = rest[:16], rest[16:]
    member = lax.axis_index("mem")
    per_device = tgt_lens.shape[1] // lax.axis_size("mem")
    pick = lambda table: lax.dynamic_slice_in_dim(table[0], member * per_device, per_device, 0)
    lengths, spans, offsets = pick(tgt_lens), pick(src_lens), pick(src_offsets)
    norms = jnp.stack(weights[10:], axis=1)
    norms = jnp.pad(norms, ((0, 0), (0, NORM - norms.shape[1])))
    gathered, all_memory = gather_any(weights[:10], norms, memory)
    W = gathered.reshape(512, LANES)
    mat = lambda i: W[:, NORM + SLAB * i : NORM + SLAB * (i + 1)]
    wsq, wsk, wsv, wso, wcq, wck, wcv, wco = [mat(i) for i in range(8)]
    w1 = W[:, NORM + 8 * SLAB : NORM + 12 * SLAB]
    w2 = gathered[:, :, NORM + 12 * SLAB :].reshape(32, 16, 4, SLAB).transpose(0, 2, 1, 3).reshape(2048, SLAB)
    ga, sa, gc, sc, gf, sf = [W[:, i].astype(jnp.float32) for i in range(6)]
    rows = target_in.shape[0]
    starts = jnp.cumsum(lengths) - lengths
    position = lax.iota(jnp.int32, rows)
    sentence = jnp.sum((position[:, None] >= starts[None, :]).astype(jnp.int32), axis=1) - 1
    picker = sentence[:, None] == lax.iota(jnp.int32, per_device)[None, :]
    choose = lambda v: jnp.sum(jnp.where(picker, v[None, :], 0), axis=1)
    self_low, self_high = choose(starts), position + 1
    cross_low = choose(offsets)
    cross_high = cross_low + choose(spans)
    low = jnp.bfloat16
    q, k, v = [matmul(target_in, w).astype(low) for w in (wsq, wsk, wsv)]
    o_self_f, tot_self = attend(q, k, v, self_low, self_high)
    o_self = o_self_f.astype(low)
    after_self, pull_self = jax.vjp(layer_norm, target_in.astype(jnp.float32) + matmul(o_self, wso), ga, sa)
    a_b = after_self.astype(low)
    qc = matmul(a_b, wcq).astype(low)
    kc, vc = matmul(all_memory, wck).astype(low), matmul(all_memory, wcv).astype(low)
    cut = lambda v: v.reshape((4, -1) + v.shape[1:])
    o_c_f, tot_c = lax.map(
        lambda p: attend(p[0], kc, vc, p[1], p[2]), (cut(qc), cut(cross_low), cut(cross_high))
    )
    o_c_f, tot_c = o_c_f.reshape(rows, -1), tot_c.reshape(rows, -1)
    o_c = o_c_f.astype(low)
    after_cross, pull_cross = jax.vjp(layer_norm, after_self + matmul(o_c, wco), gc, sc)
    c_b = after_cross.astype(low)
    hidden = matmul(c_b, w1)
    activated, pull_silu = jax.vjp(jax.nn.silu, hidden)
    act = activated.astype(low)
    final, pull_ffn = jax.vjp(layer_norm, after_cross + matmul(act, w2), gf, sf)
    d_pre_out, g_gf, g_sf = pull_ffn(out_grad.astype(jnp.float32))
    d_branch = d_pre_out.astype(low)
    g_w2 = left_grad(act, d_branch)
    d_hidden = pull_silu(back_through(d_branch, w2))[0].astype(low)
    g_w1 = left_grad(c_b, d_hidden)
    d_pre_cross, g_gc, g_sc = pull_cross(d_pre_out + back_through(d_hidden, w1))
    d_cb = d_pre_cross.astype(low)
    g_wco = left_grad(o_c, d_cb)
    d_oc = back_through(d_cb, wco).astype(low)

    def piece(carry, p):
        dq, dk, dv = attend_back(p[0], kc, vc, p[1], p[2], p[3], p[4], p[5])
        return (carry[0] + dk, carry[1] + dv), dq

    empty = jnp.zeros(kc.shape, jnp.bfloat16)
    (dk_c, dv_c), dq_c = lax.scan(
        piece,
        (empty, empty),
        tuple(cut(v) for v in (qc, cross_low, cross_high, d_oc, o_c_f, tot_c)),
    )
    dq_c = dq_c.reshape(rows, -1)
    g_wcq, g_wck, g_wcv = left_grad(a_b, dq_c), left_grad(all_memory, dk_c), left_grad(all_memory, dv_c)
    mem_grad = back_through(dk_c, wck) + back_through(dv_c, wcv)
    d_pre_self, g_ga, g_sa = pull_self(d_pre_cross + back_through(dq_c, wcq))
    d_sb = d_pre_self.astype(low)
    g_wso = left_grad(o_self, d_sb)
    d_os = back_through(d_sb, wso).astype(low)
    dq, dk, dv = attend_back(q, k, v, self_low, self_high, d_os, o_self_f, tot_self)
    g_wsq, g_wsk, g_wsv = left_grad(target_in, dq), left_grad(target_in, dk), left_grad(target_in, dv)
    target_grad = d_pre_self + back_through(dq, wsq) + back_through(dk, wsk) + back_through(dv, wsv)
    n_g = jnp.pad(jnp.stack([g_ga, g_sa, g_gc, g_sc, g_gf, g_sf], axis=1), ((0, 0), (0, NORM - 6)))
    g_w2p = g_w2.reshape(32, 4, 16, SLAB).transpose(0, 2, 1, 3).reshape(512, 4 * SLAB)
    grads = jnp.concatenate([g.astype(low) for g in (n_g, g_wsq, g_wsk, g_wsv, g_wso, g_wcq, g_wck, g_wcv, g_wco, g_w1, g_w2p)], axis=1)
    part = lambda i, n=1: out[:, NORM + SLAB * i : NORM + SLAB * (i + n)]
    out, w2_grad, mem_out = scatter_any(grads, mem_grad.astype(low))
    return (final.astype(low), target_grad, mem_out) + tuple(part(i) for i in range(8)) + (part(8, 4), w2_grad) + tuple(out[:, i] for i in range(6))


TILE = 128
RT = 256
CHUNK = 256
EPS = 1e-05
HIDE = -1e30
LOW = jnp.bfloat16
F32 = jnp.float32
DEV = 32
CUT = NORM + 12 * SLAB


def mm(a, b):
    return jnp.dot(a, b, preferred_element_type=F32)


def mmt(a, b):
    return lax.dot_general(a, b, (((1,), (1,)), ((), ())), preferred_element_type=F32)


def tmm(a, b):
    return lax.dot_general(a, b, (((0,), (0,)), ((), ())), preferred_element_type=F32)


def lane_iota(shape):
    return lax.broadcasted_iota(jnp.int32, shape, len(shape) - 1)


def row_iota(shape):
    return lax.broadcasted_iota(jnp.int32, shape, 0)


def halves():
    lane = lane_iota((1, TILE))
    even = jnp.where(lane < 64, 1.0, 0.0).astype(LOW)
    odd = jnp.where(lane < 64, 0.0, 1.0).astype(LOW)
    return even, odd


def stacked(block, even, odd):
    return jnp.concatenate([block * even, block * odd], axis=0)


def fold(pair):
    lane = lane_iota((TILE, TILE))
    return jnp.where(lane < 64, pair[:TILE], pair[TILE:])


def totals_block(even, odd):
    wide = lambda v: jnp.broadcast_to(v, (TILE, TILE))
    return jnp.concatenate([wide(even), wide(odd)], axis=0)


def corr_block():
    lane = lane_iota((TILE, TILE))
    a = jnp.where(lane < 2, 1.0, 0.0).astype(LOW)
    b = jnp.where((lane >= 64) & (lane < 66), 1.0, 0.0).astype(LOW)
    return jnp.concatenate([a, b], axis=0)


def tile_forward(rows, keys, bias, q, k, v, num, tot):
    even, odd = halves()
    ones = totals_block(even, odd)
    bias2 = jnp.concatenate([bias, bias], axis=1)
    for h in range(4):
        cols = pl.ds(TILE * h, TILE)
        s = mmt(q[rows, cols], stacked(k[keys, cols], even, odd))
        e = jnp.exp(s + bias2).astype(LOW)
        both = mm(e, jnp.concatenate([stacked(v[keys, cols], even, odd), ones], axis=1))
        num[rows, cols] += both[:, :TILE]
        tot[rows, cols] += both[:, TILE:]


def tile_backward(rows, keys, bias, q, k, v, dnx, dq, dk, dv):
    even, odd = halves()
    ones = corr_block()
    bias2 = jnp.concatenate([bias, bias], axis=1)
    for h in range(4):
        cols = pl.ds(TILE * h, TILE)
        qb = q[rows, cols]
        ks = stacked(k[keys, cols], even, odd)
        e = jnp.exp(mmt(qb, ks) + bias2)
        vs = jnp.concatenate([stacked(v[keys, cols], even, odd), ones], axis=1)
        flow = mmt(dnx[rows, pl.ds(2 * TILE * h, 2 * TILE)], vs)
        ds = (e * flow).astype(LOW)
        dq[rows, cols] += mm(ds, ks)
        dk[keys, cols] += fold(tmm(ds, qb))
        dv[keys, cols] += fold(tmm(e.astype(LOW), dnx[rows, pl.ds(2 * TILE * h, TILE)]))


def each(count, body):
    def step(i, carry):
        body(i)
        return carry
    if isinstance(count, int) and count <= 2:
        for i in range(count):
            body(i)
        return
    lax.fori_loop(0, count, step, 0, unroll=8 if isinstance(count, int) else 1)


def zero(ref, step=128):
    def body(i):
        rows = pl.ds(pl.multiple_of(i * step, step), step)
        ref[rows] = jnp.zeros((step,) + ref.shape[1:], ref.dtype)
    each(ref.shape[0] // step, body)


def columns(part, width=256):
    return pl.ds(pl.multiple_of(part * width, width), width)


def block(i, width=TILE):
    return pl.ds(pl.multiple_of(i * width, width), width)


def back_norm(u, gain, xh, r):
    gu = u * gain
    a = jnp.mean(gu, axis=1, keepdims=True)
    b = jnp.mean(gu * xh, axis=1, keepdims=True)
    return (gu - a - xh * b) * r


def out_back(g_b, weight_rows, num, tot, dnx):
    lane = lane_iota((TILE, TILE))
    same = jnp.where((lane < 64) == (row_iota((TILE, TILE)) < 64), 1.0, 0.0).astype(LOW)

    def body(n):
        up = mmt(g_b[...], weight_rows(n)).astype(LOW).astype(F32)
        for h in range(2):
            cols = pl.ds(pl.multiple_of(n * 256 + h * TILE, TILE), TILE)
            wide = lambda k: pl.ds(pl.multiple_of(n * 512 + h * 256 + k * TILE, TILE), TILE)
            d = up[:, h * TILE:(h + 1) * TILE]
            t = tot[:, cols]
            dnx[:, wide(0)] = (d / t).astype(LOW)
            p = d * num[:, cols]
            p1 = p.astype(LOW)
            p2 = (p - p1.astype(F32)).astype(LOW)
            corr = -(mm(p1, same) + mm(p2, same)) / t
            c1 = corr.astype(LOW)
            c2 = (corr - c1.astype(F32)).astype(LOW)
            place = lane_iota(c1.shape) % 64
            nothing = jnp.zeros_like(c1)
            dnx[:, wide(1)] = jnp.where(place == 0, c1, jnp.where(place == 1, c2, nothing))
    each(2, body)


def divide(num, tot, out, rows_all):
    def body(i):
        r = block(i, 64)
        o = num[r] / tot[r]
        num[r] = o
        out[r] = o.astype(LOW)
    each(rows_all // 64, body)


def normalize(y):
    mean = jnp.mean(y, axis=1, keepdims=True)
    centre = y - mean
    r = lax.rsqrt(jnp.mean(centre * centre, axis=1, keepdims=True) + EPS)
    return centre * r, r


def compute_kernel(lens_ref, spans_ref, offs_ref, out_grad, memory, gathered, after_ref, low_ref, gains_ref,
                   layer_out, grads, mem_grads, dpre_out, ng_out, *scratch):
    (w, w2, og, mem, qc, kc, vc, big, act, dhid, dv, num_c, tot_c, xh2, t1, dpre, dq, rs2,
     oc_b, a_b, c_b, g_b, dnx, ng, gb, lout, low_c, high_c, memc, sel, idx,
     starts, packed, in_sem, w_sem, out_sem) = scratch
    n_src = mem.shape[0]
    rows_all = og.shape[0]
    n_sent = starts.shape[0] - 1
    member = lax.axis_index("mem")
    base = member * n_sent

    loads = {}

    def load(name, src, dst, sem):
        loads[name] = pltpu.make_async_copy(src, dst, sem)
        loads[name].start()

    def load_slab(i, count=1):
        lanes = pl.ds(NORM + SLAB * i, SLAB * count)
        load(i, gathered.at[:, :, lanes], w.at[:, :, lanes], w_sem.at[i])

    load("a", low_ref, a_b, in_sem.at[0])
    load_slab(4)
    load("mem", memory, mem, in_sem.at[1])
    load_slab(5)
    load_slab(6)

    def load_rest():
        load("t1", after_ref, t1, in_sem.at[3])
        load("gb", gains_ref, gb, in_sem.at[4])
        load_slab(7)
        load_slab(8, 4)
        for k in range(4):
            load(("w2", k), gathered.at[:, :, pl.ds(CUT + SLAB * k, SLAB)], w2.at[:, k], w_sem.at[13 + k])
        load("og", out_grad, og, in_sem.at[2])

    outs = []

    def send(src, dst):
        copy = pltpu.make_async_copy(src, dst, out_sem.at[len(outs)])
        copy.start()
        outs.append(copy)

    def weight(i, part=None, width=256):
        if part is None:
            return w[:, :, pl.ds(NORM + SLAB * i, SLAB)].reshape(SLAB, SLAB)
        start = pl.multiple_of(NORM + SLAB * i + part * width, TILE)
        return w[:, :, pl.ds(start, width)].reshape(SLAB, width)

    def weight_rows(i, part, width=256, lanes=SLAB):
        devs = pl.ds(pl.multiple_of(part * (width // ROWS), width // ROWS), width // ROWS)
        return w[devs, :, pl.ds(NORM + SLAB * i, lanes)].reshape(width, lanes)

    def put_weight(i, part, value, width=256):
        start = pl.multiple_of(NORM + SLAB * i + part * width, TILE)
        w[:, :, pl.ds(start, width)] = value.astype(LOW).reshape(DEV, ROWS, width)

    def count(j, at):
        starts[j] = at
        return at + lens_ref[0, base + j]
    starts[n_sent] = lax.fori_loop(0, n_sent, count, jnp.int32(0))

    def count_packed(j, at):
        packed[j] = at
        return at + spans_ref[0, base + j]
    n_keys = lax.fori_loop(0, n_sent, count_packed, jnp.int32(0))
    packed[n_sent] = n_keys
    chunks = (n_keys + CHUNK - 1) // CHUNK

    def lows(i):
        row = i * TILE + row_iota((TILE, TILE))
        nothing = jnp.zeros((TILE, TILE), jnp.int32)

        def pick(j, found):
            here_on = row >= starts[j]
            values = (packed[j], packed[j + 1])
            return tuple(jnp.where(here_on, v, f) for v, f in zip(values, found))
        low_c[block(i)], high_c[block(i)] = lax.fori_loop(0, n_sent, pick, (nothing, nothing))
    each(rows_all // TILE, lows)
    zero(num_c)
    zero(tot_c)
    ng[...] = jnp.zeros_like(ng)

    def last_at(table, row):
        def pick(j, found):
            return jnp.where(starts[j] <= row, table(j), found)
        return lax.fori_loop(0, n_sent, pick, jnp.int32(0))

    def tiles(body, bias, first, last):
        def outer(i, carry):
            def inner(kt, carry):
                body(block(i, RT), block(kt), bias(i, kt))
                return carry
            return lax.fori_loop(first(i) // TILE, (last(i) - 1) // TILE + 1, inner, carry)
        lax.fori_loop(0, rows_all // RT, outer, 0)

    def cross_tiles(body):
        def bias(i, kt):
            key = kt * TILE + lane_iota((RT, TILE))
            r = block(i, RT)
            return jnp.where((key >= low_c[r]) & (key < high_c[r]), 0.0, HIDE)
        tiles(body, bias, lambda i: last_at(lambda j: packed[j], i * RT),
              lambda i: last_at(lambda j: packed[j + 1], (i + 1) * RT - 1))

    loads["a"].wait()
    loads[4].wait()

    def query(n):
        qc[:, columns(n)] = mm(a_b[...], weight(4, n)).astype(LOW) * jnp.asarray(0.125, LOW)
    each(2, query)
    load_rest()
    for name in ("mem", 5, 6):
        loads[name].wait()

    def choose(ct):
        r = block(ct, CHUNK)
        for g in range(n_src // TILE):
            hit = idx[r] == g * TILE + lane_iota((CHUNK, TILE))
            sel[:, g * TILE:(g + 1) * TILE] = jnp.where(hit, 1.0, 0.0).astype(LOW)

    def keys(ct):
        r = block(ct, CHUNK)
        key = ct * CHUNK + row_iota((CHUNK, TILE))

        def pick(j, found):
            return jnp.where(key >= packed[j], offs_ref[0, base + j] - packed[j] + key, found)
        at = lax.fori_loop(0, n_sent, pick, jnp.zeros((CHUNK, TILE), jnp.int32))
        idx[r] = jnp.where(key < n_keys, at, -1)
        choose(ct)

        def bring(n):
            memc[r, columns(n)] = mm(sel[...], mem[:, columns(n)]).astype(LOW)
        each(2, bring)

        def project(n):
            kc[r, columns(n)] = mm(memc[r], weight(5, n)).astype(LOW)
            vc[r, columns(n)] = mm(memc[r], weight(6, n)).astype(LOW)
        each(2, project)
    each(chunks, keys)

    cross_tiles(lambda r, k, bias: tile_forward(r, k, bias, qc, kc, vc, num_c, tot_c))
    divide(num_c, tot_c, oc_b, rows_all)
    for name in (7, "t1", "gb"):
        loads[name].wait()

    def cross_out(n):
        t1[:, columns(n)] += mm(oc_b[...], weight(7, n))
    each(2, cross_out)

    def norm_cross(i):
        r = block(i, 64)
        xh, rs = normalize(t1[r])
        xh2[r] = xh
        rs2[r] = jnp.broadcast_to(rs, (64, TILE))
        after = xh * gb[2:3] + gb[3:4]
        t1[r] = after
        c_b[r] = after.astype(LOW)
    each(rows_all // 64, norm_cross)

    loads[8].wait()

    def hidden(n):
        v = mm(c_b[...], weight(8, n))
        sig = 1.0 / (1.0 + jnp.exp(-v))
        act[:, columns(n)] = (v * sig).astype(LOW)
        big[block(n // 2, SLAB), columns(n % 2)] = sig * (1.0 + v * (1.0 - sig))
    each(8, hidden)
    for k in range(4):
        loads[("w2", k)].wait()

    def ffn_out(n):
        cols = columns(n)
        t1[:, cols] += mm(act[...], w2[:, :, :, cols].reshape(4 * SLAB, 256))
    each(2, ffn_out)
    loads["og"].wait()

    def norm_ffn(i):
        r = block(i, 64)
        xh, rs = normalize(t1[r])
        gain = gb[4:5]
        lout[r] = (xh * gain + gb[5:6]).astype(LOW)
        u = og[r].astype(F32)
        ng[4:5] += jnp.sum(u * xh, axis=0, keepdims=True)
        ng[5:6] += jnp.sum(u, axis=0, keepdims=True)
        d = back_norm(u, gain, xh, rs)
        dpre[r] = d
        g_b[r] = d.astype(LOW)
    each(rows_all // 64, norm_ffn)
    send(lout, layer_out)

    def hidden_back(n):
        devs = pl.ds(pl.multiple_of(n * 4, 4), 4)
        part = mmt(g_b[...], w2[devs].reshape(256, SLAB))
        d = (part * big[block(n // 2, SLAB), columns(n % 2)]).astype(LOW)
        dhid[:, columns(n)] = d
        w2[devs] = tmm(act[:, columns(n)], g_b[...]).astype(LOW).reshape(4, 4, ROWS, SLAB)
    each(8, hidden_back)
    for k in range(4):
        send(w2.at[:, k], grads.at[:, :, pl.ds(CUT + SLAB * k, SLAB)])

    def input_back(n):
        dpre[:, columns(n)] += mmt(dhid[...], weight_rows(8, n, 256, 4 * SLAB))
    each(2, input_back)

    def first_grad(n):
        put_weight(8, n, tmm(c_b[...], dhid[:, columns(n)]))
    each(8, first_grad)
    lanes = pl.ds(NORM + SLAB * 8, 4 * SLAB)
    send(w.at[:, :, lanes], grads.at[:, :, lanes])

    def back_cross(i):
        r = block(i, 64)
        u, xh = dpre[r], xh2[r]
        ng[2:3] += jnp.sum(u * xh, axis=0, keepdims=True)
        ng[3:4] += jnp.sum(u, axis=0, keepdims=True)
        d = back_norm(u, gb[2:3], xh, rs2[r][:, :1])
        dpre[r] = d
        g_b[r] = d.astype(LOW)
    each(rows_all // 64, back_cross)

    out_back(g_b, lambda n: weight_rows(7, n), num_c, tot_c, dnx)

    def out_grad_store(n):
        put_weight(7, n, tmm(oc_b[...], g_b[:, columns(n)]))
    each(2, out_grad_store)

    def send_slab(i):
        lanes = pl.ds(NORM + SLAB * i, SLAB)
        send(w.at[:, :, lanes], grads.at[:, :, lanes])

    send_slab(7)
    zero(dq)

    def clear(ct):
        r = block(ct, CHUNK)
        big[r] = jnp.zeros((CHUNK, SLAB), F32)
        dv[r] = jnp.zeros((CHUNK, SLAB), F32)
    each(chunks, clear)
    cross_tiles(lambda r, k, bias: tile_backward(r, k, bias, qc, kc, vc, dnx, dq, big, dv))

    def scaled(src, dst, factor, step=64):
        def body(i):
            r = block(i, step)
            dst[r] = (src[r] * factor).astype(LOW)
        each(src.shape[0] // step, body)

    scaled(dq, qc, 0.125)

    def query_back(n):
        dpre[:, columns(n)] += mmt(qc[...], weight_rows(4, n))
    each(2, query_back)

    send(dpre, dpre_out)

    def query_grad(n):
        put_weight(4, n, tmm(a_b[...], qc[:, columns(n)]))
    each(2, query_grad)
    send_slab(4)

    zero(num_c)
    zero(tot_c)

    def memory_back(ct):
        r = block(ct, CHUNK)
        kc[r] = big[r].astype(LOW)
        vc[r] = dv[r].astype(LOW)

        def key_grad(n):
            cols = columns(n)
            num_c[:, cols] += tmm(memc[r], kc[r, cols])
            tot_c[:, cols] += tmm(memc[r], vc[r, cols])
        each(2, key_grad)

        def rows_grad(n):
            memc[r, columns(n)] = (
                mmt(kc[r], weight_rows(5, n)) + mmt(vc[r], weight_rows(6, n))).astype(LOW)
        each(2, rows_grad)
        choose(ct)

        def spread(n):
            rows = block(n, 256)
            found = tmm(sel[:, columns(n)], memc[r]).astype(LOW)
            mem[rows] = jnp.where(ct == 0, found, mem[rows] + found)
        each(n_src // 256, spread)
    each(chunks, memory_back)
    send(mem, mem_grads)

    def key_store(n):
        put_weight(5, n, num_c[:, columns(n)])
        put_weight(6, n, tot_c[:, columns(n)])
    each(2, key_store)
    send_slab(5)
    send_slab(6)

    send(ng, ng_out)
    for copy in outs:
        copy.wait()


def state_shapes(rows):
    full = lambda dtype, lanes=SLAB, n=rows: jax.ShapeDtypeStruct((n, lanes), dtype)
    return (
        full(F32),
        full(F32),
        full(F32, TILE),
        full(F32),
        full(F32),
        full(LOW),
        full(LOW),
        full(LOW),
        full(LOW),
        full(F32, SLAB, 8),
        full(F32, SLAB, 8),
        full(jnp.int32, TILE),
    )


def compute(lens, spans, offs, out_grad, memory, gathered, after, after_low, gains):
    rows, n_src = out_grad.shape[0], memory.shape[0]
    n_sent = 16
    n_keys = n_sent * 112
    any_space = pl.BlockSpec(memory_space=pl.ANY)
    smem = pl.BlockSpec(memory_space=pltpu.SMEM)
    dma = pltpu.SemaphoreType.DMA
    f32 = lambda *s: pltpu.VMEM(s, F32)
    low = lambda *s: pltpu.VMEM(s, LOW)
    return pl.pallas_call(
        compute_kernel,
        out_shape=(
            jax.ShapeDtypeStruct((rows, SLAB), LOW),
            jax.ShapeDtypeStruct((DEV, ROWS, LANES), LOW),
            jax.ShapeDtypeStruct((n_src, SLAB), LOW),
            jax.ShapeDtypeStruct((rows, SLAB), F32),
            jax.ShapeDtypeStruct((8, SLAB), F32),
        ),
        in_specs=[smem] * 3 + [any_space] * 6,
        out_specs=(any_space,) * 5,
        scratch_shapes=[
            low(DEV, ROWS, CUT),
            low(DEV, 4, ROWS, SLAB),
            low(rows, SLAB),
            low(n_src, SLAB),
            low(rows, SLAB),
            low(n_keys, SLAB),
            low(n_keys, SLAB),
            f32(4 * SLAB, SLAB),
            low(rows, 4 * SLAB),
            low(rows, 4 * SLAB),
            f32(n_keys, SLAB),
            f32(rows, SLAB),
            f32(rows, SLAB),
            f32(rows, SLAB),
            f32(rows, SLAB),
            f32(rows, SLAB),
            f32(rows, SLAB),
            f32(rows, TILE),
            low(rows, SLAB),
            low(rows, SLAB),
            low(rows, SLAB),
            low(rows, SLAB),
            low(rows, 2 * SLAB),
            f32(8, SLAB),
            f32(8, SLAB),
            low(rows, SLAB),
            pltpu.VMEM((rows, TILE), jnp.int32),
            pltpu.VMEM((rows, TILE), jnp.int32),
            low(n_keys, SLAB),
            low(CHUNK, n_src),
            pltpu.VMEM((n_keys, TILE), jnp.int32),
            pltpu.SMEM((n_sent + 1,), jnp.int32),
            pltpu.SMEM((n_sent + 1,), jnp.int32),
            dma((5,)),
            dma((17,)),
            dma((32,)),
        ],
        compiler_params=pltpu.CompilerParams(vmem_limit_bytes=60 << 20),
        name="compute",
    )(lens, spans, offs, out_grad, memory, gathered, after, after_low, gains)
def scatter_rounds(share=0.35):
    spans = []
    for at, tiles in ((33, 6), (39, 8), (47, 8), (17, 16), (0, 11), (11, 6)):
        split = at + max(1, round(tiles * share))
        spans.append((at * 128, split * 128, (at + tiles) * 128))
    return tuple(spans)


SCATTER_ROUNDS = scatter_rounds()
Z_FIRST = (55 * 128, 60 * 128, 65 * 128)
SELF_LANES = NORM + 4 * SLAB
SELF_ROUNDS = (4, 5)


def scatter_kernel(grads, mem_grads, gathered, target, *rest):
    state, (out_ref, mem_ref, target_ref), rest = rest[:12], rest[12:15], rest[15:]
    (acc, from_core, from_first, from_second, from_z, macc, mfrom_core, mfrom_y), rest = rest[:8], rest[8:]
    held, rest = rest[:12], rest[12:]
    (w, tgt, gs, dq, dk, dv, dnx, g_b, out, mem_out), rest = rest[:10], rest[10:]
    (target_grad, from_zc, from_fc, from_sc), rest = rest[:4], rest[4:]
    (out_sems, own_sems, mown_sem, state_sems, core_s, core_r, first_s, first_r,
     second_s, second_r, zs_s, zs_r, mem_s, mem_r, zc_s, zc_r, fc_s, fc_r, sc_s, sc_r) = rest
    dpre, xh1, rs1, num_s, tot_s, qs, ks, vs, o_b, gb, ng, low_s = held
    z, x, y, c = here()
    xp, yp, cp_ = device(z, 1 - x, y, c), device(z, x, 1 - y, c), device(z, x, y, 1 - c)
    zp = [device((z + k) % 4, x, y, c) for k in (1, 2, 3)]
    count = len(SCATTER_ROUNDS)
    core_sems, first_sems, second_sems = (core_s, core_r), (first_s, first_r), (second_s, second_r)
    z_sems, mem_sems = (zs_s, zs_r), (mem_s, mem_r)
    sent = []

    def go(copy):
        copy.start()
        sent.append(copy)

    def span(r, part=None):
        a, m, b = Z_FIRST if r == count else SCATTER_ROUNDS[r]
        return {None: (a, b - a), 0: (a, m - a), 1: (m, b - m)}[part]

    def own(r):
        a, n = span(r)
        return pltpu.make_async_copy(
            grads.at[:, :, :, c, :, pl.ds(a, n)], acc.at[:, :, :, :, pl.ds(a, n)], own_sems.at[r])

    def core(r):
        a, n = span(r)
        source = gs if r in SELF_ROUNDS else grads
        return remote(source.at[:, :, :, 1 - c, :, pl.ds(a, n)],
                      from_core.at[:, :, :, :, pl.ds(a, n)], core_sems, r, cp_)

    def first(r, part):
        lanes = pl.ds(*span(r, part))
        src = acc.at[:, :, 1 - y, :, lanes] if part == 0 else acc.at[:, 1 - x, :, :, lanes]
        return remote(src, from_first.at[:, :, :, lanes], first_sems, (r, part),
                      yp if part == 0 else xp)

    def second(r, part):
        lanes = pl.ds(*span(r, part))
        src = acc.at[:, 1 - x, y, :, lanes] if part == 0 else acc.at[:, x, 1 - y, :, lanes]
        return remote(src, from_second.at[:, :, lanes], second_sems, (r, part),
                      xp if part == 0 else yp)

    def along(r, k):
        lanes = pl.ds(*span(r))
        return remote(acc.at[(z + k + 1) % 4, x, y, :, lanes], from_z.at[k, :, lanes], z_sems,
                      (r, k), zp[k])

    mem_own = pltpu.make_async_copy(mem_grads.at[:, c], macc, mown_sem)
    mem_core = remote(mem_grads.at[:, 1 - c], mfrom_core, mem_sems, 0, cp_)
    mem_far = remote(macc.at[1 - y], mfrom_y, mem_sems, 1, yp)

    def bring(i, src, dst):
        copy = pltpu.make_async_copy(src, dst, state_sems.at[i])
        copy.start()
        return copy

    early = [r for r in range(count) if r not in SELF_ROUNDS]
    own(0).start()
    mem_own.start()
    for r in [count] + early[1:]:
        own(r).start()
    copies = [bring(i, src, dst) for i, (src, dst) in enumerate(zip(state, held))]
    copies.append(bring(12, gathered.at[:, :, pl.ds(NORM, 4 * SLAB)], w))
    copies.append(bring(13, target, tgt))
    greet([xp, yp, cp_] + zp)
    go(core(early[0]))
    go(mem_core)
    for r in [count] + early[1:]:
        go(core(r))

    def add_core(r):
        if r not in SELF_ROUNDS:
            own(r).wait()
        core(r).wait_recv()
        for part in (0, 1):
            lanes = pl.ds(*span(r, part))
            for theirs in (True, False):
                def body(zi, carry, part=part, lanes=lanes, theirs=theirs):
                    for o in (0, 1):
                        if part == 0:
                            xi, yi = o, (1 - y) if theirs else y
                        else:
                            xi, yi = (1 - x) if theirs else x, o
                        mine = gs[zi, xi, yi, c, :, lanes] if r in SELF_ROUNDS else acc[zi, xi, yi, :, lanes]
                        acc[zi, xi, yi, :, lanes] = mine + from_core[zi, xi, yi, :, lanes]
                    return carry
                lax.fori_loop(0, 4, body, 0)
                if theirs:
                    go(first(r, part))

    def add_first(r):
        for part in (0, 1):
            first(r, part).wait_recv()
            lanes = pl.ds(*span(r, part))
            for theirs in (True, False):
                def body(zi, carry, part=part, lanes=lanes, theirs=theirs):
                    if part == 0:
                        xi, yi = (1 - x) if theirs else x, y
                        slot = xi
                    else:
                        xi, yi = x, (1 - y) if theirs else y
                        slot = yi
                    acc[zi, xi, yi, :, lanes] = (
                        acc[zi, xi, yi, :, lanes] + from_first[zi, slot, :, lanes])
                    return carry
                lax.fori_loop(0, 4, body, 0)
                if theirs:
                    go(second(r, part))

    def add_second(r):
        for part in (0, 1):
            second(r, part).wait_recv()
            lanes = pl.ds(*span(r, part))

            def body(zi, carry, lanes=lanes):
                acc[zi, x, y, :, lanes] = acc[zi, x, y, :, lanes] + from_second[zi, :, lanes]
                return carry
            lax.fori_loop(0, 4, body, 0)
        for k in (1, 0, 2):
            go(along(r, k))

    def add_z(r):
        lanes = pl.ds(*span(r))
        total = acc[z, x, y, :, lanes].astype(jnp.float32)
        for k in (0, 2, 1):
            along(r, k).wait_recv()
            total = total + from_z[k, :, lanes].astype(jnp.float32)
        out[:, lanes] = total

    lanes_c = pl.ds(*span(count))
    cut_c = [pl.ds(*span(count, part)) for part in (0, 1)]
    width_c = [span(count, part)[1] for part in (0, 1)]

    def far_c(k):
        return remote(acc.at[(z + k + 1) % 4, :, :, :, lanes_c], from_zc.at[k], (zc_s, zc_r), k, zp[k])

    def first_c(part):
        src = acc.at[z, 1 - x, :, :, cut_c[0]] if part == 0 else acc.at[z, :, 1 - y, :, cut_c[1]]
        return remote(src, from_fc.at[part, :, :, pl.ds(0, width_c[part])], (fc_s, fc_r), part,
                      xp if part == 0 else yp)

    def second_c(part):
        src = acc.at[z, x, 1 - y, :, cut_c[0]] if part == 0 else acc.at[z, 1 - x, y, :, cut_c[1]]
        return remote(src, from_sc.at[part, :, pl.ds(0, width_c[part])], (sc_s, sc_r), part,
                      yp if part == 0 else xp)

    def add_core_c():
        own(count).wait()
        core(count).wait_recv()
        for k in (0, 2, 1, 3):
            zi = (z + k + 1) % 4
            for xi in (0, 1):
                for yi in (0, 1):
                    acc[zi, xi, yi, :, lanes_c] = (
                        acc[zi, xi, yi, :, lanes_c] + from_core[zi, xi, yi, :, lanes_c])
            if k < 3:
                go(far_c(k))

    def add_far_c():
        for k in (0, 2, 1):
            far_c(k).wait_recv()
        for xi in (0, 1):
            for yi in (0, 1):
                total = acc[z, xi, yi, :, lanes_c].astype(F32)
                for k in range(3):
                    total = total + from_zc[k, xi, yi].astype(F32)
                acc[z, xi, yi, :, lanes_c] = total.astype(LOW)
        for part in (0, 1):
            go(first_c(part))

    def add_first_c():
        for part in (0, 1):
            first_c(part).wait_recv()
            for o in (0, 1):
                xi, yi = (x, o) if part == 0 else (o, y)
                acc[z, xi, yi, :, cut_c[part]] = (
                    acc[z, xi, yi, :, cut_c[part]] + from_fc[part, o, :, pl.ds(0, width_c[part])])
            go(second_c(part))

    def end_c():
        for part in (0, 1):
            second_c(part).wait_recv()
            out[:, cut_c[part]] = (acc[z, x, y, :, cut_c[part]].astype(F32)
                                   + from_sc[part, :, pl.ds(0, width_c[part])].astype(F32))

    def memory_core():
        mem_own.wait()
        mem_core.wait_recv()
        for theirs in (True, False):
            side = (1 - y) if theirs else y

            def body(i, carry, side=side):
                rows = pl.ds(pl.multiple_of(i * 64, 64), 64)
                macc[side, rows] = macc[side, rows] + mfrom_core[side, rows]
                return carry
            lax.fori_loop(0, 8, body, 0)
            if theirs:
                go(mem_far)

    def memory_end():
        mem_far.wait_recv()

        def body(i, carry):
            rows = pl.ds(pl.multiple_of(i * 64, 64), 64)
            mem_out[rows] = macc[y, rows].astype(jnp.float32) + mfrom_y[rows].astype(jnp.float32)
            return carry
        lax.fori_loop(0, 8, body, 0)

    def weight_rows(i, part):
        devs = pl.ds(part * 16, 16)
        return w[devs, :, pl.ds(SLAB * i, SLAB)].reshape(256, SLAB)

    def put(i, n, value):
        gs[:, :, :, :, :, pl.ds(NORM + SLAB * i + 256 * n, 256)] = value.astype(LOW).reshape(4, 2, 2, 2, ROWS, 256)

    rows_all = tgt.shape[0]

    def norm_back(i):
        r = block(i, 64)
        u, xh = dpre[r], xh1[r]
        ng[0:1] += jnp.sum(u * xh, axis=0, keepdims=True)
        ng[1:2] += jnp.sum(u, axis=0, keepdims=True)
        d = back_norm(u, gb[0:1], xh, rs1[r][:, :1])
        dpre[r] = d
        g_b[r] = d.astype(LOW)

    def self_norm():
        for copy in copies:
            copy.wait()
        each(rows_all // 64, norm_back)

    def self_out():
        out_back(g_b, lambda n: weight_rows(3, n), num_s, tot_s, dnx)
        for n in (0, 1):
            put(3, n, tmm(o_b[...], g_b[:, pl.ds(256 * n, 256)]))
        for ref in (dq, dk, dv):
            zero(ref)

    def self_tiles(i, first, last):
        def inner(kt, carry):
            r = pl.ds(i * RT, RT)
            key = kt * TILE + lane_iota((RT, TILE))
            row = i * RT + row_iota((RT, TILE))
            bias = jnp.where((key >= low_s[r]) & (key <= row), 0.0, HIDE)
            tile_backward(r, block(kt), bias, qs, ks, vs, dnx, dq, dk, dv)
            return carry
        lax.fori_loop(first, last, inner, 0)

    def self_grads():
        def lower(i):
            r = block(i, 64)
            qs[r] = (dq[r] * 0.125).astype(LOW)
            ks[r] = dk[r].astype(LOW)
            vs[r] = dv[r].astype(LOW)
        each(rows_all // 64, lower)
        for i, src in ((0, qs), (1, ks), (2, vs)):
            for n in (0, 1):
                put(i, n, tmm(tgt[...], src[:, pl.ds(256 * n, 256)]))
        inside = lane_iota((8, TILE)) < ROWS
        for d in range(DEV):
            one = ng[:, pl.ds(TILE * (d // 8), TILE)]
            one = pltpu.roll(one, (TILE - ROWS * (d % 8)) % TILE, 1) if d % 8 else one
            one = jnp.concatenate([jnp.where(inside, one, 0.0), jnp.zeros((8, TILE), F32)], axis=0)
            gs[d // 8, d // 4 % 2, d // 2 % 2, d % 2, :, pl.ds(0, NORM)] = one.astype(LOW)
        for r in SELF_ROUNDS:
            go(core(r))

    def self_target():
        for n in (0, 1):
            total = mmt(qs[...], weight_rows(0, n)) + mmt(ks[...], weight_rows(1, n))
            cols = pl.ds(256 * n, 256)
            target_grad[:, cols] = dpre[:, cols] + total + mmt(vs[...], weight_rows(2, n))

    add_core(0)
    memory_core()
    add_core_c()
    add_core(1)
    self_norm()
    add_first(0)
    add_core(2)
    self_out()
    add_second(0)
    add_first(1)
    add_core(3)
    self_tiles(0, 0, 2)
    add_second(1)
    add_first(2)
    self_tiles(1, 0, 4)
    add_z(0)
    add_second(2)
    add_first(3)
    add_far_c()
    self_grads()
    add_core(4)
    add_core(5)
    self_target()
    to_target = pltpu.make_async_copy(target_grad, target_ref, out_sems.at[0])
    to_target.start()
    add_first_c()
    memory_end()
    to_memory = pltpu.make_async_copy(mem_out, mem_ref, out_sems.at[1])
    to_memory.start()
    add_z(1)
    add_second(3)
    add_first(4)
    add_first(5)
    add_z(2)
    add_second(4)
    add_z(3)
    end_c()
    add_second(5)
    add_z(4)
    add_z(5)
    to_rows = pltpu.make_async_copy(out, out_ref, out_sems.at[2])
    to_rows.start()
    for copy in (to_target, to_memory, to_rows):
        copy.wait()
    for copy in sent:
        copy.wait_send()


def scatter_all(grads, mem_grads, gathered, target, state):
    any_space = pl.BlockSpec(memory_space=pl.ANY)
    dma = pltpu.SemaphoreType.DMA
    n = len(SCATTER_ROUNDS)
    rows = mem_grads.shape[2]
    wide = Z_FIRST[2] - Z_FIRST[0]
    low = lambda *s: pltpu.VMEM(s, LOW)
    f32 = lambda *s: pltpu.VMEM(s, F32)
    return pl.pallas_call(
        scatter_kernel,
        out_shape=(
            jax.ShapeDtypeStruct((ROWS, LANES), F32),
            jax.ShapeDtypeStruct((rows, SLAB), F32),
            jax.ShapeDtypeStruct((rows, SLAB), F32),
        ),
        in_specs=[any_space] * 16,
        out_specs=(any_space,) * 3,
        scratch_shapes=[
            low(4, 2, 2, ROWS, LANES),
            low(4, 2, 2, ROWS, LANES),
            low(4, 2, ROWS, LANES),
            low(4, ROWS, LANES),
            low(3, ROWS, LANES),
            low(2, rows, SLAB),
            low(2, rows, SLAB),
            low(rows, SLAB),
        ]
        + [pltpu.VMEM(s.shape, s.dtype) for s in state_shapes(rows)]
        + [
            low(32, ROWS, 4 * SLAB),
            low(rows, SLAB),
            low(4, 2, 2, 2, ROWS, SELF_LANES),
            f32(rows, SLAB),
            f32(rows, SLAB),
            f32(rows, SLAB),
            low(rows, 2 * SLAB),
            low(rows, SLAB),
            f32(ROWS, LANES),
            f32(rows, SLAB),
            f32(rows, SLAB),
            low(3, 2, 2, ROWS, wide),
            low(2, 2, ROWS, wide),
            low(2, ROWS, wide),
            dma((3,)),
            dma((n + 1,)),
            dma(()),
            dma((14,)),
            dma((n + 1,)),
            dma((n + 1,)),
            dma((n, 2)),
            dma((n, 2)),
            dma((n, 2)),
            dma((n, 2)),
            dma((n, 3)),
            dma((n, 3)),
            dma((2,)),
            dma((2,)),
            dma((3,)),
            dma((3,)),
            dma((2,)),
            dma((2,)),
            dma((2,)),
            dma((2,)),
        ],
        compiler_params=pltpu.CompilerParams(
            collective_id=2, has_side_effects=True, vmem_limit_bytes=56 << 20),
        name="scatter",
    )(grads, mem_grads, gathered, target, *state)


def finish_kernel(rows_ref, mem_ref, target_ref, *rest):
    outs, (rows, mem, target, in_sems, out_sems) = rest[:18], rest[18:]
    copies = []
    loads = []
    half = target.shape[0] // 2
    pieces = [pl.ds(0, half), pl.ds(half, half)]
    cuts_ = [(NORM + SLAB * i, SLAB) for i in range(8)] + [(NORM + SLAB * 8, 4 * SLAB)]
    cuts_ += [(NORM + SLAB * (12 + k), SLAB) for k in range(4)]

    def load(src, dst):
        copy = pltpu.make_async_copy(src, dst, in_sems.at[len(loads)])
        copy.start()
        loads.append(copy)

    def bring(src, dst):
        copy = pltpu.make_async_copy(src, dst, out_sems.at[len(copies)])
        copy.start()
        copies.append(copy)

    for p in pieces:
        load(target_ref.at[p], target.at[p])
        load(mem_ref.at[p], mem.at[p])
    load(rows_ref, rows)
    for i, p in enumerate(pieces):
        loads[2 * i].wait()
        bring(target.at[p], outs[0].at[p])
        loads[2 * i + 1].wait()
        bring(mem.at[p], outs[1].at[p])
    loads[4].wait()
    for i, (start, width) in enumerate(cuts_):
        dst = outs[2 + i] if i < 9 else outs[11].at[pl.ds(ROWS * (i - 9), ROWS)]
        bring(rows.at[:, pl.ds(start, width)], dst)
    for i in range(6):
        outs[12 + i][...] = rows[i, pl.ds(0, ROWS)]
    for copy in copies:
        copy.wait()


def finish(rows, mem, target):
    any_space = pl.BlockSpec(memory_space=pl.ANY)
    shape = lambda *s: jax.ShapeDtypeStruct(s, F32)
    return pl.pallas_call(
        finish_kernel,
        out_shape=(shape(*target.shape), shape(*mem.shape))
        + (shape(ROWS, SLAB),) * 8
        + (shape(ROWS, 4 * SLAB), shape(4 * ROWS, SLAB))
        + (shape(ROWS),) * 6,
        in_specs=[any_space] * 3,
        out_specs=(any_space,) * 12 + (pl.BlockSpec(memory_space=pltpu.VMEM),) * 6,
        scratch_shapes=[
            pltpu.VMEM(rows.shape, F32),
            pltpu.VMEM(mem.shape, F32),
            pltpu.VMEM(target.shape, F32),
            pltpu.SemaphoreType.DMA((5,)),
            pltpu.SemaphoreType.DMA((17,)),
        ],
        name="finish",
    )(rows, mem, target)


def local(target_in, memory, out_grad, *rest):
    fast = two_by_two((lax.axis_size("dp"), lax.axis_size("mem")))
    if not fast:
        return plain(target_in, memory, out_grad, *rest)
    weights, tables = rest[:16], rest[16:]
    norms = sum(
        jnp.pad(one[None, :], ((i, ROWS - 1 - i), (0, NORM - ROWS)))
        for i, one in enumerate(weights[10:])
    )
    gathered, all_memory, saved = gather_all(weights[:10], norms, memory, tables[0], target_in)
    after, after_low, xh1, rs1, num, tot, q, k, v, o, gains, low_s = saved
    layer_out, grads, mem_grads, d_after, norm_grads = compute(
        *tables, out_grad, all_memory, gathered, after, after_low, gains
    )
    state = (d_after, xh1, rs1, num, tot, q, k, v, o, gains, norm_grads, low_s)
    rows = target_in.shape[0]
    out, mem_out, target_grad = scatter_all(
        grads.reshape(4, 2, 2, 2, ROWS, LANES),
        mem_grads.reshape(2, 2, rows, SLAB),
        gathered,
        target_in,
        state,
    )
    return (layer_out,) + tuple(finish(out, mem_out, target_grad))


def solution(mesh):
    both = P(("dp", "mem"), None)
    flat = P(("dp", "mem"))
    in_specs = (both,) * 13 + (flat,) * 6 + (P("dp", None),) * 3
    out_specs = (both,) * 13 + (flat,) * 6
    return jax.shard_map(local, mesh=mesh, in_specs=in_specs, out_specs=out_specs, check_vma=False)
```

```python
import functools

import jax
import jax.numpy as jnp
from jax import lax
from jax.experimental import pallas as pl
from jax.experimental.pallas import tpu as pltpu
from jax.sharding import PartitionSpec as P

MESH = pl.DeviceIdType.MESH
SLAB = 512
NORM = 128
LANES = NORM + 16 * SLAB
ROWS = 16


def here():
    dp, mem = lax.axis_index("dp"), lax.axis_index("mem")
    return dp // 2, dp % 2, mem // 2, mem % 2


def device(z, x, y, c):
    return (z * 2 + x, y * 2 + c)


def greet(peers):
    barrier = pltpu.get_barrier_semaphore()
    for peer in peers:
        pl.semaphore_signal(barrier, inc=1, device_id=peer, device_id_type=MESH)
    pl.semaphore_wait(barrier, len(peers))


def remote(src, dst, sems, index, peer):
    send, recv = sems
    return pltpu.make_async_remote_copy(
        src_ref=src,
        dst_ref=dst,
        send_sem=send.at[index],
        recv_sem=recv.at[index],
        device_id=peer,
        device_id_type=MESH,
    )


def cuts(widths, share):
    spans, at = [], 0
    for tiles in widths:
        n = tiles * 128
        spans.append((at, at + max(1, round(tiles * share)) * 128, at + n))
        at += n
    return tuple(spans)


GATHER_ROUNDS = cuts((17, 36), 0.22)
Z_LAST = (53 * 128, 59 * 128, 65 * 128)


def gather_kernel(*refs):
    shards, memory_ref, lens_ref, target = refs[:10], *refs[10:13]
    params, refs = refs[13:19], refs[19:]
    out, mem_out = refs[:2]
    state_out, refs = refs[2:14], refs[14:]
    local_sem, mem_local = refs[:2]
    z_sems, first_sems, second_sems = refs[2:4], refs[4:6], refs[6:8]
    across, mems = refs[8:10], refs[10:12]
    stage, mem_stage = refs[12:14]
    state, refs = refs[14:26], refs[26:]
    after, a_b, xh1, rs1, num, tot, qs, ks, vs, o_b, gb, low_s = state
    w, norms, tgt, starts, state_sems, rows, refs = *refs[:6], refs[6:]
    cf_sems, cs_sems, cz_sems, co_sems = refs[:2], refs[2:4], refs[4:6], refs[6:8]
    z, x, y, c = here()
    xp, yp, cp_ = device(z, 1 - x, y, c), device(z, x, 1 - y, c), device(z, x, y, 1 - c)
    own = out.at[z, x, y, c]
    rounds = range(len(GATHER_ROUNDS))

    local = []

    def bring(src, start, width):
        local.append(
            pltpu.make_async_copy(src, stage.at[:, pl.ds(start, width)], local_sem.at[len(local)])
        )

    for i in range(8):
        bring(shards[i], NORM + SLAB * i, SLAB)
    bring(shards[8], NORM + SLAB * 8, 4 * SLAB)
    for k in range(4):
        bring(shards[9].at[pl.ds(ROWS * k, ROWS)], NORM + SLAB * (12 + k), SLAB)
    for one in local:
        one.start()
    keep = pltpu.make_async_copy(memory_ref, mem_stage, mem_local.at[0])
    keep.start()
    zn = [device((z + k) % 4, x, y, c) for k in (1, 3)]
    rows[...] = jnp.zeros_like(rows)
    for i, one in enumerate(params):
        rows[i : i + 1, :ROWS] = one[...].astype(F32)
    stage[:, :NORM] = rows[...].astype(LOW)
    greet([xp, yp, cp_] + zn)
    for one in local:
        one.wait()
    own_out = pltpu.make_async_copy(stage, own, mem_local.at[1])
    own_out.start()

    def column(slot):
        return z if slot == 0 else (z - slot if slot < 4 else z + (slot - 3))

    def there(slot):
        return None if slot == 0 else (z >= slot if slot < 4 else z <= 6 - slot)

    def both(a, b):
        return b if a is None else (a if b is None else jnp.logical_and(a, b))

    def guarded(cond, body):
        if cond is None:
            body()
        else:
            pl.when(cond)(body)

    sent = []

    def go(make, cond=None):
        guarded(cond, lambda: make().start())
        sent.append((cond, make))

    def along(slot, r, up):
        a, _, b = GATHER_ROUNDS[r]
        ref = out.at[column(slot), x, y, c, :, pl.ds(a, b - a)]
        src = stage.at[:, pl.ds(a, b - a)] if slot == 0 else ref
        d = 0 if slot == 0 else (slot if slot < 4 else slot - 3)
        peer = device((z + (1 if up else 3)) % 4, x, y, c)
        return remote(src, ref, z_sems, (0 if up else 1, d, r), peer)

    def arrived(slot, r):
        a, _, b = GATHER_ROUNDS[r]
        ref = out.at[column(slot), x, y, c, :, pl.ds(a, b - a)]
        up = slot < 4
        index = (0 if up else 1, (slot if up else slot - 3) - 1, r)
        return remote(ref, ref, z_sems, index, xp)

    def first(slot, r, part, arriving=False):
        a, m, b = GATHER_ROUNDS[r]
        zz = column(slot)
        if part == 0:
            ref = out.at[zz, (1 - x) if arriving else x, y, c, :, pl.ds(a, m - a)]
        else:
            ref = out.at[zz, x, (1 - y) if arriving else y, c, :, pl.ds(m, b - m)]
        lanes = pl.ds(a, m - a) if part == 0 else pl.ds(m, b - m)
        src = stage.at[:, lanes] if slot == 0 and not arriving else ref
        return remote(src, ref, first_sems, (slot, part, r), xp if part == 0 else yp)

    def second(slot, r, part, hop, arriving=False):
        a, m, b = GATHER_ROUNDS[r]
        zz = column(slot)
        if part == 0:
            side = (1 - x) if hop else x
            ref = out.at[zz, side, (1 - y) if arriving else y, c, :, pl.ds(a, m - a)]
        else:
            side = (1 - y) if hop else y
            ref = out.at[zz, (1 - x) if arriving else x, side, c, :, pl.ds(m, b - m)]
        lanes = pl.ds(a, m - a) if part == 0 else pl.ds(m, b - m)
        src = stage.at[:, lanes] if slot == 0 and not (arriving or hop) else ref
        return remote(src, ref, second_sems, (slot, part, hop, r), yp if part == 0 else xp)

    def over(slot, r, arriving=False):
        a, _, b = GATHER_ROUNDS[r]
        ref = out.at[column(slot), :, :, (1 - c) if arriving else c, :, pl.ds(a, b - a)]
        return remote(ref, ref, across, (slot, r), cp_)

    def spread(slot, r):
        cond = there(slot)
        for part in (1, 0):
            go(functools.partial(first, slot, r, part), cond)
        for part in (1, 0):
            go(functools.partial(second, slot, r, part, 0), cond)

    def from_z(d, r):
            for slot in (d, d + 3):
                cond = there(slot)
                guarded(cond, lambda slot=slot, r=r: arrived(slot, r).wait_recv())
                if d < 3:
                    onward = z < 3 if slot < 4 else z > 0
                    go(functools.partial(along, slot, r, slot < 4), both(cond, onward))
                spread(slot, r)

    def pass_on(slots, r):
            for slot in slots:
                cond = there(slot)
                for part in (1, 0):
                    guarded(cond, lambda s=slot, r=r, p=part: first(s, r, p, True).wait_recv())
                    go(functools.partial(second, slot, r, part, 1), cond)

    def hand_over(slots, r):
            for slot in slots:
                cond = there(slot)
                for part in (0, 1):
                    for hop in (0, 1):
                        guarded(cond, lambda s=slot, r=r, p=part, h=hop: second(s, r, p, h, True).wait_recv())
                go(functools.partial(over, slot, r), cond)

    cut_c = [pl.ds(Z_LAST[p], Z_LAST[p + 1] - Z_LAST[p]) for p in (0, 1)]
    lanes_c = pl.ds(Z_LAST[0], Z_LAST[2] - Z_LAST[0])

    def first_c(part, arriving=False):
        if part == 0:
            ref = out.at[z, (1 - x) if arriving else x, y, c, :, cut_c[0]]
        else:
            ref = out.at[z, x, (1 - y) if arriving else y, c, :, cut_c[1]]
        src = ref if arriving else stage.at[:, cut_c[part]]
        return remote(src, ref, cf_sems, part, xp if part == 0 else yp)

    def second_c(part, hop, arriving=False):
        if part == 0:
            ref = out.at[z, (1 - x) if hop else x, (1 - y) if arriving else y, c, :, cut_c[0]]
        else:
            ref = out.at[z, (1 - x) if arriving else x, (1 - y) if hop else y, c, :, cut_c[1]]
        src = ref if arriving or hop else stage.at[:, cut_c[part]]
        return remote(src, ref, cs_sems, (part, hop), yp if part == 0 else xp)

    def along_c(slot, up):
        ref = out.at[column(slot), :, :, c, :, lanes_c]
        d = 0 if slot == 0 else (slot if slot < 4 else slot - 3)
        peer = device((z + (1 if up else 3)) % 4, x, y, c)
        return remote(ref, ref, cz_sems, (0 if up else 1, d), peer)

    def arrived_c(slot):
        ref = out.at[column(slot), :, :, c, :, lanes_c]
        up = slot < 4
        return remote(ref, ref, cz_sems, (0 if up else 1, (slot if up else slot - 3) - 1), xp)

    def over_c(slot, arriving=False):
        ref = out.at[column(slot), :, :, (1 - c) if arriving else c, :, lanes_c]
        return remote(ref, ref, co_sems, slot, cp_)

    def pass_on_c():
        for part in (0, 1):
            first_c(part, True).wait_recv()
            go(functools.partial(second_c, part, 1))

    def plane_c():
        own_out.wait()
        for part in (0, 1):
            for hop in (0, 1):
                second_c(part, hop, True).wait_recv()
        go(functools.partial(along_c, 0, True), z < 3)
        go(functools.partial(along_c, 0, False), z > 0)
        go(functools.partial(over_c, 0))

    def from_z_c(d):
        for slot in (d, d + 3):
            cond = there(slot)
            guarded(cond, lambda slot=slot: arrived_c(slot).wait_recv())
            if d < 3:
                onward = z < 3 if slot < 4 else z > 0
                go(functools.partial(along_c, slot, slot < 4), both(cond, onward))
            go(functools.partial(over_c, slot), cond)

    for r in rounds:
        go(functools.partial(along, 0, r, True), z < 3)
        go(functools.partial(along, 0, r, False), z > 0)
        spread(0, r)
        if r == 0:
            for part in (0, 1):
                go(functools.partial(first_c, part))
            for part in (0, 1):
                go(functools.partial(second_c, part, 0))
    mem_own = mem_out.at[y, c]

    def memory_rows():
        keep.wait()
        kept = pltpu.make_async_copy(mem_stage, mem_own, mem_local.at[2])
        kept.start()
        go(lambda: remote(mem_stage, mem_own, mems, 0, yp))
        go(lambda: remote(mem_stage, mem_own, mems, 1, cp_))
        return kept

    def memory_far():
        far = mem_out.at[1 - y, c]
        remote(far, far, mems, 0, yp).wait_recv()
        go(lambda: remote(far, far, mems, 2, cp_))

    everyone = (0, 1, 4, 2, 5, 3, 6)

    def all_over(r):
        for slot in everyone:
            guarded(there(slot), lambda s=slot: over(s, r, True).wait_recv())

    rows_all = tgt.shape[0]
    n_sent = starts.shape[0]
    loads = [pltpu.make_async_copy(target, tgt, state_sems.at[12])]
    loads.append(pltpu.make_async_copy(out.at[:, :, :, :, :, pl.ds(NORM, 4 * SLAB)], w, state_sems.at[13]))
    loads.append(pltpu.make_async_copy(out.at[:, :, :, :, :, pl.ds(0, NORM)], norms, state_sems.at[14]))
    saves = [pltpu.make_async_copy(src, dst, state_sems.at[i]) for i, (src, dst) in enumerate(zip(state, state_out))]

    def weight(i, n):
        return w[:, :, :, :, :, pl.ds(SLAB * i + 256 * n, 256)].reshape(SLAB, 256)

    def prepare():
        base = lax.axis_index("mem") * n_sent

        def count(j, at):
            starts[j] = at
            return at + lens_ref[0, base + j]
        lax.fori_loop(0, n_sent, count, jnp.int32(0))
        for i in range(rows_all // TILE):
            row = i * TILE + row_iota((TILE, TILE))
            found = jnp.zeros((TILE, TILE), jnp.int32)
            for j in range(n_sent):
                found = jnp.where(row >= starts[j], starts[j], found)
            low_s[pl.ds(i * TILE, TILE)] = found
        zero(num)
        zero(tot)

    def project():
        for one in loads:
            one.wait()
        for j in range(SLAB // TILE):
            total = jnp.zeros((8, TILE), F32)
            for k in range(8):
                d = 8 * j + k
                one = norms[d // 8, d // 4 % 2, d // 2 % 2, d % 2].astype(F32)[:8]
                total = total + (pltpu.roll(one, ROWS * k, 1) if k else one)
            gb[:, pl.ds(TILE * j, TILE)] = total
        for i, dst in ((0, qs), (1, ks), (2, vs)):
            for n in (0, 1):
                value = mm(tgt[...], weight(i, n)).astype(LOW)
                dst[:, pl.ds(256 * n, 256)] = value * jnp.asarray(0.125, LOW) if i == 0 else value

    def self_tiles(i, first_tile, last_tile):
        def inner(kt, carry):
            r = pl.ds(i * RT, RT)
            key = kt * TILE + lane_iota((RT, TILE))
            row = i * RT + row_iota((RT, TILE))
            bias = jnp.where((key >= low_s[r]) & (key <= row), 0.0, HIDE)
            tile_forward(r, block(kt), bias, qs, ks, vs, num, tot)
            return carry
        lax.fori_loop(first_tile, last_tile, inner, 0)

    def project_out():
        divide(num, tot, o_b, rows_all)
        for n in (0, 1):
            cols = pl.ds(256 * n, 256)
            after[:, cols] = tgt[:, cols].astype(F32) + mm(o_b[...], weight(3, n))

    def norm_rows(i):
        r = block(i, 64)
        xh, rs = normalize(after[r])
        xh1[r] = xh
        rs1[r] = jnp.broadcast_to(rs, (64, TILE))
        value = xh * gb[0:1] + gb[1:2]
        after[r] = value
        a_b[r] = value.astype(LOW)

    loads[0].start()
    prepare()
    from_z(1, 0)
    pass_on_c()
    from_z(1, 1)
    pass_on((0,), 0)
    plane_c()
    from_z(2, 0)
    pass_on((0,), 1)
    pass_on((1, 4), 0)
    from_z(3, 0)
    from_z(2, 1)
    pass_on((2, 5), 0)
    hand_over((0,), 0)
    from_z_c(1)
    pass_on((1, 4), 1)
    pass_on((3, 6), 0)
    kept = memory_rows()
    hand_over((1, 4), 0)
    hand_over((2, 5), 0)
    from_z(3, 1)
    from_z_c(2)
    hand_over((3, 6), 0)
    all_over(0)
    loads[1].start()
    loads[2].start()
    pass_on((2, 5), 1)
    from_z_c(3)
    project()
    hand_over((0,), 1)
    self_tiles(0, 0, 2)
    pass_on((3, 6), 1)
    self_tiles(1, 0, 4)
    hand_over((1, 4), 1)
    memory_far()
    project_out()
    each(rows_all // 64, norm_rows)
    hand_over((2, 5), 1)
    hand_over((3, 6), 1)
    for one in saves:
        one.start()
    all_over(1)
    for slot in everyone:
        guarded(there(slot), lambda s=slot: over_c(s, True).wait_recv())
    for one in saves:
        one.wait()
    for i, side in ((1, y), (2, 1 - y)):
        last = mem_out.at[side, 1 - c]
        remote(last, last, mems, i, cp_).wait_recv()
    kept.wait()
    for cond, make in sent:
        guarded(cond, lambda make=make: make().wait_send())


def gather_all(shards, params, memory, lens, target):
    any_space = pl.BlockSpec(memory_space=pl.ANY)
    dma = pltpu.SemaphoreType.DMA
    n = len(GATHER_ROUNDS)
    both = lambda *s: [dma(s), dma(s)]
    state = forward_shapes(target.shape[0])
    low = lambda *s: pltpu.VMEM(s, LOW)
    gathered, whole_memory, *saved = pl.pallas_call(
        gather_kernel,
        out_shape=(
            jax.ShapeDtypeStruct((4, 2, 2, 2, ROWS, LANES), jnp.bfloat16),
            jax.ShapeDtypeStruct((2, 2) + memory.shape, jnp.bfloat16),
        )
        + state,
        in_specs=[any_space] * 11
        + [pl.BlockSpec(memory_space=pltpu.SMEM), any_space]
        + [pl.BlockSpec(memory_space=pltpu.VMEM)] * 6,
        out_specs=(any_space,) * 14,
        scratch_shapes=[dma((14,)), dma((3,))]
        + both(2, 3, n) + both(7, 2, n) + both(7, 2, 2, n) + both(7, n) + both(3)
        + [low(ROWS, LANES), low(*memory.shape)]
        + [pltpu.VMEM(s.shape, s.dtype) for s in state]
        + [
            low(4, 2, 2, 2, ROWS, 4 * SLAB),
            low(4, 2, 2, 2, ROWS, NORM),
            low(*target.shape),
            pltpu.SMEM((16,), jnp.int32),
            dma((15,)),
            pltpu.VMEM((ROWS, NORM), F32),
        ]
        + both(2) + both(2, 2) + both(2, 3) + both(7),
        compiler_params=pltpu.CompilerParams(
            collective_id=1, has_side_effects=True, vmem_limit_bytes=60 << 20),
        name="gather",
    )(*shards, memory, lens, target, *[p[None, :] for p in params])
    return gathered.reshape(32, ROWS, LANES), whole_memory.reshape(-1, SLAB), saved


def forward_shapes(rows):
    full = lambda dtype, lanes=SLAB, n=rows: jax.ShapeDtypeStruct((n, lanes), dtype)
    return (
        full(F32),
        full(LOW),
        full(F32),
        full(F32, TILE),
        full(F32),
        full(F32),
        full(LOW),
        full(LOW),
        full(LOW),
        full(LOW),
        full(F32, SLAB, 8),
        full(jnp.int32, TILE),
    )


def two_by_two(mesh_axes):
    return mesh_axes == (8, 4)


def gather_any(shards, norms, memory):
    everyone = ("dp", "mem")
    packed = jnp.concatenate([norms] + list(shards[:9]), axis=1)
    rows = lax.all_gather(packed, everyone, axis=0, tiled=True).reshape(32, ROWS, -1)
    last = lax.all_gather(shards[9], everyone, axis=0, tiled=True)
    last = last.reshape(32, 4, ROWS, SLAB).transpose(0, 2, 1, 3).reshape(32, ROWS, 4 * SLAB)
    return (
        jnp.concatenate([rows, last], axis=2),
        lax.all_gather(memory, "mem", axis=0, tiled=True),
    )


def scatter_any(grads, mem_grads):
    everyone = ("dp", "mem")
    wide = grads.reshape(32, ROWS, LANES).astype(jnp.float32)
    cut = LANES - 4 * SLAB
    rows = lax.psum_scatter(
        wide[:, :, :cut].reshape(512, cut), everyone, scatter_dimension=0, tiled=True
    )
    last = wide[:, :, cut:].reshape(32, ROWS, 4, SLAB).transpose(0, 2, 1, 3).reshape(2048, SLAB)
    last = lax.psum_scatter(last, everyone, scatter_dimension=0, tiled=True)
    mem = lax.psum_scatter(
        mem_grads.astype(jnp.float32), "mem", scatter_dimension=0, tiled=True
    )
    return rows, last, mem
HEADS = 8
HEAD = 64
eps_norm = 1e-05
score_scale = 0.125


def layer_norm(values, gain, shift):
    centre = values - jnp.mean(values, axis=-1, keepdims=True)
    spread = jnp.mean(centre * centre, axis=-1, keepdims=True)
    return centre * lax.rsqrt(spread + eps_norm) * gain + shift


def head_split(values):
    return values.reshape(values.shape[0], HEADS, HEAD)


def matmul(left, right):
    return jnp.dot(left, right, preferred_element_type=jnp.float32)


def left_grad(inputs, grads):
    return jnp.einsum("ra,rb->ab", inputs, grads, preferred_element_type=jnp.float32)


def back_through(grads, weight):
    return jnp.einsum("rb,ab->ra", grads, weight, preferred_element_type=jnp.float32)


def exp_scores(q_block, keys, low_edge, high_edge):
    raw = jnp.einsum("qhd,khd->hqk", head_split(q_block), head_split(keys),
                     preferred_element_type=jnp.float32) * score_scale
    position = lax.broadcasted_iota(jnp.int32, (q_block.shape[0], keys.shape[0]), 1)
    allowed = (position >= low_edge[:, None]) & (position < high_edge[:, None])
    return jnp.where(allowed[None], jnp.exp(raw), 0.0)


def attend(queries, keys, values, low_edge, high_edge):
    expo = exp_scores(queries, keys, low_edge, high_edge)
    numer = jnp.einsum("hqk,khd->qhd", expo.astype(jnp.bfloat16), head_split(values),
                       preferred_element_type=jnp.float32)
    totals = jnp.sum(expo, axis=2).T
    return (numer / totals[:, :, None]).reshape(queries.shape[0], -1), totals


def attend_back(queries, keys, values, low_edge, high_edge, upstream, output, totals):
    expo = exp_scores(queries, keys, low_edge, high_edge)
    up = head_split(upstream.astype(jnp.float32))
    numer_grad = (up / totals[:, :, None]).astype(jnp.bfloat16)
    corr = -jnp.sum(up * head_split(output), axis=2) / totals
    flow = jnp.einsum("qhd,khd->hqk", numer_grad, head_split(values),
                      preferred_element_type=jnp.float32) + corr.T[:, :, None]
    ds = (expo * flow).astype(jnp.bfloat16)
    dq = jnp.einsum("hqk,khd->qhd", ds, head_split(keys), preferred_element_type=jnp.float32)
    dk = jnp.einsum("hqk,qhd->khd", ds, head_split(queries), preferred_element_type=jnp.float32)
    dv = jnp.einsum("hqk,qhd->khd", expo.astype(jnp.bfloat16), numer_grad,
                    preferred_element_type=jnp.float32)
    flat = lambda v: v.reshape(v.shape[0], -1)
    return ((flat(dq) * score_scale).astype(jnp.bfloat16), (flat(dk) * score_scale).astype(jnp.bfloat16),
            flat(dv).astype(jnp.bfloat16))


def plain(target_in, memory, out_grad, *rest):
    weights, (tgt_lens, src_lens, src_offsets) = rest[:16], rest[16:]
    member = lax.axis_index("mem")
    per_device = tgt_lens.shape[1] // lax.axis_size("mem")
    pick = lambda table: lax.dynamic_slice_in_dim(table[0], member * per_device, per_device, 0)
    lengths, spans, offsets = pick(tgt_lens), pick(src_lens), pick(src_offsets)
    norms = jnp.stack(weights[10:], axis=1)
    norms = jnp.pad(norms, ((0, 0), (0, NORM - norms.shape[1])))
    gathered, all_memory = gather_any(weights[:10], norms, memory)
    W = gathered.reshape(512, LANES)
    mat = lambda i: W[:, NORM + SLAB * i : NORM + SLAB * (i + 1)]
    wsq, wsk, wsv, wso, wcq, wck, wcv, wco = [mat(i) for i in range(8)]
    w1 = W[:, NORM + 8 * SLAB : NORM + 12 * SLAB]
    w2 = gathered[:, :, NORM + 12 * SLAB :].reshape(32, 16, 4, SLAB).transpose(0, 2, 1, 3).reshape(2048, SLAB)
    ga, sa, gc, sc, gf, sf = [W[:, i].astype(jnp.float32) for i in range(6)]
    rows = target_in.shape[0]
    starts = jnp.cumsum(lengths) - lengths
    position = lax.iota(jnp.int32, rows)
    sentence = jnp.sum((position[:, None] >= starts[None, :]).astype(jnp.int32), axis=1) - 1
    picker = sentence[:, None] == lax.iota(jnp.int32, per_device)[None, :]
    choose = lambda v: jnp.sum(jnp.where(picker, v[None, :], 0), axis=1)
    self_low, self_high = choose(starts), position + 1
    cross_low = choose(offsets)
    cross_high = cross_low + choose(spans)
    low = jnp.bfloat16
    q, k, v = [matmul(target_in, w).astype(low) for w in (wsq, wsk, wsv)]
    o_self_f, tot_self = attend(q, k, v, self_low, self_high)
    o_self = o_self_f.astype(low)
    after_self, pull_self = jax.vjp(layer_norm, target_in.astype(jnp.float32) + matmul(o_self, wso), ga, sa)
    a_b = after_self.astype(low)
    qc = matmul(a_b, wcq).astype(low)
    kc, vc = matmul(all_memory, wck).astype(low), matmul(all_memory, wcv).astype(low)
    cut = lambda v: v.reshape((4, -1) + v.shape[1:])
    o_c_f, tot_c = lax.map(
        lambda p: attend(p[0], kc, vc, p[1], p[2]), (cut(qc), cut(cross_low), cut(cross_high))
    )
    o_c_f, tot_c = o_c_f.reshape(rows, -1), tot_c.reshape(rows, -1)
    o_c = o_c_f.astype(low)
    after_cross, pull_cross = jax.vjp(layer_norm, after_self + matmul(o_c, wco), gc, sc)
    c_b = after_cross.astype(low)
    hidden = matmul(c_b, w1)
    activated, pull_silu = jax.vjp(jax.nn.silu, hidden)
    act = activated.astype(low)
    final, pull_ffn = jax.vjp(layer_norm, after_cross + matmul(act, w2), gf, sf)
    d_pre_out, g_gf, g_sf = pull_ffn(out_grad.astype(jnp.float32))
    d_branch = d_pre_out.astype(low)
    g_w2 = left_grad(act, d_branch)
    d_hidden = pull_silu(back_through(d_branch, w2))[0].astype(low)
    g_w1 = left_grad(c_b, d_hidden)
    d_pre_cross, g_gc, g_sc = pull_cross(d_pre_out + back_through(d_hidden, w1))
    d_cb = d_pre_cross.astype(low)
    g_wco = left_grad(o_c, d_cb)
    d_oc = back_through(d_cb, wco).astype(low)

    def piece(carry, p):
        dq, dk, dv = attend_back(p[0], kc, vc, p[1], p[2], p[3], p[4], p[5])
        return (carry[0] + dk, carry[1] + dv), dq

    empty = jnp.zeros(kc.shape, jnp.bfloat16)
    (dk_c, dv_c), dq_c = lax.scan(
        piece,
        (empty, empty),
        tuple(cut(v) for v in (qc, cross_low, cross_high, d_oc, o_c_f, tot_c)),
    )
    dq_c = dq_c.reshape(rows, -1)
    g_wcq, g_wck, g_wcv = left_grad(a_b, dq_c), left_grad(all_memory, dk_c), left_grad(all_memory, dv_c)
    mem_grad = back_through(dk_c, wck) + back_through(dv_c, wcv)
    d_pre_self, g_ga, g_sa = pull_self(d_pre_cross + back_through(dq_c, wcq))
    d_sb = d_pre_self.astype(low)
    g_wso = left_grad(o_self, d_sb)
    d_os = back_through(d_sb, wso).astype(low)
    dq, dk, dv = attend_back(q, k, v, self_low, self_high, d_os, o_self_f, tot_self)
    g_wsq, g_wsk, g_wsv = left_grad(target_in, dq), left_grad(target_in, dk), left_grad(target_in, dv)
    target_grad = d_pre_self + back_through(dq, wsq) + back_through(dk, wsk) + back_through(dv, wsv)
    n_g = jnp.pad(jnp.stack([g_ga, g_sa, g_gc, g_sc, g_gf, g_sf], axis=1), ((0, 0), (0, NORM - 6)))
    g_w2p = g_w2.reshape(32, 4, 16, SLAB).transpose(0, 2, 1, 3).reshape(512, 4 * SLAB)
    grads = jnp.concatenate([g.astype(low) for g in (n_g, g_wsq, g_wsk, g_wsv, g_wso, g_wcq, g_wck, g_wcv, g_wco, g_w1, g_w2p)], axis=1)
    part = lambda i, n=1: out[:, NORM + SLAB * i : NORM + SLAB * (i + n)]
    out, w2_grad, mem_out = scatter_any(grads, mem_grad.astype(low))
    return (final.astype(low), target_grad, mem_out) + tuple(part(i) for i in range(8)) + (part(8, 4), w2_grad) + tuple(out[:, i] for i in range(6))


TILE = 128
RT = 256
RC = 512
CHUNK = 256
EPS = 1e-05
HIDE = -1e30
LOW = jnp.bfloat16
F32 = jnp.float32
DEV = 32
CUT = NORM + 12 * SLAB


def mm(a, b):
    return jnp.dot(a, b, preferred_element_type=F32)


def mmt(a, b):
    return lax.dot_general(a, b, (((1,), (1,)), ((), ())), preferred_element_type=F32)


def tmm(a, b):
    return lax.dot_general(a, b, (((0,), (0,)), ((), ())), preferred_element_type=F32)


def lane_iota(shape):
    return lax.broadcasted_iota(jnp.int32, shape, len(shape) - 1)


def row_iota(shape):
    return lax.broadcasted_iota(jnp.int32, shape, 0)


def halves():
    lane = lane_iota((1, TILE))
    even = jnp.where(lane < 64, 1.0, 0.0).astype(LOW)
    odd = jnp.where(lane < 64, 0.0, 1.0).astype(LOW)
    return even, odd


def stacked(block, even, odd):
    return jnp.concatenate([block * even, block * odd], axis=0)


def fold(pair):
    lane = lane_iota((TILE, TILE))
    return jnp.where(lane < 64, pair[:TILE], pair[TILE:])


def totals_block(even, odd):
    wide = lambda v: jnp.broadcast_to(v, (TILE, TILE))
    return jnp.concatenate([wide(even), wide(odd)], axis=0)


def corr_block():
    lane = lane_iota((TILE, TILE))
    a = jnp.where(lane < 2, 1.0, 0.0).astype(LOW)
    b = jnp.where((lane >= 64) & (lane < 66), 1.0, 0.0).astype(LOW)
    return jnp.concatenate([a, b], axis=0)


def tile_forward(rows, keys, bias, q, k, v, num, tot):
    even, odd = halves()
    ones = totals_block(even, odd)
    bias2 = jnp.concatenate([bias, bias], axis=1)
    for h in range(4):
        cols = pl.ds(TILE * h, TILE)
        s = mmt(q[rows, cols], stacked(k[keys, cols], even, odd))
        e = jnp.exp(s + bias2).astype(LOW)
        both = mm(e, jnp.concatenate([stacked(v[keys, cols], even, odd), ones], axis=1))
        num[rows, cols] += both[:, :TILE]
        tot[rows, cols] += both[:, TILE:]


def tile_backward(rows, keys, bias, q, k, v, dnx, dq, dk, dv):
    even, odd = halves()
    ones = corr_block()
    bias2 = jnp.concatenate([bias, bias], axis=1)
    for h in range(4):
        cols = pl.ds(TILE * h, TILE)
        qb = q[rows, cols]
        ks = stacked(k[keys, cols], even, odd)
        e = jnp.exp(mmt(qb, ks) + bias2)
        vs = jnp.concatenate([stacked(v[keys, cols], even, odd), ones], axis=1)
        flow = mmt(dnx[rows, pl.ds(2 * TILE * h, 2 * TILE)], vs)
        ds = (e * flow).astype(LOW)
        dq[rows, cols] += mm(ds, ks)
        dk[keys, cols] += fold(tmm(ds, qb))
        dv[keys, cols] += fold(tmm(e.astype(LOW), dnx[rows, pl.ds(2 * TILE * h, TILE)]))


def each(count, body):
    def step(i, carry):
        body(i)
        return carry
    if isinstance(count, int) and count <= 2:
        for i in range(count):
            body(i)
        return
    lax.fori_loop(0, count, step, 0, unroll=8 if isinstance(count, int) else 1)


def zero(ref, step=128):
    def body(i):
        rows = pl.ds(pl.multiple_of(i * step, step), step)
        ref[rows] = jnp.zeros((step,) + ref.shape[1:], ref.dtype)
    each(ref.shape[0] // step, body)


def columns(part, width=256):
    return pl.ds(pl.multiple_of(part * width, width), width)


def block(i, width=TILE):
    return pl.ds(pl.multiple_of(i * width, width), width)


def back_norm(u, gain, xh, r):
    gu = u * gain
    a = jnp.mean(gu, axis=1, keepdims=True)
    b = jnp.mean(gu * xh, axis=1, keepdims=True)
    return (gu - a - xh * b) * r


def out_back(g_b, weight_rows, num, tot, dnx):
    lane = lane_iota((TILE, TILE))
    same = jnp.where((lane < 64) == (row_iota((TILE, TILE)) < 64), 1.0, 0.0).astype(LOW)

    def body(n):
        up = mmt(g_b[...], weight_rows(n)).astype(LOW).astype(F32)
        for h in range(2):
            cols = pl.ds(pl.multiple_of(n * 256 + h * TILE, TILE), TILE)
            wide = lambda k: pl.ds(pl.multiple_of(n * 512 + h * 256 + k * TILE, TILE), TILE)
            d = up[:, h * TILE:(h + 1) * TILE]
            t = tot[:, cols]
            dnx[:, wide(0)] = (d / t).astype(LOW)
            p = d * num[:, cols]
            p1 = p.astype(LOW)
            p2 = (p - p1.astype(F32)).astype(LOW)
            corr = -(mm(p1, same) + mm(p2, same)) / t
            c1 = corr.astype(LOW)
            c2 = (corr - c1.astype(F32)).astype(LOW)
            place = lane_iota(c1.shape) % 64
            nothing = jnp.zeros_like(c1)
            dnx[:, wide(1)] = jnp.where(place == 0, c1, jnp.where(place == 1, c2, nothing))
    each(2, body)


def divide(num, tot, out, rows_all):
    def body(i):
        r = block(i, 64)
        o = num[r] / tot[r]
        num[r] = o
        out[r] = o.astype(LOW)
    each(rows_all // 64, body)


def normalize(y):
    mean = jnp.mean(y, axis=1, keepdims=True)
    centre = y - mean
    r = lax.rsqrt(jnp.mean(centre * centre, axis=1, keepdims=True) + EPS)
    return centre * r, r


def compute_kernel(lens_ref, spans_ref, offs_ref, out_grad, memory, gathered, after_ref, low_ref, gains_ref,
                   layer_out, grads, mem_grads, dpre_out, ng_out, *scratch):
    (w, w2, og, mem, qc, kc, vc, big, act, dhid, dv, num_c, tot_c, xh2, t1, dpre, dq, rs2,
     oc_b, a_b, c_b, g_b, dnx, ng, gb, lout, low_c, high_c, memc, sel, idx,
     starts, packed, in_sem, w_sem, out_sem) = scratch
    n_src = mem.shape[0]
    rows_all = og.shape[0]
    n_sent = starts.shape[0] - 1
    member = lax.axis_index("mem")
    base = member * n_sent

    loads = {}

    def load(name, src, dst, sem):
        loads[name] = pltpu.make_async_copy(src, dst, sem)
        loads[name].start()

    def load_slab(i, count=1):
        lanes = pl.ds(NORM + SLAB * i, SLAB * count)
        load(i, gathered.at[:, :, lanes], w.at[:, :, lanes], w_sem.at[i])

    load("a", low_ref, a_b, in_sem.at[0])
    load_slab(4)
    load("mem", memory, mem, in_sem.at[1])
    load_slab(5)
    load_slab(6)

    def load_rest():
        load("t1", after_ref, t1, in_sem.at[3])
        load("gb", gains_ref, gb, in_sem.at[4])
        load_slab(7)
        load_slab(8, 4)
        for k in range(4):
            load(("w2", k), gathered.at[:, :, pl.ds(CUT + SLAB * k, SLAB)], w2.at[:, k], w_sem.at[13 + k])
        load("og", out_grad, og, in_sem.at[2])

    outs = []

    def send(src, dst):
        copy = pltpu.make_async_copy(src, dst, out_sem.at[len(outs)])
        copy.start()
        outs.append(copy)

    def weight(i, part=None, width=256):
        if part is None:
            return w[:, :, pl.ds(NORM + SLAB * i, SLAB)].reshape(SLAB, SLAB)
        start = pl.multiple_of(NORM + SLAB * i + part * width, TILE)
        return w[:, :, pl.ds(start, width)].reshape(SLAB, width)

    def weight_rows(i, part, width=256, lanes=SLAB):
        devs = pl.ds(pl.multiple_of(part * (width // ROWS), width // ROWS), width // ROWS)
        return w[devs, :, pl.ds(NORM + SLAB * i, lanes)].reshape(width, lanes)

    def put_weight(i, part, value, width=256):
        start = pl.multiple_of(NORM + SLAB * i + part * width, TILE)
        w[:, :, pl.ds(start, width)] = value.astype(LOW).reshape(DEV, ROWS, width)

    def count(j, at):
        starts[j] = at
        return at + lens_ref[0, base + j]
    starts[n_sent] = lax.fori_loop(0, n_sent, count, jnp.int32(0))

    def count_packed(j, at):
        packed[j] = at
        return at + spans_ref[0, base + j]
    n_keys = lax.fori_loop(0, n_sent, count_packed, jnp.int32(0))
    packed[n_sent] = n_keys
    chunks = (n_keys + CHUNK - 1) // CHUNK

    def lows(i):
        row = i * TILE + row_iota((TILE, TILE))
        nothing = jnp.zeros((TILE, TILE), jnp.int32)

        def pick(j, found):
            here_on = row >= starts[j]
            values = (packed[j], packed[j + 1])
            return tuple(jnp.where(here_on, v, f) for v, f in zip(values, found))
        low_c[block(i)], high_c[block(i)] = lax.fori_loop(0, n_sent, pick, (nothing, nothing))
    each(rows_all // TILE, lows)
    zero(num_c)
    zero(tot_c)
    ng[...] = jnp.zeros_like(ng)

    def last_at(table, row):
        def pick(j, found):
            return jnp.where(starts[j] <= row, table(j), found)
        return lax.fori_loop(0, n_sent, pick, jnp.int32(0))

    def tiles(body, bias, first, last):
        def outer(i, carry):
            def inner(kt, carry):
                body(block(i, RC), block(kt), bias(i, kt))
                return carry
            return lax.fori_loop(first(i) // TILE, (last(i) - 1) // TILE + 1, inner, carry)
        lax.fori_loop(0, rows_all // RC, outer, 0)

    def cross_tiles(body):
        def bias(i, kt):
            key = kt * TILE + lane_iota((RC, TILE))
            r = block(i, RC)
            return jnp.where((key >= low_c[r]) & (key < high_c[r]), 0.0, HIDE)
        tiles(body, bias, lambda i: last_at(lambda j: packed[j], i * RC),
              lambda i: last_at(lambda j: packed[j + 1], (i + 1) * RC - 1))

    loads["a"].wait()
    loads[4].wait()

    def query(n):
        qc[:, columns(n)] = mm(a_b[...], weight(4, n)).astype(LOW) * jnp.asarray(0.125, LOW)
    each(2, query)
    load_rest()
    for name in ("mem", 5, 6):
        loads[name].wait()

    def choose(ct):
        r = block(ct, CHUNK)
        for g in range(n_src // TILE):
            hit = idx[r] == g * TILE + lane_iota((CHUNK, TILE))
            sel[:, g * TILE:(g + 1) * TILE] = jnp.where(hit, 1.0, 0.0).astype(LOW)

    def keys(ct):
        r = block(ct, CHUNK)
        key = ct * CHUNK + row_iota((CHUNK, TILE))

        def pick(j, found):
            return jnp.where(key >= packed[j], offs_ref[0, base + j] - packed[j] + key, found)
        at = lax.fori_loop(0, n_sent, pick, jnp.zeros((CHUNK, TILE), jnp.int32))
        idx[r] = jnp.where(key < n_keys, at, -1)
        choose(ct)

        def bring(n):
            memc[r, columns(n)] = mm(sel[...], mem[:, columns(n)]).astype(LOW)
        each(2, bring)

        def project(n):
            kc[r, columns(n)] = mm(memc[r], weight(5, n)).astype(LOW)
            vc[r, columns(n)] = mm(memc[r], weight(6, n)).astype(LOW)
        each(2, project)
    each(chunks, keys)

    cross_tiles(lambda r, k, bias: tile_forward(r, k, bias, qc, kc, vc, num_c, tot_c))
    divide(num_c, tot_c, oc_b, rows_all)
    for name in (7, "t1", "gb"):
        loads[name].wait()

    def cross_out(n):
        t1[:, columns(n)] += mm(oc_b[...], weight(7, n))
    each(2, cross_out)

    def norm_cross(i):
        r = block(i, 64)
        xh, rs = normalize(t1[r])
        xh2[r] = xh
        rs2[r] = jnp.broadcast_to(rs, (64, TILE))
        after = xh * gb[2:3] + gb[3:4]
        t1[r] = after
        c_b[r] = after.astype(LOW)
    each(rows_all // 64, norm_cross)

    loads[8].wait()

    def hidden(n):
        v = mm(c_b[...], weight(8, n))
        sig = 1.0 / (1.0 + jnp.exp(-v))
        act[:, columns(n)] = (v * sig).astype(LOW)
        big[block(n // 2, SLAB), columns(n % 2)] = sig * (1.0 + v * (1.0 - sig))
    each(8, hidden)
    for k in range(4):
        loads[("w2", k)].wait()

    def ffn_out(n):
        cols = columns(n)
        t1[:, cols] += mm(act[...], w2[:, :, :, cols].reshape(4 * SLAB, 256))
    each(2, ffn_out)
    loads["og"].wait()

    def norm_ffn(i):
        r = block(i, 64)
        xh, rs = normalize(t1[r])
        gain = gb[4:5]
        lout[r] = (xh * gain + gb[5:6]).astype(LOW)
        u = og[r].astype(F32)
        ng[4:5] += jnp.sum(u * xh, axis=0, keepdims=True)
        ng[5:6] += jnp.sum(u, axis=0, keepdims=True)
        d = back_norm(u, gain, xh, rs)
        dpre[r] = d
        g_b[r] = d.astype(LOW)
    each(rows_all // 64, norm_ffn)
    send(lout, layer_out)

    def hidden_back(n):
        devs = pl.ds(pl.multiple_of(n * 4, 4), 4)
        part = mmt(g_b[...], w2[devs].reshape(256, SLAB))
        d = (part * big[block(n // 2, SLAB), columns(n % 2)]).astype(LOW)
        dhid[:, columns(n)] = d
        w2[devs] = tmm(act[:, columns(n)], g_b[...]).astype(LOW).reshape(4, 4, ROWS, SLAB)
    each(8, hidden_back)
    for k in range(4):
        send(w2.at[:, k], grads.at[:, :, pl.ds(CUT + SLAB * k, SLAB)])

    def input_back(n):
        dpre[:, columns(n)] += mmt(dhid[...], weight_rows(8, n, 256, 4 * SLAB))
    each(2, input_back)

    def first_grad(n):
        put_weight(8, n, tmm(c_b[...], dhid[:, columns(n)]))
    each(8, first_grad)
    lanes = pl.ds(NORM + SLAB * 8, 4 * SLAB)
    send(w.at[:, :, lanes], grads.at[:, :, lanes])

    def back_cross(i):
        r = block(i, 64)
        u, xh = dpre[r], xh2[r]
        ng[2:3] += jnp.sum(u * xh, axis=0, keepdims=True)
        ng[3:4] += jnp.sum(u, axis=0, keepdims=True)
        d = back_norm(u, gb[2:3], xh, rs2[r][:, :1])
        dpre[r] = d
        g_b[r] = d.astype(LOW)
    each(rows_all // 64, back_cross)

    out_back(g_b, lambda n: weight_rows(7, n), num_c, tot_c, dnx)

    def out_grad_store(n):
        put_weight(7, n, tmm(oc_b[...], g_b[:, columns(n)]))
    each(2, out_grad_store)

    def send_slab(i):
        lanes = pl.ds(NORM + SLAB * i, SLAB)
        send(w.at[:, :, lanes], grads.at[:, :, lanes])

    send_slab(7)
    zero(dq)

    def clear(ct):
        r = block(ct, CHUNK)
        big[r] = jnp.zeros((CHUNK, SLAB), F32)
        dv[r] = jnp.zeros((CHUNK, SLAB), F32)
    each(chunks, clear)
    cross_tiles(lambda r, k, bias: tile_backward(r, k, bias, qc, kc, vc, dnx, dq, big, dv))

    def scaled(src, dst, factor, step=64):
        def body(i):
            r = block(i, step)
            dst[r] = (src[r] * factor).astype(LOW)
        each(src.shape[0] // step, body)

    scaled(dq, qc, 0.125)

    def query_back(n):
        dpre[:, columns(n)] += mmt(qc[...], weight_rows(4, n))
    each(2, query_back)

    send(dpre, dpre_out)

    def query_grad(n):
        put_weight(4, n, tmm(a_b[...], qc[:, columns(n)]))
    each(2, query_grad)
    send_slab(4)

    zero(num_c)
    zero(tot_c)

    def memory_back(ct):
        r = block(ct, CHUNK)
        kc[r] = big[r].astype(LOW)
        vc[r] = dv[r].astype(LOW)

        def key_grad(n):
            cols = columns(n)
            num_c[:, cols] += tmm(memc[r], kc[r, cols])
            tot_c[:, cols] += tmm(memc[r], vc[r, cols])
        each(2, key_grad)

        def rows_grad(n):
            memc[r, columns(n)] = (
                mmt(kc[r], weight_rows(5, n)) + mmt(vc[r], weight_rows(6, n))).astype(LOW)
        each(2, rows_grad)
        choose(ct)

        def spread(n):
            rows = block(n, 256)
            found = tmm(sel[:, columns(n)], memc[r]).astype(LOW)
            mem[rows] = jnp.where(ct == 0, found, mem[rows] + found)
        each(n_src // 256, spread)
    each(chunks, memory_back)
    send(mem, mem_grads)

    def key_store(n):
        put_weight(5, n, num_c[:, columns(n)])
        put_weight(6, n, tot_c[:, columns(n)])
    each(2, key_store)
    send_slab(5)
    send_slab(6)

    send(ng, ng_out)
    for copy in outs:
        copy.wait()


def state_shapes(rows):
    full = lambda dtype, lanes=SLAB, n=rows: jax.ShapeDtypeStruct((n, lanes), dtype)
    return (
        full(F32),
        full(F32),
        full(F32, TILE),
        full(F32),
        full(F32),
        full(LOW),
        full(LOW),
        full(LOW),
        full(LOW),
        full(F32, SLAB, 8),
        full(F32, SLAB, 8),
        full(jnp.int32, TILE),
    )


def compute(lens, spans, offs, out_grad, memory, gathered, after, after_low, gains):
    rows, n_src = out_grad.shape[0], memory.shape[0]
    n_sent = 16
    n_keys = n_sent * 112
    any_space = pl.BlockSpec(memory_space=pl.ANY)
    smem = pl.BlockSpec(memory_space=pltpu.SMEM)
    dma = pltpu.SemaphoreType.DMA
    f32 = lambda *s: pltpu.VMEM(s, F32)
    low = lambda *s: pltpu.VMEM(s, LOW)
    return pl.pallas_call(
        compute_kernel,
        out_shape=(
            jax.ShapeDtypeStruct((rows, SLAB), LOW),
            jax.ShapeDtypeStruct((DEV, ROWS, LANES), LOW),
            jax.ShapeDtypeStruct((n_src, SLAB), LOW),
            jax.ShapeDtypeStruct((rows, SLAB), F32),
            jax.ShapeDtypeStruct((8, SLAB), F32),
        ),
        in_specs=[smem] * 3 + [any_space] * 6,
        out_specs=(any_space,) * 5,
        scratch_shapes=[
            low(DEV, ROWS, CUT),
            low(DEV, 4, ROWS, SLAB),
            low(rows, SLAB),
            low(n_src, SLAB),
            low(rows, SLAB),
            low(n_keys, SLAB),
            low(n_keys, SLAB),
            f32(4 * SLAB, SLAB),
            low(rows, 4 * SLAB),
            low(rows, 4 * SLAB),
            f32(n_keys, SLAB),
            f32(rows, SLAB),
            f32(rows, SLAB),
            f32(rows, SLAB),
            f32(rows, SLAB),
            f32(rows, SLAB),
            f32(rows, SLAB),
            f32(rows, TILE),
            low(rows, SLAB),
            low(rows, SLAB),
            low(rows, SLAB),
            low(rows, SLAB),
            low(rows, 2 * SLAB),
            f32(8, SLAB),
            f32(8, SLAB),
            low(rows, SLAB),
            pltpu.VMEM((rows, TILE), jnp.int32),
            pltpu.VMEM((rows, TILE), jnp.int32),
            low(n_keys, SLAB),
            low(CHUNK, n_src),
            pltpu.VMEM((n_keys, TILE), jnp.int32),
            pltpu.SMEM((n_sent + 1,), jnp.int32),
            pltpu.SMEM((n_sent + 1,), jnp.int32),
            dma((5,)),
            dma((17,)),
            dma((32,)),
        ],
        compiler_params=pltpu.CompilerParams(vmem_limit_bytes=60 << 20),
        name="compute",
    )(lens, spans, offs, out_grad, memory, gathered, after, after_low, gains)
def scatter_rounds(share=0.35):
    spans = []
    for at, tiles in ((33, 6), (39, 8), (47, 8), (17, 16), (0, 11), (11, 6)):
        split = at + max(1, round(tiles * share))
        spans.append((at * 128, split * 128, (at + tiles) * 128))
    return tuple(spans)


SCATTER_ROUNDS = scatter_rounds()
Z_FIRST = (55 * 128, 60 * 128, 65 * 128)
SELF_LANES = NORM + 4 * SLAB
SELF_ROUNDS = (4, 5)


def scatter_kernel(grads, mem_grads, gathered, target, *rest):
    state, (out_ref, mem_ref, target_ref), rest = rest[:12], rest[12:15], rest[15:]
    (acc, from_core, from_first, from_second, from_z, macc, mfrom_core, mfrom_y), rest = rest[:8], rest[8:]
    held, rest = rest[:12], rest[12:]
    (w, tgt, gs, dq, dk, dv, dnx, g_b, out, mem_out), rest = rest[:10], rest[10:]
    (target_grad, from_zc, from_fc, from_sc), rest = rest[:4], rest[4:]
    (out_sems, own_sems, mown_sem, state_sems, core_s, core_r, first_s, first_r,
     second_s, second_r, zs_s, zs_r, mem_s, mem_r, zc_s, zc_r, fc_s, fc_r, sc_s, sc_r) = rest
    dpre, xh1, rs1, num_s, tot_s, qs, ks, vs, o_b, gb, ng, low_s = held
    z, x, y, c = here()
    xp, yp, cp_ = device(z, 1 - x, y, c), device(z, x, 1 - y, c), device(z, x, y, 1 - c)
    zp = [device((z + k) % 4, x, y, c) for k in (1, 2, 3)]
    count = len(SCATTER_ROUNDS)
    core_sems, first_sems, second_sems = (core_s, core_r), (first_s, first_r), (second_s, second_r)
    z_sems, mem_sems = (zs_s, zs_r), (mem_s, mem_r)
    sent = []

    def go(copy):
        copy.start()
        sent.append(copy)

    def span(r, part=None):
        a, m, b = Z_FIRST if r == count else SCATTER_ROUNDS[r]
        return {None: (a, b - a), 0: (a, m - a), 1: (m, b - m)}[part]

    def own(r):
        a, n = span(r)
        return pltpu.make_async_copy(
            grads.at[:, :, :, c, :, pl.ds(a, n)], acc.at[:, :, :, :, pl.ds(a, n)], own_sems.at[r])

    def core(r):
        a, n = span(r)
        source = gs if r in SELF_ROUNDS else grads
        return remote(source.at[:, :, :, 1 - c, :, pl.ds(a, n)],
                      from_core.at[:, :, :, :, pl.ds(a, n)], core_sems, r, cp_)

    def first(r, part):
        lanes = pl.ds(*span(r, part))
        src = acc.at[:, :, 1 - y, :, lanes] if part == 0 else acc.at[:, 1 - x, :, :, lanes]
        return remote(src, from_first.at[:, :, :, lanes], first_sems, (r, part),
                      yp if part == 0 else xp)

    def second(r, part):
        lanes = pl.ds(*span(r, part))
        src = acc.at[:, 1 - x, y, :, lanes] if part == 0 else acc.at[:, x, 1 - y, :, lanes]
        return remote(src, from_second.at[:, :, lanes], second_sems, (r, part),
                      xp if part == 0 else yp)

    def along(r, k):
        lanes = pl.ds(*span(r))
        return remote(acc.at[(z + k + 1) % 4, x, y, :, lanes], from_z.at[k, :, lanes], z_sems,
                      (r, k), zp[k])

    mem_own = pltpu.make_async_copy(mem_grads.at[:, c], macc, mown_sem)
    mem_core = remote(mem_grads.at[:, 1 - c], mfrom_core, mem_sems, 0, cp_)
    mem_far = remote(macc.at[1 - y], mfrom_y, mem_sems, 1, yp)

    def bring(i, src, dst):
        copy = pltpu.make_async_copy(src, dst, state_sems.at[i])
        copy.start()
        return copy

    early = [r for r in range(count) if r not in SELF_ROUNDS]
    own(0).start()
    mem_own.start()
    for r in [count] + early[1:]:
        own(r).start()
    copies = [bring(i, src, dst) for i, (src, dst) in enumerate(zip(state, held))]
    copies.append(bring(12, gathered.at[:, :, pl.ds(NORM, 4 * SLAB)], w))
    copies.append(bring(13, target, tgt))
    greet([xp, yp, cp_] + zp)
    go(core(early[0]))
    go(mem_core)
    for r in [count] + early[1:]:
        go(core(r))

    def add_core(r):
        if r not in SELF_ROUNDS:
            own(r).wait()
        core(r).wait_recv()
        for part in (0, 1):
            lanes = pl.ds(*span(r, part))
            for theirs in (True, False):
                def body(zi, carry, part=part, lanes=lanes, theirs=theirs):
                    for o in (0, 1):
                        if part == 0:
                            xi, yi = o, (1 - y) if theirs else y
                        else:
                            xi, yi = (1 - x) if theirs else x, o
                        mine = gs[zi, xi, yi, c, :, lanes] if r in SELF_ROUNDS else acc[zi, xi, yi, :, lanes]
                        acc[zi, xi, yi, :, lanes] = mine + from_core[zi, xi, yi, :, lanes]
                    return carry
                lax.fori_loop(0, 4, body, 0)
                if theirs:
                    go(first(r, part))

    def add_first(r):
        for part in (0, 1):
            first(r, part).wait_recv()
            lanes = pl.ds(*span(r, part))
            for theirs in (True, False):
                def body(zi, carry, part=part, lanes=lanes, theirs=theirs):
                    if part == 0:
                        xi, yi = (1 - x) if theirs else x, y
                        slot = xi
                    else:
                        xi, yi = x, (1 - y) if theirs else y
                        slot = yi
                    acc[zi, xi, yi, :, lanes] = (
                        acc[zi, xi, yi, :, lanes] + from_first[zi, slot, :, lanes])
                    return carry
                lax.fori_loop(0, 4, body, 0)
                if theirs:
                    go(second(r, part))

    def add_second(r):
        for part in (0, 1):
            second(r, part).wait_recv()
            lanes = pl.ds(*span(r, part))

            def body(zi, carry, lanes=lanes):
                acc[zi, x, y, :, lanes] = acc[zi, x, y, :, lanes] + from_second[zi, :, lanes]
                return carry
            lax.fori_loop(0, 4, body, 0)
        for k in (1, 0, 2):
            go(along(r, k))

    def add_z(r):
        lanes = pl.ds(*span(r))
        total = acc[z, x, y, :, lanes].astype(jnp.float32)
        for k in (0, 2, 1):
            along(r, k).wait_recv()
            total = total + from_z[k, :, lanes].astype(jnp.float32)
        out[:, lanes] = total

    lanes_c = pl.ds(*span(count))
    cut_c = [pl.ds(*span(count, part)) for part in (0, 1)]
    width_c = [span(count, part)[1] for part in (0, 1)]

    def far_c(k):
        return remote(acc.at[(z + k + 1) % 4, :, :, :, lanes_c], from_zc.at[k], (zc_s, zc_r), k, zp[k])

    def first_c(part):
        src = acc.at[z, 1 - x, :, :, cut_c[0]] if part == 0 else acc.at[z, :, 1 - y, :, cut_c[1]]
        return remote(src, from_fc.at[part, :, :, pl.ds(0, width_c[part])], (fc_s, fc_r), part,
                      xp if part == 0 else yp)

    def second_c(part):
        src = acc.at[z, x, 1 - y, :, cut_c[0]] if part == 0 else acc.at[z, 1 - x, y, :, cut_c[1]]
        return remote(src, from_sc.at[part, :, pl.ds(0, width_c[part])], (sc_s, sc_r), part,
                      yp if part == 0 else xp)

    def add_core_c():
        own(count).wait()
        core(count).wait_recv()
        for k in (0, 2, 1, 3):
            zi = (z + k + 1) % 4
            for xi in (0, 1):
                for yi in (0, 1):
                    acc[zi, xi, yi, :, lanes_c] = (
                        acc[zi, xi, yi, :, lanes_c] + from_core[zi, xi, yi, :, lanes_c])
            if k < 3:
                go(far_c(k))

    def add_far_c():
        for k in (0, 2, 1):
            far_c(k).wait_recv()
        for xi in (0, 1):
            for yi in (0, 1):
                total = acc[z, xi, yi, :, lanes_c].astype(F32)
                for k in range(3):
                    total = total + from_zc[k, xi, yi].astype(F32)
                acc[z, xi, yi, :, lanes_c] = total.astype(LOW)
        for part in (0, 1):
            go(first_c(part))

    def add_first_c():
        for part in (0, 1):
            first_c(part).wait_recv()
            for o in (0, 1):
                xi, yi = (x, o) if part == 0 else (o, y)
                acc[z, xi, yi, :, cut_c[part]] = (
                    acc[z, xi, yi, :, cut_c[part]] + from_fc[part, o, :, pl.ds(0, width_c[part])])
            go(second_c(part))

    def end_c():
        for part in (0, 1):
            second_c(part).wait_recv()
            out[:, cut_c[part]] = (acc[z, x, y, :, cut_c[part]].astype(F32)
                                   + from_sc[part, :, pl.ds(0, width_c[part])].astype(F32))

    def memory_core():
        mem_own.wait()
        mem_core.wait_recv()
        for theirs in (True, False):
            side = (1 - y) if theirs else y

            def body(i, carry, side=side):
                rows = pl.ds(pl.multiple_of(i * 64, 64), 64)
                macc[side, rows] = macc[side, rows] + mfrom_core[side, rows]
                return carry
            lax.fori_loop(0, 8, body, 0)
            if theirs:
                go(mem_far)

    def memory_end():
        mem_far.wait_recv()

        def body(i, carry):
            rows = pl.ds(pl.multiple_of(i * 64, 64), 64)
            mem_out[rows] = macc[y, rows].astype(jnp.float32) + mfrom_y[rows].astype(jnp.float32)
            return carry
        lax.fori_loop(0, 8, body, 0)

    def weight_rows(i, part):
        devs = pl.ds(part * 16, 16)
        return w[devs, :, pl.ds(SLAB * i, SLAB)].reshape(256, SLAB)

    def put(i, n, value):
        gs[:, :, :, :, :, pl.ds(NORM + SLAB * i + 256 * n, 256)] = value.astype(LOW).reshape(4, 2, 2, 2, ROWS, 256)

    rows_all = tgt.shape[0]

    def norm_back(i):
        r = block(i, 64)
        u, xh = dpre[r], xh1[r]
        ng[0:1] += jnp.sum(u * xh, axis=0, keepdims=True)
        ng[1:2] += jnp.sum(u, axis=0, keepdims=True)
        d = back_norm(u, gb[0:1], xh, rs1[r][:, :1])
        dpre[r] = d
        g_b[r] = d.astype(LOW)

    def self_norm():
        for copy in copies:
            copy.wait()
        each(rows_all // 64, norm_back)

    def self_out():
        out_back(g_b, lambda n: weight_rows(3, n), num_s, tot_s, dnx)
        for n in (0, 1):
            put(3, n, tmm(o_b[...], g_b[:, pl.ds(256 * n, 256)]))
        for ref in (dq, dk, dv):
            zero(ref)

    def self_tiles(i, first, last):
        def inner(kt, carry):
            r = pl.ds(i * RT, RT)
            key = kt * TILE + lane_iota((RT, TILE))
            row = i * RT + row_iota((RT, TILE))
            bias = jnp.where((key >= low_s[r]) & (key <= row), 0.0, HIDE)
            tile_backward(r, block(kt), bias, qs, ks, vs, dnx, dq, dk, dv)
            return carry
        lax.fori_loop(first, last, inner, 0)

    def self_grads():
        def lower(i):
            r = block(i, 64)
            qs[r] = (dq[r] * 0.125).astype(LOW)
            ks[r] = dk[r].astype(LOW)
            vs[r] = dv[r].astype(LOW)
        each(rows_all // 64, lower)
        for i, src in ((0, qs), (1, ks), (2, vs)):
            for n in (0, 1):
                put(i, n, tmm(tgt[...], src[:, pl.ds(256 * n, 256)]))
        inside = lane_iota((8, TILE)) < ROWS
        for d in range(DEV):
            one = ng[:, pl.ds(TILE * (d // 8), TILE)]
            one = pltpu.roll(one, (TILE - ROWS * (d % 8)) % TILE, 1) if d % 8 else one
            one = jnp.concatenate([jnp.where(inside, one, 0.0), jnp.zeros((8, TILE), F32)], axis=0)
            gs[d // 8, d // 4 % 2, d // 2 % 2, d % 2, :, pl.ds(0, NORM)] = one.astype(LOW)
        for r in SELF_ROUNDS:
            go(core(r))

    def self_target():
        for n in (0, 1):
            total = mmt(qs[...], weight_rows(0, n)) + mmt(ks[...], weight_rows(1, n))
            cols = pl.ds(256 * n, 256)
            target_grad[:, cols] = dpre[:, cols] + total + mmt(vs[...], weight_rows(2, n))

    add_core(0)
    memory_core()
    add_core_c()
    add_core(1)
    self_norm()
    add_first(0)
    add_core(2)
    self_out()
    add_second(0)
    add_first(1)
    add_core(3)
    self_tiles(0, 0, 2)
    add_second(1)
    add_first(2)
    self_tiles(1, 0, 4)
    add_z(0)
    add_second(2)
    add_first(3)
    add_far_c()
    self_grads()
    add_core(4)
    add_core(5)
    self_target()
    to_target = pltpu.make_async_copy(target_grad, target_ref, out_sems.at[0])
    to_target.start()
    add_first_c()
    memory_end()
    to_memory = pltpu.make_async_copy(mem_out, mem_ref, out_sems.at[1])
    to_memory.start()
    add_z(1)
    add_second(3)
    add_first(4)
    add_first(5)
    add_z(2)
    add_second(4)
    add_z(3)
    end_c()
    add_second(5)
    add_z(4)
    add_z(5)
    to_rows = pltpu.make_async_copy(out, out_ref, out_sems.at[2])
    to_rows.start()
    for copy in (to_target, to_memory, to_rows):
        copy.wait()
    for copy in sent:
        copy.wait_send()


def scatter_all(grads, mem_grads, gathered, target, state):
    any_space = pl.BlockSpec(memory_space=pl.ANY)
    dma = pltpu.SemaphoreType.DMA
    n = len(SCATTER_ROUNDS)
    rows = mem_grads.shape[2]
    wide = Z_FIRST[2] - Z_FIRST[0]
    low = lambda *s: pltpu.VMEM(s, LOW)
    f32 = lambda *s: pltpu.VMEM(s, F32)
    return pl.pallas_call(
        scatter_kernel,
        out_shape=(
            jax.ShapeDtypeStruct((ROWS, LANES), F32),
            jax.ShapeDtypeStruct((rows, SLAB), F32),
            jax.ShapeDtypeStruct((rows, SLAB), F32),
        ),
        in_specs=[any_space] * 16,
        out_specs=(any_space,) * 3,
        scratch_shapes=[
            low(4, 2, 2, ROWS, LANES),
            low(4, 2, 2, ROWS, LANES),
            low(4, 2, ROWS, LANES),
            low(4, ROWS, LANES),
            low(3, ROWS, LANES),
            low(2, rows, SLAB),
            low(2, rows, SLAB),
            low(rows, SLAB),
        ]
        + [pltpu.VMEM(s.shape, s.dtype) for s in state_shapes(rows)]
        + [
            low(32, ROWS, 4 * SLAB),
            low(rows, SLAB),
            low(4, 2, 2, 2, ROWS, SELF_LANES),
            f32(rows, SLAB),
            f32(rows, SLAB),
            f32(rows, SLAB),
            low(rows, 2 * SLAB),
            low(rows, SLAB),
            f32(ROWS, LANES),
            f32(rows, SLAB),
            f32(rows, SLAB),
            low(3, 2, 2, ROWS, wide),
            low(2, 2, ROWS, wide),
            low(2, ROWS, wide),
            dma((3,)),
            dma((n + 1,)),
            dma(()),
            dma((14,)),
            dma((n + 1,)),
            dma((n + 1,)),
            dma((n, 2)),
            dma((n, 2)),
            dma((n, 2)),
            dma((n, 2)),
            dma((n, 3)),
            dma((n, 3)),
            dma((2,)),
            dma((2,)),
            dma((3,)),
            dma((3,)),
            dma((2,)),
            dma((2,)),
            dma((2,)),
            dma((2,)),
        ],
        compiler_params=pltpu.CompilerParams(
            collective_id=2, has_side_effects=True, vmem_limit_bytes=56 << 20),
        name="scatter",
    )(grads, mem_grads, gathered, target, *state)


def finish_kernel(rows_ref, mem_ref, target_ref, *rest):
    outs, (rows, mem, target, in_sems, out_sems) = rest[:18], rest[18:]
    copies = []
    loads = []
    half = target.shape[0] // 2
    pieces = [pl.ds(0, half), pl.ds(half, half)]
    cuts_ = [(NORM + SLAB * i, SLAB) for i in range(8)] + [(NORM + SLAB * 8, 4 * SLAB)]
    cuts_ += [(NORM + SLAB * (12 + k), SLAB) for k in range(4)]

    def load(src, dst):
        copy = pltpu.make_async_copy(src, dst, in_sems.at[len(loads)])
        copy.start()
        loads.append(copy)

    def bring(src, dst):
        copy = pltpu.make_async_copy(src, dst, out_sems.at[len(copies)])
        copy.start()
        copies.append(copy)

    for p in pieces:
        load(target_ref.at[p], target.at[p])
        load(mem_ref.at[p], mem.at[p])
    load(rows_ref, rows)
    for i, p in enumerate(pieces):
        loads[2 * i].wait()
        bring(target.at[p], outs[0].at[p])
        loads[2 * i + 1].wait()
        bring(mem.at[p], outs[1].at[p])
    loads[4].wait()
    for i, (start, width) in enumerate(cuts_):
        dst = outs[2 + i] if i < 9 else outs[11].at[pl.ds(ROWS * (i - 9), ROWS)]
        bring(rows.at[:, pl.ds(start, width)], dst)
    for i in range(6):
        outs[12 + i][...] = rows[i, pl.ds(0, ROWS)]
    for copy in copies:
        copy.wait()


def finish(rows, mem, target):
    any_space = pl.BlockSpec(memory_space=pl.ANY)
    shape = lambda *s: jax.ShapeDtypeStruct(s, F32)
    return pl.pallas_call(
        finish_kernel,
        out_shape=(shape(*target.shape), shape(*mem.shape))
        + (shape(ROWS, SLAB),) * 8
        + (shape(ROWS, 4 * SLAB), shape(4 * ROWS, SLAB))
        + (shape(ROWS),) * 6,
        in_specs=[any_space] * 3,
        out_specs=(any_space,) * 12 + (pl.BlockSpec(memory_space=pltpu.VMEM),) * 6,
        scratch_shapes=[
            pltpu.VMEM(rows.shape, F32),
            pltpu.VMEM(mem.shape, F32),
            pltpu.VMEM(target.shape, F32),
            pltpu.SemaphoreType.DMA((5,)),
            pltpu.SemaphoreType.DMA((17,)),
        ],
        name="finish",
    )(rows, mem, target)


def local(target_in, memory, out_grad, *rest):
    fast = two_by_two((lax.axis_size("dp"), lax.axis_size("mem")))
    if not fast:
        return plain(target_in, memory, out_grad, *rest)
    weights, tables = rest[:16], rest[16:]
    gathered, all_memory, saved = gather_all(
        weights[:10], weights[10:], memory, tables[0], target_in
    )
    after, after_low, xh1, rs1, num, tot, q, k, v, o, gains, low_s = saved
    layer_out, grads, mem_grads, d_after, norm_grads = compute(
        *tables, out_grad, all_memory, gathered, after, after_low, gains
    )
    state = (d_after, xh1, rs1, num, tot, q, k, v, o, gains, norm_grads, low_s)
    rows = target_in.shape[0]
    out, mem_out, target_grad = scatter_all(
        grads.reshape(4, 2, 2, 2, ROWS, LANES),
        mem_grads.reshape(2, 2, rows, SLAB),
        gathered,
        target_in,
        state,
    )
    return (layer_out,) + tuple(finish(out, mem_out, target_grad))


def solution(mesh):
    both = P(("dp", "mem"), None)
    flat = P(("dp", "mem"))
    in_specs = (both,) * 13 + (flat,) * 6 + (P("dp", None),) * 3
    out_specs = (both,) * 13 + (flat,) * 6
    return jax.shard_map(local, mesh=mesh, in_specs=in_specs, out_specs=out_specs, check_vma=False)
```

```python
import functools

import jax
import jax.numpy as jnp
from jax import lax
from jax.experimental import pallas as pl
from jax.experimental.pallas import tpu as pltpu
from jax.sharding import PartitionSpec as P

MESH = pl.DeviceIdType.MESH
SLAB = 512
NORM = 128
LANES = NORM + 16 * SLAB
ROWS = 16


def here():
    dp, mem = lax.axis_index("dp"), lax.axis_index("mem")
    return dp // 2, dp % 2, mem // 2, mem % 2


def device(z, x, y, c):
    return (z * 2 + x, y * 2 + c)


def greet(peers):
    barrier = pltpu.get_barrier_semaphore()
    for peer in peers:
        pl.semaphore_signal(barrier, inc=1, device_id=peer, device_id_type=MESH)
    pl.semaphore_wait(barrier, len(peers))


def remote(src, dst, sems, index, peer):
    send, recv = sems
    return pltpu.make_async_remote_copy(
        src_ref=src,
        dst_ref=dst,
        send_sem=send.at[index],
        recv_sem=recv.at[index],
        device_id=peer,
        device_id_type=MESH,
    )


def cuts(widths, share):
    spans, at = [], 0
    for tiles in widths:
        n = tiles * 128
        spans.append((at, at + max(1, round(tiles * share)) * 128, at + n))
        at += n
    return tuple(spans)


GATHER_ROUNDS = cuts((17, 36), 0.22)
Z_LAST = (53 * 128, 59 * 128, 65 * 128)


def gather_kernel(*refs):
    shards, memory_ref, lens_ref, target = refs[:10], *refs[10:13]
    params, refs = refs[13:19], refs[19:]
    out, mem_out = refs[:2]
    state_out, refs = refs[2:14], refs[14:]
    local_sem, mem_local = refs[:2]
    z_sems, first_sems, second_sems = refs[2:4], refs[4:6], refs[6:8]
    across, mems = refs[8:10], refs[10:12]
    stage, mem_stage = refs[12:14]
    state, refs = refs[14:26], refs[26:]
    after, a_b, xh1, rs1, num, tot, qs, ks, vs, o_b, gb, low_s = state
    w, norms, tgt, starts, state_sems, rows, refs = *refs[:6], refs[6:]
    cf_sems, cs_sems, cz_sems, co_sems = refs[:2], refs[2:4], refs[4:6], refs[6:8]
    z, x, y, c = here()
    xp, yp, cp_ = device(z, 1 - x, y, c), device(z, x, 1 - y, c), device(z, x, y, 1 - c)
    own = out.at[z, x, y, c]
    rounds = range(len(GATHER_ROUNDS))

    local = []

    def bring(src, start, width):
        local.append(
            pltpu.make_async_copy(src, stage.at[:, pl.ds(start, width)], local_sem.at[len(local)])
        )

    for i in range(8):
        bring(shards[i], NORM + SLAB * i, SLAB)
    bring(shards[8], NORM + SLAB * 8, 4 * SLAB)
    for k in range(4):
        bring(shards[9].at[pl.ds(ROWS * k, ROWS)], NORM + SLAB * (12 + k), SLAB)
    for one in local:
        one.start()
    keep = pltpu.make_async_copy(memory_ref, mem_stage, mem_local.at[0])
    keep.start()
    zn = [device((z + k) % 4, x, y, c) for k in (1, 3)]
    rows[...] = jnp.zeros_like(rows)
    for i, one in enumerate(params):
        rows[i : i + 1, :ROWS] = one[...].astype(F32)
    stage[:, :NORM] = rows[...].astype(LOW)
    greet([xp, yp, cp_] + zn)
    for one in local:
        one.wait()
    own_out = pltpu.make_async_copy(stage, own, mem_local.at[1])
    own_out.start()

    def column(slot):
        return z if slot == 0 else (z - slot if slot < 4 else z + (slot - 3))

    def there(slot):
        return None if slot == 0 else (z >= slot if slot < 4 else z <= 6 - slot)

    def both(a, b):
        return b if a is None else (a if b is None else jnp.logical_and(a, b))

    def guarded(cond, body):
        if cond is None:
            body()
        else:
            pl.when(cond)(body)

    sent = []

    def go(make, cond=None):
        guarded(cond, lambda: make().start())
        sent.append((cond, make))

    def along(slot, r, up):
        a, _, b = GATHER_ROUNDS[r]
        ref = out.at[column(slot), x, y, c, :, pl.ds(a, b - a)]
        src = stage.at[:, pl.ds(a, b - a)] if slot == 0 else ref
        d = 0 if slot == 0 else (slot if slot < 4 else slot - 3)
        peer = device((z + (1 if up else 3)) % 4, x, y, c)
        return remote(src, ref, z_sems, (0 if up else 1, d, r), peer)

    def arrived(slot, r):
        a, _, b = GATHER_ROUNDS[r]
        ref = out.at[column(slot), x, y, c, :, pl.ds(a, b - a)]
        up = slot < 4
        index = (0 if up else 1, (slot if up else slot - 3) - 1, r)
        return remote(ref, ref, z_sems, index, xp)

    def first(slot, r, part, arriving=False):
        a, m, b = GATHER_ROUNDS[r]
        zz = column(slot)
        if part == 0:
            ref = out.at[zz, (1 - x) if arriving else x, y, c, :, pl.ds(a, m - a)]
        else:
            ref = out.at[zz, x, (1 - y) if arriving else y, c, :, pl.ds(m, b - m)]
        lanes = pl.ds(a, m - a) if part == 0 else pl.ds(m, b - m)
        src = stage.at[:, lanes] if slot == 0 and not arriving else ref
        return remote(src, ref, first_sems, (slot, part, r), xp if part == 0 else yp)

    def second(slot, r, part, hop, arriving=False):
        a, m, b = GATHER_ROUNDS[r]
        zz = column(slot)
        if part == 0:
            side = (1 - x) if hop else x
            ref = out.at[zz, side, (1 - y) if arriving else y, c, :, pl.ds(a, m - a)]
        else:
            side = (1 - y) if hop else y
            ref = out.at[zz, (1 - x) if arriving else x, side, c, :, pl.ds(m, b - m)]
        lanes = pl.ds(a, m - a) if part == 0 else pl.ds(m, b - m)
        src = stage.at[:, lanes] if slot == 0 and not (arriving or hop) else ref
        return remote(src, ref, second_sems, (slot, part, hop, r), yp if part == 0 else xp)

    def over(slot, r, arriving=False):
        a, _, b = GATHER_ROUNDS[r]
        ref = out.at[column(slot), :, :, (1 - c) if arriving else c, :, pl.ds(a, b - a)]
        return remote(ref, ref, across, (slot, r), cp_)

    def spread(slot, r):
        cond = there(slot)
        for part in (1, 0):
            go(functools.partial(first, slot, r, part), cond)
        for part in (1, 0):
            go(functools.partial(second, slot, r, part, 0), cond)

    def from_z(d, r):
            for slot in (d, d + 3):
                cond = there(slot)
                guarded(cond, lambda slot=slot, r=r: arrived(slot, r).wait_recv())
                if d < 3:
                    onward = z < 3 if slot < 4 else z > 0
                    go(functools.partial(along, slot, r, slot < 4), both(cond, onward))
                spread(slot, r)

    def pass_on(slots, r):
            for slot in slots:
                cond = there(slot)
                for part in (1, 0):
                    guarded(cond, lambda s=slot, r=r, p=part: first(s, r, p, True).wait_recv())
                    go(functools.partial(second, slot, r, part, 1), cond)

    def hand_over(slots, r):
            for slot in slots:
                cond = there(slot)
                for part in (0, 1):
                    for hop in (0, 1):
                        guarded(cond, lambda s=slot, r=r, p=part, h=hop: second(s, r, p, h, True).wait_recv())
                go(functools.partial(over, slot, r), cond)

    cut_c = [pl.ds(Z_LAST[p], Z_LAST[p + 1] - Z_LAST[p]) for p in (0, 1)]
    lanes_c = pl.ds(Z_LAST[0], Z_LAST[2] - Z_LAST[0])

    def first_c(part, arriving=False):
        if part == 0:
            ref = out.at[z, (1 - x) if arriving else x, y, c, :, cut_c[0]]
        else:
            ref = out.at[z, x, (1 - y) if arriving else y, c, :, cut_c[1]]
        src = ref if arriving else stage.at[:, cut_c[part]]
        return remote(src, ref, cf_sems, part, xp if part == 0 else yp)

    def second_c(part, hop, arriving=False):
        if part == 0:
            ref = out.at[z, (1 - x) if hop else x, (1 - y) if arriving else y, c, :, cut_c[0]]
        else:
            ref = out.at[z, (1 - x) if arriving else x, (1 - y) if hop else y, c, :, cut_c[1]]
        src = ref if arriving or hop else stage.at[:, cut_c[part]]
        return remote(src, ref, cs_sems, (part, hop), yp if part == 0 else xp)

    def along_c(slot, up):
        ref = out.at[column(slot), :, :, c, :, lanes_c]
        d = 0 if slot == 0 else (slot if slot < 4 else slot - 3)
        peer = device((z + (1 if up else 3)) % 4, x, y, c)
        return remote(ref, ref, cz_sems, (0 if up else 1, d), peer)

    def arrived_c(slot):
        ref = out.at[column(slot), :, :, c, :, lanes_c]
        up = slot < 4
        return remote(ref, ref, cz_sems, (0 if up else 1, (slot if up else slot - 3) - 1), xp)

    def over_c(slot, arriving=False):
        ref = out.at[column(slot), :, :, (1 - c) if arriving else c, :, lanes_c]
        return remote(ref, ref, co_sems, slot, cp_)

    def pass_on_c():
        for part in (0, 1):
            first_c(part, True).wait_recv()
            go(functools.partial(second_c, part, 1))

    def plane_c():
        own_out.wait()
        for part in (0, 1):
            for hop in (0, 1):
                second_c(part, hop, True).wait_recv()
        go(functools.partial(along_c, 0, True), z < 3)
        go(functools.partial(along_c, 0, False), z > 0)
        go(functools.partial(over_c, 0))

    def from_z_c(d):
        for slot in (d, d + 3):
            cond = there(slot)
            guarded(cond, lambda slot=slot: arrived_c(slot).wait_recv())
            if d < 3:
                onward = z < 3 if slot < 4 else z > 0
                go(functools.partial(along_c, slot, slot < 4), both(cond, onward))
            go(functools.partial(over_c, slot), cond)

    for r in rounds:
        go(functools.partial(along, 0, r, True), z < 3)
        go(functools.partial(along, 0, r, False), z > 0)
        spread(0, r)
        if r == 0:
            for part in (0, 1):
                go(functools.partial(first_c, part))
            for part in (0, 1):
                go(functools.partial(second_c, part, 0))
    mem_own = mem_out.at[y, c]

    def memory_rows():
        keep.wait()
        kept = pltpu.make_async_copy(mem_stage, mem_own, mem_local.at[2])
        kept.start()
        go(lambda: remote(mem_stage, mem_own, mems, 0, yp))
        go(lambda: remote(mem_stage, mem_own, mems, 1, cp_))
        return kept

    def memory_far():
        far = mem_out.at[1 - y, c]
        remote(far, far, mems, 0, yp).wait_recv()
        go(lambda: remote(far, far, mems, 2, cp_))

    everyone = (0, 1, 4, 2, 5, 3, 6)

    def all_over(r):
        for slot in everyone:
            guarded(there(slot), lambda s=slot: over(s, r, True).wait_recv())

    rows_all = tgt.shape[0]
    n_sent = starts.shape[0]
    loads = [pltpu.make_async_copy(target, tgt, state_sems.at[12])]
    loads.append(pltpu.make_async_copy(out.at[:, :, :, :, :, pl.ds(NORM, 4 * SLAB)], w, state_sems.at[13]))
    loads.append(pltpu.make_async_copy(out.at[:, :, :, :, :, pl.ds(0, NORM)], norms, state_sems.at[14]))
    saves = [pltpu.make_async_copy(src, dst, state_sems.at[i]) for i, (src, dst) in enumerate(zip(state, state_out))]

    def weight(i, n):
        return w[:, :, :, :, :, pl.ds(SLAB * i + 256 * n, 256)].reshape(SLAB, 256)

    def prepare():
        base = lax.axis_index("mem") * n_sent

        def count(j, at):
            starts[j] = at
            return at + lens_ref[0, base + j]
        lax.fori_loop(0, n_sent, count, jnp.int32(0))
        for i in range(rows_all // TILE):
            row = i * TILE + row_iota((TILE, TILE))
            found = jnp.zeros((TILE, TILE), jnp.int32)
            for j in range(n_sent):
                found = jnp.where(row >= starts[j], starts[j], found)
            low_s[pl.ds(i * TILE, TILE)] = found
        zero(num)
        zero(tot)

    def project():
        for one in loads:
            one.wait()
        for j in range(SLAB // TILE):
            total = jnp.zeros((8, TILE), F32)
            for k in range(8):
                d = 8 * j + k
                one = norms[d // 8, d // 4 % 2, d // 2 % 2, d % 2].astype(F32)[:8]
                total = total + (pltpu.roll(one, ROWS * k, 1) if k else one)
            gb[:, pl.ds(TILE * j, TILE)] = total
        for i, dst in ((0, qs), (1, ks), (2, vs)):
            for n in (0, 1):
                value = mm(tgt[...], weight(i, n)).astype(LOW)
                dst[:, pl.ds(256 * n, 256)] = value * jnp.asarray(0.125, LOW) if i == 0 else value

    def self_tiles(i, first_tile, last_tile):
        def inner(kt, carry):
            r = pl.ds(i * RT, RT)
            key = kt * TILE + lane_iota((RT, TILE))
            row = i * RT + row_iota((RT, TILE))
            bias = jnp.where((key >= low_s[r]) & (key <= row), 0.0, HIDE)
            tile_forward(r, block(kt), bias, qs, ks, vs, num, tot)
            return carry
        lax.fori_loop(first_tile, last_tile, inner, 0)

    def project_out():
        divide(num, tot, o_b, rows_all)
        for n in (0, 1):
            cols = pl.ds(256 * n, 256)
            after[:, cols] = tgt[:, cols].astype(F32) + mm(o_b[...], weight(3, n))

    def norm_rows(i):
        r = block(i, 64)
        xh, rs = normalize(after[r])
        xh1[r] = xh
        rs1[r] = jnp.broadcast_to(rs, (64, TILE))
        value = xh * gb[0:1] + gb[1:2]
        after[r] = value
        a_b[r] = value.astype(LOW)

    loads[0].start()
    prepare()
    from_z(1, 0)
    pass_on_c()
    from_z(1, 1)
    pass_on((0,), 0)
    plane_c()
    from_z(2, 0)
    pass_on((0,), 1)
    pass_on((1, 4), 0)
    from_z(3, 0)
    from_z(2, 1)
    pass_on((2, 5), 0)
    hand_over((0,), 0)
    from_z_c(1)
    pass_on((1, 4), 1)
    pass_on((3, 6), 0)
    kept = memory_rows()
    hand_over((1, 4), 0)
    hand_over((2, 5), 0)
    from_z(3, 1)
    from_z_c(2)
    hand_over((3, 6), 0)
    all_over(0)
    loads[1].start()
    loads[2].start()
    pass_on((2, 5), 1)
    from_z_c(3)
    project()
    hand_over((0,), 1)
    self_tiles(0, 0, 2)
    pass_on((3, 6), 1)
    self_tiles(1, 0, 4)
    hand_over((1, 4), 1)
    memory_far()
    project_out()
    each(rows_all // 64, norm_rows)
    hand_over((2, 5), 1)
    hand_over((3, 6), 1)
    for one in saves:
        one.start()
    all_over(1)
    for slot in everyone:
        guarded(there(slot), lambda s=slot: over_c(s, True).wait_recv())
    for one in saves:
        one.wait()
    for i, side in ((1, y), (2, 1 - y)):
        last = mem_out.at[side, 1 - c]
        remote(last, last, mems, i, cp_).wait_recv()
    kept.wait()
    for cond, make in sent:
        guarded(cond, lambda make=make: make().wait_send())


def gather_all(shards, params, memory, lens, target):
    any_space = pl.BlockSpec(memory_space=pl.ANY)
    dma = pltpu.SemaphoreType.DMA
    n = len(GATHER_ROUNDS)
    both = lambda *s: [dma(s), dma(s)]
    state = forward_shapes(target.shape[0])
    low = lambda *s: pltpu.VMEM(s, LOW)
    gathered, whole_memory, *saved = pl.pallas_call(
        gather_kernel,
        out_shape=(
            jax.ShapeDtypeStruct((4, 2, 2, 2, ROWS, LANES), jnp.bfloat16),
            jax.ShapeDtypeStruct((2, 2) + memory.shape, jnp.bfloat16),
        )
        + state,
        in_specs=[any_space] * 11
        + [pl.BlockSpec(memory_space=pltpu.SMEM), any_space]
        + [pl.BlockSpec(memory_space=pltpu.VMEM)] * 6,
        out_specs=(any_space,) * 14,
        scratch_shapes=[dma((14,)), dma((3,))]
        + both(2, 3, n) + both(7, 2, n) + both(7, 2, 2, n) + both(7, n) + both(3)
        + [low(ROWS, LANES), low(*memory.shape)]
        + [pltpu.VMEM(s.shape, s.dtype) for s in state]
        + [
            low(4, 2, 2, 2, ROWS, 4 * SLAB),
            low(4, 2, 2, 2, ROWS, NORM),
            low(*target.shape),
            pltpu.SMEM((16,), jnp.int32),
            dma((15,)),
            pltpu.VMEM((ROWS, NORM), F32),
        ]
        + both(2) + both(2, 2) + both(2, 3) + both(7),
        compiler_params=pltpu.CompilerParams(
            collective_id=1, has_side_effects=True, vmem_limit_bytes=60 << 20),
        name="gather",
    )(*shards, memory, lens, target, *[p[None, :] for p in params])
    return gathered.reshape(32, ROWS, LANES), whole_memory.reshape(-1, SLAB), saved


def forward_shapes(rows):
    full = lambda dtype, lanes=SLAB, n=rows: jax.ShapeDtypeStruct((n, lanes), dtype)
    return (
        full(F32),
        full(LOW),
        full(F32),
        full(F32, TILE),
        full(F32),
        full(F32),
        full(LOW),
        full(LOW),
        full(LOW),
        full(LOW),
        full(F32, SLAB, 8),
        full(jnp.int32, TILE),
    )


def two_by_two(mesh_axes):
    return mesh_axes == (8, 4)


def gather_any(shards, norms, memory):
    everyone = ("dp", "mem")
    packed = jnp.concatenate([norms] + list(shards[:9]), axis=1)
    rows = lax.all_gather(packed, everyone, axis=0, tiled=True).reshape(32, ROWS, -1)
    last = lax.all_gather(shards[9], everyone, axis=0, tiled=True)
    last = last.reshape(32, 4, ROWS, SLAB).transpose(0, 2, 1, 3).reshape(32, ROWS, 4 * SLAB)
    return (
        jnp.concatenate([rows, last], axis=2),
        lax.all_gather(memory, "mem", axis=0, tiled=True),
    )


def scatter_any(grads, mem_grads):
    everyone = ("dp", "mem")
    wide = grads.reshape(32, ROWS, LANES).astype(jnp.float32)
    cut = LANES - 4 * SLAB
    rows = lax.psum_scatter(
        wide[:, :, :cut].reshape(512, cut), everyone, scatter_dimension=0, tiled=True
    )
    last = wide[:, :, cut:].reshape(32, ROWS, 4, SLAB).transpose(0, 2, 1, 3).reshape(2048, SLAB)
    last = lax.psum_scatter(last, everyone, scatter_dimension=0, tiled=True)
    mem = lax.psum_scatter(
        mem_grads.astype(jnp.float32), "mem", scatter_dimension=0, tiled=True
    )
    return rows, last, mem
HEADS = 8
HEAD = 64
eps_norm = 1e-05
score_scale = 0.125


def layer_norm(values, gain, shift):
    centre = values - jnp.mean(values, axis=-1, keepdims=True)
    spread = jnp.mean(centre * centre, axis=-1, keepdims=True)
    return centre * lax.rsqrt(spread + eps_norm) * gain + shift


def head_split(values):
    return values.reshape(values.shape[0], HEADS, HEAD)


def matmul(left, right):
    return jnp.dot(left, right, preferred_element_type=jnp.float32)


def left_grad(inputs, grads):
    return jnp.einsum("ra,rb->ab", inputs, grads, preferred_element_type=jnp.float32)


def back_through(grads, weight):
    return jnp.einsum("rb,ab->ra", grads, weight, preferred_element_type=jnp.float32)


def exp_scores(q_block, keys, low_edge, high_edge):
    raw = jnp.einsum("qhd,khd->hqk", head_split(q_block), head_split(keys),
                     preferred_element_type=jnp.float32) * score_scale
    position = lax.broadcasted_iota(jnp.int32, (q_block.shape[0], keys.shape[0]), 1)
    allowed = (position >= low_edge[:, None]) & (position < high_edge[:, None])
    return jnp.where(allowed[None], jnp.exp(raw), 0.0)


def attend(queries, keys, values, low_edge, high_edge):
    expo = exp_scores(queries, keys, low_edge, high_edge)
    numer = jnp.einsum("hqk,khd->qhd", expo.astype(jnp.bfloat16), head_split(values),
                       preferred_element_type=jnp.float32)
    totals = jnp.sum(expo, axis=2).T
    return (numer / totals[:, :, None]).reshape(queries.shape[0], -1), totals


def attend_back(queries, keys, values, low_edge, high_edge, upstream, output, totals):
    expo = exp_scores(queries, keys, low_edge, high_edge)
    up = head_split(upstream.astype(jnp.float32))
    numer_grad = (up / totals[:, :, None]).astype(jnp.bfloat16)
    corr = -jnp.sum(up * head_split(output), axis=2) / totals
    flow = jnp.einsum("qhd,khd->hqk", numer_grad, head_split(values),
                      preferred_element_type=jnp.float32) + corr.T[:, :, None]
    ds = (expo * flow).astype(jnp.bfloat16)
    dq = jnp.einsum("hqk,khd->qhd", ds, head_split(keys), preferred_element_type=jnp.float32)
    dk = jnp.einsum("hqk,qhd->khd", ds, head_split(queries), preferred_element_type=jnp.float32)
    dv = jnp.einsum("hqk,qhd->khd", expo.astype(jnp.bfloat16), numer_grad,
                    preferred_element_type=jnp.float32)
    flat = lambda v: v.reshape(v.shape[0], -1)
    return ((flat(dq) * score_scale).astype(jnp.bfloat16), (flat(dk) * score_scale).astype(jnp.bfloat16),
            flat(dv).astype(jnp.bfloat16))


def plain(target_in, memory, out_grad, *rest):
    weights, (tgt_lens, src_lens, src_offsets) = rest[:16], rest[16:]
    member = lax.axis_index("mem")
    per_device = tgt_lens.shape[1] // lax.axis_size("mem")
    pick = lambda table: lax.dynamic_slice_in_dim(table[0], member * per_device, per_device, 0)
    lengths, spans, offsets = pick(tgt_lens), pick(src_lens), pick(src_offsets)
    norms = jnp.stack(weights[10:], axis=1)
    norms = jnp.pad(norms, ((0, 0), (0, NORM - norms.shape[1])))
    gathered, all_memory = gather_any(weights[:10], norms, memory)
    W = gathered.reshape(512, LANES)
    mat = lambda i: W[:, NORM + SLAB * i : NORM + SLAB * (i + 1)]
    wsq, wsk, wsv, wso, wcq, wck, wcv, wco = [mat(i) for i in range(8)]
    w1 = W[:, NORM + 8 * SLAB : NORM + 12 * SLAB]
    w2 = gathered[:, :, NORM + 12 * SLAB :].reshape(32, 16, 4, SLAB).transpose(0, 2, 1, 3).reshape(2048, SLAB)
    ga, sa, gc, sc, gf, sf = [W[:, i].astype(jnp.float32) for i in range(6)]
    rows = target_in.shape[0]
    starts = jnp.cumsum(lengths) - lengths
    position = lax.iota(jnp.int32, rows)
    sentence = jnp.sum((position[:, None] >= starts[None, :]).astype(jnp.int32), axis=1) - 1
    picker = sentence[:, None] == lax.iota(jnp.int32, per_device)[None, :]
    choose = lambda v: jnp.sum(jnp.where(picker, v[None, :], 0), axis=1)
    self_low, self_high = choose(starts), position + 1
    cross_low = choose(offsets)
    cross_high = cross_low + choose(spans)
    low = jnp.bfloat16
    q, k, v = [matmul(target_in, w).astype(low) for w in (wsq, wsk, wsv)]
    o_self_f, tot_self = attend(q, k, v, self_low, self_high)
    o_self = o_self_f.astype(low)
    after_self, pull_self = jax.vjp(layer_norm, target_in.astype(jnp.float32) + matmul(o_self, wso), ga, sa)
    a_b = after_self.astype(low)
    qc = matmul(a_b, wcq).astype(low)
    kc, vc = matmul(all_memory, wck).astype(low), matmul(all_memory, wcv).astype(low)
    cut = lambda v: v.reshape((4, -1) + v.shape[1:])
    o_c_f, tot_c = lax.map(
        lambda p: attend(p[0], kc, vc, p[1], p[2]), (cut(qc), cut(cross_low), cut(cross_high))
    )
    o_c_f, tot_c = o_c_f.reshape(rows, -1), tot_c.reshape(rows, -1)
    o_c = o_c_f.astype(low)
    after_cross, pull_cross = jax.vjp(layer_norm, after_self + matmul(o_c, wco), gc, sc)
    c_b = after_cross.astype(low)
    hidden = matmul(c_b, w1)
    activated, pull_silu = jax.vjp(jax.nn.silu, hidden)
    act = activated.astype(low)
    final, pull_ffn = jax.vjp(layer_norm, after_cross + matmul(act, w2), gf, sf)
    d_pre_out, g_gf, g_sf = pull_ffn(out_grad.astype(jnp.float32))
    d_branch = d_pre_out.astype(low)
    g_w2 = left_grad(act, d_branch)
    d_hidden = pull_silu(back_through(d_branch, w2))[0].astype(low)
    g_w1 = left_grad(c_b, d_hidden)
    d_pre_cross, g_gc, g_sc = pull_cross(d_pre_out + back_through(d_hidden, w1))
    d_cb = d_pre_cross.astype(low)
    g_wco = left_grad(o_c, d_cb)
    d_oc = back_through(d_cb, wco).astype(low)

    def piece(carry, p):
        dq, dk, dv = attend_back(p[0], kc, vc, p[1], p[2], p[3], p[4], p[5])
        return (carry[0] + dk, carry[1] + dv), dq

    empty = jnp.zeros(kc.shape, jnp.bfloat16)
    (dk_c, dv_c), dq_c = lax.scan(
        piece,
        (empty, empty),
        tuple(cut(v) for v in (qc, cross_low, cross_high, d_oc, o_c_f, tot_c)),
    )
    dq_c = dq_c.reshape(rows, -1)
    g_wcq, g_wck, g_wcv = left_grad(a_b, dq_c), left_grad(all_memory, dk_c), left_grad(all_memory, dv_c)
    mem_grad = back_through(dk_c, wck) + back_through(dv_c, wcv)
    d_pre_self, g_ga, g_sa = pull_self(d_pre_cross + back_through(dq_c, wcq))
    d_sb = d_pre_self.astype(low)
    g_wso = left_grad(o_self, d_sb)
    d_os = back_through(d_sb, wso).astype(low)
    dq, dk, dv = attend_back(q, k, v, self_low, self_high, d_os, o_self_f, tot_self)
    g_wsq, g_wsk, g_wsv = left_grad(target_in, dq), left_grad(target_in, dk), left_grad(target_in, dv)
    target_grad = d_pre_self + back_through(dq, wsq) + back_through(dk, wsk) + back_through(dv, wsv)
    n_g = jnp.pad(jnp.stack([g_ga, g_sa, g_gc, g_sc, g_gf, g_sf], axis=1), ((0, 0), (0, NORM - 6)))
    g_w2p = g_w2.reshape(32, 4, 16, SLAB).transpose(0, 2, 1, 3).reshape(512, 4 * SLAB)
    grads = jnp.concatenate([g.astype(low) for g in (n_g, g_wsq, g_wsk, g_wsv, g_wso, g_wcq, g_wck, g_wcv, g_wco, g_w1, g_w2p)], axis=1)
    part = lambda i, n=1: out[:, NORM + SLAB * i : NORM + SLAB * (i + n)]
    out, w2_grad, mem_out = scatter_any(grads, mem_grad.astype(low))
    return (final.astype(low), target_grad, mem_out) + tuple(part(i) for i in range(8)) + (part(8, 4), w2_grad) + tuple(out[:, i] for i in range(6))


TILE = 128
RT = 256
RC = 512
CHUNK = 256
EPS = 1e-05
HIDE = -1e30
LOW = jnp.bfloat16
F32 = jnp.float32
DEV = 32
CUT = NORM + 12 * SLAB


def mm(a, b):
    return jnp.dot(a, b, preferred_element_type=F32)


def mmt(a, b):
    return lax.dot_general(a, b, (((1,), (1,)), ((), ())), preferred_element_type=F32)


def tmm(a, b):
    return lax.dot_general(a, b, (((0,), (0,)), ((), ())), preferred_element_type=F32)


def lane_iota(shape):
    return lax.broadcasted_iota(jnp.int32, shape, len(shape) - 1)


def row_iota(shape):
    return lax.broadcasted_iota(jnp.int32, shape, 0)


def halves():
    lane = lane_iota((1, TILE))
    even = jnp.where(lane < 64, 1.0, 0.0).astype(LOW)
    odd = jnp.where(lane < 64, 0.0, 1.0).astype(LOW)
    return even, odd


def stacked(block, even, odd):
    return jnp.concatenate([block * even, block * odd], axis=0)


def fold(pair):
    lane = lane_iota((TILE, TILE))
    return jnp.where(lane < 64, pair[:TILE], pair[TILE:])


def totals_block(even, odd):
    wide = lambda v: jnp.broadcast_to(v, (TILE, TILE))
    return jnp.concatenate([wide(even), wide(odd)], axis=0)


def corr_block():
    lane = lane_iota((TILE, TILE))
    a = jnp.where(lane < 2, 1.0, 0.0).astype(LOW)
    b = jnp.where((lane >= 64) & (lane < 66), 1.0, 0.0).astype(LOW)
    return jnp.concatenate([a, b], axis=0)


def tile_forward(rows, keys, bias, q, k, v, num, tot):
    even, odd = halves()
    ones = totals_block(even, odd)
    bias2 = jnp.concatenate([bias, bias], axis=1)
    for h in range(4):
        cols = pl.ds(TILE * h, TILE)
        s = mmt(q[rows, cols], stacked(k[keys, cols], even, odd))
        e = jnp.exp(s + bias2).astype(LOW)
        both = mm(e, jnp.concatenate([stacked(v[keys, cols], even, odd), ones], axis=1))
        num[rows, cols] += both[:, :TILE]
        tot[rows, cols] += both[:, TILE:]


def tile_backward(rows, keys, bias, q, k, v, dnx, dq, dk, dv):
    even, odd = halves()
    ones = corr_block()
    bias2 = jnp.concatenate([bias, bias], axis=1)
    for h in range(4):
        cols = pl.ds(TILE * h, TILE)
        qb = q[rows, cols]
        ks = stacked(k[keys, cols], even, odd)
        e = jnp.exp(mmt(qb, ks) + bias2)
        vs = jnp.concatenate([stacked(v[keys, cols], even, odd), ones], axis=1)
        flow = mmt(dnx[rows, pl.ds(2 * TILE * h, 2 * TILE)], vs)
        ds = (e * flow).astype(LOW)
        dq[rows, cols] += mm(ds, ks)
        dk[keys, cols] += fold(tmm(ds, qb))
        dv[keys, cols] += fold(tmm(e.astype(LOW), dnx[rows, pl.ds(2 * TILE * h, TILE)]))


def each(count, body):
    def step(i, carry):
        body(i)
        return carry
    if isinstance(count, int) and count <= 2:
        for i in range(count):
            body(i)
        return
    lax.fori_loop(0, count, step, 0, unroll=8 if isinstance(count, int) else 1)


def zero(ref, step=128):
    def body(i):
        rows = pl.ds(pl.multiple_of(i * step, step), step)
        ref[rows] = jnp.zeros((step,) + ref.shape[1:], ref.dtype)
    each(ref.shape[0] // step, body)


def columns(part, width=256):
    return pl.ds(pl.multiple_of(part * width, width), width)


def block(i, width=TILE):
    return pl.ds(pl.multiple_of(i * width, width), width)


def back_norm(u, gain, xh, r):
    gu = u * gain
    a = jnp.mean(gu, axis=1, keepdims=True)
    b = jnp.mean(gu * xh, axis=1, keepdims=True)
    return (gu - a - xh * b) * r


def out_back(g_b, weight_rows, num, tot, dnx):
    lane = lane_iota((TILE, TILE))
    same = jnp.where((lane < 64) == (row_iota((TILE, TILE)) < 64), 1.0, 0.0).astype(LOW)

    def body(n):
        up = mmt(g_b[...], weight_rows(n)).astype(LOW).astype(F32)
        for h in range(2):
            cols = pl.ds(pl.multiple_of(n * 256 + h * TILE, TILE), TILE)
            wide = lambda k: pl.ds(pl.multiple_of(n * 512 + h * 256 + k * TILE, TILE), TILE)
            d = up[:, h * TILE:(h + 1) * TILE]
            t = tot[:, cols]
            dnx[:, wide(0)] = (d / t).astype(LOW)
            p = d * num[:, cols]
            p1 = p.astype(LOW)
            p2 = (p - p1.astype(F32)).astype(LOW)
            corr = -(mm(p1, same) + mm(p2, same)) / t
            c1 = corr.astype(LOW)
            c2 = (corr - c1.astype(F32)).astype(LOW)
            place = lane_iota(c1.shape) % 64
            nothing = jnp.zeros_like(c1)
            dnx[:, wide(1)] = jnp.where(place == 0, c1, jnp.where(place == 1, c2, nothing))
    each(2, body)


def divide(num, tot, out, rows_all):
    def body(i):
        r = block(i, 64)
        o = num[r] / tot[r]
        num[r] = o
        out[r] = o.astype(LOW)
    each(rows_all // 64, body)


def normalize(y):
    mean = jnp.mean(y, axis=1, keepdims=True)
    centre = y - mean
    r = lax.rsqrt(jnp.mean(centre * centre, axis=1, keepdims=True) + EPS)
    return centre * r, r


def compute_kernel(lens_ref, spans_ref, offs_ref, out_grad, memory, gathered, after_ref, low_ref, gains_ref,
                   layer_out, grads, mem_grads, dpre_out, ng_out, *scratch):
    (w, w2, og, mem, qc, kc, vc, big, act, dhid, dv, num_c, tot_c, xh2, t1, dpre, dq, rs2,
     oc_b, a_b, c_b, g_b, dnx, ng, gb, lout, low_c, high_c, memc, sel, idx,
     starts, packed, in_sem, w_sem, out_sem) = scratch
    n_src = mem.shape[0]
    rows_all = og.shape[0]
    n_sent = starts.shape[0] - 1
    member = lax.axis_index("mem")
    base = member * n_sent

    loads = {}

    def load(name, src, dst, sem):
        loads[name] = pltpu.make_async_copy(src, dst, sem)
        loads[name].start()

    def load_slab(i, count=1):
        lanes = pl.ds(NORM + SLAB * i, SLAB * count)
        load(i, gathered.at[:, :, lanes], w.at[:, :, lanes], w_sem.at[i])

    load("a", low_ref, a_b, in_sem.at[0])
    load_slab(4)
    load("mem", memory, mem, in_sem.at[1])
    load_slab(5)
    load_slab(6)

    def load_rest():
        load("t1", after_ref, t1, in_sem.at[3])
        load("gb", gains_ref, gb, in_sem.at[4])
        load_slab(7)
        load_slab(8, 4)
        for k in range(4):
            load(("w2", k), gathered.at[:, :, pl.ds(CUT + SLAB * k, SLAB)], w2.at[:, k], w_sem.at[13 + k])
        load("og", out_grad, og, in_sem.at[2])

    outs = []

    def send(src, dst):
        copy = pltpu.make_async_copy(src, dst, out_sem.at[len(outs)])
        copy.start()
        outs.append(copy)

    def weight(i, part=None, width=256):
        if part is None:
            return w[:, :, pl.ds(NORM + SLAB * i, SLAB)].reshape(SLAB, SLAB)
        start = pl.multiple_of(NORM + SLAB * i + part * width, TILE)
        return w[:, :, pl.ds(start, width)].reshape(SLAB, width)

    def weight_rows(i, part, width=256, lanes=SLAB):
        devs = pl.ds(pl.multiple_of(part * (width // ROWS), width // ROWS), width // ROWS)
        return w[devs, :, pl.ds(NORM + SLAB * i, lanes)].reshape(width, lanes)

    def put_weight(i, part, value, width=256):
        start = pl.multiple_of(NORM + SLAB * i + part * width, TILE)
        w[:, :, pl.ds(start, width)] = value.astype(LOW).reshape(DEV, ROWS, width)

    def count(j, at):
        starts[j] = at
        return at + lens_ref[0, base + j]
    starts[n_sent] = lax.fori_loop(0, n_sent, count, jnp.int32(0))

    def count_packed(j, at):
        packed[j] = at
        return at + spans_ref[0, base + j]
    n_keys = lax.fori_loop(0, n_sent, count_packed, jnp.int32(0))
    packed[n_sent] = n_keys
    chunks = (n_keys + CHUNK - 1) // CHUNK

    def lows(i):
        row = i * TILE + row_iota((TILE, TILE))
        nothing = jnp.zeros((TILE, TILE), jnp.int32)

        def pick(j, found):
            here_on = row >= starts[j]
            values = (packed[j], packed[j + 1])
            return tuple(jnp.where(here_on, v, f) for v, f in zip(values, found))
        low_c[block(i)], high_c[block(i)] = lax.fori_loop(0, n_sent, pick, (nothing, nothing))
    each(rows_all // TILE, lows)
    zero(num_c)
    zero(tot_c)
    ng[...] = jnp.zeros_like(ng)

    def last_at(table, row):
        def pick(j, found):
            return jnp.where(starts[j] <= row, table(j), found)
        return lax.fori_loop(0, n_sent, pick, jnp.int32(0))

    def tiles(body, bias, first, last):
        def outer(i, carry):
            def inner(kt, carry):
                body(block(i, RC), block(kt), bias(i, kt))
                return carry
            return lax.fori_loop(first(i) // TILE, (last(i) - 1) // TILE + 1, inner, carry)
        lax.fori_loop(0, rows_all // RC, outer, 0)

    def cross_tiles(body):
        def bias(i, kt):
            key = kt * TILE + lane_iota((RC, TILE))
            r = block(i, RC)
            return jnp.where((key >= low_c[r]) & (key < high_c[r]), 0.0, HIDE)
        tiles(body, bias, lambda i: last_at(lambda j: packed[j], i * RC),
              lambda i: last_at(lambda j: packed[j + 1], (i + 1) * RC - 1))

    loads["a"].wait()
    loads[4].wait()

    def query(n):
        qc[:, columns(n)] = mm(a_b[...], weight(4, n)).astype(LOW) * jnp.asarray(0.125, LOW)
    each(2, query)
    load_rest()
    for name in ("mem", 5, 6):
        loads[name].wait()

    def choose(ct):
        r = block(ct, CHUNK)
        for g in range(n_src // TILE):
            hit = idx[r] == g * TILE + lane_iota((CHUNK, TILE))
            sel[:, g * TILE:(g + 1) * TILE] = jnp.where(hit, 1.0, 0.0).astype(LOW)

    def keys(ct):
        r = block(ct, CHUNK)
        key = ct * CHUNK + row_iota((CHUNK, TILE))

        def pick(j, found):
            return jnp.where(key >= packed[j], offs_ref[0, base + j] - packed[j] + key, found)
        at = lax.fori_loop(0, n_sent, pick, jnp.zeros((CHUNK, TILE), jnp.int32))
        idx[r] = jnp.where(key < n_keys, at, -1)
        choose(ct)

        def bring(n):
            memc[r, columns(n)] = mm(sel[...], mem[:, columns(n)]).astype(LOW)
        each(2, bring)

        def project(n):
            kc[r, columns(n)] = mm(memc[r], weight(5, n)).astype(LOW)
            vc[r, columns(n)] = mm(memc[r], weight(6, n)).astype(LOW)
        each(2, project)
    each(chunks, keys)

    cross_tiles(lambda r, k, bias: tile_forward(r, k, bias, qc, kc, vc, num_c, tot_c))
    divide(num_c, tot_c, oc_b, rows_all)
    for name in (7, "t1", "gb"):
        loads[name].wait()

    def cross_out(n):
        t1[:, columns(n)] += mm(oc_b[...], weight(7, n))
    each(2, cross_out)

    def norm_cross(i):
        r = block(i, 64)
        xh, rs = normalize(t1[r])
        xh2[r] = xh
        rs2[r] = jnp.broadcast_to(rs, (64, TILE))
        after = xh * gb[2:3] + gb[3:4]
        t1[r] = after
        c_b[r] = after.astype(LOW)
    each(rows_all // 64, norm_cross)

    loads[8].wait()

    def hidden(n):
        v = mm(c_b[...], weight(8, n))
        sig = 1.0 / (1.0 + jnp.exp(-v))
        act[:, columns(n)] = (v * sig).astype(LOW)
        big[block(n // 2, SLAB), columns(n % 2)] = sig * (1.0 + v * (1.0 - sig))
    each(8, hidden)
    for k in range(4):
        loads[("w2", k)].wait()

    def ffn_out(n):
        cols = columns(n)
        t1[:, cols] += mm(act[...], w2[:, :, :, cols].reshape(4 * SLAB, 256))
    each(2, ffn_out)
    loads["og"].wait()

    def norm_ffn(i):
        r = block(i, 64)
        xh, rs = normalize(t1[r])
        gain = gb[4:5]
        lout[r] = (xh * gain + gb[5:6]).astype(LOW)
        u = og[r].astype(F32)
        ng[4:5] += jnp.sum(u * xh, axis=0, keepdims=True)
        ng[5:6] += jnp.sum(u, axis=0, keepdims=True)
        d = back_norm(u, gain, xh, rs)
        dpre[r] = d
        g_b[r] = d.astype(LOW)
    each(rows_all // 64, norm_ffn)
    send(lout, layer_out)

    def hidden_back(n):
        devs = pl.ds(pl.multiple_of(n * 4, 4), 4)
        part = mmt(g_b[...], w2[devs].reshape(256, SLAB))
        d = (part * big[block(n // 2, SLAB), columns(n % 2)]).astype(LOW)
        dhid[:, columns(n)] = d
        w2[devs] = tmm(act[:, columns(n)], g_b[...]).astype(LOW).reshape(4, 4, ROWS, SLAB)
    each(8, hidden_back)
    for k in range(4):
        send(w2.at[:, k], grads.at[:, :, pl.ds(CUT + SLAB * k, SLAB)])

    def input_back(n):
        dpre[:, columns(n)] += mmt(dhid[...], weight_rows(8, n, 256, 4 * SLAB))
    each(2, input_back)

    def first_grad(n):
        put_weight(8, n, tmm(c_b[...], dhid[:, columns(n)]))
    each(8, first_grad)
    lanes = pl.ds(NORM + SLAB * 8, 4 * SLAB)
    send(w.at[:, :, lanes], grads.at[:, :, lanes])

    def back_cross(i):
        r = block(i, 64)
        u, xh = dpre[r], xh2[r]
        ng[2:3] += jnp.sum(u * xh, axis=0, keepdims=True)
        ng[3:4] += jnp.sum(u, axis=0, keepdims=True)
        d = back_norm(u, gb[2:3], xh, rs2[r][:, :1])
        dpre[r] = d
        g_b[r] = d.astype(LOW)
    each(rows_all // 64, back_cross)

    out_back(g_b, lambda n: weight_rows(7, n), num_c, tot_c, dnx)

    def out_grad_store(n):
        put_weight(7, n, tmm(oc_b[...], g_b[:, columns(n)]))
    each(2, out_grad_store)

    def send_slab(i):
        lanes = pl.ds(NORM + SLAB * i, SLAB)
        send(w.at[:, :, lanes], grads.at[:, :, lanes])

    send_slab(7)
    zero(dq)

    def clear(ct):
        r = block(ct, CHUNK)
        big[r] = jnp.zeros((CHUNK, SLAB), F32)
        dv[r] = jnp.zeros((CHUNK, SLAB), F32)
    each(chunks, clear)
    cross_tiles(lambda r, k, bias: tile_backward(r, k, bias, qc, kc, vc, dnx, dq, big, dv))

    def scaled(src, dst, factor, step=64):
        def body(i):
            r = block(i, step)
            dst[r] = (src[r] * factor).astype(LOW)
        each(src.shape[0] // step, body)

    scaled(dq, qc, 0.125)

    def query_back(n):
        dpre[:, columns(n)] += mmt(qc[...], weight_rows(4, n))
    each(2, query_back)

    send(dpre, dpre_out)

    def query_grad(n):
        put_weight(4, n, tmm(a_b[...], qc[:, columns(n)]))
    each(2, query_grad)
    send_slab(4)

    zero(num_c)
    zero(tot_c)

    def memory_back(ct):
        r = block(ct, CHUNK)
        kc[r] = big[r].astype(LOW)
        vc[r] = dv[r].astype(LOW)

        def key_grad(n):
            cols = columns(n)
            num_c[:, cols] += tmm(memc[r], kc[r, cols])
            tot_c[:, cols] += tmm(memc[r], vc[r, cols])
        each(2, key_grad)

        def rows_grad(n):
            memc[r, columns(n)] = (
                mmt(kc[r], weight_rows(5, n)) + mmt(vc[r], weight_rows(6, n))).astype(LOW)
        each(2, rows_grad)
        choose(ct)

        def spread(n):
            rows = block(n, 256)
            found = tmm(sel[:, columns(n)], memc[r]).astype(LOW)
            mem[rows] = jnp.where(ct == 0, found, mem[rows] + found)
        each(n_src // 256, spread)
    each(chunks, memory_back)
    send(mem, mem_grads)

    def key_store(n):
        put_weight(5, n, num_c[:, columns(n)])
        put_weight(6, n, tot_c[:, columns(n)])
    each(2, key_store)
    send_slab(5)
    send_slab(6)

    send(ng, ng_out)
    for copy in outs:
        copy.wait()


def state_shapes(rows):
    full = lambda dtype, lanes=SLAB, n=rows: jax.ShapeDtypeStruct((n, lanes), dtype)
    return (
        full(F32),
        full(F32),
        full(F32, TILE),
        full(F32),
        full(F32),
        full(LOW),
        full(LOW),
        full(LOW),
        full(LOW),
        full(F32, SLAB, 8),
        full(F32, SLAB, 8),
        full(jnp.int32, TILE),
    )


def compute(lens, spans, offs, out_grad, memory, gathered, after, after_low, gains):
    rows, n_src = out_grad.shape[0], memory.shape[0]
    n_sent = 16
    n_keys = n_sent * 112
    any_space = pl.BlockSpec(memory_space=pl.ANY)
    smem = pl.BlockSpec(memory_space=pltpu.SMEM)
    dma = pltpu.SemaphoreType.DMA
    f32 = lambda *s: pltpu.VMEM(s, F32)
    low = lambda *s: pltpu.VMEM(s, LOW)
    return pl.pallas_call(
        compute_kernel,
        out_shape=(
            jax.ShapeDtypeStruct((rows, SLAB), LOW),
            jax.ShapeDtypeStruct((DEV, ROWS, LANES), LOW),
            jax.ShapeDtypeStruct((n_src, SLAB), LOW),
            jax.ShapeDtypeStruct((rows, SLAB), F32),
            jax.ShapeDtypeStruct((8, SLAB), F32),
        ),
        in_specs=[smem] * 3 + [any_space] * 6,
        out_specs=(any_space,) * 5,
        scratch_shapes=[
            low(DEV, ROWS, CUT),
            low(DEV, 4, ROWS, SLAB),
            low(rows, SLAB),
            low(n_src, SLAB),
            low(rows, SLAB),
            low(n_keys, SLAB),
            low(n_keys, SLAB),
            f32(4 * SLAB, SLAB),
            low(rows, 4 * SLAB),
            low(rows, 4 * SLAB),
            f32(n_keys, SLAB),
            f32(rows, SLAB),
            f32(rows, SLAB),
            f32(rows, SLAB),
            f32(rows, SLAB),
            f32(rows, SLAB),
            f32(rows, SLAB),
            f32(rows, TILE),
            low(rows, SLAB),
            low(rows, SLAB),
            low(rows, SLAB),
            low(rows, SLAB),
            low(rows, 2 * SLAB),
            f32(8, SLAB),
            f32(8, SLAB),
            low(rows, SLAB),
            pltpu.VMEM((rows, TILE), jnp.int32),
            pltpu.VMEM((rows, TILE), jnp.int32),
            low(n_keys, SLAB),
            low(CHUNK, n_src),
            pltpu.VMEM((n_keys, TILE), jnp.int32),
            pltpu.SMEM((n_sent + 1,), jnp.int32),
            pltpu.SMEM((n_sent + 1,), jnp.int32),
            dma((5,)),
            dma((17,)),
            dma((32,)),
        ],
        compiler_params=pltpu.CompilerParams(vmem_limit_bytes=60 << 20),
        name="compute",
    )(lens, spans, offs, out_grad, memory, gathered, after, after_low, gains)
def scatter_rounds(share=0.42):
    spans = []
    for at, tiles in ((33, 6), (39, 7), (46, 7), (17, 16), (0, 11), (11, 6)):
        split = at + max(1, round(tiles * share))
        spans.append((at * 128, split * 128, (at + tiles) * 128))
    return tuple(spans)


SCATTER_ROUNDS = scatter_rounds()
Z_FIRST = (53 * 128, 59 * 128, 65 * 128)
SELF_LANES = NORM + 4 * SLAB
SELF_ROUNDS = (4, 5)


def scatter_kernel(grads, mem_grads, gathered, target, *rest):
    state, (out_ref, mem_ref, target_ref), rest = rest[:12], rest[12:15], rest[15:]
    (acc, from_core, from_first, from_second, from_z, macc, mfrom_core, mfrom_y), rest = rest[:8], rest[8:]
    held, rest = rest[:12], rest[12:]
    (w, tgt, gs, dq, dk, dv, dnx, g_b, out, mem_out), rest = rest[:10], rest[10:]
    (target_grad, from_zc, from_fc, from_sc), rest = rest[:4], rest[4:]
    (out_sems, own_sems, mown_sem, state_sems, core_s, core_r, first_s, first_r,
     second_s, second_r, zs_s, zs_r, mem_s, mem_r, zc_s, zc_r, fc_s, fc_r, sc_s, sc_r) = rest
    dpre, xh1, rs1, num_s, tot_s, qs, ks, vs, o_b, gb, ng, low_s = held
    z, x, y, c = here()
    xp, yp, cp_ = device(z, 1 - x, y, c), device(z, x, 1 - y, c), device(z, x, y, 1 - c)
    zp = [device((z + k) % 4, x, y, c) for k in (1, 2, 3)]
    count = len(SCATTER_ROUNDS)
    core_sems, first_sems, second_sems = (core_s, core_r), (first_s, first_r), (second_s, second_r)
    z_sems, mem_sems = (zs_s, zs_r), (mem_s, mem_r)
    sent = []

    def go(copy):
        copy.start()
        sent.append(copy)

    def span(r, part=None):
        a, m, b = Z_FIRST if r == count else SCATTER_ROUNDS[r]
        return {None: (a, b - a), 0: (a, m - a), 1: (m, b - m)}[part]

    def own(r):
        a, n = span(r)
        return pltpu.make_async_copy(
            grads.at[:, :, :, c, :, pl.ds(a, n)], acc.at[:, :, :, :, pl.ds(a, n)], own_sems.at[r])

    def core(r):
        a, n = span(r)
        source = gs if r in SELF_ROUNDS else grads
        return remote(source.at[:, :, :, 1 - c, :, pl.ds(a, n)],
                      from_core.at[:, :, :, :, pl.ds(a, n)], core_sems, r, cp_)

    def first(r, part):
        lanes = pl.ds(*span(r, part))
        src = acc.at[:, :, 1 - y, :, lanes] if part == 0 else acc.at[:, 1 - x, :, :, lanes]
        return remote(src, from_first.at[:, :, :, lanes], first_sems, (r, part),
                      yp if part == 0 else xp)

    def second(r, part):
        lanes = pl.ds(*span(r, part))
        src = acc.at[:, 1 - x, y, :, lanes] if part == 0 else acc.at[:, x, 1 - y, :, lanes]
        return remote(src, from_second.at[:, :, lanes], second_sems, (r, part),
                      xp if part == 0 else yp)

    def along(r, k):
        lanes = pl.ds(*span(r))
        return remote(acc.at[(z + k + 1) % 4, x, y, :, lanes], from_z.at[k, :, lanes], z_sems,
                      (r, k), zp[k])

    mem_own = pltpu.make_async_copy(mem_grads.at[:, c], macc, mown_sem)
    mem_core = remote(mem_grads.at[:, 1 - c], mfrom_core, mem_sems, 0, cp_)
    mem_far = remote(macc.at[1 - y], mfrom_y, mem_sems, 1, yp)

    def bring(i, src, dst):
        copy = pltpu.make_async_copy(src, dst, state_sems.at[i])
        copy.start()
        return copy

    early = [r for r in range(count) if r not in SELF_ROUNDS]
    own(0).start()
    mem_own.start()
    for r in [count] + early[1:]:
        own(r).start()
    copies = [bring(i, src, dst) for i, (src, dst) in enumerate(zip(state, held))]
    copies.append(bring(12, gathered.at[:, :, pl.ds(NORM, 4 * SLAB)], w))
    copies.append(bring(13, target, tgt))
    greet([xp, yp, cp_] + zp)
    go(core(early[0]))
    go(mem_core)
    for r in [count] + early[1:]:
        go(core(r))

    def add_core(r):
        if r not in SELF_ROUNDS:
            own(r).wait()
        core(r).wait_recv()
        for part in (0, 1):
            lanes = pl.ds(*span(r, part))
            for theirs in (True, False):
                def body(zi, carry, part=part, lanes=lanes, theirs=theirs):
                    for o in (0, 1):
                        if part == 0:
                            xi, yi = o, (1 - y) if theirs else y
                        else:
                            xi, yi = (1 - x) if theirs else x, o
                        mine = gs[zi, xi, yi, c, :, lanes] if r in SELF_ROUNDS else acc[zi, xi, yi, :, lanes]
                        acc[zi, xi, yi, :, lanes] = mine + from_core[zi, xi, yi, :, lanes]
                    return carry
                lax.fori_loop(0, 4, body, 0)
                if theirs:
                    go(first(r, part))

    def add_first(r):
        for part in (0, 1):
            first(r, part).wait_recv()
            lanes = pl.ds(*span(r, part))
            for theirs in (True, False):
                def body(zi, carry, part=part, lanes=lanes, theirs=theirs):
                    if part == 0:
                        xi, yi = (1 - x) if theirs else x, y
                        slot = xi
                    else:
                        xi, yi = x, (1 - y) if theirs else y
                        slot = yi
                    acc[zi, xi, yi, :, lanes] = (
                        acc[zi, xi, yi, :, lanes] + from_first[zi, slot, :, lanes])
                    return carry
                lax.fori_loop(0, 4, body, 0)
                if theirs:
                    go(second(r, part))

    def add_second(r):
        for part in (0, 1):
            second(r, part).wait_recv()
            lanes = pl.ds(*span(r, part))

            def body(zi, carry, lanes=lanes):
                acc[zi, x, y, :, lanes] = acc[zi, x, y, :, lanes] + from_second[zi, :, lanes]
                return carry
            lax.fori_loop(0, 4, body, 0)
        for k in (1, 0, 2):
            go(along(r, k))

    def add_z(r):
        lanes = pl.ds(*span(r))
        total = acc[z, x, y, :, lanes].astype(jnp.float32)
        for k in (0, 2, 1):
            along(r, k).wait_recv()
            total = total + from_z[k, :, lanes].astype(jnp.float32)
        out[:, lanes] = total

    lanes_c = pl.ds(*span(count))
    cut_c = [pl.ds(*span(count, part)) for part in (0, 1)]
    width_c = [span(count, part)[1] for part in (0, 1)]

    def far_c(k):
        return remote(acc.at[(z + k + 1) % 4, :, :, :, lanes_c], from_zc.at[k], (zc_s, zc_r), k, zp[k])

    def first_c(part):
        src = acc.at[z, 1 - x, :, :, cut_c[0]] if part == 0 else acc.at[z, :, 1 - y, :, cut_c[1]]
        return remote(src, from_fc.at[part, :, :, pl.ds(0, width_c[part])], (fc_s, fc_r), part,
                      xp if part == 0 else yp)

    def second_c(part):
        src = acc.at[z, x, 1 - y, :, cut_c[0]] if part == 0 else acc.at[z, 1 - x, y, :, cut_c[1]]
        return remote(src, from_sc.at[part, :, pl.ds(0, width_c[part])], (sc_s, sc_r), part,
                      yp if part == 0 else xp)

    def add_core_c():
        own(count).wait()
        core(count).wait_recv()
        for k in (0, 2, 1, 3):
            zi = (z + k + 1) % 4
            for xi in (0, 1):
                for yi in (0, 1):
                    acc[zi, xi, yi, :, lanes_c] = (
                        acc[zi, xi, yi, :, lanes_c] + from_core[zi, xi, yi, :, lanes_c])
            if k < 3:
                go(far_c(k))

    def add_far_c():
        for k in (0, 2, 1):
            far_c(k).wait_recv()
        for xi in (0, 1):
            for yi in (0, 1):
                total = acc[z, xi, yi, :, lanes_c].astype(F32)
                for k in range(3):
                    total = total + from_zc[k, xi, yi].astype(F32)
                acc[z, xi, yi, :, lanes_c] = total.astype(LOW)
        for part in (0, 1):
            go(first_c(part))

    def add_first_c():
        for part in (0, 1):
            first_c(part).wait_recv()
            for o in (0, 1):
                xi, yi = (x, o) if part == 0 else (o, y)
                acc[z, xi, yi, :, cut_c[part]] = (
                    acc[z, xi, yi, :, cut_c[part]] + from_fc[part, o, :, pl.ds(0, width_c[part])])
            go(second_c(part))

    def end_c():
        for part in (0, 1):
            second_c(part).wait_recv()
            out[:, cut_c[part]] = (acc[z, x, y, :, cut_c[part]].astype(F32)
                                   + from_sc[part, :, pl.ds(0, width_c[part])].astype(F32))

    def memory_core():
        mem_own.wait()
        mem_core.wait_recv()
        for theirs in (True, False):
            side = (1 - y) if theirs else y

            def body(i, carry, side=side):
                rows = pl.ds(pl.multiple_of(i * 64, 64), 64)
                macc[side, rows] = macc[side, rows] + mfrom_core[side, rows]
                return carry
            lax.fori_loop(0, 8, body, 0)
            if theirs:
                go(mem_far)

    def memory_end():
        mem_far.wait_recv()

        def body(i, carry):
            rows = pl.ds(pl.multiple_of(i * 64, 64), 64)
            mem_out[rows] = macc[y, rows].astype(jnp.float32) + mfrom_y[rows].astype(jnp.float32)
            return carry
        lax.fori_loop(0, 8, body, 0)

    def weight_rows(i, part):
        devs = pl.ds(part * 16, 16)
        return w[devs, :, pl.ds(SLAB * i, SLAB)].reshape(256, SLAB)

    def put(i, n, value):
        gs[:, :, :, :, :, pl.ds(NORM + SLAB * i + 256 * n, 256)] = value.astype(LOW).reshape(4, 2, 2, 2, ROWS, 256)

    rows_all = tgt.shape[0]

    def norm_back(i):
        r = block(i, 64)
        u, xh = dpre[r], xh1[r]
        ng[0:1] += jnp.sum(u * xh, axis=0, keepdims=True)
        ng[1:2] += jnp.sum(u, axis=0, keepdims=True)
        d = back_norm(u, gb[0:1], xh, rs1[r][:, :1])
        dpre[r] = d
        g_b[r] = d.astype(LOW)

    def self_norm():
        for copy in copies:
            copy.wait()
        each(rows_all // 64, norm_back)

    def self_out():
        out_back(g_b, lambda n: weight_rows(3, n), num_s, tot_s, dnx)
        for n in (0, 1):
            put(3, n, tmm(o_b[...], g_b[:, pl.ds(256 * n, 256)]))
        for ref in (dq, dk, dv):
            zero(ref)

    def self_tiles(i, first, last):
        def inner(kt, carry):
            r = pl.ds(i * RT, RT)
            key = kt * TILE + lane_iota((RT, TILE))
            row = i * RT + row_iota((RT, TILE))
            bias = jnp.where((key >= low_s[r]) & (key <= row), 0.0, HIDE)
            tile_backward(r, block(kt), bias, qs, ks, vs, dnx, dq, dk, dv)
            return carry
        lax.fori_loop(first, last, inner, 0)

    def self_grads():
        def lower(i):
            r = block(i, 64)
            qs[r] = (dq[r] * 0.125).astype(LOW)
            ks[r] = dk[r].astype(LOW)
            vs[r] = dv[r].astype(LOW)
        each(rows_all // 64, lower)
        for i, src in ((0, qs), (1, ks), (2, vs)):
            for n in (0, 1):
                put(i, n, tmm(tgt[...], src[:, pl.ds(256 * n, 256)]))
        inside = lane_iota((8, TILE)) < ROWS
        for d in range(DEV):
            one = ng[:, pl.ds(TILE * (d // 8), TILE)]
            one = pltpu.roll(one, (TILE - ROWS * (d % 8)) % TILE, 1) if d % 8 else one
            one = jnp.concatenate([jnp.where(inside, one, 0.0), jnp.zeros((8, TILE), F32)], axis=0)
            gs[d // 8, d // 4 % 2, d // 2 % 2, d % 2, :, pl.ds(0, NORM)] = one.astype(LOW)
        for r in SELF_ROUNDS:
            go(core(r))

    def self_target():
        for n in (0, 1):
            total = mmt(qs[...], weight_rows(0, n)) + mmt(ks[...], weight_rows(1, n))
            cols = pl.ds(256 * n, 256)
            target_grad[:, cols] = dpre[:, cols] + total + mmt(vs[...], weight_rows(2, n))

    add_core(0)
    memory_core()
    add_core_c()
    add_core(1)
    self_norm()
    add_first(0)
    add_core(2)
    self_out()
    add_second(0)
    add_first(1)
    add_core(3)
    self_tiles(0, 0, 2)
    add_second(1)
    add_first(2)
    self_tiles(1, 0, 4)
    add_z(0)
    add_second(2)
    add_first(3)
    add_far_c()
    self_grads()
    add_core(4)
    add_core(5)
    self_target()
    to_target = pltpu.make_async_copy(target_grad, target_ref, out_sems.at[0])
    to_target.start()
    add_first_c()
    memory_end()
    to_memory = pltpu.make_async_copy(mem_out, mem_ref, out_sems.at[1])
    to_memory.start()
    add_z(1)
    add_second(3)
    add_first(4)
    add_first(5)
    add_z(2)
    add_second(4)
    add_z(3)
    end_c()
    add_second(5)
    add_z(4)
    add_z(5)
    to_rows = pltpu.make_async_copy(out, out_ref, out_sems.at[2])
    to_rows.start()
    for copy in (to_target, to_memory, to_rows):
        copy.wait()
    for copy in sent:
        copy.wait_send()


def scatter_all(grads, mem_grads, gathered, target, state):
    any_space = pl.BlockSpec(memory_space=pl.ANY)
    dma = pltpu.SemaphoreType.DMA
    n = len(SCATTER_ROUNDS)
    rows = mem_grads.shape[2]
    wide = Z_FIRST[2] - Z_FIRST[0]
    low = lambda *s: pltpu.VMEM(s, LOW)
    f32 = lambda *s: pltpu.VMEM(s, F32)
    return pl.pallas_call(
        scatter_kernel,
        out_shape=(
            jax.ShapeDtypeStruct((ROWS, LANES), F32),
            jax.ShapeDtypeStruct((rows, SLAB), F32),
            jax.ShapeDtypeStruct((rows, SLAB), F32),
        ),
        in_specs=[any_space] * 16,
        out_specs=(any_space,) * 3,
        scratch_shapes=[
            low(4, 2, 2, ROWS, LANES),
            low(4, 2, 2, ROWS, LANES),
            low(4, 2, ROWS, LANES),
            low(4, ROWS, LANES),
            low(3, ROWS, LANES),
            low(2, rows, SLAB),
            low(2, rows, SLAB),
            low(rows, SLAB),
        ]
        + [pltpu.VMEM(s.shape, s.dtype) for s in state_shapes(rows)]
        + [
            low(32, ROWS, 4 * SLAB),
            low(rows, SLAB),
            low(4, 2, 2, 2, ROWS, SELF_LANES),
            f32(rows, SLAB),
            f32(rows, SLAB),
            f32(rows, SLAB),
            low(rows, 2 * SLAB),
            low(rows, SLAB),
            f32(ROWS, LANES),
            f32(rows, SLAB),
            f32(rows, SLAB),
            low(3, 2, 2, ROWS, wide),
            low(2, 2, ROWS, wide),
            low(2, ROWS, wide),
            dma((3,)),
            dma((n + 1,)),
            dma(()),
            dma((14,)),
            dma((n + 1,)),
            dma((n + 1,)),
            dma((n, 2)),
            dma((n, 2)),
            dma((n, 2)),
            dma((n, 2)),
            dma((n, 3)),
            dma((n, 3)),
            dma((2,)),
            dma((2,)),
            dma((3,)),
            dma((3,)),
            dma((2,)),
            dma((2,)),
            dma((2,)),
            dma((2,)),
        ],
        compiler_params=pltpu.CompilerParams(
            collective_id=2, has_side_effects=True, vmem_limit_bytes=56 << 20),
        name="scatter",
    )(grads, mem_grads, gathered, target, *state)


def finish_kernel(rows_ref, mem_ref, target_ref, *rest):
    outs, (rows, mem, target, in_sems, out_sems) = rest[:18], rest[18:]
    copies = []
    loads = []
    half = target.shape[0] // 2
    pieces = [pl.ds(0, half), pl.ds(half, half)]
    cuts_ = [(NORM + SLAB * i, SLAB) for i in range(8)] + [(NORM + SLAB * 8, 4 * SLAB)]
    cuts_ += [(NORM + SLAB * (12 + k), SLAB) for k in range(4)]

    def load(src, dst):
        copy = pltpu.make_async_copy(src, dst, in_sems.at[len(loads)])
        copy.start()
        loads.append(copy)

    def bring(src, dst):
        copy = pltpu.make_async_copy(src, dst, out_sems.at[len(copies)])
        copy.start()
        copies.append(copy)

    for p in pieces:
        load(target_ref.at[p], target.at[p])
        load(mem_ref.at[p], mem.at[p])
    load(rows_ref, rows)
    for i, p in enumerate(pieces):
        loads[2 * i].wait()
        bring(target.at[p], outs[0].at[p])
        loads[2 * i + 1].wait()
        bring(mem.at[p], outs[1].at[p])
    loads[4].wait()
    for i, (start, width) in enumerate(cuts_):
        dst = outs[2 + i] if i < 9 else outs[11].at[pl.ds(ROWS * (i - 9), ROWS)]
        bring(rows.at[:, pl.ds(start, width)], dst)
    for i in range(6):
        outs[12 + i][...] = rows[i, pl.ds(0, ROWS)]
    for copy in copies:
        copy.wait()


def finish(rows, mem, target):
    any_space = pl.BlockSpec(memory_space=pl.ANY)
    shape = lambda *s: jax.ShapeDtypeStruct(s, F32)
    return pl.pallas_call(
        finish_kernel,
        out_shape=(shape(*target.shape), shape(*mem.shape))
        + (shape(ROWS, SLAB),) * 8
        + (shape(ROWS, 4 * SLAB), shape(4 * ROWS, SLAB))
        + (shape(ROWS),) * 6,
        in_specs=[any_space] * 3,
        out_specs=(any_space,) * 12 + (pl.BlockSpec(memory_space=pltpu.VMEM),) * 6,
        scratch_shapes=[
            pltpu.VMEM(rows.shape, F32),
            pltpu.VMEM(mem.shape, F32),
            pltpu.VMEM(target.shape, F32),
            pltpu.SemaphoreType.DMA((5,)),
            pltpu.SemaphoreType.DMA((17,)),
        ],
        name="finish",
    )(rows, mem, target)


def local(target_in, memory, out_grad, *rest):
    fast = two_by_two((lax.axis_size("dp"), lax.axis_size("mem")))
    if not fast:
        return plain(target_in, memory, out_grad, *rest)
    weights, tables = rest[:16], rest[16:]
    gathered, all_memory, saved = gather_all(
        weights[:10], weights[10:], memory, tables[0], target_in
    )
    after, after_low, xh1, rs1, num, tot, q, k, v, o, gains, low_s = saved
    layer_out, grads, mem_grads, d_after, norm_grads = compute(
        *tables, out_grad, all_memory, gathered, after, after_low, gains
    )
    state = (d_after, xh1, rs1, num, tot, q, k, v, o, gains, norm_grads, low_s)
    rows = target_in.shape[0]
    out, mem_out, target_grad = scatter_all(
        grads.reshape(4, 2, 2, 2, ROWS, LANES),
        mem_grads.reshape(2, 2, rows, SLAB),
        gathered,
        target_in,
        state,
    )
    return (layer_out,) + tuple(finish(out, mem_out, target_grad))


def solution(mesh):
    both = P(("dp", "mem"), None)
    flat = P(("dp", "mem"))
    in_specs = (both,) * 13 + (flat,) * 6 + (P("dp", None),) * 3
    out_specs = (both,) * 13 + (flat,) * 6
    return jax.shard_map(local, mesh=mesh, in_specs=in_specs, out_specs=out_specs, check_vma=False)
```

```python
import functools

import jax
import jax.numpy as jnp
from jax import lax
from jax.experimental import pallas as pl
from jax.experimental.pallas import tpu as pltpu
from jax.sharding import PartitionSpec as P

MESH = pl.DeviceIdType.MESH
SLAB = 512
NORM = 128
LANES = NORM + 16 * SLAB
ROWS = 16


def here():
    dp, mem = lax.axis_index("dp"), lax.axis_index("mem")
    return dp // 2, dp % 2, mem // 2, mem % 2


def device(z, x, y, c):
    return (z * 2 + x, y * 2 + c)


def greet(peers):
    barrier = pltpu.get_barrier_semaphore()
    for peer in peers:
        pl.semaphore_signal(barrier, inc=1, device_id=peer, device_id_type=MESH)
    pl.semaphore_wait(barrier, len(peers))


def remote(src, dst, sems, index, peer):
    send, recv = sems
    return pltpu.make_async_remote_copy(
        src_ref=src,
        dst_ref=dst,
        send_sem=send.at[index],
        recv_sem=recv.at[index],
        device_id=peer,
        device_id_type=MESH,
    )


def cuts(widths, share):
    spans, at = [], 0
    for tiles in widths:
        n = tiles * 128
        spans.append((at, at + max(1, round(tiles * share)) * 128, at + n))
        at += n
    return tuple(spans)


GATHER_ROUNDS = cuts((17, 36), 0.22)
Z_LAST = (53 * 128, 59 * 128, 65 * 128)


def gather_kernel(*refs):
    shards, memory_ref, lens_ref, target = refs[:10], *refs[10:13]
    params, refs = refs[13:19], refs[19:]
    out, mem_out = refs[:2]
    state_out, refs = refs[2:14], refs[14:]
    local_sem, mem_local = refs[:2]
    z_sems, first_sems, second_sems = refs[2:4], refs[4:6], refs[6:8]
    across, mems = refs[8:10], refs[10:12]
    stage, mem_stage = refs[12:14]
    state, refs = refs[14:26], refs[26:]
    after, a_b, xh1, rs1, num, tot, qs, ks, vs, o_b, gb, low_s = state
    w, norms, tgt, starts, state_sems, rows, refs = *refs[:6], refs[6:]
    cf_sems, cs_sems, cz_sems, co_sems = refs[:2], refs[2:4], refs[4:6], refs[6:8]
    z, x, y, c = here()
    xp, yp, cp_ = device(z, 1 - x, y, c), device(z, x, 1 - y, c), device(z, x, y, 1 - c)
    own = out.at[z, x, y, c]
    rounds = range(len(GATHER_ROUNDS))

    local = []

    def bring(src, start, width):
        local.append(
            pltpu.make_async_copy(src, stage.at[:, pl.ds(start, width)], local_sem.at[len(local)])
        )

    for i in range(8):
        bring(shards[i], NORM + SLAB * i, SLAB)
    bring(shards[8], NORM + SLAB * 8, 4 * SLAB)
    for k in range(4):
        bring(shards[9].at[pl.ds(ROWS * k, ROWS)], NORM + SLAB * (12 + k), SLAB)
    for one in local:
        one.start()
    keep = pltpu.make_async_copy(memory_ref, mem_stage, mem_local.at[0])
    keep.start()
    zn = [device((z + k) % 4, x, y, c) for k in (1, 3)]
    rows[...] = jnp.zeros_like(rows)
    for i, one in enumerate(params):
        rows[i : i + 1, :ROWS] = one[...].astype(F32)
    stage[:, :NORM] = rows[...].astype(LOW)
    greet([xp, yp, cp_] + zn)
    for one in local:
        one.wait()
    own_out = pltpu.make_async_copy(stage, own, mem_local.at[1])
    own_out.start()

    def column(slot):
        return z if slot == 0 else (z - slot if slot < 4 else z + (slot - 3))

    def there(slot):
        return None if slot == 0 else (z >= slot if slot < 4 else z <= 6 - slot)

    def both(a, b):
        return b if a is None else (a if b is None else jnp.logical_and(a, b))

    def guarded(cond, body):
        if cond is None:
            body()
        else:
            pl.when(cond)(body)

    sent = []

    def go(make, cond=None):
        guarded(cond, lambda: make().start())
        sent.append((cond, make))

    def along(slot, r, up):
        a, _, b = GATHER_ROUNDS[r]
        ref = out.at[column(slot), x, y, c, :, pl.ds(a, b - a)]
        src = stage.at[:, pl.ds(a, b - a)] if slot == 0 else ref
        d = 0 if slot == 0 else (slot if slot < 4 else slot - 3)
        peer = device((z + (1 if up else 3)) % 4, x, y, c)
        return remote(src, ref, z_sems, (0 if up else 1, d, r), peer)

    def arrived(slot, r):
        a, _, b = GATHER_ROUNDS[r]
        ref = out.at[column(slot), x, y, c, :, pl.ds(a, b - a)]
        up = slot < 4
        index = (0 if up else 1, (slot if up else slot - 3) - 1, r)
        return remote(ref, ref, z_sems, index, xp)

    def first(slot, r, part, arriving=False):
        a, m, b = GATHER_ROUNDS[r]
        zz = column(slot)
        if part == 0:
            ref = out.at[zz, (1 - x) if arriving else x, y, c, :, pl.ds(a, m - a)]
        else:
            ref = out.at[zz, x, (1 - y) if arriving else y, c, :, pl.ds(m, b - m)]
        lanes = pl.ds(a, m - a) if part == 0 else pl.ds(m, b - m)
        src = stage.at[:, lanes] if slot == 0 and not arriving else ref
        return remote(src, ref, first_sems, (slot, part, r), xp if part == 0 else yp)

    def second(slot, r, part, hop, arriving=False):
        a, m, b = GATHER_ROUNDS[r]
        zz = column(slot)
        if part == 0:
            side = (1 - x) if hop else x
            ref = out.at[zz, side, (1 - y) if arriving else y, c, :, pl.ds(a, m - a)]
        else:
            side = (1 - y) if hop else y
            ref = out.at[zz, (1 - x) if arriving else x, side, c, :, pl.ds(m, b - m)]
        lanes = pl.ds(a, m - a) if part == 0 else pl.ds(m, b - m)
        src = stage.at[:, lanes] if slot == 0 and not (arriving or hop) else ref
        return remote(src, ref, second_sems, (slot, part, hop, r), yp if part == 0 else xp)

    def over(slot, r, arriving=False):
        a, _, b = GATHER_ROUNDS[r]
        ref = out.at[column(slot), :, :, (1 - c) if arriving else c, :, pl.ds(a, b - a)]
        return remote(ref, ref, across, (slot, r), cp_)

    def spread(slot, r):
        cond = there(slot)
        for part in (1, 0):
            go(functools.partial(first, slot, r, part), cond)
        for part in (1, 0):
            go(functools.partial(second, slot, r, part, 0), cond)

    def from_z(d, r):
            for slot in (d, d + 3):
                cond = there(slot)
                guarded(cond, lambda slot=slot, r=r: arrived(slot, r).wait_recv())
                if d < 3:
                    onward = z < 3 if slot < 4 else z > 0
                    go(functools.partial(along, slot, r, slot < 4), both(cond, onward))
                spread(slot, r)

    def pass_on(slots, r):
            for slot in slots:
                cond = there(slot)
                for part in (1, 0):
                    guarded(cond, lambda s=slot, r=r, p=part: first(s, r, p, True).wait_recv())
                    go(functools.partial(second, slot, r, part, 1), cond)

    def hand_over(slots, r):
            for slot in slots:
                cond = there(slot)
                for part in (0, 1):
                    for hop in (0, 1):
                        guarded(cond, lambda s=slot, r=r, p=part, h=hop: second(s, r, p, h, True).wait_recv())
                go(functools.partial(over, slot, r), cond)

    cut_c = [pl.ds(Z_LAST[p], Z_LAST[p + 1] - Z_LAST[p]) for p in (0, 1)]
    lanes_c = pl.ds(Z_LAST[0], Z_LAST[2] - Z_LAST[0])

    def first_c(part, arriving=False):
        if part == 0:
            ref = out.at[z, (1 - x) if arriving else x, y, c, :, cut_c[0]]
        else:
            ref = out.at[z, x, (1 - y) if arriving else y, c, :, cut_c[1]]
        src = ref if arriving else stage.at[:, cut_c[part]]
        return remote(src, ref, cf_sems, part, xp if part == 0 else yp)

    def second_c(part, hop, arriving=False):
        if part == 0:
            ref = out.at[z, (1 - x) if hop else x, (1 - y) if arriving else y, c, :, cut_c[0]]
        else:
            ref = out.at[z, (1 - x) if arriving else x, (1 - y) if hop else y, c, :, cut_c[1]]
        src = ref if arriving or hop else stage.at[:, cut_c[part]]
        return remote(src, ref, cs_sems, (part, hop), yp if part == 0 else xp)

    def along_c(slot, up):
        ref = out.at[column(slot), :, :, c, :, lanes_c]
        d = 0 if slot == 0 else (slot if slot < 4 else slot - 3)
        peer = device((z + (1 if up else 3)) % 4, x, y, c)
        return remote(ref, ref, cz_sems, (0 if up else 1, d), peer)

    def arrived_c(slot):
        ref = out.at[column(slot), :, :, c, :, lanes_c]
        up = slot < 4
        return remote(ref, ref, cz_sems, (0 if up else 1, (slot if up else slot - 3) - 1), xp)

    def over_c(slot, arriving=False):
        ref = out.at[column(slot), :, :, (1 - c) if arriving else c, :, lanes_c]
        return remote(ref, ref, co_sems, slot, cp_)

    def pass_on_c():
        for part in (0, 1):
            first_c(part, True).wait_recv()
            go(functools.partial(second_c, part, 1))

    def plane_c():
        own_out.wait()
        for part in (0, 1):
            for hop in (0, 1):
                second_c(part, hop, True).wait_recv()
        go(functools.partial(along_c, 0, True), z < 3)
        go(functools.partial(along_c, 0, False), z > 0)
        go(functools.partial(over_c, 0))

    def from_z_c(d):
        for slot in (d, d + 3):
            cond = there(slot)
            guarded(cond, lambda slot=slot: arrived_c(slot).wait_recv())
            if d < 3:
                onward = z < 3 if slot < 4 else z > 0
                go(functools.partial(along_c, slot, slot < 4), both(cond, onward))
            go(functools.partial(over_c, slot), cond)

    for r in rounds:
        go(functools.partial(along, 0, r, True), z < 3)
        go(functools.partial(along, 0, r, False), z > 0)
        spread(0, r)
        if r == 0:
            for part in (0, 1):
                go(functools.partial(first_c, part))
            for part in (0, 1):
                go(functools.partial(second_c, part, 0))
    mem_own = mem_out.at[y, c]

    def memory_rows():
        keep.wait()
        kept = pltpu.make_async_copy(mem_stage, mem_own, mem_local.at[2])
        kept.start()
        go(lambda: remote(mem_stage, mem_own, mems, 0, yp))
        go(lambda: remote(mem_stage, mem_own, mems, 1, cp_))
        return kept

    def memory_far():
        far = mem_out.at[1 - y, c]
        remote(far, far, mems, 0, yp).wait_recv()
        go(lambda: remote(far, far, mems, 2, cp_))

    everyone = (0, 1, 4, 2, 5, 3, 6)

    def all_over(r):
        for slot in everyone:
            guarded(there(slot), lambda s=slot: over(s, r, True).wait_recv())

    rows_all = tgt.shape[0]
    n_sent = starts.shape[0]
    loads = [pltpu.make_async_copy(target, tgt, state_sems.at[12])]
    loads.append(pltpu.make_async_copy(out.at[:, :, :, :, :, pl.ds(NORM, 4 * SLAB)], w, state_sems.at[13]))
    loads.append(pltpu.make_async_copy(out.at[:, :, :, :, :, pl.ds(0, NORM)], norms, state_sems.at[14]))
    saves = [pltpu.make_async_copy(src, dst, state_sems.at[i]) for i, (src, dst) in enumerate(zip(state, state_out))]

    def weight(i, n):
        return w[:, :, :, :, :, pl.ds(SLAB * i + 256 * n, 256)].reshape(SLAB, 256)

    def prepare():
        base = lax.axis_index("mem") * n_sent

        def count(j, at):
            starts[j] = at
            return at + lens_ref[0, base + j]
        lax.fori_loop(0, n_sent, count, jnp.int32(0))
        for i in range(rows_all // TILE):
            row = i * TILE + row_iota((TILE, TILE))
            found = jnp.zeros((TILE, TILE), jnp.int32)
            for j in range(n_sent):
                found = jnp.where(row >= starts[j], starts[j], found)
            low_s[pl.ds(i * TILE, TILE)] = found
        zero(num)
        zero(tot)

    def project():
        for one in loads:
            one.wait()
        for j in range(SLAB // TILE):
            total = jnp.zeros((8, TILE), F32)
            for k in range(8):
                d = 8 * j + k
                one = norms[d // 8, d // 4 % 2, d // 2 % 2, d % 2].astype(F32)[:8]
                total = total + (pltpu.roll(one, ROWS * k, 1) if k else one)
            gb[:, pl.ds(TILE * j, TILE)] = total
        for i, dst in ((0, qs), (1, ks), (2, vs)):
            for n in (0, 1):
                value = mm(tgt[...], weight(i, n)).astype(LOW)
                dst[:, pl.ds(256 * n, 256)] = value * jnp.asarray(0.125, LOW) if i == 0 else value

    def self_tiles(i, first_tile, last_tile):
        def inner(kt, carry):
            r = pl.ds(i * RC, RC)
            key = kt * TILE + lane_iota((RC, TILE))
            row = i * RC + row_iota((RC, TILE))
            bias = jnp.where((key >= low_s[r]) & (key <= row), 0.0, HIDE)
            tile_forward(r, block(kt), bias, qs, ks, vs, num, tot)
            return carry
        lax.fori_loop(first_tile, last_tile, inner, 0)

    def project_out():
        divide(num, tot, o_b, rows_all)
        for n in (0, 1):
            cols = pl.ds(256 * n, 256)
            after[:, cols] = tgt[:, cols].astype(F32) + mm(o_b[...], weight(3, n))

    def norm_rows(i):
        r = block(i, 64)
        xh, rs = normalize(after[r])
        xh1[r] = xh
        rs1[r] = jnp.broadcast_to(rs, (64, TILE))
        value = xh * gb[0:1] + gb[1:2]
        after[r] = value
        a_b[r] = value.astype(LOW)

    loads[0].start()
    prepare()
    from_z(1, 0)
    pass_on_c()
    from_z(1, 1)
    pass_on((0,), 0)
    plane_c()
    from_z(2, 0)
    pass_on((0,), 1)
    pass_on((1, 4), 0)
    from_z(3, 0)
    from_z(2, 1)
    pass_on((2, 5), 0)
    hand_over((0,), 0)
    from_z_c(1)
    pass_on((1, 4), 1)
    pass_on((3, 6), 0)
    kept = memory_rows()
    hand_over((1, 4), 0)
    hand_over((2, 5), 0)
    from_z(3, 1)
    from_z_c(2)
    hand_over((3, 6), 0)
    all_over(0)
    loads[1].start()
    loads[2].start()
    pass_on((2, 5), 1)
    from_z_c(3)
    project()
    hand_over((0,), 1)
    self_tiles(0, 0, 2)
    pass_on((3, 6), 1)
    self_tiles(0, 2, 4)
    hand_over((1, 4), 1)
    memory_far()
    project_out()
    each(rows_all // 64, norm_rows)
    hand_over((2, 5), 1)
    hand_over((3, 6), 1)
    for one in saves:
        one.start()
    all_over(1)
    for slot in everyone:
        guarded(there(slot), lambda s=slot: over_c(s, True).wait_recv())
    for one in saves:
        one.wait()
    for i, side in ((1, y), (2, 1 - y)):
        last = mem_out.at[side, 1 - c]
        remote(last, last, mems, i, cp_).wait_recv()
    kept.wait()
    for cond, make in sent:
        guarded(cond, lambda make=make: make().wait_send())


def gather_all(shards, params, memory, lens, target):
    any_space = pl.BlockSpec(memory_space=pl.ANY)
    dma = pltpu.SemaphoreType.DMA
    n = len(GATHER_ROUNDS)
    both = lambda *s: [dma(s), dma(s)]
    state = forward_shapes(target.shape[0])
    low = lambda *s: pltpu.VMEM(s, LOW)
    gathered, whole_memory, *saved = pl.pallas_call(
        gather_kernel,
        out_shape=(
            jax.ShapeDtypeStruct((4, 2, 2, 2, ROWS, LANES), jnp.bfloat16),
            jax.ShapeDtypeStruct((2, 2) + memory.shape, jnp.bfloat16),
        )
        + state,
        in_specs=[any_space] * 11
        + [pl.BlockSpec(memory_space=pltpu.SMEM), any_space]
        + [pl.BlockSpec(memory_space=pltpu.VMEM)] * 6,
        out_specs=(any_space,) * 14,
        scratch_shapes=[dma((14,)), dma((3,))]
        + both(2, 3, n) + both(7, 2, n) + both(7, 2, 2, n) + both(7, n) + both(3)
        + [low(ROWS, LANES), low(*memory.shape)]
        + [pltpu.VMEM(s.shape, s.dtype) for s in state]
        + [
            low(4, 2, 2, 2, ROWS, 4 * SLAB),
            low(4, 2, 2, 2, ROWS, NORM),
            low(*target.shape),
            pltpu.SMEM((16,), jnp.int32),
            dma((15,)),
            pltpu.VMEM((ROWS, NORM), F32),
        ]
        + both(2) + both(2, 2) + both(2, 3) + both(7),
        compiler_params=pltpu.CompilerParams(
            collective_id=1, has_side_effects=True, vmem_limit_bytes=60 << 20),
        name="gather",
    )(*shards, memory, lens, target, *[p[None, :] for p in params])
    return gathered.reshape(32, ROWS, LANES), whole_memory.reshape(-1, SLAB), saved


def forward_shapes(rows):
    full = lambda dtype, lanes=SLAB, n=rows: jax.ShapeDtypeStruct((n, lanes), dtype)
    return (
        full(F32),
        full(LOW),
        full(F32),
        full(F32, TILE),
        full(F32),
        full(F32),
        full(LOW),
        full(LOW),
        full(LOW),
        full(LOW),
        full(F32, SLAB, 8),
        full(jnp.int32, TILE),
    )


def two_by_two(mesh_axes):
    return mesh_axes == (8, 4)


def gather_any(shards, norms, memory):
    everyone = ("dp", "mem")
    packed = jnp.concatenate([norms] + list(shards[:9]), axis=1)
    rows = lax.all_gather(packed, everyone, axis=0, tiled=True).reshape(32, ROWS, -1)
    last = lax.all_gather(shards[9], everyone, axis=0, tiled=True)
    last = last.reshape(32, 4, ROWS, SLAB).transpose(0, 2, 1, 3).reshape(32, ROWS, 4 * SLAB)
    return (
        jnp.concatenate([rows, last], axis=2),
        lax.all_gather(memory, "mem", axis=0, tiled=True),
    )


def scatter_any(grads, mem_grads):
    everyone = ("dp", "mem")
    wide = grads.reshape(32, ROWS, LANES).astype(jnp.float32)
    cut = LANES - 4 * SLAB
    rows = lax.psum_scatter(
        wide[:, :, :cut].reshape(512, cut), everyone, scatter_dimension=0, tiled=True
    )
    last = wide[:, :, cut:].reshape(32, ROWS, 4, SLAB).transpose(0, 2, 1, 3).reshape(2048, SLAB)
    last = lax.psum_scatter(last, everyone, scatter_dimension=0, tiled=True)
    mem = lax.psum_scatter(
        mem_grads.astype(jnp.float32), "mem", scatter_dimension=0, tiled=True
    )
    return rows, last, mem
HEADS = 8
HEAD = 64
eps_norm = 1e-05
score_scale = 0.125


def layer_norm(values, gain, shift):
    centre = values - jnp.mean(values, axis=-1, keepdims=True)
    spread = jnp.mean(centre * centre, axis=-1, keepdims=True)
    return centre * lax.rsqrt(spread + eps_norm) * gain + shift


def head_split(values):
    return values.reshape(values.shape[0], HEADS, HEAD)


def matmul(left, right):
    return jnp.dot(left, right, preferred_element_type=jnp.float32)


def left_grad(inputs, grads):
    return jnp.einsum("ra,rb->ab", inputs, grads, preferred_element_type=jnp.float32)


def back_through(grads, weight):
    return jnp.einsum("rb,ab->ra", grads, weight, preferred_element_type=jnp.float32)


def exp_scores(q_block, keys, low_edge, high_edge):
    raw = jnp.einsum("qhd,khd->hqk", head_split(q_block), head_split(keys),
                     preferred_element_type=jnp.float32) * score_scale
    position = lax.broadcasted_iota(jnp.int32, (q_block.shape[0], keys.shape[0]), 1)
    allowed = (position >= low_edge[:, None]) & (position < high_edge[:, None])
    return jnp.where(allowed[None], jnp.exp(raw), 0.0)


def attend(queries, keys, values, low_edge, high_edge):
    expo = exp_scores(queries, keys, low_edge, high_edge)
    numer = jnp.einsum("hqk,khd->qhd", expo.astype(jnp.bfloat16), head_split(values),
                       preferred_element_type=jnp.float32)
    totals = jnp.sum(expo, axis=2).T
    return (numer / totals[:, :, None]).reshape(queries.shape[0], -1), totals


def attend_back(queries, keys, values, low_edge, high_edge, upstream, output, totals):
    expo = exp_scores(queries, keys, low_edge, high_edge)
    up = head_split(upstream.astype(jnp.float32))
    numer_grad = (up / totals[:, :, None]).astype(jnp.bfloat16)
    corr = -jnp.sum(up * head_split(output), axis=2) / totals
    flow = jnp.einsum("qhd,khd->hqk", numer_grad, head_split(values),
                      preferred_element_type=jnp.float32) + corr.T[:, :, None]
    ds = (expo * flow).astype(jnp.bfloat16)
    dq = jnp.einsum("hqk,khd->qhd", ds, head_split(keys), preferred_element_type=jnp.float32)
    dk = jnp.einsum("hqk,qhd->khd", ds, head_split(queries), preferred_element_type=jnp.float32)
    dv = jnp.einsum("hqk,qhd->khd", expo.astype(jnp.bfloat16), numer_grad,
                    preferred_element_type=jnp.float32)
    flat = lambda v: v.reshape(v.shape[0], -1)
    return ((flat(dq) * score_scale).astype(jnp.bfloat16), (flat(dk) * score_scale).astype(jnp.bfloat16),
            flat(dv).astype(jnp.bfloat16))


def plain(target_in, memory, out_grad, *rest):
    weights, (tgt_lens, src_lens, src_offsets) = rest[:16], rest[16:]
    member = lax.axis_index("mem")
    per_device = tgt_lens.shape[1] // lax.axis_size("mem")
    pick = lambda table: lax.dynamic_slice_in_dim(table[0], member * per_device, per_device, 0)
    lengths, spans, offsets = pick(tgt_lens), pick(src_lens), pick(src_offsets)
    norms = jnp.stack(weights[10:], axis=1)
    norms = jnp.pad(norms, ((0, 0), (0, NORM - norms.shape[1])))
    gathered, all_memory = gather_any(weights[:10], norms, memory)
    W = gathered.reshape(512, LANES)
    mat = lambda i: W[:, NORM + SLAB * i : NORM + SLAB * (i + 1)]
    wsq, wsk, wsv, wso, wcq, wck, wcv, wco = [mat(i) for i in range(8)]
    w1 = W[:, NORM + 8 * SLAB : NORM + 12 * SLAB]
    w2 = gathered[:, :, NORM + 12 * SLAB :].reshape(32, 16, 4, SLAB).transpose(0, 2, 1, 3).reshape(2048, SLAB)
    ga, sa, gc, sc, gf, sf = [W[:, i].astype(jnp.float32) for i in range(6)]
    rows = target_in.shape[0]
    starts = jnp.cumsum(lengths) - lengths
    position = lax.iota(jnp.int32, rows)
    sentence = jnp.sum((position[:, None] >= starts[None, :]).astype(jnp.int32), axis=1) - 1
    picker = sentence[:, None] == lax.iota(jnp.int32, per_device)[None, :]
    choose = lambda v: jnp.sum(jnp.where(picker, v[None, :], 0), axis=1)
    self_low, self_high = choose(starts), position + 1
    cross_low = choose(offsets)
    cross_high = cross_low + choose(spans)
    low = jnp.bfloat16
    q, k, v = [matmul(target_in, w).astype(low) for w in (wsq, wsk, wsv)]
    o_self_f, tot_self = attend(q, k, v, self_low, self_high)
    o_self = o_self_f.astype(low)
    after_self, pull_self = jax.vjp(layer_norm, target_in.astype(jnp.float32) + matmul(o_self, wso), ga, sa)
    a_b = after_self.astype(low)
    qc = matmul(a_b, wcq).astype(low)
    kc, vc = matmul(all_memory, wck).astype(low), matmul(all_memory, wcv).astype(low)
    cut = lambda v: v.reshape((4, -1) + v.shape[1:])
    o_c_f, tot_c = lax.map(
        lambda p: attend(p[0], kc, vc, p[1], p[2]), (cut(qc), cut(cross_low), cut(cross_high))
    )
    o_c_f, tot_c = o_c_f.reshape(rows, -1), tot_c.reshape(rows, -1)
    o_c = o_c_f.astype(low)
    after_cross, pull_cross = jax.vjp(layer_norm, after_self + matmul(o_c, wco), gc, sc)
    c_b = after_cross.astype(low)
    hidden = matmul(c_b, w1)
    activated, pull_silu = jax.vjp(jax.nn.silu, hidden)
    act = activated.astype(low)
    final, pull_ffn = jax.vjp(layer_norm, after_cross + matmul(act, w2), gf, sf)
    d_pre_out, g_gf, g_sf = pull_ffn(out_grad.astype(jnp.float32))
    d_branch = d_pre_out.astype(low)
    g_w2 = left_grad(act, d_branch)
    d_hidden = pull_silu(back_through(d_branch, w2))[0].astype(low)
    g_w1 = left_grad(c_b, d_hidden)
    d_pre_cross, g_gc, g_sc = pull_cross(d_pre_out + back_through(d_hidden, w1))
    d_cb = d_pre_cross.astype(low)
    g_wco = left_grad(o_c, d_cb)
    d_oc = back_through(d_cb, wco).astype(low)

    def piece(carry, p):
        dq, dk, dv = attend_back(p[0], kc, vc, p[1], p[2], p[3], p[4], p[5])
        return (carry[0] + dk, carry[1] + dv), dq

    empty = jnp.zeros(kc.shape, jnp.bfloat16)
    (dk_c, dv_c), dq_c = lax.scan(
        piece,
        (empty, empty),
        tuple(cut(v) for v in (qc, cross_low, cross_high, d_oc, o_c_f, tot_c)),
    )
    dq_c = dq_c.reshape(rows, -1)
    g_wcq, g_wck, g_wcv = left_grad(a_b, dq_c), left_grad(all_memory, dk_c), left_grad(all_memory, dv_c)
    mem_grad = back_through(dk_c, wck) + back_through(dv_c, wcv)
    d_pre_self, g_ga, g_sa = pull_self(d_pre_cross + back_through(dq_c, wcq))
    d_sb = d_pre_self.astype(low)
    g_wso = left_grad(o_self, d_sb)
    d_os = back_through(d_sb, wso).astype(low)
    dq, dk, dv = attend_back(q, k, v, self_low, self_high, d_os, o_self_f, tot_self)
    g_wsq, g_wsk, g_wsv = left_grad(target_in, dq), left_grad(target_in, dk), left_grad(target_in, dv)
    target_grad = d_pre_self + back_through(dq, wsq) + back_through(dk, wsk) + back_through(dv, wsv)
    n_g = jnp.pad(jnp.stack([g_ga, g_sa, g_gc, g_sc, g_gf, g_sf], axis=1), ((0, 0), (0, NORM - 6)))
    g_w2p = g_w2.reshape(32, 4, 16, SLAB).transpose(0, 2, 1, 3).reshape(512, 4 * SLAB)
    grads = jnp.concatenate([g.astype(low) for g in (n_g, g_wsq, g_wsk, g_wsv, g_wso, g_wcq, g_wck, g_wcv, g_wco, g_w1, g_w2p)], axis=1)
    part = lambda i, n=1: out[:, NORM + SLAB * i : NORM + SLAB * (i + n)]
    out, w2_grad, mem_out = scatter_any(grads, mem_grad.astype(low))
    return (final.astype(low), target_grad, mem_out) + tuple(part(i) for i in range(8)) + (part(8, 4), w2_grad) + tuple(out[:, i] for i in range(6))


TILE = 128
RT = 256
RC = 512
CHUNK = 256
EPS = 1e-05
HIDE = -1e30
LOW = jnp.bfloat16
F32 = jnp.float32
DEV = 32
CUT = NORM + 12 * SLAB


def mm(a, b):
    return jnp.dot(a, b, preferred_element_type=F32)


def mmt(a, b):
    return lax.dot_general(a, b, (((1,), (1,)), ((), ())), preferred_element_type=F32)


def tmm(a, b):
    return lax.dot_general(a, b, (((0,), (0,)), ((), ())), preferred_element_type=F32)


def lane_iota(shape):
    return lax.broadcasted_iota(jnp.int32, shape, len(shape) - 1)


def row_iota(shape):
    return lax.broadcasted_iota(jnp.int32, shape, 0)


def halves():
    lane = lane_iota((1, TILE))
    even = jnp.where(lane < 64, 1.0, 0.0).astype(LOW)
    odd = jnp.where(lane < 64, 0.0, 1.0).astype(LOW)
    return even, odd


def stacked(block, even, odd):
    return jnp.concatenate([block * even, block * odd], axis=0)


def fold(pair):
    lane = lane_iota((TILE, TILE))
    return jnp.where(lane < 64, pair[:TILE], pair[TILE:])


def totals_block(even, odd):
    wide = lambda v: jnp.broadcast_to(v, (TILE, TILE))
    return jnp.concatenate([wide(even), wide(odd)], axis=0)


def corr_block():
    lane = lane_iota((TILE, TILE))
    a = jnp.where(lane < 2, 1.0, 0.0).astype(LOW)
    b = jnp.where((lane >= 64) & (lane < 66), 1.0, 0.0).astype(LOW)
    return jnp.concatenate([a, b], axis=0)


def tile_forward(rows, keys, bias, q, k, v, num, tot):
    even, odd = halves()
    ones = totals_block(even, odd)
    bias2 = jnp.concatenate([bias, bias], axis=1)
    for h in range(4):
        cols = pl.ds(TILE * h, TILE)
        s = mmt(q[rows, cols], stacked(k[keys, cols], even, odd))
        e = jnp.exp(s + bias2).astype(LOW)
        both = mm(e, jnp.concatenate([stacked(v[keys, cols], even, odd), ones], axis=1))
        num[rows, cols] += both[:, :TILE]
        tot[rows, cols] += both[:, TILE:]


def tile_backward(rows, keys, bias, q, k, v, dnx, dq, dk, dv):
    even, odd = halves()
    ones = corr_block()
    bias2 = jnp.concatenate([bias, bias], axis=1)
    for h in range(4):
        cols = pl.ds(TILE * h, TILE)
        qb = q[rows, cols]
        ks = stacked(k[keys, cols], even, odd)
        e = jnp.exp(mmt(qb, ks) + bias2)
        vs = jnp.concatenate([stacked(v[keys, cols], even, odd), ones], axis=1)
        flow = mmt(dnx[rows, pl.ds(2 * TILE * h, 2 * TILE)], vs)
        ds = (e * flow).astype(LOW)
        dq[rows, cols] += mm(ds, ks)
        dk[keys, cols] += fold(tmm(ds, qb))
        dv[keys, cols] += fold(tmm(e.astype(LOW), dnx[rows, pl.ds(2 * TILE * h, TILE)]))


def each(count, body):
    def step(i, carry):
        body(i)
        return carry
    if isinstance(count, int) and count <= 2:
        for i in range(count):
            body(i)
        return
    lax.fori_loop(0, count, step, 0, unroll=8 if isinstance(count, int) else 1)


def zero(ref, step=128):
    def body(i):
        rows = pl.ds(pl.multiple_of(i * step, step), step)
        ref[rows] = jnp.zeros((step,) + ref.shape[1:], ref.dtype)
    each(ref.shape[0] // step, body)


def columns(part, width=256):
    return pl.ds(pl.multiple_of(part * width, width), width)


def block(i, width=TILE):
    return pl.ds(pl.multiple_of(i * width, width), width)


def back_norm(u, gain, xh, r):
    gu = u * gain
    a = jnp.mean(gu, axis=1, keepdims=True)
    b = jnp.mean(gu * xh, axis=1, keepdims=True)
    return (gu - a - xh * b) * r


def out_back(g_b, weight_rows, num, tot, dnx):
    lane = lane_iota((TILE, TILE))
    same = jnp.where((lane < 64) == (row_iota((TILE, TILE)) < 64), 1.0, 0.0).astype(LOW)

    def body(n):
        up = mmt(g_b[...], weight_rows(n)).astype(LOW).astype(F32)
        for h in range(2):
            cols = pl.ds(pl.multiple_of(n * 256 + h * TILE, TILE), TILE)
            wide = lambda k: pl.ds(pl.multiple_of(n * 512 + h * 256 + k * TILE, TILE), TILE)
            d = up[:, h * TILE:(h + 1) * TILE]
            t = tot[:, cols]
            dnx[:, wide(0)] = (d / t).astype(LOW)
            p = d * num[:, cols]
            p1 = p.astype(LOW)
            p2 = (p - p1.astype(F32)).astype(LOW)
            corr = -(mm(p1, same) + mm(p2, same)) / t
            c1 = corr.astype(LOW)
            c2 = (corr - c1.astype(F32)).astype(LOW)
            place = lane_iota(c1.shape) % 64
            nothing = jnp.zeros_like(c1)
            dnx[:, wide(1)] = jnp.where(place == 0, c1, jnp.where(place == 1, c2, nothing))
    each(2, body)


def divide(num, tot, out, rows_all):
    def body(i):
        r = block(i, 64)
        o = num[r] / tot[r]
        num[r] = o
        out[r] = o.astype(LOW)
    each(rows_all // 64, body)


def normalize(y):
    mean = jnp.mean(y, axis=1, keepdims=True)
    centre = y - mean
    r = lax.rsqrt(jnp.mean(centre * centre, axis=1, keepdims=True) + EPS)
    return centre * r, r


def compute_kernel(lens_ref, spans_ref, offs_ref, out_grad, memory, gathered, after_ref, low_ref, gains_ref,
                   layer_out, grads, mem_grads, dpre_out, ng_out, *scratch):
    (w, w2, og, mem, qc, kc, vc, big, act, dhid, dv, num_c, tot_c, xh2, t1, dpre, dq, rs2,
     oc_b, a_b, c_b, g_b, dnx, ng, gb, lout, low_c, high_c, memc, sel, idx,
     starts, packed, in_sem, w_sem, out_sem) = scratch
    n_src = mem.shape[0]
    rows_all = og.shape[0]
    n_sent = starts.shape[0] - 1
    member = lax.axis_index("mem")
    base = member * n_sent

    loads = {}

    def load(name, src, dst, sem):
        loads[name] = pltpu.make_async_copy(src, dst, sem)
        loads[name].start()

    def load_slab(i, count=1):
        lanes = pl.ds(NORM + SLAB * i, SLAB * count)
        load(i, gathered.at[:, :, lanes], w.at[:, :, lanes], w_sem.at[i])

    load("a", low_ref, a_b, in_sem.at[0])
    load_slab(4)
    load("mem", memory, mem, in_sem.at[1])
    load_slab(5)
    load_slab(6)

    def load_rest():
        load("t1", after_ref, t1, in_sem.at[3])
        load("gb", gains_ref, gb, in_sem.at[4])
        load_slab(7)
        load_slab(8, 4)
        for k in range(4):
            load(("w2", k), gathered.at[:, :, pl.ds(CUT + SLAB * k, SLAB)], w2.at[:, k], w_sem.at[13 + k])
        load("og", out_grad, og, in_sem.at[2])

    outs = []

    def send(src, dst):
        copy = pltpu.make_async_copy(src, dst, out_sem.at[len(outs)])
        copy.start()
        outs.append(copy)

    def weight(i, part=None, width=256):
        if part is None:
            return w[:, :, pl.ds(NORM + SLAB * i, SLAB)].reshape(SLAB, SLAB)
        start = pl.multiple_of(NORM + SLAB * i + part * width, TILE)
        return w[:, :, pl.ds(start, width)].reshape(SLAB, width)

    def weight_rows(i, part, width=256, lanes=SLAB):
        devs = pl.ds(pl.multiple_of(part * (width // ROWS), width // ROWS), width // ROWS)
        return w[devs, :, pl.ds(NORM + SLAB * i, lanes)].reshape(width, lanes)

    def put_weight(i, part, value, width=256):
        start = pl.multiple_of(NORM + SLAB * i + part * width, TILE)
        w[:, :, pl.ds(start, width)] = value.astype(LOW).reshape(DEV, ROWS, width)

    def count(j, at):
        starts[j] = at
        return at + lens_ref[0, base + j]
    starts[n_sent] = lax.fori_loop(0, n_sent, count, jnp.int32(0))

    def count_packed(j, at):
        packed[j] = at
        return at + spans_ref[0, base + j]
    n_keys = lax.fori_loop(0, n_sent, count_packed, jnp.int32(0))
    packed[n_sent] = n_keys
    chunks = (n_keys + CHUNK - 1) // CHUNK

    def lows(i):
        row = i * TILE + row_iota((TILE, TILE))
        nothing = jnp.zeros((TILE, TILE), jnp.int32)

        def pick(j, found):
            here_on = row >= starts[j]
            values = (packed[j], packed[j + 1])
            return tuple(jnp.where(here_on, v, f) for v, f in zip(values, found))
        low_c[block(i)], high_c[block(i)] = lax.fori_loop(0, n_sent, pick, (nothing, nothing))
    each(rows_all // TILE, lows)
    zero(num_c)
    zero(tot_c)
    ng[...] = jnp.zeros_like(ng)

    def last_at(table, row):
        def pick(j, found):
            return jnp.where(starts[j] <= row, table(j), found)
        return lax.fori_loop(0, n_sent, pick, jnp.int32(0))

    def tiles(body, bias, first, last):
        def outer(i, carry):
            def inner(kt, carry):
                body(block(i, RC), block(kt), bias(i, kt))
                return carry
            return lax.fori_loop(first(i) // TILE, (last(i) - 1) // TILE + 1, inner, carry)
        lax.fori_loop(0, rows_all // RC, outer, 0)

    def cross_tiles(body):
        def bias(i, kt):
            key = kt * TILE + lane_iota((RC, TILE))
            r = block(i, RC)
            return jnp.where((key >= low_c[r]) & (key < high_c[r]), 0.0, HIDE)
        tiles(body, bias, lambda i: last_at(lambda j: packed[j], i * RC),
              lambda i: last_at(lambda j: packed[j + 1], (i + 1) * RC - 1))

    loads["a"].wait()
    loads[4].wait()

    def query(n):
        qc[:, columns(n)] = mm(a_b[...], weight(4, n)).astype(LOW) * jnp.asarray(0.125, LOW)
    each(2, query)
    load_rest()
    for name in ("mem", 5, 6):
        loads[name].wait()

    def choose(ct):
        r = block(ct, CHUNK)
        for g in range(n_src // TILE):
            hit = idx[r] == g * TILE + lane_iota((CHUNK, TILE))
            sel[:, g * TILE:(g + 1) * TILE] = jnp.where(hit, 1.0, 0.0).astype(LOW)

    def keys(ct):
        r = block(ct, CHUNK)
        key = ct * CHUNK + row_iota((CHUNK, TILE))

        def pick(j, found):
            return jnp.where(key >= packed[j], offs_ref[0, base + j] - packed[j] + key, found)
        at = lax.fori_loop(0, n_sent, pick, jnp.zeros((CHUNK, TILE), jnp.int32))
        idx[r] = jnp.where(key < n_keys, at, -1)
        choose(ct)

        def bring(n):
            memc[r, columns(n)] = mm(sel[...], mem[:, columns(n)]).astype(LOW)
        each(2, bring)

        def project(n):
            kc[r, columns(n)] = mm(memc[r], weight(5, n)).astype(LOW)
            vc[r, columns(n)] = mm(memc[r], weight(6, n)).astype(LOW)
        each(2, project)
    each(chunks, keys)

    cross_tiles(lambda r, k, bias: tile_forward(r, k, bias, qc, kc, vc, num_c, tot_c))
    divide(num_c, tot_c, oc_b, rows_all)
    for name in (7, "t1", "gb"):
        loads[name].wait()

    def cross_out(n):
        t1[:, columns(n)] += mm(oc_b[...], weight(7, n))
    each(2, cross_out)

    def norm_cross(i):
        r = block(i, 64)
        xh, rs = normalize(t1[r])
        xh2[r] = xh
        rs2[r] = jnp.broadcast_to(rs, (64, TILE))
        after = xh * gb[2:3] + gb[3:4]
        t1[r] = after
        c_b[r] = after.astype(LOW)
    each(rows_all // 64, norm_cross)

    loads[8].wait()

    def hidden(n):
        v = mm(c_b[...], weight(8, n))
        sig = 1.0 / (1.0 + jnp.exp(-v))
        act[:, columns(n)] = (v * sig).astype(LOW)
        big[block(n // 2, SLAB), columns(n % 2)] = sig * (1.0 + v * (1.0 - sig))
    each(8, hidden)
    for k in range(4):
        loads[("w2", k)].wait()

    def ffn_out(n):
        cols = columns(n)
        t1[:, cols] += mm(act[...], w2[:, :, :, cols].reshape(4 * SLAB, 256))
    each(2, ffn_out)
    loads["og"].wait()

    def norm_ffn(i):
        r = block(i, 64)
        xh, rs = normalize(t1[r])
        gain = gb[4:5]
        lout[r] = (xh * gain + gb[5:6]).astype(LOW)
        u = og[r].astype(F32)
        ng[4:5] += jnp.sum(u * xh, axis=0, keepdims=True)
        ng[5:6] += jnp.sum(u, axis=0, keepdims=True)
        d = back_norm(u, gain, xh, rs)
        dpre[r] = d
        g_b[r] = d.astype(LOW)
    each(rows_all // 64, norm_ffn)
    send(lout, layer_out)

    def hidden_back(n):
        devs = pl.ds(pl.multiple_of(n * 4, 4), 4)
        part = mmt(g_b[...], w2[devs].reshape(256, SLAB))
        d = (part * big[block(n // 2, SLAB), columns(n % 2)]).astype(LOW)
        dhid[:, columns(n)] = d
        w2[devs] = tmm(act[:, columns(n)], g_b[...]).astype(LOW).reshape(4, 4, ROWS, SLAB)
    each(8, hidden_back)
    for k in range(4):
        send(w2.at[:, k], grads.at[:, :, pl.ds(CUT + SLAB * k, SLAB)])

    def input_back(n):
        dpre[:, columns(n)] += mmt(dhid[...], weight_rows(8, n, 256, 4 * SLAB))
    each(2, input_back)

    def first_grad(n):
        put_weight(8, n, tmm(c_b[...], dhid[:, columns(n)]))
    each(8, first_grad)
    lanes = pl.ds(NORM + SLAB * 8, 4 * SLAB)
    send(w.at[:, :, lanes], grads.at[:, :, lanes])

    def back_cross(i):
        r = block(i, 64)
        u, xh = dpre[r], xh2[r]
        ng[2:3] += jnp.sum(u * xh, axis=0, keepdims=True)
        ng[3:4] += jnp.sum(u, axis=0, keepdims=True)
        d = back_norm(u, gb[2:3], xh, rs2[r][:, :1])
        dpre[r] = d
        g_b[r] = d.astype(LOW)
    each(rows_all // 64, back_cross)

    out_back(g_b, lambda n: weight_rows(7, n), num_c, tot_c, dnx)

    def out_grad_store(n):
        put_weight(7, n, tmm(oc_b[...], g_b[:, columns(n)]))
    each(2, out_grad_store)

    def send_slab(i):
        lanes = pl.ds(NORM + SLAB * i, SLAB)
        send(w.at[:, :, lanes], grads.at[:, :, lanes])

    send_slab(7)
    zero(dq)

    def clear(ct):
        r = block(ct, CHUNK)
        big[r] = jnp.zeros((CHUNK, SLAB), F32)
        dv[r] = jnp.zeros((CHUNK, SLAB), F32)
    each(chunks, clear)
    cross_tiles(lambda r, k, bias: tile_backward(r, k, bias, qc, kc, vc, dnx, dq, big, dv))

    def scaled(src, dst, factor, step=64):
        def body(i):
            r = block(i, step)
            dst[r] = (src[r] * factor).astype(LOW)
        each(src.shape[0] // step, body)

    scaled(dq, qc, 0.125)

    def query_back(n):
        dpre[:, columns(n)] += mmt(qc[...], weight_rows(4, n))
    each(2, query_back)

    send(dpre, dpre_out)

    def query_grad(n):
        put_weight(4, n, tmm(a_b[...], qc[:, columns(n)]))
    each(2, query_grad)
    send_slab(4)

    zero(num_c)
    zero(tot_c)

    def memory_back(ct):
        r = block(ct, CHUNK)
        kc[r] = big[r].astype(LOW)
        vc[r] = dv[r].astype(LOW)

        def key_grad(n):
            cols = columns(n)
            num_c[:, cols] += tmm(memc[r], kc[r, cols])
            tot_c[:, cols] += tmm(memc[r], vc[r, cols])
        each(2, key_grad)

        def rows_grad(n):
            memc[r, columns(n)] = (
                mmt(kc[r], weight_rows(5, n)) + mmt(vc[r], weight_rows(6, n))).astype(LOW)
        each(2, rows_grad)
        choose(ct)

        def spread(n):
            rows = block(n, 256)
            found = tmm(sel[:, columns(n)], memc[r]).astype(LOW)
            mem[rows] = jnp.where(ct == 0, found, mem[rows] + found)
        each(n_src // 256, spread)
    each(chunks, memory_back)
    send(mem, mem_grads)

    def key_store(n):
        put_weight(5, n, num_c[:, columns(n)])
        put_weight(6, n, tot_c[:, columns(n)])
    each(2, key_store)
    send_slab(5)
    send_slab(6)

    send(ng, ng_out)
    for copy in outs:
        copy.wait()


def state_shapes(rows):
    full = lambda dtype, lanes=SLAB, n=rows: jax.ShapeDtypeStruct((n, lanes), dtype)
    return (
        full(F32),
        full(F32),
        full(F32, TILE),
        full(F32),
        full(F32),
        full(LOW),
        full(LOW),
        full(LOW),
        full(LOW),
        full(F32, SLAB, 8),
        full(F32, SLAB, 8),
        full(jnp.int32, TILE),
    )


def compute(lens, spans, offs, out_grad, memory, gathered, after, after_low, gains):
    rows, n_src = out_grad.shape[0], memory.shape[0]
    n_sent = 16
    n_keys = n_sent * 112
    any_space = pl.BlockSpec(memory_space=pl.ANY)
    smem = pl.BlockSpec(memory_space=pltpu.SMEM)
    dma = pltpu.SemaphoreType.DMA
    f32 = lambda *s: pltpu.VMEM(s, F32)
    low = lambda *s: pltpu.VMEM(s, LOW)
    return pl.pallas_call(
        compute_kernel,
        out_shape=(
            jax.ShapeDtypeStruct((rows, SLAB), LOW),
            jax.ShapeDtypeStruct((DEV, ROWS, LANES), LOW),
            jax.ShapeDtypeStruct((n_src, SLAB), LOW),
            jax.ShapeDtypeStruct((rows, SLAB), F32),
            jax.ShapeDtypeStruct((8, SLAB), F32),
        ),
        in_specs=[smem] * 3 + [any_space] * 6,
        out_specs=(any_space,) * 5,
        scratch_shapes=[
            low(DEV, ROWS, CUT),
            low(DEV, 4, ROWS, SLAB),
            low(rows, SLAB),
            low(n_src, SLAB),
            low(rows, SLAB),
            low(n_keys, SLAB),
            low(n_keys, SLAB),
            f32(4 * SLAB, SLAB),
            low(rows, 4 * SLAB),
            low(rows, 4 * SLAB),
            f32(n_keys, SLAB),
            f32(rows, SLAB),
            f32(rows, SLAB),
            f32(rows, SLAB),
            f32(rows, SLAB),
            f32(rows, SLAB),
            f32(rows, SLAB),
            f32(rows, TILE),
            low(rows, SLAB),
            low(rows, SLAB),
            low(rows, SLAB),
            low(rows, SLAB),
            low(rows, 2 * SLAB),
            f32(8, SLAB),
            f32(8, SLAB),
            low(rows, SLAB),
            pltpu.VMEM((rows, TILE), jnp.int32),
            pltpu.VMEM((rows, TILE), jnp.int32),
            low(n_keys, SLAB),
            low(CHUNK, n_src),
            pltpu.VMEM((n_keys, TILE), jnp.int32),
            pltpu.SMEM((n_sent + 1,), jnp.int32),
            pltpu.SMEM((n_sent + 1,), jnp.int32),
            dma((5,)),
            dma((17,)),
            dma((32,)),
        ],
        compiler_params=pltpu.CompilerParams(vmem_limit_bytes=60 << 20),
        name="compute",
    )(lens, spans, offs, out_grad, memory, gathered, after, after_low, gains)
def scatter_rounds(share=0.42):
    spans = []
    for at, tiles in ((33, 6), (39, 7), (46, 7), (17, 16), (0, 11), (11, 6)):
        split = at + max(1, round(tiles * share))
        spans.append((at * 128, split * 128, (at + tiles) * 128))
    return tuple(spans)


SCATTER_ROUNDS = scatter_rounds()
Z_FIRST = (53 * 128, 59 * 128, 65 * 128)
SELF_LANES = NORM + 4 * SLAB
SELF_ROUNDS = (4, 5)


def scatter_kernel(grads, mem_grads, gathered, target, *rest):
    state, (out_ref, mem_ref, target_ref), rest = rest[:12], rest[12:15], rest[15:]
    (acc, from_core, from_first, from_second, from_z, macc, mfrom_core, mfrom_y), rest = rest[:8], rest[8:]
    held, rest = rest[:12], rest[12:]
    (w, tgt, gs, dq, dk, dv, dnx, g_b, out, mem_out), rest = rest[:10], rest[10:]
    (target_grad, from_zc, from_fc, from_sc), rest = rest[:4], rest[4:]
    (out_sems, own_sems, mown_sem, state_sems, core_s, core_r, first_s, first_r,
     second_s, second_r, zs_s, zs_r, mem_s, mem_r, zc_s, zc_r, fc_s, fc_r, sc_s, sc_r) = rest
    dpre, xh1, rs1, num_s, tot_s, qs, ks, vs, o_b, gb, ng, low_s = held
    z, x, y, c = here()
    xp, yp, cp_ = device(z, 1 - x, y, c), device(z, x, 1 - y, c), device(z, x, y, 1 - c)
    zp = [device((z + k) % 4, x, y, c) for k in (1, 2, 3)]
    count = len(SCATTER_ROUNDS)
    core_sems, first_sems, second_sems = (core_s, core_r), (first_s, first_r), (second_s, second_r)
    z_sems, mem_sems = (zs_s, zs_r), (mem_s, mem_r)
    sent = []

    def go(copy):
        copy.start()
        sent.append(copy)

    def span(r, part=None):
        a, m, b = Z_FIRST if r == count else SCATTER_ROUNDS[r]
        return {None: (a, b - a), 0: (a, m - a), 1: (m, b - m)}[part]

    def own(r):
        a, n = span(r)
        return pltpu.make_async_copy(
            grads.at[:, :, :, c, :, pl.ds(a, n)], acc.at[:, :, :, :, pl.ds(a, n)], own_sems.at[r])

    def core(r):
        a, n = span(r)
        source = gs if r in SELF_ROUNDS else grads
        return remote(source.at[:, :, :, 1 - c, :, pl.ds(a, n)],
                      from_core.at[:, :, :, :, pl.ds(a, n)], core_sems, r, cp_)

    def first(r, part):
        lanes = pl.ds(*span(r, part))
        src = acc.at[:, :, 1 - y, :, lanes] if part == 0 else acc.at[:, 1 - x, :, :, lanes]
        return remote(src, from_first.at[:, :, :, lanes], first_sems, (r, part),
                      yp if part == 0 else xp)

    def second(r, part):
        lanes = pl.ds(*span(r, part))
        src = acc.at[:, 1 - x, y, :, lanes] if part == 0 else acc.at[:, x, 1 - y, :, lanes]
        return remote(src, from_second.at[:, :, lanes], second_sems, (r, part),
                      xp if part == 0 else yp)

    def along(r, k):
        lanes = pl.ds(*span(r))
        return remote(acc.at[(z + k + 1) % 4, x, y, :, lanes], from_z.at[k, :, lanes], z_sems,
                      (r, k), zp[k])

    mem_own = pltpu.make_async_copy(mem_grads.at[:, c], macc, mown_sem)
    mem_core = remote(mem_grads.at[:, 1 - c], mfrom_core, mem_sems, 0, cp_)
    mem_far = remote(macc.at[1 - y], mfrom_y, mem_sems, 1, yp)

    def bring(i, src, dst):
        copy = pltpu.make_async_copy(src, dst, state_sems.at[i])
        copy.start()
        return copy

    early = [r for r in range(count) if r not in SELF_ROUNDS]
    own(0).start()
    mem_own.start()
    for r in [count] + early[1:]:
        own(r).start()
    copies = [bring(i, src, dst) for i, (src, dst) in enumerate(zip(state, held))]
    copies.append(bring(12, gathered.at[:, :, pl.ds(NORM, 4 * SLAB)], w))
    copies.append(bring(13, target, tgt))
    greet([xp, yp, cp_] + zp)
    go(core(early[0]))
    go(mem_core)
    for r in [count] + early[1:]:
        go(core(r))

    def add_core(r):
        if r not in SELF_ROUNDS:
            own(r).wait()
        core(r).wait_recv()
        for part in (0, 1):
            lanes = pl.ds(*span(r, part))
            for theirs in (True, False):
                def body(zi, carry, part=part, lanes=lanes, theirs=theirs):
                    for o in (0, 1):
                        if part == 0:
                            xi, yi = o, (1 - y) if theirs else y
                        else:
                            xi, yi = (1 - x) if theirs else x, o
                        mine = gs[zi, xi, yi, c, :, lanes] if r in SELF_ROUNDS else acc[zi, xi, yi, :, lanes]
                        acc[zi, xi, yi, :, lanes] = mine + from_core[zi, xi, yi, :, lanes]
                    return carry
                lax.fori_loop(0, 4, body, 0)
                if theirs:
                    go(first(r, part))

    def add_first(r):
        for part in (0, 1):
            first(r, part).wait_recv()
            lanes = pl.ds(*span(r, part))
            for theirs in (True, False):
                def body(zi, carry, part=part, lanes=lanes, theirs=theirs):
                    if part == 0:
                        xi, yi = (1 - x) if theirs else x, y
                        slot = xi
                    else:
                        xi, yi = x, (1 - y) if theirs else y
                        slot = yi
                    acc[zi, xi, yi, :, lanes] = (
                        acc[zi, xi, yi, :, lanes] + from_first[zi, slot, :, lanes])
                    return carry
                lax.fori_loop(0, 4, body, 0)
                if theirs:
                    go(second(r, part))

    def add_second(r):
        for part in (0, 1):
            second(r, part).wait_recv()
            lanes = pl.ds(*span(r, part))

            def body(zi, carry, lanes=lanes):
                acc[zi, x, y, :, lanes] = acc[zi, x, y, :, lanes] + from_second[zi, :, lanes]
                return carry
            lax.fori_loop(0, 4, body, 0)
        for k in (1, 0, 2):
            go(along(r, k))

    def add_z(r):
        lanes = pl.ds(*span(r))
        total = acc[z, x, y, :, lanes].astype(jnp.float32)
        for k in (0, 2, 1):
            along(r, k).wait_recv()
            total = total + from_z[k, :, lanes].astype(jnp.float32)
        out[:, lanes] = total

    lanes_c = pl.ds(*span(count))
    cut_c = [pl.ds(*span(count, part)) for part in (0, 1)]
    width_c = [span(count, part)[1] for part in (0, 1)]

    def far_c(k):
        return remote(acc.at[(z + k + 1) % 4, :, :, :, lanes_c], from_zc.at[k], (zc_s, zc_r), k, zp[k])

    def first_c(part):
        src = acc.at[z, 1 - x, :, :, cut_c[0]] if part == 0 else acc.at[z, :, 1 - y, :, cut_c[1]]
        return remote(src, from_fc.at[part, :, :, pl.ds(0, width_c[part])], (fc_s, fc_r), part,
                      xp if part == 0 else yp)

    def second_c(part):
        src = acc.at[z, x, 1 - y, :, cut_c[0]] if part == 0 else acc.at[z, 1 - x, y, :, cut_c[1]]
        return remote(src, from_sc.at[part, :, pl.ds(0, width_c[part])], (sc_s, sc_r), part,
                      yp if part == 0 else xp)

    def add_core_c():
        own(count).wait()
        core(count).wait_recv()
        for k in (0, 2, 1, 3):
            zi = (z + k + 1) % 4
            for xi in (0, 1):
                for yi in (0, 1):
                    acc[zi, xi, yi, :, lanes_c] = (
                        acc[zi, xi, yi, :, lanes_c] + from_core[zi, xi, yi, :, lanes_c])
            if k < 3:
                go(far_c(k))

    def add_far_c():
        for k in (0, 2, 1):
            far_c(k).wait_recv()
        for xi in (0, 1):
            for yi in (0, 1):
                total = acc[z, xi, yi, :, lanes_c].astype(F32)
                for k in range(3):
                    total = total + from_zc[k, xi, yi].astype(F32)
                acc[z, xi, yi, :, lanes_c] = total.astype(LOW)
        for part in (0, 1):
            go(first_c(part))

    def add_first_c():
        for part in (0, 1):
            first_c(part).wait_recv()
            for o in (0, 1):
                xi, yi = (x, o) if part == 0 else (o, y)
                acc[z, xi, yi, :, cut_c[part]] = (
                    acc[z, xi, yi, :, cut_c[part]] + from_fc[part, o, :, pl.ds(0, width_c[part])])
            go(second_c(part))

    def end_c():
        for part in (0, 1):
            second_c(part).wait_recv()
            out[:, cut_c[part]] = (acc[z, x, y, :, cut_c[part]].astype(F32)
                                   + from_sc[part, :, pl.ds(0, width_c[part])].astype(F32))

    def memory_core():
        mem_own.wait()
        mem_core.wait_recv()
        for theirs in (True, False):
            side = (1 - y) if theirs else y

            def body(i, carry, side=side):
                rows = pl.ds(pl.multiple_of(i * 64, 64), 64)
                macc[side, rows] = macc[side, rows] + mfrom_core[side, rows]
                return carry
            lax.fori_loop(0, 8, body, 0)
            if theirs:
                go(mem_far)

    def memory_end():
        mem_far.wait_recv()

        def body(i, carry):
            rows = pl.ds(pl.multiple_of(i * 64, 64), 64)
            mem_out[rows] = macc[y, rows].astype(jnp.float32) + mfrom_y[rows].astype(jnp.float32)
            return carry
        lax.fori_loop(0, 8, body, 0)

    def weight_rows(i, part):
        devs = pl.ds(part * 16, 16)
        return w[devs, :, pl.ds(SLAB * i, SLAB)].reshape(256, SLAB)

    def put(i, n, value):
        gs[:, :, :, :, :, pl.ds(NORM + SLAB * i + 256 * n, 256)] = value.astype(LOW).reshape(4, 2, 2, 2, ROWS, 256)

    rows_all = tgt.shape[0]

    def norm_back(i):
        r = block(i, 64)
        u, xh = dpre[r], xh1[r]
        ng[0:1] += jnp.sum(u * xh, axis=0, keepdims=True)
        ng[1:2] += jnp.sum(u, axis=0, keepdims=True)
        d = back_norm(u, gb[0:1], xh, rs1[r][:, :1])
        dpre[r] = d
        g_b[r] = d.astype(LOW)

    def self_norm():
        for copy in copies:
            copy.wait()
        each(rows_all // 64, norm_back)

    def self_out():
        out_back(g_b, lambda n: weight_rows(3, n), num_s, tot_s, dnx)
        for n in (0, 1):
            put(3, n, tmm(o_b[...], g_b[:, pl.ds(256 * n, 256)]))
        for ref in (dq, dk, dv):
            zero(ref)

    def self_tiles(i, first, last):
        def inner(kt, carry):
            r = pl.ds(i * RC, RC)
            key = kt * TILE + lane_iota((RC, TILE))
            row = i * RC + row_iota((RC, TILE))
            bias = jnp.where((key >= low_s[r]) & (key <= row), 0.0, HIDE)
            tile_backward(r, block(kt), bias, qs, ks, vs, dnx, dq, dk, dv)
            return carry
        lax.fori_loop(first, last, inner, 0)

    def self_grads():
        def lower(i):
            r = block(i, 64)
            qs[r] = (dq[r] * 0.125).astype(LOW)
            ks[r] = dk[r].astype(LOW)
            vs[r] = dv[r].astype(LOW)
        each(rows_all // 64, lower)
        for i, src in ((0, qs), (1, ks), (2, vs)):
            for n in (0, 1):
                put(i, n, tmm(tgt[...], src[:, pl.ds(256 * n, 256)]))
        inside = lane_iota((8, TILE)) < ROWS
        for d in range(DEV):
            one = ng[:, pl.ds(TILE * (d // 8), TILE)]
            one = pltpu.roll(one, (TILE - ROWS * (d % 8)) % TILE, 1) if d % 8 else one
            one = jnp.concatenate([jnp.where(inside, one, 0.0), jnp.zeros((8, TILE), F32)], axis=0)
            gs[d // 8, d // 4 % 2, d // 2 % 2, d % 2, :, pl.ds(0, NORM)] = one.astype(LOW)
        for r in SELF_ROUNDS:
            go(core(r))

    def self_target():
        for n in (0, 1):
            total = mmt(qs[...], weight_rows(0, n)) + mmt(ks[...], weight_rows(1, n))
            cols = pl.ds(256 * n, 256)
            target_grad[:, cols] = dpre[:, cols] + total + mmt(vs[...], weight_rows(2, n))

    add_core(0)
    memory_core()
    add_core_c()
    add_core(1)
    self_norm()
    add_first(0)
    add_core(2)
    self_out()
    add_second(0)
    add_first(1)
    add_core(3)
    self_tiles(0, 0, 2)
    add_second(1)
    add_first(2)
    self_tiles(0, 2, 4)
    add_z(0)
    add_second(2)
    add_first(3)
    add_far_c()
    self_grads()
    add_core(4)
    add_core(5)
    self_target()
    to_target = pltpu.make_async_copy(target_grad, target_ref, out_sems.at[0])
    to_target.start()
    add_first_c()
    memory_end()
    to_memory = pltpu.make_async_copy(mem_out, mem_ref, out_sems.at[1])
    to_memory.start()
    add_z(1)
    add_second(3)
    add_first(4)
    add_first(5)
    add_z(2)
    add_second(4)
    add_z(3)
    end_c()
    add_second(5)
    add_z(4)
    add_z(5)
    to_rows = pltpu.make_async_copy(out, out_ref, out_sems.at[2])
    to_rows.start()
    for copy in (to_target, to_memory, to_rows):
        copy.wait()
    for copy in sent:
        copy.wait_send()


def scatter_all(grads, mem_grads, gathered, target, state):
    any_space = pl.BlockSpec(memory_space=pl.ANY)
    dma = pltpu.SemaphoreType.DMA
    n = len(SCATTER_ROUNDS)
    rows = mem_grads.shape[2]
    wide = Z_FIRST[2] - Z_FIRST[0]
    low = lambda *s: pltpu.VMEM(s, LOW)
    f32 = lambda *s: pltpu.VMEM(s, F32)
    return pl.pallas_call(
        scatter_kernel,
        out_shape=(
            jax.ShapeDtypeStruct((ROWS, LANES), F32),
            jax.ShapeDtypeStruct((rows, SLAB), F32),
            jax.ShapeDtypeStruct((rows, SLAB), F32),
        ),
        in_specs=[any_space] * 16,
        out_specs=(any_space,) * 3,
        scratch_shapes=[
            low(4, 2, 2, ROWS, LANES),
            low(4, 2, 2, ROWS, LANES),
            low(4, 2, ROWS, LANES),
            low(4, ROWS, LANES),
            low(3, ROWS, LANES),
            low(2, rows, SLAB),
            low(2, rows, SLAB),
            low(rows, SLAB),
        ]
        + [pltpu.VMEM(s.shape, s.dtype) for s in state_shapes(rows)]
        + [
            low(32, ROWS, 4 * SLAB),
            low(rows, SLAB),
            low(4, 2, 2, 2, ROWS, SELF_LANES),
            f32(rows, SLAB),
            f32(rows, SLAB),
            f32(rows, SLAB),
            low(rows, 2 * SLAB),
            low(rows, SLAB),
            f32(ROWS, LANES),
            f32(rows, SLAB),
            f32(rows, SLAB),
            low(3, 2, 2, ROWS, wide),
            low(2, 2, ROWS, wide),
            low(2, ROWS, wide),
            dma((3,)),
            dma((n + 1,)),
            dma(()),
            dma((14,)),
            dma((n + 1,)),
            dma((n + 1,)),
            dma((n, 2)),
            dma((n, 2)),
            dma((n, 2)),
            dma((n, 2)),
            dma((n, 3)),
            dma((n, 3)),
            dma((2,)),
            dma((2,)),
            dma((3,)),
            dma((3,)),
            dma((2,)),
            dma((2,)),
            dma((2,)),
            dma((2,)),
        ],
        compiler_params=pltpu.CompilerParams(
            collective_id=2, has_side_effects=True, vmem_limit_bytes=56 << 20),
        name="scatter",
    )(grads, mem_grads, gathered, target, *state)


def finish_kernel(rows_ref, mem_ref, target_ref, *rest):
    outs, (rows, mem, target, in_sems, out_sems) = rest[:18], rest[18:]
    copies = []
    loads = []
    half = target.shape[0] // 2
    pieces = [pl.ds(0, half), pl.ds(half, half)]
    cuts_ = [(NORM + SLAB * i, SLAB) for i in range(8)] + [(NORM + SLAB * 8, 4 * SLAB)]
    cuts_ += [(NORM + SLAB * (12 + k), SLAB) for k in range(4)]

    def load(src, dst):
        copy = pltpu.make_async_copy(src, dst, in_sems.at[len(loads)])
        copy.start()
        loads.append(copy)

    def bring(src, dst):
        copy = pltpu.make_async_copy(src, dst, out_sems.at[len(copies)])
        copy.start()
        copies.append(copy)

    for p in pieces:
        load(target_ref.at[p], target.at[p])
        load(mem_ref.at[p], mem.at[p])
    load(rows_ref, rows)
    for i, p in enumerate(pieces):
        loads[2 * i].wait()
        bring(target.at[p], outs[0].at[p])
        loads[2 * i + 1].wait()
        bring(mem.at[p], outs[1].at[p])
    loads[4].wait()
    for i, (start, width) in enumerate(cuts_):
        dst = outs[2 + i] if i < 9 else outs[11].at[pl.ds(ROWS * (i - 9), ROWS)]
        bring(rows.at[:, pl.ds(start, width)], dst)
    for i in range(6):
        outs[12 + i][...] = rows[i, pl.ds(0, ROWS)]
    for copy in copies:
        copy.wait()


def finish(rows, mem, target):
    any_space = pl.BlockSpec(memory_space=pl.ANY)
    shape = lambda *s: jax.ShapeDtypeStruct(s, F32)
    return pl.pallas_call(
        finish_kernel,
        out_shape=(shape(*target.shape), shape(*mem.shape))
        + (shape(ROWS, SLAB),) * 8
        + (shape(ROWS, 4 * SLAB), shape(4 * ROWS, SLAB))
        + (shape(ROWS),) * 6,
        in_specs=[any_space] * 3,
        out_specs=(any_space,) * 12 + (pl.BlockSpec(memory_space=pltpu.VMEM),) * 6,
        scratch_shapes=[
            pltpu.VMEM(rows.shape, F32),
            pltpu.VMEM(mem.shape, F32),
            pltpu.VMEM(target.shape, F32),
            pltpu.SemaphoreType.DMA((5,)),
            pltpu.SemaphoreType.DMA((17,)),
        ],
        name="finish",
    )(rows, mem, target)


def local(target_in, memory, out_grad, *rest):
    fast = two_by_two((lax.axis_size("dp"), lax.axis_size("mem")))
    if not fast:
        return plain(target_in, memory, out_grad, *rest)
    weights, tables = rest[:16], rest[16:]
    gathered, all_memory, saved = gather_all(
        weights[:10], weights[10:], memory, tables[0], target_in
    )
    after, after_low, xh1, rs1, num, tot, q, k, v, o, gains, low_s = saved
    layer_out, grads, mem_grads, d_after, norm_grads = compute(
        *tables, out_grad, all_memory, gathered, after, after_low, gains
    )
    state = (d_after, xh1, rs1, num, tot, q, k, v, o, gains, norm_grads, low_s)
    rows = target_in.shape[0]
    out, mem_out, target_grad = scatter_all(
        grads.reshape(4, 2, 2, 2, ROWS, LANES),
        mem_grads.reshape(2, 2, rows, SLAB),
        gathered,
        target_in,
        state,
    )
    return (layer_out,) + tuple(finish(out, mem_out, target_grad))


def solution(mesh):
    both = P(("dp", "mem"), None)
    flat = P(("dp", "mem"))
    in_specs = (both,) * 13 + (flat,) * 6 + (P("dp", None),) * 3
    out_specs = (both,) * 13 + (flat,) * 6
    return jax.shard_map(local, mesh=mesh, in_specs=in_specs, out_specs=out_specs, check_vma=False)
```
